32 devices in a mesh: dp: 8 (over z, core), expert: 4 (over y, x).
Axes of the slice: x: 2, y: 2, z: 4, core: 2. Of those that a mesh axis runs over, the one named last changes fastest.
Arguments:
- tokens: bfloat16 [8192, 1024], P(('dp', 'expert')), may hold values from -6 to 6
- cotangent: bfloat16 [8192, 1024], P(('dp', 'expert')), may hold values from -6 to 6
- qkv_weight: bfloat16 [1024, 3072], P(('dp', 'expert')), may hold values from -0.1875 to 0.1875
- out_weight: bfloat16 [1024, 1024], P(('dp', 'expert')), may hold values from -0.75 to 0.75
- router_weight: bfloat16 [1024, 4], P(('dp', 'expert')), may hold values from -0.1875 to 0.1875
- first_gain: bfloat16 [1024], P(('dp', 'expert')), may hold values from 0.5 to 1.5
- second_gain: bfloat16 [1024], P(('dp', 'expert')), may hold values from 0.5 to 1.5
- bias_table: bfloat16 [512], P(('dp', 'expert')), may hold values from -4 to 4
- gate_weight: bfloat16 [4, 1024, 2816], P('expert', 'dp'), may hold values from -0.1875 to 0.1875
- up_weight: bfloat16 [4, 1024, 2816], P('expert', 'dp'), may hold values from -0.1875 to 0.1875
- down_weight: bfloat16 [4, 2816, 1024], P('expert', 'dp'), may hold values from -0.109375 to 0.109375
- lengths: int32 [8, 4], P('dp', 'expert'), may hold values from 1 to 256, 768 in all within a row
- routes: int32 [8192, 2], P(('dp', 'expert')), may hold values from 0 to 3, all different within a row; in each aligned block of 256 rows (0 to 255, 256 to 511, ...) at most 256 rows name the same one
- priority: int32 [8, 1024], P('dp', 'expert'), may hold values from 0 to 1023, each once within a row
Outputs:
- output: bfloat16 [8192, 1024], P(('dp', 'expert'))
- grad_tokens: float32 [8192, 1024], P(('dp', 'expert'))
- grad_qkv_weight: float32 [1024, 3072], P(('dp', 'expert'))
- output_weight_gradient: float32 [1024, 1024], P(('dp', 'expert'))
- grad_router_weight: float32 [1024, 4], P(('dp', 'expert'))
- grad_first_gain: float32 [1024], P(('dp', 'expert'))
- grad_second_gain: float32 [1024], P(('dp', 'expert'))
- grad_bias_table: float32 [512], P(('dp', 'expert'))
- grad_gate_weight: float32 [4, 1024, 2816], P('expert', 'dp')
- grad_up_weight: float32 [4, 1024, 2816], P('expert', 'dp')
- grad_down_weight: float32 [4, 2816, 1024], P('expert', 'dp')
The draws below stay inside these ranges and needn't reach their ends.
Inputs may be any that keep to these rules, and one draw needn't show every extreme that they name: The lengths of the 4 sequences of one group sum to 768, and one of them is 256. `routes`: A slot's two experts differ. Among the 256 slots of one device no expert is named more than 256 times; on some device one expert is named exactly 256 times. `priority`: each row is a permutation.
All inputs are finite; a program needn't handle non-finite values.
Results may differ from the reference program's by a relative error of at most 0.02.
Values may be sent and summed in bfloat16 or wider, within the bound.
A program may use at most 192 MiB of HBM per device.

```python
import math
import jax
import jax.numpy as jnp
import numpy as np
from jax import lax

D = 1024
HEADS = 16
HD = 64
FF = 2816
BUCKETS = 32
SEQ = 256
EXPERTS = 4
TOKENS = 8192
GROUP_TOKENS = 1024
CAP = 480
SLOT = 256
N_DP = 8
N_EXPERT = 4


def level_of(stream_key, dims, shards, low, largest):
    loudness = 1.0
    for position, blocks in shards:
        draws = jax.random.uniform(jax.random.fold_in(jax.random.fold_in(stream_key, 6), position), (blocks,), jnp.float32, low / len(shards), largest / len(shards))
        loudness = loudness * jnp.repeat(jnp.exp(draws), dims[position] // blocks).reshape((-1,) + (1,) * (len(dims) - 1 - position))
    return loudness


def split_up(count, total, reach, lean):
    loads = [(1 << 20) // math.isqrt(standing ** lean) + 1 for standing in range(2, count + 1)]
    surplus, given = total - reach - (count - 1), [1] * (count - 1)
    while surplus > 0:
        movable = [i for i in range(count - 1) if given[i] < reach]
        pool, left = sum([loads[i] for i in movable]), surplus
        for i in movable:
            extra = min(reach - given[i], max(1, left * loads[i] // pool), surplus)
            given[i] = given[i] + extra
            surplus = surplus - extra
    return np.array([reach] + given)


def uneven_parts(own_key, count, total, most, lean):
    if count == 2:
        one = jax.random.randint(own_key, (), max(1, total - most), min(most, total - 1) + 1)
        return jnp.stack([one, total - one])
    sizes = jnp.asarray(split_up(count, total, most, lean), jnp.int32)
    couples = (count - 1) // 2
    donor, receiver = sizes[1:1 + 2 * couples:2], sizes[2:2 + 2 * couples:2]
    room = jnp.minimum(donor - 1, most - receiver)
    passed = jax.random.randint(jax.random.fold_in(own_key, 1), (couples,), 0, 1 << 20) % (room + 1)
    sizes = sizes.at[1:1 + 2 * couples:2].set(donor - passed).at[2:2 + 2 * couples:2].set(receiver + passed)
    return sizes[jax.random.permutation(jax.random.fold_in(own_key, 2), count)]


def assign_block(stream_key, own, number, rows, count, top, reach, skew):
    order = jax.random.permutation(stream_key, count)
    packed, common = portions_of(count, rows * top, reach, skew, True), portions_of(count, rows * top, reach, skew, False)
    places = jnp.arange(count)

    def named(sizes, turn):
        used = int((sizes > 0).sum())
        fixed = max(1, used // 4)
        passed = fixed + (places - fixed + turn * (used - fixed)) % max(1, count - fixed)
        return jnp.zeros((count,), jnp.int32).at[order[jnp.where(places < fixed, places, passed)]].set(jnp.asarray(sizes, jnp.int32))

    sizes = jnp.where(number % 4 == 0, named(packed, number // 4), named(common, number - number // 4 - 1))
    mixed = jax.random.permutation(jax.random.fold_in(own, 3), count)
    donor, taker = mixed[0:count // 2 * 2:2], mixed[1:count // 2 * 2:2]
    margin = jnp.minimum(sizes[donor] - 1, reach - sizes[taker]) // 2
    margin = jnp.where((donor == order[0]) | (taker == order[0]) | (sizes[taker] == 0), 0, jnp.maximum(margin, 0))
    passed = jax.random.randint(jax.random.fold_in(own, 4), (count // 2,), 0, 1 << 20) % (margin + 1)
    sizes = sizes.at[donor].add(-passed).at[taker].add(passed)
    members = jnp.searchsorted(jnp.cumsum(sizes), jnp.arange(rows * top), side="right").astype(jnp.int32)
    table = members.reshape(top, rows).T
    table = table[jax.random.permutation(jax.random.fold_in(own, 1), rows)]
    turn = jax.random.randint(jax.random.fold_in(own, 2), (rows, 1), 0, top)
    return jnp.take_along_axis(table, (jnp.arange(top)[None, :] + turn) % top, axis=1)


def portions_of(amount, total, bound, slope, full):
    portions = [(1 << 20) // math.isqrt(grade ** slope) + 1 for grade in range(1, amount + 1)]
    largest = bound if full else min(bound, max(-(-total // amount), total * portions[0] // sum(portions)))
    least = 1 if total - largest >= amount - 1 else 0
    given, rest = [largest] + [least] * (amount - 1), total - largest - least * (amount - 1)
    while rest > 0:
        free = [i for i in range(1, amount) if given[i] < largest] or [i for i in range(1, amount) if given[i] < bound]
        whole, budget = sum([portions[i] for i in free]), rest
        for i in free:
            extra = min(bound - given[i], max(1, budget * portions[i] // whole), rest)
            given[i] = given[i] + extra
            rest = rest - extra
    return np.array(given)


def normal_values(stream_key, shape, spread, reach, cuts=(), kind=jnp.bfloat16):
    loudness = level_of(stream_key, shape, cuts, -0.22, 0.18) if cuts else 1.0
    array = jax.random.normal(stream_key, shape, jnp.float32) * spread * loudness
    return jnp.minimum(jnp.maximum(array, -reach), reach).astype(kind)


def setup_inputs(seed: int = 0) -> dict:
    keys = jax.random.split(jax.random.key(seed), 15)
    tokens = normal_values(keys[0], (TOKENS, D), 1.0, 6.0, ((0, 32),))
    cotangent = normal_values(keys[1], (TOKENS, D), 1.0, 6.0, ((0, 32),))
    qkv_weight = normal_values(keys[2], (D, 3 * D), D ** -0.5, 0.1875, ((0, 32),))
    out_weight = normal_values(keys[3], (D, D), (D // 16) ** -0.5, 0.75, ((0, 32),))
    router_weight = normal_values(keys[4], (D, EXPERTS), D ** -0.5, 0.1875, ((0, 32),))
    first_gain = jnp.clip(1.0 + 0.1 * jax.random.normal(keys[5], (D,), jnp.float32), 0.5, 1.5).astype(jnp.bfloat16)
    second_gain = jnp.clip(1.0 + 0.1 * jax.random.normal(keys[6], (D,), jnp.float32), 0.5, 1.5).astype(jnp.bfloat16)
    bias_table = normal_values(keys[7], (HEADS * BUCKETS,), 1.0, 4.0, ((0, 32),))
    gate_weight = normal_values(keys[8], (EXPERTS, D, FF), D ** -0.5, 0.1875, ((0, 4), (1, 8)))
    up_weight = normal_values(keys[9], (EXPERTS, D, FF), D ** -0.5, 0.1875, ((0, 4), (1, 8)))
    down_weight = normal_values(keys[10], (EXPERTS, FF, D), FF ** -0.5, 0.109375, ((0, 4), (1, 8)))
    lengths = jax.vmap(lambda own: uneven_parts(own, N_EXPERT, 3 * SEQ * N_EXPERT // 4, SEQ, 0))(jax.random.split(keys[11], N_DP)).reshape((N_DP, N_EXPERT)).astype(jnp.int32)
    routes_keys = jax.random.split(jax.random.fold_in(keys[12], 1), TOKENS // SEQ)
    routes_turns = jax.random.permutation(jax.random.fold_in(keys[12], 3), TOKENS // SEQ)
    routes = jax.vmap(lambda own, number: assign_block(jax.random.fold_in(keys[12], 2), own, number, SEQ, EXPERTS, 2, SLOT, 2))(routes_keys, routes_turns).reshape((TOKENS, 2))
    priority = jax.vmap(lambda own: jax.random.permutation(own, GROUP_TOKENS))(jax.random.split(keys[13], N_DP)).reshape((N_DP, GROUP_TOKENS)).astype(jnp.int32)
    return dict(tokens=tokens, cotangent=cotangent, qkv_weight=qkv_weight, out_weight=out_weight, router_weight=router_weight, first_gain=first_gain, second_gain=second_gain, bias_table=bias_table, gate_weight=gate_weight, up_weight=up_weight, down_weight=down_weight, lengths=lengths, routes=routes, priority=priority)


epsilon = 1e-06
masked_value = -1e+30
max_distance = 128.0
largest_value = lax.Precision.HIGHEST

@jax.custom_vjp
def low(v):
    return lax.optimization_barrier(v.astype(jnp.bfloat16)).astype(jnp.float32)

@jax.custom_vjp
def low_back(v):
    return v

def low_keep(v):
    return (low(v), None)

def low_pass(kept, grad):
    return (grad,)

def back_keep(v):
    return (v, None)

def back_low(kept, grad):
    return (low(grad),)
low.defvjp(low_keep, low_pass)
low_back.defvjp(back_keep, back_low)

def rounded(value_in):
    return low(low_back(value_in))

def bucket_table(seq_slots, bucket_count):
    halfway = bucket_count // 2
    exact_span = bucket_count // 4
    offset = np.arange(seq_slots)[:, None] - np.arange(seq_slots)[None, :]
    distance = np.abs(offset)
    log_part = np.log(np.maximum(distance, 1) / float(exact_span)) / np.log(max_distance / exact_span)
    far_bucket = np.minimum(exact_span + np.floor(log_part * exact_span).astype(np.int64), halfway - 1)
    inside = np.where(distance < exact_span, distance, far_bucket)
    return (np.where(offset < 0, halfway, 0) + inside).astype(np.int32)

def expert_assignment(group_routes, group_rank, group_lengths):
    group_tokens = group_routes.shape[0]
    group_slot = jnp.arange(group_tokens, dtype=jnp.int32) % SEQ
    group_valid = group_slot < jnp.repeat(group_lengths, SEQ)
    inverse = jnp.zeros((group_tokens,), jnp.int32).at[group_rank].set(jnp.arange(group_tokens, dtype=jnp.int32))
    order_routes = jnp.concatenate([group_routes[inverse, 0], group_routes[inverse, 1]])
    order_valid = jnp.concatenate([group_valid[inverse], group_valid[inverse]])
    expert_range = jnp.arange(EXPERTS, dtype=jnp.int32)
    order_onehot = ((order_routes[:, None] == expert_range[None, :]) & order_valid[:, None]).astype(jnp.int32)
    earlier = jnp.cumsum(order_onehot, axis=0) - order_onehot
    order_pos = lax.optimization_barrier(jnp.sum(earlier * order_onehot, axis=1))
    positions = jnp.stack([order_pos[group_rank], order_pos[group_tokens + group_rank]], axis=1)
    kept_mask = group_valid[:, None] & (positions < CAP)
    target = jnp.where(kept_mask, group_routes * CAP + positions, EXPERTS * CAP).astype(jnp.int32)
    owners = jnp.repeat(jnp.arange(group_tokens, dtype=jnp.int32), 2)
    token_of = jnp.full((EXPERTS * CAP,), group_tokens, jnp.int32).at[target.reshape(-1)].set(owners, mode='drop')
    return (target, kept_mask, token_of)

def reference(tokens, cotangent, qkv_weight, out_weight, router_weight, first_gain, second_gain, bias_table, gate_weight, up_weight, down_weight, lengths, routes, priority):
    sequence_count = N_DP * N_EXPERT
    group_tokens = N_EXPERT * SEQ
    valid_mask = jnp.arange(TOKENS, dtype=jnp.int32) % SEQ < jnp.repeat(lengths.reshape(-1), SEQ)
    valid_float = valid_mask.astype(jnp.float32)
    target, kept_mask, token_of = jax.vmap(expert_assignment)(routes.reshape(N_DP, group_tokens, 2), priority, lengths)
    kept_float = kept_mask.astype(jnp.float32)
    indicator_matrix = jnp.asarray((bucket_table(SEQ, BUCKETS)[None, :, :] == np.arange(BUCKETS)[:, None, None]).astype(np.float32))
    picker = (routes[:, :, None] == jnp.arange(EXPERTS, dtype=jnp.int32)[None, None, :]).astype(jnp.float32)
    key_live = jnp.arange(SEQ, dtype=jnp.int32)[None, :] < lengths.reshape(-1)[:, None]
    score_scale = 1.0 / math.sqrt(HD)

    def forward(token_rows, qkv_matrix, out_matrix, router_matrix, first_scale, second_scale, bias_values, gate_matrix, up_matrix, down_matrix):
        per_head_bias = bias_values.reshape(HEADS, BUCKETS)
        position_bias_matrix = jnp.einsum('crd,wc->wrd', indicator_matrix, per_head_bias, precision=largest_value)

        def attend(pieces):
            seq_rows, live_keys = pieces
            inverse_rms = lax.rsqrt(lax.optimization_barrier(jnp.mean(seq_rows * seq_rows, axis=1, keepdims=True)) + epsilon)
            normed = low(seq_rows * inverse_rms * first_scale)
            qkv_rows = rounded(jnp.dot(normed, qkv_matrix, precision=largest_value))
            queries = qkv_rows[:, :D].reshape(SEQ, HEADS, HD)
            keys_all = qkv_rows[:, D:2 * D].reshape(SEQ, HEADS, HD)
            values_all = qkv_rows[:, 2 * D:].reshape(SEQ, HEADS, HD)
            scores = jnp.einsum('qhd,khd->hqk', queries, keys_all, precision=largest_value) * score_scale + position_bias_matrix
            scores = jnp.where(live_keys[None, None, :], low_back(scores), masked_value)
            attn_probs = low(jax.nn.softmax(scores, axis=2))
            attended = rounded(jnp.einsum('hqk,khd->qhd', attn_probs, values_all, precision=largest_value).reshape(SEQ, D))
            return seq_rows + low_back(jnp.dot(attended, out_matrix, precision=largest_value))
        residual = lax.map(jax.checkpoint(attend), (token_rows.reshape(sequence_count, SEQ, D), key_live)).reshape(TOKENS, D)
        inverse_two = lax.rsqrt(lax.optimization_barrier(jnp.mean(residual * residual, axis=1, keepdims=True)) + epsilon)
        normed_two = low(residual * inverse_two * second_scale)
        logits = jnp.dot(normed_two, router_matrix, precision=largest_value)
        chosen = jnp.einsum('se,sje->sj', logits, picker, precision=largest_value)
        gate_probs = jax.nn.softmax(chosen, axis=1)

        def experts(pieces):
            rows_group, gates_group, target_group, kept_group, token_group = pieces
            extended = jnp.concatenate([rows_group, jnp.zeros((1, D), rows_group.dtype)])
            buffer = low_back(extended[token_group].reshape(EXPERTS, CAP, D))
            gate_in = low_back(jnp.einsum('ecd,edf->ecf', buffer, gate_matrix, precision=largest_value))
            up_in = low_back(jnp.einsum('ecd,edf->ecf', buffer, up_matrix, precision=largest_value))
            hidden = low(jax.nn.gelu(gate_in, approximate=True) * up_in)
            expert_out = rounded(jnp.einsum('ecf,efd->ecd', hidden, down_matrix, precision=largest_value)).reshape(EXPERTS * CAP, D)
            out_extended = jnp.concatenate([expert_out, jnp.zeros((1, D), expert_out.dtype)])
            pair_out = out_extended[target_group]
            return lax.optimization_barrier(jnp.sum(pair_out * (kept_group * gates_group)[:, :, None], axis=1))
        expert_mix = lax.map(jax.checkpoint(experts), (normed_two.reshape(N_DP, group_tokens, D), gate_probs.reshape(N_DP, group_tokens, 2), target, kept_float, token_of)).reshape(TOKENS, D)
        return valid_float[:, None] * (residual + expert_mix)
    inputs = tuple((argument.astype(jnp.float32) for argument in (tokens, qkv_weight, out_weight, router_weight, first_gain, second_gain, bias_table, gate_weight, up_weight, down_weight)))
    output, pullback = jax.vjp(forward, *inputs)
    gradients = pullback(cotangent.astype(jnp.float32))
    return (output.astype(jnp.bfloat16), gradients[0], gradients[1], gradients[2], gradients[3], gradients[4], gradients[5], gradients[6], gradients[7], gradients[8], gradients[9])
```

```python
import functools
import math

import jax
import jax.numpy as jnp
import numpy as np
from jax import lax
from jax.experimental import pallas as pl
from jax.experimental.pallas import tpu as pltpu
from jax.sharding import PartitionSpec as P

HEADS = 16
HD = 64
BUCKETS = 32
CAP = 480
PAIRS = HEADS // 2
LANES = 2 * HD

epsilon = 1e-06
masked_value = -1e30
max_distance = 128.0
SCALE = 1.0 / math.sqrt(HD)
MB = 1 << 20
F32 = jnp.float32
BF16 = jnp.bfloat16


def bucket_of(offset, bucket_count):
    halfway = bucket_count // 2
    exact_span = bucket_count // 4
    distance = np.abs(offset)
    log_part = np.log(np.maximum(distance, 1) / float(exact_span)) / np.log(
        max_distance / exact_span
    )
    far_bucket = np.minimum(
        exact_span + np.floor(log_part * exact_span).astype(np.int64), halfway - 1
    )
    inside = np.where(distance < exact_span, distance, far_bucket)
    return np.where(offset < 0, halfway, 0) + inside


def diagonal_onehot(ahead):
    return (bucket_of(-ahead, BUCKETS)[None, :] == np.arange(BUCKETS)[:, None]).astype(np.float32)


def dot(a, b):
    return jnp.dot(a, b, preferred_element_type=F32)


def dot_nt(a, b):
    return lax.dot_general(a, b, (((1,), (1,)), ((), ())), preferred_element_type=F32)


def dot_tn(a, b):
    return lax.dot_general(a, b, (((0,), (0,)), ((), ())), preferred_element_type=F32)


def two_halves(value):
    high = value.astype(BF16)
    return high, (value - high.astype(F32)).astype(BF16)


def columns(index, width):
    return pl.ds(pl.multiple_of(index * width, width), width)


VMEM_SPEC = pl.BlockSpec(memory_space=pltpu.VMEM)


ANY_SPEC = pl.BlockSpec(memory_space=pl.ANY)
MESH = pl.DeviceIdType.MESH
DMA = pltpu.SemaphoreType.DMA


def call(kernel, out_shape, scratch, vmem, flops, *args, stay=(), land=(), link=None):
    nbytes = sum(a.size * a.dtype.itemsize for a in args)
    params = dict(vmem_limit_bytes=vmem)
    if link is not None:
        params.update(collective_id=link, has_side_effects=True)
    return pl.pallas_call(
        kernel,
        out_shape=out_shape,
        in_specs=[ANY_SPEC if i in stay else VMEM_SPEC for i in range(len(args))],
        out_specs=tuple(ANY_SPEC if i in land else VMEM_SPEC for i in range(len(out_shape))),
        scratch_shapes=scratch,
        compiler_params=pltpu.CompilerParams(**params),
        cost_estimate=pl.CostEstimate(flops=flops, bytes_accessed=nbytes, transcendentals=0),
    )(*args)


def here():
    d, e = lax.axis_index("dp"), lax.axis_index("expert")
    return d, e, d // 2, lax.rem(d, 2)


def flipped(value, bits):
    low, high = lax.rem(value, 2), value // 2
    low = 1 - low if bits & 1 else low
    high = 1 - high if bits & 2 else high
    return 2 * high + low


def meet(partners):
    barrier = pltpu.get_barrier_semaphore()
    for partner in partners:
        pl.semaphore_signal(barrier, inc=1, device_id=partner, device_id_type=MESH)
    pl.semaphore_wait(barrier, len(partners))


def push(src, dst, send, recv, to):
    copy = pltpu.make_async_remote_copy(
        src_ref=src, dst_ref=dst, send_sem=send, recv_sem=recv, device_id=to, device_id_type=MESH
    )
    copy.start()
    return copy


def group(d, e):
    return [None] + [(d, flipped(e, q)) for q in (1, 2, 3)]


class Spread:
    def __init__(self, src, dst, send, recv, d, e):
        self.src, self.dst, self.send, self.recv = src, dst, send, recv
        self.to = group(d, e)
        self.half = src.shape[0] // 2
        self.copies = {}

    def part(self, ref, half):
        return ref.at[pl.ds(half * self.half, self.half)]

    def start(self):
        for turn in range(2):
            for q in (1, 2):
                half = turn if q == 1 else 1 - turn
                at = 2 * (q - 1) + half
                self.copies[q, half] = push(
                    self.part(self.src, half),
                    self.part(self.dst.at[q], half),
                    self.send.at[at],
                    self.recv.at[at],
                    self.to[q],
                )

    def forward(self):
        for q, half, across, at in ((1, 0, 2, 4), (2, 1, 1, 5)):
            self.copies[q, half].wait_recv()
            self.copies[3, half] = push(
                self.part(self.dst.at[q], half),
                self.part(self.dst.at[3], half),
                self.send.at[at],
                self.recv.at[at],
                self.to[across],
            )

    def finish(self):
        for q, half in ((1, 1), (2, 0), (3, 0), (3, 1)):
            self.copies[q, half].wait_recv()
        for copy in self.copies.values():
            copy.wait_send()


class Swap:
    def __init__(self, src, dst, send, recv, d, e):
        self.src, self.dst, self.send, self.recv = src, dst, send, recv
        self.to = group(d, e)
        self.copies = {}

    def start(self, q):
        self.copies[q] = push(
            self.src.at[q], self.dst.at[q], self.send.at[q], self.recv.at[q], self.to[q]
        )

    def finish(self):
        for copy in self.copies.values():
            copy.wait_recv()
        for copy in self.copies.values():
            copy.wait_send()


def gather_weights_kernel(own, full, local, send, recv):
    d, e, z, c = here()
    share = own.shape[0]
    other = 2 * z + 1 - c
    to_x, to_y, to_core = (d, flipped(e, 1)), (d, flipped(e, 2)), (other, e)
    to_z = [None] + [(2 * flipped(z, k) + c, e) for k in (1, 2, 3)]
    meet([to_x, to_y, to_core] + to_z[1:])

    def item(k, q):
        row = (2 * flipped(z, k) + c) * 4 + flipped(e, q)
        return full.at[pl.ds(pl.multiple_of(row * share, share), share)]

    def pass_on(src, k, q, way, at, to):
        return push(src, item(k, q), send.at[way, at], recv.at[way, at], to)

    z_way, x_way, y_way, across_way, core_way = range(5)
    mine = pltpu.make_async_copy(own, item(0, 0), local.at[0])
    mine.start()
    copies = []
    from_z, from_x, from_y, across, from_core = {}, {}, {}, {}, {}
    for k in (1, 2, 3):
        from_z[k] = pass_on(own, 0, 0, z_way, k, to_z[k])
    for k in range(4):
        src = own
        if k:
            from_z[k].wait_recv()
            src = item(k, 0)
        from_x[k] = pass_on(src, k, 0, x_way, k, to_x)
        from_y[k] = pass_on(src, k, 0, y_way, k, to_y)
        from_core[k, 0] = pass_on(src, k, 0, core_way, k, to_core)
    for k in range(4):
        from_x[k].wait_recv()
        from_core[k, 1] = pass_on(item(k, 1), k, 1, core_way, 4 + k, to_core)
        if k % 2 == 0:
            across[k] = pass_on(item(k, 1), k, 1, across_way, k, to_y)
        from_y[k].wait_recv()
        from_core[k, 2] = pass_on(item(k, 2), k, 2, core_way, 8 + k, to_core)
        if k % 2 == 1:
            across[k] = pass_on(item(k, 2), k, 2, across_way, k, to_x)
    for k in range(4):
        across[k].wait_recv()
        from_core[k, 3] = pass_on(item(k, 3), k, 3, core_way, 12 + k, to_core)
    for copy in from_core.values():
        copy.wait_recv()
    for copies in (from_z, from_x, from_y, across, from_core):
        for copy in copies.values():
            copy.wait_send()
    mine.wait()


def gather_weights(own):
    shape = (32 * own.shape[0], own.shape[1])
    return call(
        gather_weights_kernel,
        (jax.ShapeDtypeStruct(shape, BF16),),
        [DMA((1,)), DMA((5, 16)), DMA((5, 16))],
        16 * MB,
        0,
        own,
        stay=(0,),
        land=(0,),
        link=0,
    )[0]


def attention_forward_kernel(experts, *refs):
    fast = len(refs) > 16
    tokens, weights, heads, hot, length = refs[:5]
    refs = refs[5:]
    if fast:
        cotangent, meta = refs[:2]
        refs = refs[2:]
    qkv, attended, probs, resid, normed_two, small = refs[:6]
    normed, diagonals = refs[-2:]
    if fast:
        rows_full, cots_full, meta_full, local, send, recv = refs[6:-2]
        d, e, _, _ = here()
        meet(group(d, e)[1:])
        rows_spread = Spread(normed_two, rows_full, send.at[0], recv.at[0], d, e)
        cots_spread = Spread(cotangent, cots_full, send.at[1], recv.at[1], d, e)
        cots_spread.start()
        meta_copies = [
            push(meta, meta_full.at[q], send.at[2, q], recv.at[2, q], group(d, e)[q])
            for q in (1, 2, 3)
        ]
        own_copies = [
            pltpu.make_async_copy(cotangent, cots_full.at[0], local.at[0]),
            pltpu.make_async_copy(meta, meta_full.at[0], local.at[1]),
        ]
        for copy in own_copies:
            copy.start()
    slots, width = tokens.shape
    small[...] = jnp.transpose(weights[:, 4 * width :].astype(F32))[: small.shape[0], :]
    x = tokens[...].astype(F32)
    inv_one = lax.rsqrt(jnp.mean(x * x, axis=1, keepdims=True) + epsilon)
    normed[...] = (x * inv_one * small[experts : experts + 1, :]).astype(BF16)
    spread_bias = heads[...].astype(F32) * small[experts + 2 : experts + 3, :]
    diagonals[...] = dot(spread_bias.astype(BF16), hot[...])

    @pl.loop(0, 3 * width // 512)
    def _(j):
        qkv[:, columns(j, 512)] = dot(normed[...], weights[:, columns(j, 512)]).astype(BF16)

    lane = lax.broadcasted_iota(jnp.int32, (slots, LANES), 1)
    first = lane < HD
    live = lax.broadcasted_iota(jnp.int32, (slots, slots), 1) < length[0, 0]

    def attend(pair):
        q = qkv[:, columns(pair, LANES)]
        k = qkv[:, columns(PAIRS + pair, LANES)]
        v = qkv[:, columns(2 * PAIRS + pair, LANES)]
        outs = []
        for half in range(2):
            head = 2 * pair + half
            own = first if half == 0 else jnp.logical_not(first)
            row = jnp.broadcast_to(diagonals[pl.ds(head, 1), :], (slots, 2 * slots))
            bias = pltpu.roll(row, 0, 1, stride=1, stride_axis=0)[:, :slots]
            scores = dot_nt(jnp.where(own, q, jnp.zeros_like(q)), k) * SCALE + bias
            scores = jnp.where(live, scores, masked_value)
            exponent = jnp.exp(scores - jnp.max(scores, axis=1, keepdims=True))
            low = (exponent / jnp.sum(exponent, axis=1, keepdims=True)).astype(BF16)
            probs[head] = low
            outs.append(dot(low, v))
        attended[:, columns(pair, LANES)] = jnp.where(first, outs[0], outs[1]).astype(BF16)

    pl.loop(0, PAIRS // 2)(attend)
    if fast:
        cots_spread.forward()
    pl.loop(PAIRS // 2, PAIRS)(attend)

    @pl.loop(0, width // 512)
    def _(j):
        resid[:, columns(j, 512)] = tokens[:, columns(j, 512)].astype(F32) + dot(
            attended[...], weights[:, columns(3 * width // 512 + j, 512)]
        )

    r = resid[...]
    inv_two = lax.rsqrt(jnp.mean(r * r, axis=1, keepdims=True) + epsilon)
    normed_two[...] = (r * inv_two * small[experts + 1 : experts + 2, :]).astype(BF16)
    if fast:
        rows_spread.start()
        own_rows = pltpu.make_async_copy(normed_two, rows_full.at[0], local.at[2])
        own_rows.start()
        rows_spread.forward()
        for copy in own_copies:
            copy.wait()
        for copy in meta_copies:
            copy.wait()
        cots_spread.finish()
        own_rows.wait()
        rows_spread.finish()


def attention_forward(fast, experts, tokens, weights, heads, hot, length, cotangent, meta):
    slots, width = tokens.shape
    small_rows = -(-(experts + 3) // 8) * 8
    shapes = (
        jax.ShapeDtypeStruct((slots, 3 * width), BF16),
        jax.ShapeDtypeStruct((slots, width), BF16),
        jax.ShapeDtypeStruct((HEADS, slots, slots), BF16),
        jax.ShapeDtypeStruct((slots, width), F32),
        jax.ShapeDtypeStruct((slots, width), BF16),
        jax.ShapeDtypeStruct((small_rows, width), F32),
    )
    scratch = [pltpu.VMEM((slots, width), BF16), pltpu.VMEM((HEADS, 2 * slots), F32)]
    args = (tokens, weights, heads, hot, length)
    options = {}
    if fast:
        args = args + (cotangent, meta)
        shapes = shapes + (
            jax.ShapeDtypeStruct((experts, slots, width), BF16),
            jax.ShapeDtypeStruct((experts, slots, width), BF16),
            jax.ShapeDtypeStruct((experts,) + meta.shape, jnp.int32),
        )
        scratch = [DMA((3,)), DMA((3, 6)), DMA((3, 6))] + scratch
        options = dict(stay=(5, 6), land=(6, 7, 8), link=1)
    return call(
        functools.partial(attention_forward_kernel, experts),
        shapes,
        scratch,
        48 * MB,
        2 * slots * width * (4 * width + 2 * slots),
        *args,
        **options,
    )


def pair_gates(logits, route_zero, route_one):
    experts = logits.shape[0]
    which = lax.broadcasted_iota(jnp.int32, logits.shape, 0)
    zero = jnp.sum(jnp.where(which == route_zero, logits, 0.0), axis=0, keepdims=True)
    one = jnp.sum(jnp.where(which == route_one, logits, 0.0), axis=0, keepdims=True)
    top = jnp.maximum(zero, one)
    zero, one = jnp.exp(zero - top), jnp.exp(one - top)
    total = zero + one
    return zero / total, one / total


def dispatch_kernel(
    rows, cots, meta, small, own, buffer, scaled, plain, select, gate_column, acc, acc_cot, rank
):
    blocks, slots = rows.shape[0], rows.shape[1]
    expert = own[0, 0]
    total_zero = jnp.zeros((1, 1), F32)
    acc[...] = jnp.zeros_like(acc)
    acc_cot[...] = jnp.zeros_like(acc_cot)
    gate_column[...] = jnp.zeros_like(gate_column)

    def names(block):
        info = meta[block]
        valid = info[3:4, :] > 0
        zero = jnp.logical_and(valid, info[0:1, :] == expert)
        one = jnp.logical_and(valid, info[1:2, :] == expert)
        return info, zero, one

    row_of = lax.broadcasted_iota(jnp.int32, (16, slots), 0)
    for block in range(blocks):
        _, zero, _ = names(block)
        total_zero = total_zero + jnp.sum(zero.astype(F32), axis=1, keepdims=True)
        rank[block] = jnp.transpose(meta[block].astype(F32))

    for block in range(blocks):
        info, zero, one = names(block)
        mine = info[2:3, :].astype(F32)

        def earlier(other, counts):
            _, other_zero, other_one = names(other)
            marks = jnp.where(row_of == 0, other_zero.astype(F32), 0.0) + jnp.where(
                row_of == 1, other_one.astype(F32), 0.0
            )
            before = (rank[other][:, 2:3] < mine).astype(F32).astype(BF16)
            return counts + dot(marks.astype(BF16), before)

        counts = lax.fori_loop(0, blocks, earlier, jnp.zeros((16, slots), F32))
        place = jnp.where(
            zero, counts[0:1, :], jnp.where(one, counts[1:2, :] + total_zero, -1.0)
        ).astype(jnp.int32)
        hot = lax.broadcasted_iota(jnp.int32, (CAP, slots), 0) == place
        picked = hot.astype(F32).astype(BF16)
        select[block] = picked
        logits = dot_nt(small[...].astype(BF16), rows[block])
        gate_zero, gate_one = pair_gates(logits, info[0:1, :], info[1:2, :])
        gate = jnp.where(zero, gate_zero, jnp.where(one, gate_one, 0.0))
        gate_column[...] += jnp.sum(jnp.where(hot, gate, 0.0), axis=1, keepdims=True)
        acc[...] += dot(picked, rows[block])
        acc_cot[...] += dot(picked, cots[block])

    buffer[...] = acc[...].astype(BF16)
    plain[...] = acc_cot[...].astype(BF16)
    scaled[...] = (acc_cot[...] * gate_column[:, 0:1]).astype(BF16)


def dispatch(rows, cots, meta, small, own):
    blocks, slots, width = rows.shape
    shapes = (
        jax.ShapeDtypeStruct((CAP, width), BF16),
        jax.ShapeDtypeStruct((CAP, width), BF16),
        jax.ShapeDtypeStruct((CAP, width), BF16),
        jax.ShapeDtypeStruct((blocks, CAP, slots), BF16),
        jax.ShapeDtypeStruct((CAP, 128), F32),
    )
    return call(
        dispatch_kernel,
        shapes,
        [
            pltpu.VMEM((CAP, width), F32),
            pltpu.VMEM((CAP, width), F32),
            pltpu.VMEM((blocks, slots, meta.shape[1]), F32),
        ],
        56 * MB,
        4 * CAP * blocks * slots * width,
        rows,
        cots,
        meta,
        small,
        own,
    )


CHUNK = 256
GELU_A = math.sqrt(2.0 / math.pi)
GELU_B = 0.044715


def expert_chunk(buffer, scaled, gate, up, down):
    gate_in, up_in = dot(buffer, gate), dot(buffer, up)
    square = gate_in * gate_in
    wave = jnp.tanh(GELU_A * gate_in * (1.0 + GELU_B * square))
    half = 0.5 * (1.0 + wave)
    activated = gate_in * half
    slope = half + (0.5 * GELU_A) * gate_in * (1.0 - wave * wave) * (1.0 + 3.0 * GELU_B * square)
    hidden = (activated * up_in).astype(BF16)
    grad_hidden = dot_nt(scaled, down)
    grad_gate_in = (grad_hidden * up_in * slope).astype(BF16)
    grad_up_in = (grad_hidden * activated).astype(BF16)
    grad_buffer = dot_nt(grad_gate_in, gate) + dot_nt(grad_up_in, up)
    return (
        dot(hidden, down),
        grad_buffer,
        dot_tn(buffer, grad_gate_in),
        dot_tn(buffer, grad_up_in),
        dot_tn(hidden, scaled),
    )


def expert_kernel(
    buffer,
    scaled,
    plain,
    gate,
    up,
    down,
    out,
    grad_buffer,
    inner,
    grad_gate,
    grad_up,
    grad_down,
    acc_out,
    acc_grad,
):
    step = pl.program_id(0)

    @pl.when(step == 0)
    def _():
        acc_out[...] = jnp.zeros_like(acc_out)
        acc_grad[...] = jnp.zeros_like(acc_grad)

    more_out, more_grad, d_gate, d_up, d_down = expert_chunk(
        buffer[...], scaled[...], gate[...], up[...], down[...]
    )
    acc_out[...] += more_out
    acc_grad[...] += more_grad
    grad_gate[...] = d_gate.astype(BF16)
    grad_up[...] = d_up.astype(BF16)
    grad_down[...] = d_down.astype(BF16)

    @pl.when(step == pl.num_programs(0) - 1)
    def _():
        low = acc_out[...].astype(BF16)
        out[...] = low
        grad_buffer[...] = acc_grad[...].astype(BF16)
        inner[...] = jnp.broadcast_to(
            jnp.sum(low.astype(F32) * plain[...].astype(F32), axis=1, keepdims=True), inner.shape
        )


def experts(buffer, scaled, plain, gate, up, down):
    rows, width = buffer.shape
    hidden = gate.shape[1]
    whole = pl.BlockSpec((rows, width), lambda j: (0, 0))
    tall = pl.BlockSpec((width, CHUNK), lambda j: (0, j))
    wide = pl.BlockSpec((CHUNK, width), lambda j: (j, 0))
    shapes = (
        jax.ShapeDtypeStruct((rows, width), BF16),
        jax.ShapeDtypeStruct((rows, width), BF16),
        jax.ShapeDtypeStruct((rows, 128), F32),
        jax.ShapeDtypeStruct((width, hidden), BF16),
        jax.ShapeDtypeStruct((width, hidden), BF16),
        jax.ShapeDtypeStruct((hidden, width), BF16),
    )
    return pl.pallas_call(
        expert_kernel,
        out_shape=shapes,
        grid=(hidden // CHUNK,),
        in_specs=[whole, whole, whole, tall, tall, wide],
        out_specs=(whole, whole, pl.BlockSpec((rows, 128), lambda j: (0, 0)), tall, tall, wide),
        scratch_shapes=[pltpu.VMEM((rows, width), F32), pltpu.VMEM((rows, width), F32)],
        compiler_params=pltpu.CompilerParams(
            vmem_limit_bytes=48 * MB, dimension_semantics=("arbitrary",)
        ),
        cost_estimate=pl.CostEstimate(
            flops=18 * rows * width * hidden,
            bytes_accessed=12 * width * hidden,
            transcendentals=rows * hidden,
        ),
    )(buffer, scaled, plain, gate, up, down)


def give_back_kernel(fast, select, out, grad_buffer, inner, gate_column, *refs):
    mixed = refs[0]
    grads, inner_rows = refs[-2:]
    blocks = select.shape[0]
    order = range(blocks)
    if fast:
        returned, inner_full, local, send, recv = refs[1:-2]
        d, e, _, _ = here()
        meet(group(d, e)[1:])
        swap = Swap(grads, returned, send.at[0], recv.at[0], d, e)
        inner_swap = Swap(inner_rows, inner_full, send.at[1], recv.at[1], d, e)
        order = (3, 1, 2, 0)
    for block in order:
        row = jnp.sum(select[block].astype(F32) * inner[:, 0:1], axis=0, keepdims=True)
        inner_rows[block] = jnp.broadcast_to(row, inner_rows.shape[1:])
        grads[block] = dot_tn(select[block], grad_buffer[...]).astype(BF16)
        if fast and block:
            inner_swap.start(block)
            swap.start(block)
    if fast:
        own_copies = [
            pltpu.make_async_copy(grads.at[0], returned.at[0], local.at[0]),
            pltpu.make_async_copy(inner_rows.at[0], inner_full.at[0], local.at[1]),
        ]
        for copy in own_copies:
            copy.start()
    weighted = (out[...].astype(F32) * gate_column[:, 0:1]).astype(BF16)
    for block in order:
        mixed[block] = dot_tn(select[block], weighted).astype(BF16)
    if fast:
        for copy in own_copies:
            copy.wait()
        inner_swap.finish()
        swap.finish()


def give_back(fast, select, out, grad_buffer, inner, gate_column):
    blocks, rows, slots = select.shape
    width = out.shape[1]
    wide = (blocks, slots, width)
    thin = (blocks, 8, slots)
    shapes = (
        jax.ShapeDtypeStruct(wide, BF16),
        jax.ShapeDtypeStruct(wide, BF16),
        jax.ShapeDtypeStruct(thin, F32),
    )
    scratch, options = [], {}
    if fast:
        scratch = [DMA((2,)), DMA((2, 4)), DMA((2, 4)), pltpu.VMEM(wide, BF16), pltpu.VMEM(thin, F32)]
        options = dict(land=(1, 2), link=2)
    return call(
        functools.partial(give_back_kernel, fast),
        shapes,
        scratch,
        56 * MB,
        4 * rows * blocks * slots * width,
        select,
        out,
        grad_buffer,
        inner,
        gate_column,
        **options,
    )


def attention_backward_kernel(
    fast,
    experts,
    tokens,
    cotangent,
    weights,
    small,
    heads,
    hot_back,
    length,
    meta,
    own,
    returned,
    inner_rows,
    mixed,
    qkv,
    attended,
    probs,
    resid,
    normed_two,
    output,
    grad_tokens,
    grad_weights,
    grad_small,
    grad_attended,
    grad_qkv,
    branch,
    normed,
    work,
    grad_diagonals,
    *refs,
):
    slots, width = tokens.shape
    blocks = returned.shape[0]
    if fast:
        mixed_full, send, recv = refs
        d, e, _, _ = here()
        meet(group(d, e)[1:])
        swap = Swap(mixed, mixed_full, send, recv, d, e)
        for block in (3, 1, 2):
            swap.start(block)
    router_t = small[...].astype(BF16)
    keep_row = lax.broadcasted_iota(jnp.int32, (slots, 1), 0) < length[0, 0]
    logits = dot_nt(router_t, normed_two[...])
    zero_route, one_route = meta[0:1, :], meta[1:2, :]
    gate_zero, gate_one = pair_gates(logits, zero_route, one_route)
    which = lax.broadcasted_iota(jnp.int32, logits.shape, 0)
    grad_zero = jnp.zeros((1, slots), F32)
    grad_one = jnp.zeros((1, slots), F32)
    for block in range(blocks):
        row = inner_rows[block][0:1, :]
        expert = jnp.bitwise_xor(own[0, 0], block) if fast else block
        grad_zero = grad_zero + jnp.where(zero_route == expert, row, 0.0)
        grad_one = grad_one + jnp.where(one_route == expert, row, 0.0)
    shared = gate_zero * grad_zero + gate_one * grad_one
    grad_zero = gate_zero * (grad_zero - shared)
    grad_one = gate_one * (grad_one - shared)
    grad_logits = jnp.where(which == zero_route, grad_zero, 0.0) + jnp.where(
        which == one_route, grad_one, 0.0
    )
    high, rest = two_halves(grad_logits)
    grad_small[...] = dot(high, normed_two[...]) + dot(rest, normed_two[...])
    grad_normed_two = dot_tn(high, router_t) + dot_tn(rest, router_t)
    for block in range(blocks):
        grad_normed_two = grad_normed_two + returned[block].astype(F32)
    r = resid[...]
    inv_two = lax.rsqrt(jnp.mean(r * r, axis=1, keepdims=True) + epsilon)
    unit_two = r * inv_two
    grad_small[experts + 1 : experts + 2, :] = jnp.sum(
        grad_normed_two * unit_two, axis=0, keepdims=True
    )
    scaled_two = small[experts + 1 : experts + 2, :] * grad_normed_two
    grad_resid = jnp.where(keep_row, cotangent[...].astype(F32), 0.0) + inv_two * (
        scaled_two - unit_two * jnp.mean(scaled_two * unit_two, axis=1, keepdims=True)
    )
    work[...] = grad_resid
    branch[...] = grad_resid.astype(BF16)

    @pl.loop(0, width // 256)
    def _(j):
        grad_weights[:, columns(3 * width // 256 + j, 256)] = dot_tn(
            attended[...], branch[:, columns(j, 256)]
        ).astype(BF16)

    grad_attended[...] = dot_nt(branch[...], weights[:, 3 * width : 4 * width]).astype(BF16)

    lane = lax.broadcasted_iota(jnp.int32, (slots, LANES), 1)
    first = lane < HD
    square = (slots, slots)
    flip = (
        lax.broadcasted_iota(jnp.int32, square, 0) + lax.broadcasted_iota(jnp.int32, square, 1)
        == slots - 1
    )
    flip = flip.astype(F32).astype(BF16)

    @pl.loop(0, PAIRS)
    def _(pair):
        q = qkv[:, columns(pair, LANES)]
        k = qkv[:, columns(PAIRS + pair, LANES)]
        v = qkv[:, columns(2 * PAIRS + pair, LANES)]
        g = grad_attended[:, columns(pair, LANES)]
        dq, dk, dv = [], [], []
        for half in range(2):
            head = 2 * pair + half
            own = first if half == 0 else jnp.logical_not(first)
            low = probs[head]
            p = low.astype(F32)
            grad_probs = dot_nt(jnp.where(own, g, jnp.zeros_like(g)), v)
            ds = p * (grad_probs - jnp.sum(p * grad_probs, axis=1, keepdims=True))
            ds = ds.astype(BF16)
            wide = jnp.concatenate([dot(flip, ds), jnp.zeros((slots, slots), F32)], axis=1)
            skewed = pltpu.roll(wide, 0, 1, stride=1, stride_axis=0)
            grad_diagonals[pl.ds(head, 1), :] = jnp.sum(skewed, axis=0, keepdims=True)
            dq.append(dot(ds, k))
            dk.append(dot_tn(ds, q))
            dv.append(dot_tn(low, g))
        grad_qkv[:, columns(pair, LANES)] = (jnp.where(first, dq[0], dq[1]) * SCALE).astype(BF16)
        grad_qkv[:, columns(PAIRS + pair, LANES)] = (
            jnp.where(first, dk[0], dk[1]) * SCALE
        ).astype(BF16)
        grad_qkv[:, columns(2 * PAIRS + pair, LANES)] = jnp.where(first, dv[0], dv[1]).astype(BF16)

    x = tokens[...].astype(F32)
    inv_one = lax.rsqrt(jnp.mean(x * x, axis=1, keepdims=True) + epsilon)
    unit_one = x * inv_one
    normed[...] = (unit_one * small[experts : experts + 1, :]).astype(BF16)
    high, rest = two_halves(grad_diagonals[...])
    by_lane = dot_nt(high, hot_back[...]) + dot_nt(rest, hot_back[...])
    grad_small[experts + 2 : experts + 3, :] = jnp.sum(
        by_lane * heads[...].astype(F32), axis=0, keepdims=True
    )

    @pl.loop(0, 3 * width // 256)
    def _(j):
        grad_weights[:, columns(j, 256)] = dot_tn(normed[...], grad_qkv[:, columns(j, 256)]).astype(
            BF16
        )

    grad_normed = dot_nt(grad_qkv[...], weights[:, : 3 * width])
    grad_small[experts : experts + 1, :] = jnp.sum(grad_normed * unit_one, axis=0, keepdims=True)
    scaled_one = small[experts : experts + 1, :] * grad_normed
    grad_tokens[...] = work[...] + inv_one * (
        scaled_one - unit_one * jnp.mean(scaled_one * unit_one, axis=1, keepdims=True)
    )
    if fast:
        swap.finish()
    total = resid[...] + mixed[0].astype(F32)
    for block in range(1, blocks):
        total = total + (mixed_full if fast else mixed)[block].astype(F32)
    output[...] = jnp.where(keep_row, total, 0.0).astype(BF16)


def attention_backward(fast, experts, *args):
    tokens, small, mixed = args[0], args[3], args[11]
    slots, width = tokens.shape
    shapes = (
        jax.ShapeDtypeStruct((slots, width), BF16),
        jax.ShapeDtypeStruct((slots, width), F32),
        jax.ShapeDtypeStruct((width, 4 * width), BF16),
        jax.ShapeDtypeStruct(small.shape, F32),
    )
    scratch = [
        pltpu.VMEM((slots, width), BF16),
        pltpu.VMEM((slots, 3 * width), BF16),
        pltpu.VMEM((slots, width), BF16),
        pltpu.VMEM((slots, width), BF16),
        pltpu.VMEM((slots, width), F32),
        pltpu.VMEM((HEADS, 2 * slots), F32),
    ]
    options = {}
    if fast:
        scratch += [pltpu.VMEM(mixed.shape, BF16), DMA((4,)), DMA((4,))]
        options = dict(link=3)
    return call(
        functools.partial(attention_backward_kernel, fast, experts),
        shapes,
        scratch,
        60 * MB,
        4 * slots * width * (4 * width + 2 * slots),
        *args,
        **options,
    )


def add_up_kernel(
    partial,
    small,
    grad_qkv,
    grad_out,
    small_sum,
    mine,
    theirs,
    first_in,
    second_in,
    planes,
    last_in,
    smalls,
    small_in,
    local,
    send,
    recv,
    small_send,
    small_recv,
):
    d, e, z, c = here()
    share = grad_qkv.shape[0]
    quad = 4 * share
    width = grad_out.shape[1]
    other = (2 * z + 1 - c, e)
    to_x, to_y = (d, flipped(e, 1)), (d, flipped(e, 2))
    to_z = [None] + [(2 * flipped(z, k) + c, e) for k in (1, 2, 3)]
    meet([other, to_x, to_y] + to_z[1:])
    turns = (3, 2, 1, 0)

    def block(k, core):
        row = (2 * flipped(z, k) + core) * quad
        return partial.at[pl.ds(pl.multiple_of(row, quad), quad)]

    def piece(k, q):
        row = flipped(e, q) * share
        return mine.at[k, pl.ds(pl.multiple_of(row, share), share)]

    loads, from_core, firsts, seconds, lasts = {}, {}, {}, {}, {}
    for k in turns:
        from_core[k] = push(block(k, 1 - c), theirs.at[k], send.at[0, k], recv.at[0, k], other)
        loads[k] = pltpu.make_async_copy(block(k, c), mine.at[k], local.at[k])
        loads[k].start()

    small_to = [other, to_x, to_y, to_z[1], to_z[2]]
    smalls[0] = small[...]
    small_copies = []

    def small_step():
        at = len(small_copies)
        if at:
            small_copies[at - 1].wait_recv()
            smalls[at] = smalls[at - 1] + small_in[at - 1]
        if at < len(small_to):
            small_copies.append(
                push(
                    smalls.at[at],
                    small_in.at[at],
                    small_send.at[at],
                    small_recv.at[at],
                    small_to[at],
                )
            )

    def stage_one(k):
        loads[k].wait()
        from_core[k].wait_recv()

        @pl.loop(0, 4)
        def _(j):
            at = pl.ds(pl.multiple_of(j * share, share), share)
            mine[k, at] = (mine[k, at].astype(F32) + theirs[k, at].astype(F32)).astype(BF16)

        near, to = (1, to_x) if k % 2 == 0 else (2, to_y)
        firsts[k] = [
            push(piece(k, q), first_in.at[k, slot], send.at[1 + slot, k], recv.at[1 + slot, k], to)
            for slot, q in ((1, 3), (0, near))
        ]

    def stage_two(k):
        far, to = (2, to_y) if k % 2 == 0 else (1, to_x)
        for copy in firsts[k]:
            copy.wait_recv()
        source = piece(k, far)
        source[...] = (source[...].astype(F32) + first_in[k, 1].astype(F32)).astype(BF16)
        seconds[k] = push(source, second_in.at[k], send.at[3, k], recv.at[3, k], to)

    def stage_three(k):
        seconds[k].wait_recv()
        total = piece(k, 0)[...].astype(F32) + first_in[k, 0].astype(F32)
        total = total + second_in[k].astype(F32)
        if k:
            planes[k] = total.astype(BF16)
            lasts[k] = push(planes.at[k], last_in.at[k], send.at[4, k], recv.at[4, k], to_z[k])
        else:
            grad_qkv[...] = total[:, : 3 * width]
            grad_out[...] = total[:, 3 * width :]

    a, b, c_, d_ = turns
    small_step()
    stage_one(a)
    stage_one(b)
    small_step()
    stage_two(a)
    stage_one(c_)
    stage_two(b)
    small_step()
    stage_three(a)
    stage_one(d_)
    stage_two(c_)
    small_step()
    stage_three(b)
    stage_two(d_)
    small_step()
    stage_three(c_)
    stage_three(d_)
    small_step()
    small_sum[...] = smalls[len(small_to)]
    for k in turns[:-1]:
        lasts[k].wait_recv()
    total = last_in[1].astype(F32) + last_in[2].astype(F32) + last_in[3].astype(F32)
    grad_qkv[...] += total[:, : 3 * width]
    grad_out[...] += total[:, 3 * width :]
    for copies in (from_core, seconds, lasts):
        for copy in copies.values():
            copy.wait_send()
    for pair in firsts.values():
        for copy in pair:
            copy.wait_send()
    for copy in small_copies:
        copy.wait_send()


def add_up(partial, small):
    width, wide = partial.shape
    share = width // 32
    return call(
        add_up_kernel,
        (
            jax.ShapeDtypeStruct((share, 3 * width), F32),
            jax.ShapeDtypeStruct((share, width), F32),
            jax.ShapeDtypeStruct(small.shape, F32),
        ),
        [
            pltpu.VMEM((4, 4 * share, wide), BF16),
            pltpu.VMEM((4, 4 * share, wide), BF16),
            pltpu.VMEM((4, 2, share, wide), BF16),
            pltpu.VMEM((4, share, wide), BF16),
            pltpu.VMEM((4, share, wide), BF16),
            pltpu.VMEM((4, share, wide), BF16),
            pltpu.VMEM((6,) + small.shape, F32),
            pltpu.VMEM((5,) + small.shape, F32),
            DMA((4,)),
            DMA((5, 4)),
            DMA((5, 4)),
            DMA((5,)),
            DMA((5,)),
        ],
        40 * MB,
        0,
        partial,
        small,
        stay=(0,),
        link=4,
    )


def on_device(
    fast,
    tokens,
    cotangent,
    qkv_weight,
    out_weight,
    router_weight,
    first_gain,
    second_gain,
    bias_table,
    gate_weight,
    up_weight,
    down_weight,
    lengths,
    routes,
    priority,
):
    both = ("dp", "expert")
    slots, width = tokens.shape
    expert_count = lax.axis_size("expert")
    device_count = lax.axis_size("dp") * expert_count
    share, bias_share = first_gain.shape[0], bias_table.shape[0]
    device = lax.axis_index("dp") * expert_count + lax.axis_index("expert")
    own = lax.axis_index("expert").astype(jnp.int32).reshape(1, 1)
    small_rows = -(-(expert_count + 3) // 8) * 8

    def gathered(value, axes, axis=0, tiled=True):
        return lax.all_gather(value, axes, axis=axis, tiled=tiled)

    def scattered(value, axes):
        return lax.psum_scatter(value, axes, scatter_dimension=0, tiled=True).astype(F32)

    def exchanged(value):
        return lax.all_to_all(value, "expert", split_axis=0, concat_axis=0, tiled=True)

    gate_full, up_full, down_full = (
        gathered(value[0], "dp") for value in (gate_weight, up_weight, down_weight)
    )

    beside = jnp.concatenate(
        [
            router_weight,
            first_gain[:, None],
            second_gain[:, None],
            jnp.pad(bias_table, (0, share - bias_share))[:, None],
            jnp.zeros((share, 128 - expert_count - 3), BF16),
        ],
        axis=1,
    )
    weights_own = jnp.concatenate([qkv_weight, out_weight, beside], axis=1)
    lane = np.arange(width)
    flat = lane // share * bias_share + lane % share
    in_table = lane % share < bias_share
    heads = np.arange(HEADS)[:, None] == np.where(in_table, flat // BUCKETS, -1)[None, :]
    heads = jnp.asarray(heads.astype(np.float32), BF16)
    ahead = np.arange(2 * slots)

    def hot(ahead):
        return jnp.asarray(
            np.where(in_table[:, None], diagonal_onehot(ahead)[flat % BUCKETS], 0.0), BF16
        )

    valid_rows = jnp.arange(slots, dtype=jnp.int32) < lengths[0, 0]
    meta_own = jnp.concatenate(
        [
            routes.T,
            priority,
            valid_rows.astype(jnp.int32)[None, :],
            jnp.zeros((4, slots), jnp.int32),
        ],
        axis=0,
    )

    weights = gather_weights(weights_own) if fast else gathered(weights_own, both)
    qkv, attended, probs, resid, normed_two, small, *spread = attention_forward(
        fast,
        expert_count,
        tokens,
        weights,
        heads,
        hot(np.where(ahead < slots, ahead, ahead - 2 * slots)),
        lengths,
        cotangent,
        meta_own,
    )
    if fast:
        rows, cots, meta = spread
    else:
        rows, cots, meta = (
            gathered(value, "expert", tiled=False) for value in (normed_two, cotangent, meta_own)
        )
    buffer, scaled, plain, select, gate_column = dispatch(rows, cots, meta, small, own)
    expert_out, grad_buffer, inner, grad_gate, grad_up, grad_down = experts(
        buffer, scaled, plain, gate_full, up_full, down_full
    )
    mixed, returned, inner_rows = give_back(
        fast, select, expert_out, grad_buffer, inner, gate_column
    )
    if not fast:
        mixed, returned, inner_rows = exchanged(mixed), exchanged(returned), exchanged(inner_rows)
    output, grad_tokens, grad_weights, grad_small = attention_backward(
        fast,
        expert_count,
        tokens,
        cotangent,
        weights,
        small,
        heads,
        hot(ahead - (slots - 1)),
        lengths,
        meta_own,
        own,
        returned,
        inner_rows,
        mixed,
        qkv,
        attended,
        probs,
        resid,
        normed_two,
    )
    if fast:
        grad_qkv, grad_out, grad_small = add_up(grad_weights, grad_small)
    else:
        grad_weights = scattered(grad_weights, both)
        grad_qkv, grad_out = grad_weights[:, : 3 * width], grad_weights[:, 3 * width :]
        grad_small = lax.psum(grad_small, both)
    grad_small = lax.dynamic_slice(grad_small, (0, device * share), (small_rows, share))
    return (
        output,
        grad_tokens,
        grad_qkv,
        grad_out,
        grad_small[:expert_count].T,
        grad_small[expert_count],
        grad_small[expert_count + 1],
        grad_small[expert_count + 2, :bias_share],
        scattered(grad_gate, "dp")[None],
        scattered(grad_up, "dp")[None],
        scattered(grad_down, "dp")[None],
    )


def solution(mesh):
    fast = dict(mesh.shape) == {"dp": 8, "expert": 4}
    rows = P(("dp", "expert"), None)
    flat = P(("dp", "expert"))
    expert = P("expert", "dp", None)
    grid = P("dp", "expert")
    return jax.shard_map(
        functools.partial(on_device, fast),
        mesh=mesh,
        in_specs=(rows,) * 5 + (flat,) * 3 + (expert,) * 3 + (grid, rows, grid),
        out_specs=(rows,) * 5 + (flat,) * 3 + (expert,) * 3,
        check_vma=False,
    )
```

```python
import functools
import math

import jax
import jax.numpy as jnp
import numpy as np
from jax import lax
from jax.experimental import pallas as pl
from jax.experimental.pallas import tpu as pltpu
from jax.sharding import PartitionSpec as P

HEADS = 16
HD = 64
BUCKETS = 32
CAP = 480
PAIRS = HEADS // 2
LANES = 2 * HD

epsilon = 1e-06
masked_value = -1e30
max_distance = 128.0
SCALE = 1.0 / math.sqrt(HD)
MB = 1 << 20
F32 = jnp.float32
BF16 = jnp.bfloat16


def bucket_of(offset, bucket_count):
    halfway = bucket_count // 2
    exact_span = bucket_count // 4
    distance = np.abs(offset)
    log_part = np.log(np.maximum(distance, 1) / float(exact_span)) / np.log(
        max_distance / exact_span
    )
    far_bucket = np.minimum(
        exact_span + np.floor(log_part * exact_span).astype(np.int64), halfway - 1
    )
    inside = np.where(distance < exact_span, distance, far_bucket)
    return np.where(offset < 0, halfway, 0) + inside


def diagonal_onehot(ahead):
    return (bucket_of(-ahead, BUCKETS)[None, :] == np.arange(BUCKETS)[:, None]).astype(np.float32)


def dot(a, b):
    return jnp.dot(a, b, preferred_element_type=F32)


def dot_nt(a, b):
    return lax.dot_general(a, b, (((1,), (1,)), ((), ())), preferred_element_type=F32)


def dot_tn(a, b):
    return lax.dot_general(a, b, (((0,), (0,)), ((), ())), preferred_element_type=F32)


def two_halves(value):
    high = value.astype(BF16)
    return high, (value - high.astype(F32)).astype(BF16)


def columns(index, width):
    return pl.ds(pl.multiple_of(index * width, width), width)


VMEM_SPEC = pl.BlockSpec(memory_space=pltpu.VMEM)


ANY_SPEC = pl.BlockSpec(memory_space=pl.ANY)
MESH = pl.DeviceIdType.MESH
DMA = pltpu.SemaphoreType.DMA


def call(kernel, out_shape, scratch, vmem, flops, *args, stay=(), land=(), link=None):
    nbytes = sum(a.size * a.dtype.itemsize for a in args)
    params = dict(vmem_limit_bytes=vmem)
    if link is not None:
        params.update(collective_id=link, has_side_effects=True)
    return pl.pallas_call(
        kernel,
        out_shape=out_shape,
        in_specs=[ANY_SPEC if i in stay else VMEM_SPEC for i in range(len(args))],
        out_specs=tuple(ANY_SPEC if i in land else VMEM_SPEC for i in range(len(out_shape))),
        scratch_shapes=scratch,
        compiler_params=pltpu.CompilerParams(**params),
        cost_estimate=pl.CostEstimate(flops=flops, bytes_accessed=nbytes, transcendentals=0),
    )(*args)


def here():
    d, e = lax.axis_index("dp"), lax.axis_index("expert")
    return d, e, d // 2, lax.rem(d, 2)


def flipped(value, bits):
    low, high = lax.rem(value, 2), value // 2
    low = 1 - low if bits & 1 else low
    high = 1 - high if bits & 2 else high
    return 2 * high + low


def meet(partners):
    barrier = pltpu.get_barrier_semaphore()
    for partner in partners:
        pl.semaphore_signal(barrier, inc=1, device_id=partner, device_id_type=MESH)
    pl.semaphore_wait(barrier, len(partners))


def push(src, dst, send, recv, to):
    copy = pltpu.make_async_remote_copy(
        src_ref=src, dst_ref=dst, send_sem=send, recv_sem=recv, device_id=to, device_id_type=MESH
    )
    copy.start()
    return copy


def group(d, e):
    return [None] + [(d, flipped(e, q)) for q in (1, 2, 3)]


class Spread:
    def __init__(self, src, dst, send, recv, d, e):
        self.src, self.dst, self.send, self.recv = src, dst, send, recv
        self.to = group(d, e)
        self.half = src.shape[0] // 2
        self.copies = {}

    def part(self, ref, half):
        return ref.at[pl.ds(half * self.half, self.half)]

    def start(self):
        for turn in range(2):
            for q in (1, 2):
                half = turn if q == 1 else 1 - turn
                at = 2 * (q - 1) + half
                self.copies[q, half] = push(
                    self.part(self.src, half),
                    self.part(self.dst.at[q], half),
                    self.send.at[at],
                    self.recv.at[at],
                    self.to[q],
                )

    def forward(self):
        for q, half, across, at in ((1, 0, 2, 4), (2, 1, 1, 5)):
            self.copies[q, half].wait_recv()
            self.copies[3, half] = push(
                self.part(self.dst.at[q], half),
                self.part(self.dst.at[3], half),
                self.send.at[at],
                self.recv.at[at],
                self.to[across],
            )

    def finish(self):
        for q, half in ((1, 1), (2, 0), (3, 0), (3, 1)):
            self.copies[q, half].wait_recv()
        for copy in self.copies.values():
            copy.wait_send()


class Swap:
    def __init__(self, src, dst, send, recv, d, e):
        self.src, self.dst, self.send, self.recv = src, dst, send, recv
        self.to = group(d, e)
        self.copies = {}

    def start(self, q):
        self.copies[q] = push(
            self.src.at[q], self.dst.at[q], self.send.at[q], self.recv.at[q], self.to[q]
        )

    def finish(self):
        for copy in self.copies.values():
            copy.wait_recv()
        for copy in self.copies.values():
            copy.wait_send()


def gather_weights_kernel(own, full, local, send, recv):
    d, e, z, c = here()
    share = own.shape[0]
    other = 2 * z + 1 - c
    to_x, to_y, to_core = (d, flipped(e, 1)), (d, flipped(e, 2)), (other, e)
    to_z = [None] + [(2 * flipped(z, k) + c, e) for k in (1, 2, 3)]
    meet([to_x, to_y, to_core] + to_z[1:])

    def item(k, q):
        row = (2 * flipped(z, k) + c) * 4 + flipped(e, q)
        return full.at[pl.ds(pl.multiple_of(row * share, share), share)]

    def pass_on(src, k, q, way, at, to):
        return push(src, item(k, q), send.at[way, at], recv.at[way, at], to)

    z_way, x_way, y_way, across_way, core_way = range(5)
    mine = pltpu.make_async_copy(own, item(0, 0), local.at[0])
    mine.start()
    copies = []
    from_z, from_x, from_y, across, from_core = {}, {}, {}, {}, {}
    for k in (1, 2, 3):
        from_z[k] = pass_on(own, 0, 0, z_way, k, to_z[k])
    for k in range(4):
        src = own
        if k:
            from_z[k].wait_recv()
            src = item(k, 0)
        from_x[k] = pass_on(src, k, 0, x_way, k, to_x)
        from_y[k] = pass_on(src, k, 0, y_way, k, to_y)
        from_core[k, 0] = pass_on(src, k, 0, core_way, k, to_core)
    for k in range(4):
        from_x[k].wait_recv()
        from_core[k, 1] = pass_on(item(k, 1), k, 1, core_way, 4 + k, to_core)
        if k % 2 == 0:
            across[k] = pass_on(item(k, 1), k, 1, across_way, k, to_y)
        from_y[k].wait_recv()
        from_core[k, 2] = pass_on(item(k, 2), k, 2, core_way, 8 + k, to_core)
        if k % 2 == 1:
            across[k] = pass_on(item(k, 2), k, 2, across_way, k, to_x)
    for k in range(4):
        across[k].wait_recv()
        from_core[k, 3] = pass_on(item(k, 3), k, 3, core_way, 12 + k, to_core)
    for copy in from_core.values():
        copy.wait_recv()
    for copies in (from_z, from_x, from_y, across, from_core):
        for copy in copies.values():
            copy.wait_send()
    mine.wait()


def gather_weights(own):
    shape = (32 * own.shape[0], own.shape[1])
    return call(
        gather_weights_kernel,
        (jax.ShapeDtypeStruct(shape, BF16),),
        [DMA((1,)), DMA((5, 16)), DMA((5, 16))],
        16 * MB,
        0,
        own,
        stay=(0,),
        land=(0,),
        link=0,
    )[0]


class LineSum:
    def __init__(self, count, source, scratch, load):
        self.count, self.source, self.load_first = count, source, load
        scratch = list(scratch)
        self.theirs, self.landed, self.send, self.recv = scratch[:4]
        if load:
            self.loads, self.loaded = scratch[4:]
        self.d, self.e, self.z, self.core = here()
        self.other = (2 * self.z + 1 - self.core, self.e)
        self.to = [None] + [(2 * flipped(self.z, k) + self.core, self.e) for k in (1, 2, 3)]
        self.end = jnp.logical_or(self.z == 0, self.z == 3)
        self.middle = jnp.logical_not(self.end)

    @staticmethod
    def scratch(count, rows, width, load):
        shape = (count, 4, rows, width)
        parts = [pltpu.VMEM(shape, BF16), pltpu.VMEM(shape, BF16), DMA((count, 3, 4)), DMA((count, 3, 4))]
        return parts + ([pltpu.VMEM(shape, BF16), DMA((count, 4))] if load else [])

    def remote(self, i, src, dst, stage, out, into, to):
        return pltpu.make_async_remote_copy(
            src_ref=src,
            dst_ref=dst,
            send_sem=self.send.at[i, stage, out],
            recv_sem=self.recv.at[i, stage, into],
            device_id=to,
            device_id_type=MESH,
        )

    def load(self, i, k):
        return pltpu.make_async_copy(
            self.source(i, k, self.core), self.loads.at[i, k], self.loaded.at[i, k]
        )

    def swap(self, i, k):
        src = self.source(i, k, 1 - self.core)
        return self.remote(i, src, self.theirs.at[i, k], 0, k, k, self.other)

    def hand(self, i, k):
        at = 1 if k == 1 else 5 - k
        return self.remote(i, self.theirs.at[i, k], self.landed.at[i, at], 1, k, at, self.to[1])

    def handed(self, i, at):
        return self.remote(i, self.theirs.at[i, at], self.landed.at[i, at], 1, at, at, self.to[1])

    def deliver(self, i, k):
        return self.remote(i, self.theirs.at[i, k], self.landed.at[i, 0], 2, k, 0, self.to[k])

    def add(self, i, k, more):
        self.theirs[i, k] = (self.theirs[i, k].astype(F32) + more[...].astype(F32)).astype(BF16)

    def begin(self, i):
        for k in (3, 2, 1, 0):
            self.swap(i, k).start()
            if self.load_first:
                self.load(i, k).start()

    def halve(self, i):
        for k in (3, 2, 1, 0):
            if self.load_first:
                self.load(i, k).wait()
            self.swap(i, k).wait_recv()
            self.add(i, k, self.loads.at[i, k] if self.load_first else self.source(i, k, self.core))
        self.hand(i, 1).start()

        @pl.when(self.end)
        def _():
            self.hand(i, 2).start()
            self.hand(i, 3).start()

    def relay(self, i):
        @pl.when(self.middle)
        def _():
            for k in (3, 2):
                self.handed(i, k).wait_recv()
                self.add(i, k, self.landed.at[i, k])
                self.deliver(i, k).start()

    def finish(self, i):
        self.handed(i, 1).wait_recv()
        self.deliver(i, 2).wait_recv()
        return (
            self.theirs[i, 0].astype(F32)
            + self.landed[i, 0].astype(F32)
            + self.landed[i, 1].astype(F32)
        )

    def settle(self, i):
        for k in range(4):
            self.swap(i, k).wait_send()
        self.hand(i, 1).wait_send()

        @pl.when(self.end)
        def _():
            self.hand(i, 2).wait_send()
            self.hand(i, 3).wait_send()

        @pl.when(self.middle)
        def _():
            self.deliver(i, 2).wait_send()
            self.deliver(i, 3).wait_send()


class LineSpread:
    def __init__(self, own, place, scratch):
        self.own, self.place = own, place
        self.copied, self.send, self.recv = scratch
        self.d, self.e, self.z, self.core = here()
        self.other = (2 * self.z + 1 - self.core, self.e)
        self.to = [None] + [(2 * flipped(self.z, k) + self.core, self.e) for k in (1, 2, 3)]
        self.end = jnp.logical_or(self.z == 0, self.z == 3)
        self.middle = jnp.logical_not(self.end)

    @staticmethod
    def scratch(count):
        return [DMA((count,)), DMA((count, 8)), DMA((count, 8))]

    def from_chip(self, j, k, core=None):
        return self.place(j, 2 * flipped(self.z, k) + (self.core if core is None else core))

    def remote(self, j, src, dst, out, into, to):
        return pltpu.make_async_remote_copy(
            src_ref=src,
            dst_ref=dst,
            send_sem=self.send.at[j, out],
            recv_sem=self.recv.at[j, into],
            device_id=to,
            device_id_type=MESH,
        )

    def keep(self, j):
        return pltpu.make_async_copy(self.own(j), self.place(j, self.d), self.copied.at[j])

    def first(self, j, way):
        out = min(way, 2)
        into = 4 if way == 0 else way
        to = self.to[way] if way else self.other
        return self.remote(j, self.own(j), self.place(j, self.d), out, into, to)

    def share(self, j, k):
        piece = self.from_chip(j, k)
        return self.remote(j, piece, piece, 2 + k, 4 + k, self.other)

    def pass_on(self, j, k):
        piece = self.from_chip(j, k)
        return self.remote(j, piece, piece, 4 + k, 5 - k, self.to[1])

    def arrival(self, j, k):
        piece = self.from_chip(j, k)
        return self.remote(j, piece, piece, k, k, self.to[1])

    def shared(self, j, k):
        piece = self.from_chip(j, k, 1 - self.core)
        return self.remote(j, piece, piece, 4 + k if k else 0, 4 + k, self.other)

    def start(self, j):
        self.first(j, 1).start()

        @pl.when(self.middle)
        def _():
            self.first(j, 3).start()

        @pl.when(self.end)
        def _():
            self.first(j, 2).start()

        self.first(j, 0).start()
        self.keep(j).start()

    def relay(self, j):
        for k in (1, 3, 2):
            self.arrival(j, k).wait_recv()
            if k > 1:
                @pl.when(self.middle)
                def _():
                    self.pass_on(j, k).start()

            self.share(j, k).start()

    def complete(self, j):
        self.keep(j).wait()
        for k in range(4):
            self.shared(j, k).wait_recv()

    def settle(self, j):
        self.first(j, 0).wait_send()
        self.first(j, 1).wait_send()

        @pl.when(self.middle)
        def _():
            self.first(j, 3).wait_send()
            self.pass_on(j, 2).wait_send()
            self.pass_on(j, 3).wait_send()

        @pl.when(self.end)
        def _():
            self.first(j, 2).wait_send()

        for k in (1, 2, 3):
            self.share(j, k).wait_send()


def attention_forward_kernel(fast, experts, *refs):
    tokens, weights, heads, hot, length = refs[:5]
    refs = refs[5:]
    if fast:
        cotangent, meta = refs[:2]
        refs = refs[2:]
    qkv, attended, probs, resid, normed_two, small = refs[:6]
    normed, diagonals = refs[-2:]
    if fast:
        rows_full, cots_full, meta_full, local, send, recv = refs[6:-2]
        d, e, _, _ = here()
        meet(group(d, e)[1:])
        rows_spread = Spread(normed_two, rows_full, send.at[0], recv.at[0], d, e)
        cots_spread = Spread(cotangent, cots_full, send.at[1], recv.at[1], d, e)
        cots_spread.start()
        meta_copies = [
            push(meta, meta_full.at[q], send.at[2, q], recv.at[2, q], group(d, e)[q])
            for q in (1, 2, 3)
        ]
        own_copies = [
            pltpu.make_async_copy(cotangent, cots_full.at[0], local.at[0]),
            pltpu.make_async_copy(meta, meta_full.at[0], local.at[1]),
        ]
        for copy in own_copies:
            copy.start()
    slots, width = tokens.shape
    small[...] = jnp.transpose(weights[:, 4 * width :].astype(F32))[: small.shape[0], :]
    x = tokens[...].astype(F32)
    inv_one = lax.rsqrt(jnp.mean(x * x, axis=1, keepdims=True) + epsilon)
    normed[...] = (x * inv_one * small[experts : experts + 1, :]).astype(BF16)
    spread_bias = heads[...].astype(F32) * small[experts + 2 : experts + 3, :]
    diagonals[...] = dot(spread_bias.astype(BF16), hot[...])

    @pl.loop(0, 3 * width // 512)
    def _(j):
        qkv[:, columns(j, 512)] = dot(normed[...], weights[:, columns(j, 512)]).astype(BF16)

    lane = lax.broadcasted_iota(jnp.int32, (slots, LANES), 1)
    first = lane < HD
    live = lax.broadcasted_iota(jnp.int32, (slots, slots), 1) < length[0, 0]

    def attend(pair):
        q = qkv[:, columns(pair, LANES)]
        k = qkv[:, columns(PAIRS + pair, LANES)]
        v = qkv[:, columns(2 * PAIRS + pair, LANES)]
        outs = []
        for half in range(2):
            head = 2 * pair + half
            own = first if half == 0 else jnp.logical_not(first)
            row = jnp.broadcast_to(diagonals[pl.ds(head, 1), :], (slots, 2 * slots))
            bias = pltpu.roll(row, 0, 1, stride=1, stride_axis=0)[:, :slots]
            scores = dot_nt(jnp.where(own, q, jnp.zeros_like(q)), k) * SCALE + bias
            scores = jnp.where(live, scores, masked_value)
            exponent = jnp.exp(scores - jnp.max(scores, axis=1, keepdims=True))
            low = (exponent / jnp.sum(exponent, axis=1, keepdims=True)).astype(BF16)
            probs[head] = low
            outs.append(dot(low, v))
        attended[:, columns(pair, LANES)] = jnp.where(first, outs[0], outs[1]).astype(BF16)

    pl.loop(0, PAIRS // 2)(attend)
    if fast:
        cots_spread.forward()
    pl.loop(PAIRS // 2, PAIRS)(attend)

    @pl.loop(0, width // 512)
    def _(j):
        resid[:, columns(j, 512)] = tokens[:, columns(j, 512)].astype(F32) + dot(
            attended[...], weights[:, columns(3 * width // 512 + j, 512)]
        )

    r = resid[...]
    inv_two = lax.rsqrt(jnp.mean(r * r, axis=1, keepdims=True) + epsilon)
    normed_two[...] = (r * inv_two * small[experts + 1 : experts + 2, :]).astype(BF16)
    if fast:
        rows_spread.start()
        own_rows = pltpu.make_async_copy(normed_two, rows_full.at[0], local.at[2])
        own_rows.start()
        rows_spread.forward()
        for copy in own_copies:
            copy.wait()
        for copy in meta_copies:
            copy.wait()
        cots_spread.finish()
        own_rows.wait()
        rows_spread.finish()


def attention_forward(fast, experts, tokens, weights, heads, hot, length, cotangent, meta):
    slots, width = tokens.shape
    small_rows = -(-(experts + 3) // 8) * 8
    shapes = (
        jax.ShapeDtypeStruct((slots, 3 * width), BF16),
        jax.ShapeDtypeStruct((slots, width), BF16),
        jax.ShapeDtypeStruct((HEADS, slots, slots), BF16),
        jax.ShapeDtypeStruct((slots, width), F32),
        jax.ShapeDtypeStruct((slots, width), BF16),
        jax.ShapeDtypeStruct((small_rows, width), F32),
    )
    scratch = [pltpu.VMEM((slots, width), BF16), pltpu.VMEM((HEADS, 2 * slots), F32)]
    args = (tokens, weights, heads, hot, length)
    options = {}
    if fast:
        args = args + (cotangent, meta)
        shapes = shapes + (
            jax.ShapeDtypeStruct((experts, slots, width), BF16),
            jax.ShapeDtypeStruct((experts, slots, width), BF16),
            jax.ShapeDtypeStruct((experts,) + meta.shape, jnp.int32),
        )
        scratch = [DMA((3,)), DMA((3, 6)), DMA((3, 6))] + scratch
        options = dict(stay=(5, 6), land=(6, 7, 8), link=1)
    return call(
        functools.partial(attention_forward_kernel, fast, experts),
        shapes,
        scratch,
        48 * MB,
        2 * slots * width * (4 * width + 2 * slots),
        *args,
        **options,
    )


def pair_gates(logits, route_zero, route_one):
    experts = logits.shape[0]
    which = lax.broadcasted_iota(jnp.int32, logits.shape, 0)
    zero = jnp.sum(jnp.where(which == route_zero, logits, 0.0), axis=0, keepdims=True)
    one = jnp.sum(jnp.where(which == route_one, logits, 0.0), axis=0, keepdims=True)
    top = jnp.maximum(zero, one)
    zero, one = jnp.exp(zero - top), jnp.exp(one - top)
    total = zero + one
    return zero / total, one / total


def dispatch_kernel(
    rows, cots, meta, small, own, buffer, scaled, plain, select, gate_column, acc, acc_cot, rank
):
    blocks, slots = rows.shape[0], rows.shape[1]
    expert = own[0, 0]
    total_zero = jnp.zeros((1, 1), F32)
    acc[...] = jnp.zeros_like(acc)
    acc_cot[...] = jnp.zeros_like(acc_cot)
    gate_column[...] = jnp.zeros_like(gate_column)

    def names(block):
        info = meta[block]
        valid = info[3:4, :] > 0
        zero = jnp.logical_and(valid, info[0:1, :] == expert)
        one = jnp.logical_and(valid, info[1:2, :] == expert)
        return info, zero, one

    row_of = lax.broadcasted_iota(jnp.int32, (16, slots), 0)
    for block in range(blocks):
        _, zero, _ = names(block)
        total_zero = total_zero + jnp.sum(zero.astype(F32), axis=1, keepdims=True)
        rank[block] = jnp.transpose(meta[block].astype(F32))

    for block in range(blocks):
        info, zero, one = names(block)
        mine = info[2:3, :].astype(F32)

        def earlier(other, counts):
            _, other_zero, other_one = names(other)
            marks = jnp.where(row_of == 0, other_zero.astype(F32), 0.0) + jnp.where(
                row_of == 1, other_one.astype(F32), 0.0
            )
            before = (rank[other][:, 2:3] < mine).astype(F32).astype(BF16)
            return counts + dot(marks.astype(BF16), before)

        counts = lax.fori_loop(0, blocks, earlier, jnp.zeros((16, slots), F32))
        place = jnp.where(
            zero, counts[0:1, :], jnp.where(one, counts[1:2, :] + total_zero, -1.0)
        ).astype(jnp.int32)
        hot = lax.broadcasted_iota(jnp.int32, (CAP, slots), 0) == place
        picked = hot.astype(F32).astype(BF16)
        select[block] = picked
        logits = dot_nt(small[...].astype(BF16), rows[block])
        gate_zero, gate_one = pair_gates(logits, info[0:1, :], info[1:2, :])
        gate = jnp.where(zero, gate_zero, jnp.where(one, gate_one, 0.0))
        gate_column[...] += jnp.sum(jnp.where(hot, gate, 0.0), axis=1, keepdims=True)
        acc[...] += dot(picked, rows[block])
        acc_cot[...] += dot(picked, cots[block])

    buffer[...] = acc[...].astype(BF16)
    plain[...] = acc_cot[...].astype(BF16)
    scaled[...] = (acc_cot[...] * gate_column[:, 0:1]).astype(BF16)


def dispatch(rows, cots, meta, small, own):
    blocks, slots, width = rows.shape
    shapes = (
        jax.ShapeDtypeStruct((CAP, width), BF16),
        jax.ShapeDtypeStruct((CAP, width), BF16),
        jax.ShapeDtypeStruct((CAP, width), BF16),
        jax.ShapeDtypeStruct((blocks, CAP, slots), BF16),
        jax.ShapeDtypeStruct((CAP, 128), F32),
    )
    return call(
        dispatch_kernel,
        shapes,
        [
            pltpu.VMEM((CAP, width), F32),
            pltpu.VMEM((CAP, width), F32),
            pltpu.VMEM((blocks, slots, meta.shape[1]), F32),
        ],
        56 * MB,
        4 * CAP * blocks * slots * width,
        rows,
        cots,
        meta,
        small,
        own,
    )


CHUNK = 256
GELU_A = math.sqrt(2.0 / math.pi)
GELU_B = 0.044715


def expert_chunk(buffer, scaled, gate, up, down):
    gate_in, up_in = dot(buffer, gate), dot(buffer, up)
    square = gate_in * gate_in
    wave = jnp.tanh(GELU_A * gate_in * (1.0 + GELU_B * square))
    half = 0.5 * (1.0 + wave)
    activated = gate_in * half
    slope = half + (0.5 * GELU_A) * gate_in * (1.0 - wave * wave) * (1.0 + 3.0 * GELU_B * square)
    hidden = (activated * up_in).astype(BF16)
    grad_hidden = dot_nt(scaled, down)
    grad_gate_in = (grad_hidden * up_in * slope).astype(BF16)
    grad_up_in = (grad_hidden * activated).astype(BF16)
    grad_buffer = dot_nt(grad_gate_in, gate) + dot_nt(grad_up_in, up)
    return (
        dot(hidden, down),
        grad_buffer,
        dot_tn(buffer, grad_gate_in),
        dot_tn(buffer, grad_up_in),
        dot_tn(hidden, scaled),
    )


def expert_kernel(
    buffer,
    scaled,
    plain,
    gate,
    up,
    down,
    out,
    grad_buffer,
    inner,
    grad_gate,
    grad_up,
    grad_down,
    acc_out,
    acc_grad,
):
    step = pl.program_id(0)

    @pl.when(step == 0)
    def _():
        acc_out[...] = jnp.zeros_like(acc_out)
        acc_grad[...] = jnp.zeros_like(acc_grad)

    more_out, more_grad, d_gate, d_up, d_down = expert_chunk(
        buffer[...], scaled[...], gate[...], up[...], down[...]
    )
    acc_out[...] += more_out
    acc_grad[...] += more_grad
    grad_gate[...] = d_gate.astype(BF16)
    grad_up[...] = d_up.astype(BF16)
    grad_down[...] = d_down.astype(BF16)

    @pl.when(step == pl.num_programs(0) - 1)
    def _():
        low = acc_out[...].astype(BF16)
        out[...] = low
        grad_buffer[...] = acc_grad[...].astype(BF16)
        inner[...] = jnp.broadcast_to(
            jnp.sum(low.astype(F32) * plain[...].astype(F32), axis=1, keepdims=True), inner.shape
        )


def experts(buffer, scaled, plain, gate, up, down):
    rows, width = buffer.shape
    hidden = gate.shape[1]
    whole = pl.BlockSpec((rows, width), lambda j: (0, 0))
    tall = pl.BlockSpec((width, CHUNK), lambda j: (0, j))
    wide = pl.BlockSpec((CHUNK, width), lambda j: (j, 0))
    shapes = (
        jax.ShapeDtypeStruct((rows, width), BF16),
        jax.ShapeDtypeStruct((rows, width), BF16),
        jax.ShapeDtypeStruct((rows, 128), F32),
        jax.ShapeDtypeStruct((width, hidden), BF16),
        jax.ShapeDtypeStruct((width, hidden), BF16),
        jax.ShapeDtypeStruct((hidden, width), BF16),
    )
    return pl.pallas_call(
        expert_kernel,
        out_shape=shapes,
        grid=(hidden // CHUNK,),
        in_specs=[whole, whole, whole, tall, tall, wide],
        out_specs=(whole, whole, pl.BlockSpec((rows, 128), lambda j: (0, 0)), tall, tall, wide),
        scratch_shapes=[pltpu.VMEM((rows, width), F32), pltpu.VMEM((rows, width), F32)],
        compiler_params=pltpu.CompilerParams(
            vmem_limit_bytes=48 * MB, dimension_semantics=("arbitrary",)
        ),
        cost_estimate=pl.CostEstimate(
            flops=18 * rows * width * hidden,
            bytes_accessed=12 * width * hidden,
            transcendentals=rows * hidden,
        ),
    )(buffer, scaled, plain, gate, up, down)


def give_back_kernel(select, out, grad_buffer, inner, gate_column, mixed, grads, inner_rows):
    weighted = (out[...].astype(F32) * gate_column[:, 0:1]).astype(BF16)
    for block in range(select.shape[0]):
        row = jnp.sum(select[block].astype(F32) * inner[:, 0:1], axis=0, keepdims=True)
        inner_rows[block] = jnp.broadcast_to(row, inner_rows.shape[1:])
        grads[block] = dot_tn(select[block], grad_buffer[...]).astype(BF16)
        mixed[block] = dot_tn(select[block], weighted).astype(BF16)


def give_back(select, out, grad_buffer, inner, gate_column):
    blocks, rows, slots = select.shape
    width = out.shape[1]
    wide = (blocks, slots, width)
    return call(
        give_back_kernel,
        (
            jax.ShapeDtypeStruct(wide, BF16),
            jax.ShapeDtypeStruct(wide, BF16),
            jax.ShapeDtypeStruct((blocks, 8, slots), F32),
        ),
        [],
        56 * MB,
        4 * rows * blocks * slots * width,
        select,
        out,
        grad_buffer,
        inner,
        gate_column,
    )


TILE = 2 * CHUNK


def sweep_kernel(
    ready,
    summed,
    buffer,
    scaled,
    plain,
    gate_column,
    select,
    own,
    early,
    down_full,
    sums,
    rest,
    grad_down,
    mixed,
    returned,
    inner_full,
    both,
    down,
    acc_out,
    acc_grad,
    down_stage,
    grads,
    inner_rows,
    loaded,
    stored,
    local,
    swap_send,
    swap_recv,
    *scratch,
):
    tiles, width = both.shape[0], both.shape[1]
    share = own.shape[0]
    coming = tiles - ready
    d, e, z, c = here()

    def columns_of(tile):
        return pl.ds(pl.multiple_of(tile * TILE, TILE), TILE)

    def rows_of(device):
        return pl.ds(pl.multiple_of(device * share, share), share)

    spread = LineSpread(
        lambda j: own.at[:, columns_of(ready + j)],
        lambda j, device: both.at[ready + j, rows_of(device)],
        scratch[:3],
    )
    line = LineSum(
        summed,
        lambda i, k, core: both.at[i, rows_of(2 * flipped(z, k) + core)],
        scratch[3:],
        load=False,
    )
    swap = Swap(grads, returned, swap_send.at[0], swap_recv.at[0], d, e)
    inner_swap = Swap(inner_rows, inner_full, swap_send.at[1], swap_recv.at[1], d, e)
    meet(group(d, e)[1:] + [line.other] + line.to[1:])

    def early_load(t):
        return pltpu.make_async_copy(early.at[:, columns_of(t)], both.at[t], loaded.at[t])

    down_load = pltpu.make_async_copy(down_full, down, loaded.at[tiles])
    for t in range(ready):
        early_load(t).start()
        if t == 0:
            down_load.start()
    for j in range(min(2, coming)):
        spread.start(j)
    acc_out[...] = jnp.zeros_like(acc_out)
    acc_grad[...] = jnp.zeros_like(acc_grad)
    down_load.wait()

    def down_rows(t):
        return pl.ds(pl.multiple_of(t * CHUNK, CHUNK), CHUNK)

    def down_store(t, slot):
        return pltpu.make_async_copy(
            down_stage.at[slot], grad_down.at[down_rows(t)], stored.at[tiles + slot]
        )

    def rest_store(t):
        return pltpu.make_async_copy(both.at[t], rest.at[t - summed], stored.at[t])

    def between(low, value, high):
        return jnp.logical_and(value >= low, value < high)

    def tile_step(t, _):
        @pl.when(t < ready)
        def _():
            early_load(t).wait()

        @pl.when(between(0, t - 2, coming))
        def _():
            spread.relay(t - 2)

        @pl.when(between(2, t, coming))
        def _():
            spread.start(t)

        @pl.when(t >= ready)
        def _():
            spread.complete(t - ready)

        @pl.when(between(0, t - 1, summed))
        def _():
            line.halve(t - 1)

        @pl.when(between(0, t - LAG, summed))
        def _():
            line.relay(t - LAG)

        more_out, more_grad, d_gate, d_up, d_down = expert_chunk(
            buffer[...], scaled[...], both[t, :, :CHUNK], both[t, :, CHUNK:], down[down_rows(t)]
        )
        acc_out[...] += more_out
        acc_grad[...] += more_grad

        @pl.when(t >= ready)
        def _():
            spread.settle(t - ready)

        both[t, :, :CHUNK] = d_gate.astype(BF16)
        both[t, :, CHUNK:] = d_up.astype(BF16)
        slot = lax.rem(t, 2)

        @pl.when(t >= 2)
        def _():
            down_store(t - 2, slot).wait()

        down_stage[slot] = d_down.astype(BF16)
        down_store(t, slot).start()

        @pl.when(t < summed)
        def _():
            line.begin(t)

        @pl.when(t >= summed)
        def _():
            rest_store(t).start()

        return 0

    lax.fori_loop(0, tiles, tile_step, 0)

    low = acc_out[...].astype(BF16)
    inner = jnp.sum(low.astype(F32) * plain[...].astype(F32), axis=1, keepdims=True)
    grad_low = acc_grad[...].astype(BF16)
    order = (3, 1, 2, 0)
    for block in order:
        row = jnp.sum(select[block].astype(F32) * inner, axis=0, keepdims=True)
        inner_rows[block] = jnp.broadcast_to(row, inner_rows.shape[1:])
        grads[block] = dot_tn(select[block], grad_low).astype(BF16)
        if block:
            inner_swap.start(block)
            swap.start(block)
    own_copies = [
        pltpu.make_async_copy(grads.at[0], returned.at[0], local.at[0]),
        pltpu.make_async_copy(inner_rows.at[0], inner_full.at[0], local.at[1]),
    ]
    for copy in own_copies:
        copy.start()
    for i in range(tiles - 1, summed):
        line.halve(i)
    weighted = (low.astype(F32) * gate_column[:, 0:1]).astype(BF16)
    for block in order:
        mixed[block] = dot_tn(select[block], weighted).astype(BF16)

    @pl.loop(max(0, tiles - LAG), summed)
    def _(i):
        line.relay(i)

    @pl.loop(0, summed)
    def _(i):
        sums[i] = line.finish(i)
        line.settle(i)

    for t in range(tiles - 2, tiles):
        down_store(t, t % 2).wait()
    for t in range(summed, tiles):
        rest_store(t).wait()
    for copy in own_copies:
        copy.wait()
    inner_swap.finish()
    swap.finish()


LAG = 4


def sweep(ready, summed, buffer, scaled, plain, gate_column, select, own, early, down_full):
    rows, width = buffer.shape
    tiles = own.shape[1] // TILE
    share = own.shape[0]
    block = (select.shape[0], select.shape[2], width)
    thin = (select.shape[0], 8, select.shape[2])
    hidden = tiles * CHUNK
    shapes = (
        jax.ShapeDtypeStruct((summed, share, TILE), F32),
        jax.ShapeDtypeStruct((max(1, tiles - summed), width, TILE), BF16),
        jax.ShapeDtypeStruct(down_full.shape, BF16),
        jax.ShapeDtypeStruct(block, BF16),
        jax.ShapeDtypeStruct(block, BF16),
        jax.ShapeDtypeStruct(thin, F32),
    )
    scratch = [
        pltpu.VMEM((tiles, width, TILE), BF16),
        pltpu.VMEM(down_full.shape, BF16),
        pltpu.VMEM((rows, width), F32),
        pltpu.VMEM((rows, width), F32),
        pltpu.VMEM((2, CHUNK, width), BF16),
        pltpu.VMEM(block, BF16),
        pltpu.VMEM(thin, F32),
        DMA((tiles + 1,)),
        DMA((tiles + 2,)),
        DMA((2,)),
        DMA((2, 4)),
        DMA((2, 4)),
    ]
    scratch += LineSpread.scratch(tiles - ready) + LineSum.scratch(summed, share, TILE, False)
    return call(
        functools.partial(sweep_kernel, ready, summed),
        shapes,
        scratch,
        62 * MB,
        18 * rows * width * hidden,
        buffer,
        scaled,
        plain,
        gate_column,
        select,
        own,
        early,
        down_full,
        stay=(5, 6, 7),
        land=(1, 2, 4, 5),
        link=2,
    )


def down_source(array, z, share):
    def source(i, k, core):
        row = pl.multiple_of((2 * flipped(z, k) + core) * share, share)
        return array.at[pl.ds(row, share), pl.ds(pl.multiple_of(i * CHUNK, CHUNK), CHUNK)]

    return source


def attention_backward_kernel(fast, experts, down_units, *refs):
    refs = list(refs)

    def take(count):
        taken, refs[:] = refs[:count], refs[count:]
        return taken

    tokens, cotangent, weights, small, heads, hot_back, length, meta, own = take(9)
    returned, inner_rows, mixed, qkv, attended, probs, resid, normed_two = take(8)
    if fast:
        tail, grad_down = take(2)
    output, grad_tokens, grad_weights, grad_small = take(4)
    if fast:
        rest_sums, down_sums = take(2)
    grad_attended, grad_qkv, branch, normed, work, grad_diagonals = take(6)
    slots, width = tokens.shape
    blocks = returned.shape[0]
    if fast:
        mixed_full, send, recv = take(3)
        d, e, z, _ = here()
        share, down_share = width // 8, grad_down.shape[0] // 8

        def rest_source(i, k, core):
            row = pl.multiple_of((2 * flipped(z, k) + core) * share, share)
            return tail.at[i, pl.ds(row, share)]

        rest_line = LineSum(tail.shape[0], rest_source, take(6), True)
        down_line = LineSum(down_units, down_source(grad_down, z, down_share), take(6), True)
        lines = [(rest_line, i) for i in range(tail.shape[0])]
        lines += [(down_line, i) for i in range(down_units)]
        meet(group(d, e)[1:] + [rest_line.other] + rest_line.to[1:])
        for line, i in lines:
            line.begin(i)
        swap = Swap(mixed, mixed_full, send, recv, d, e)
        for block in (3, 1, 2):
            swap.start(block)
        for line, i in lines:
            line.halve(i)
    router_t = small[...].astype(BF16)
    keep_row = lax.broadcasted_iota(jnp.int32, (slots, 1), 0) < length[0, 0]
    logits = dot_nt(router_t, normed_two[...])
    zero_route, one_route = meta[0:1, :], meta[1:2, :]
    gate_zero, gate_one = pair_gates(logits, zero_route, one_route)
    which = lax.broadcasted_iota(jnp.int32, logits.shape, 0)
    grad_zero = jnp.zeros((1, slots), F32)
    grad_one = jnp.zeros((1, slots), F32)
    for block in range(blocks):
        row = inner_rows[block][0:1, :]
        expert = jnp.bitwise_xor(own[0, 0], block) if fast else block
        grad_zero = grad_zero + jnp.where(zero_route == expert, row, 0.0)
        grad_one = grad_one + jnp.where(one_route == expert, row, 0.0)
    shared = gate_zero * grad_zero + gate_one * grad_one
    grad_zero = gate_zero * (grad_zero - shared)
    grad_one = gate_one * (grad_one - shared)
    grad_logits = jnp.where(which == zero_route, grad_zero, 0.0) + jnp.where(
        which == one_route, grad_one, 0.0
    )
    high, rest = two_halves(grad_logits)
    grad_small[...] = dot(high, normed_two[...]) + dot(rest, normed_two[...])
    grad_normed_two = dot_tn(high, router_t) + dot_tn(rest, router_t)
    for block in range(blocks):
        grad_normed_two = grad_normed_two + returned[block].astype(F32)
    r = resid[...]
    inv_two = lax.rsqrt(jnp.mean(r * r, axis=1, keepdims=True) + epsilon)
    unit_two = r * inv_two
    grad_small[experts + 1 : experts + 2, :] = jnp.sum(
        grad_normed_two * unit_two, axis=0, keepdims=True
    )
    scaled_two = small[experts + 1 : experts + 2, :] * grad_normed_two
    grad_resid = jnp.where(keep_row, cotangent[...].astype(F32), 0.0) + inv_two * (
        scaled_two - unit_two * jnp.mean(scaled_two * unit_two, axis=1, keepdims=True)
    )
    work[...] = grad_resid
    branch[...] = grad_resid.astype(BF16)

    @pl.loop(0, width // 256)
    def _(j):
        grad_weights[:, columns(3 * width // 256 + j, 256)] = dot_tn(
            attended[...], branch[:, columns(j, 256)]
        ).astype(BF16)

    grad_attended[...] = dot_nt(branch[...], weights[:, 3 * width : 4 * width]).astype(BF16)

    lane = lax.broadcasted_iota(jnp.int32, (slots, LANES), 1)
    first = lane < HD
    square = (slots, slots)
    flip = (
        lax.broadcasted_iota(jnp.int32, square, 0) + lax.broadcasted_iota(jnp.int32, square, 1)
        == slots - 1
    )
    flip = flip.astype(F32).astype(BF16)

    def attend_back(pair):
        q = qkv[:, columns(pair, LANES)]
        k = qkv[:, columns(PAIRS + pair, LANES)]
        v = qkv[:, columns(2 * PAIRS + pair, LANES)]
        g = grad_attended[:, columns(pair, LANES)]
        dq, dk, dv = [], [], []
        for half in range(2):
            head = 2 * pair + half
            own = first if half == 0 else jnp.logical_not(first)
            low = probs[head]
            p = low.astype(F32)
            grad_probs = dot_nt(jnp.where(own, g, jnp.zeros_like(g)), v)
            ds = p * (grad_probs - jnp.sum(p * grad_probs, axis=1, keepdims=True))
            ds = ds.astype(BF16)
            wide = jnp.concatenate([dot(flip, ds), jnp.zeros((slots, slots), F32)], axis=1)
            skewed = pltpu.roll(wide, 0, 1, stride=1, stride_axis=0)
            grad_diagonals[pl.ds(head, 1), :] = jnp.sum(skewed, axis=0, keepdims=True)
            dq.append(dot(ds, k))
            dk.append(dot_tn(ds, q))
            dv.append(dot_tn(low, g))
        grad_qkv[:, columns(pair, LANES)] = (jnp.where(first, dq[0], dq[1]) * SCALE).astype(BF16)
        grad_qkv[:, columns(PAIRS + pair, LANES)] = (
            jnp.where(first, dk[0], dk[1]) * SCALE
        ).astype(BF16)
        grad_qkv[:, columns(2 * PAIRS + pair, LANES)] = jnp.where(first, dv[0], dv[1]).astype(BF16)

    pl.loop(0, PAIRS // 2)(attend_back)
    if fast:
        for line, i in lines[: len(lines) // 2]:
            line.relay(i)
    pl.loop(PAIRS // 2, PAIRS)(attend_back)
    if fast:
        for line, i in lines[len(lines) // 2 :]:
            line.relay(i)

    x = tokens[...].astype(F32)
    inv_one = lax.rsqrt(jnp.mean(x * x, axis=1, keepdims=True) + epsilon)
    unit_one = x * inv_one
    normed[...] = (unit_one * small[experts : experts + 1, :]).astype(BF16)
    high, rest = two_halves(grad_diagonals[...])
    by_lane = dot_nt(high, hot_back[...]) + dot_nt(rest, hot_back[...])
    grad_small[experts + 2 : experts + 3, :] = jnp.sum(
        by_lane * heads[...].astype(F32), axis=0, keepdims=True
    )

    @pl.loop(0, 3 * width // 256)
    def _(j):
        grad_weights[:, columns(j, 256)] = dot_tn(normed[...], grad_qkv[:, columns(j, 256)]).astype(
            BF16
        )

    grad_normed = dot_nt(grad_qkv[...], weights[:, : 3 * width])
    grad_small[experts : experts + 1, :] = jnp.sum(grad_normed * unit_one, axis=0, keepdims=True)
    scaled_one = small[experts : experts + 1, :] * grad_normed
    grad_tokens[...] = work[...] + inv_one * (
        scaled_one - unit_one * jnp.mean(scaled_one * unit_one, axis=1, keepdims=True)
    )
    if fast:
        for line, i in lines:
            (rest_sums if line is rest_line else down_sums)[i] = line.finish(i)
            line.settle(i)
        swap.finish()
    total = resid[...] + mixed[0].astype(F32)
    for block in range(1, blocks):
        total = total + (mixed_full if fast else mixed)[block].astype(F32)
    output[...] = jnp.where(keep_row, total, 0.0).astype(BF16)


def attention_backward(fast, experts, down_units, *args):
    tokens, small, mixed = args[0], args[3], args[11]
    slots, width = tokens.shape
    shapes = (
        jax.ShapeDtypeStruct((slots, width), BF16),
        jax.ShapeDtypeStruct((slots, width), F32),
        jax.ShapeDtypeStruct((width, 4 * width), BF16),
        jax.ShapeDtypeStruct(small.shape, F32),
    )
    scratch = [
        pltpu.VMEM((slots, width), BF16),
        pltpu.VMEM((slots, 3 * width), BF16),
        pltpu.VMEM((slots, width), BF16),
        pltpu.VMEM((slots, width), BF16),
        pltpu.VMEM((slots, width), F32),
        pltpu.VMEM((HEADS, 2 * slots), F32),
    ]
    options = {}
    if fast:
        rest, grad_down = args[-2:]
        share, down_share = width // 8, grad_down.shape[0] // 8
        shapes += (
            jax.ShapeDtypeStruct((rest.shape[0], share, TILE), F32),
            jax.ShapeDtypeStruct((down_units, down_share, CHUNK), F32),
        )
        scratch += [pltpu.VMEM(mixed.shape, BF16), DMA((4,)), DMA((4,))]
        scratch += LineSum.scratch(rest.shape[0], share, TILE, True)
        scratch += LineSum.scratch(down_units, down_share, CHUNK, True)
        options = dict(link=3, stay=(len(args) - 2, len(args) - 1))
    return call(
        functools.partial(attention_backward_kernel, fast, experts, down_units),
        shapes,
        scratch,
        62 * MB,
        4 * slots * width * (4 * width + 2 * slots),
        *args,
        **options,
    )


def add_up_kernel(
    done,
    partial,
    small,
    grad_down,
    grad_qkv,
    grad_out,
    small_sum,
    down_sums,
    mine,
    theirs,
    first_in,
    second_in,
    planes,
    last_in,
    smalls,
    small_in,
    local,
    send,
    recv,
    small_send,
    small_recv,
    *scratch,
):
    d, e, z, c = here()
    share = grad_qkv.shape[0]
    down_share = grad_down.shape[0] // 8
    whole = down_source(grad_down, z, down_share)
    line = LineSum(
        down_sums.shape[0], lambda i, k, core: whole(done + i, k, core), scratch, True
    )
    units = range(down_sums.shape[0])
    quad = 4 * share
    width = grad_out.shape[1]
    other = (2 * z + 1 - c, e)
    to_x, to_y = (d, flipped(e, 1)), (d, flipped(e, 2))
    to_z = [None] + [(2 * flipped(z, k) + c, e) for k in (1, 2, 3)]
    meet([other, to_x, to_y] + to_z[1:])
    turns = (3, 2, 1, 0)

    def block(k, core):
        row = (2 * flipped(z, k) + core) * quad
        return partial.at[pl.ds(pl.multiple_of(row, quad), quad)]

    def piece(k, q):
        row = flipped(e, q) * share
        return mine.at[k, pl.ds(pl.multiple_of(row, share), share)]

    for i in units:
        line.begin(i)
    loads, from_core, firsts, seconds, lasts = {}, {}, {}, {}, {}
    for k in turns:
        from_core[k] = push(block(k, 1 - c), theirs.at[k], send.at[0, k], recv.at[0, k], other)
        loads[k] = pltpu.make_async_copy(block(k, c), mine.at[k], local.at[k])
        loads[k].start()

    small_to = [other, to_x, to_y, to_z[1], to_z[2]]
    smalls[0] = small[...]
    small_copies = []

    def small_step():
        at = len(small_copies)
        if at:
            small_copies[at - 1].wait_recv()
            smalls[at] = smalls[at - 1] + small_in[at - 1]
        if at < len(small_to):
            small_copies.append(
                push(
                    smalls.at[at],
                    small_in.at[at],
                    small_send.at[at],
                    small_recv.at[at],
                    small_to[at],
                )
            )

    def stage_one(k):
        loads[k].wait()
        from_core[k].wait_recv()

        @pl.loop(0, 4)
        def _(j):
            at = pl.ds(pl.multiple_of(j * share, share), share)
            mine[k, at] = (mine[k, at].astype(F32) + theirs[k, at].astype(F32)).astype(BF16)

        near, to = (1, to_x) if k % 2 == 0 else (2, to_y)
        firsts[k] = [
            push(piece(k, q), first_in.at[k, slot], send.at[1 + slot, k], recv.at[1 + slot, k], to)
            for slot, q in ((1, 3), (0, near))
        ]

    def stage_two(k):
        far, to = (2, to_y) if k % 2 == 0 else (1, to_x)
        for copy in firsts[k]:
            copy.wait_recv()
        source = piece(k, far)
        source[...] = (source[...].astype(F32) + first_in[k, 1].astype(F32)).astype(BF16)
        seconds[k] = push(source, second_in.at[k], send.at[3, k], recv.at[3, k], to)

    def stage_three(k):
        seconds[k].wait_recv()
        total = piece(k, 0)[...].astype(F32) + first_in[k, 0].astype(F32)
        total = total + second_in[k].astype(F32)
        if k:
            planes[k] = total.astype(BF16)
            lasts[k] = push(planes.at[k], last_in.at[k], send.at[4, k], recv.at[4, k], to_z[k])
        else:
            grad_qkv[...] = total[:, : 3 * width]
            grad_out[...] = total[:, 3 * width :]

    a, b, c_, d_ = turns
    small_step()
    for i in units:
        line.halve(i)
    stage_one(a)
    stage_one(b)
    small_step()
    stage_two(a)
    stage_one(c_)
    stage_two(b)
    small_step()
    stage_three(a)
    for i in units[:1]:
        line.relay(i)
    stage_one(d_)
    stage_two(c_)
    small_step()
    stage_three(b)
    stage_two(d_)
    small_step()
    for i in units[1:]:
        line.relay(i)
    stage_three(c_)
    stage_three(d_)
    small_step()
    small_sum[...] = smalls[len(small_to)]
    for k in turns[:-1]:
        lasts[k].wait_recv()
    total = last_in[1].astype(F32) + last_in[2].astype(F32) + last_in[3].astype(F32)
    grad_qkv[...] += total[:, : 3 * width]
    grad_out[...] += total[:, 3 * width :]
    for i in units:
        down_sums[i] = line.finish(i)
        line.settle(i)
    for copies in (from_core, seconds, lasts):
        for copy in copies.values():
            copy.wait_send()
    for pair in firsts.values():
        for copy in pair:
            copy.wait_send()
    for copy in small_copies:
        copy.wait_send()


def add_up(done, partial, small, grad_down):
    width, wide = partial.shape
    share = width // 32
    down_share = grad_down.shape[0] // 8
    left = width // CHUNK - done
    return call(
        functools.partial(add_up_kernel, done),
        (
            jax.ShapeDtypeStruct((share, 3 * width), F32),
            jax.ShapeDtypeStruct((share, width), F32),
            jax.ShapeDtypeStruct(small.shape, F32),
            jax.ShapeDtypeStruct((left, down_share, CHUNK), F32),
        ),
        [
            pltpu.VMEM((4, 4 * share, wide), BF16),
            pltpu.VMEM((4, 4 * share, wide), BF16),
            pltpu.VMEM((4, 2, share, wide), BF16),
            pltpu.VMEM((4, share, wide), BF16),
            pltpu.VMEM((4, share, wide), BF16),
            pltpu.VMEM((4, share, wide), BF16),
            pltpu.VMEM((6,) + small.shape, F32),
            pltpu.VMEM((5,) + small.shape, F32),
            DMA((4,)),
            DMA((5, 4)),
            DMA((5, 4)),
            DMA((5,)),
            DMA((5,)),
            *LineSum.scratch(left, down_share, CHUNK, True),
        ],
        56 * MB,
        0,
        partial,
        small,
        grad_down,
        stay=(0, 2),
        link=4,
    )


READY = 4
SUMMED = 9
DOWN_EARLY = 1


def on_device(
    fast,
    tokens,
    cotangent,
    qkv_weight,
    out_weight,
    router_weight,
    first_gain,
    second_gain,
    bias_table,
    gate_weight,
    up_weight,
    down_weight,
    lengths,
    routes,
    priority,
):
    both = ("dp", "expert")
    slots, width = tokens.shape
    expert_count = lax.axis_size("expert")
    device_count = lax.axis_size("dp") * expert_count
    share, bias_share = first_gain.shape[0], bias_table.shape[0]
    device = lax.axis_index("dp") * expert_count + lax.axis_index("expert")
    own = lax.axis_index("expert").astype(jnp.int32).reshape(1, 1)
    small_rows = -(-(expert_count + 3) // 8) * 8

    def gathered(value, axes, axis=0, tiled=True):
        return lax.all_gather(value, axes, axis=axis, tiled=tiled)

    def scattered(value, axes):
        return lax.psum_scatter(value, axes, scatter_dimension=0, tiled=True).astype(F32)

    def exchanged(value):
        return lax.all_to_all(value, "expert", split_axis=0, concat_axis=0, tiled=True)

    rows_own, hidden = gate_weight.shape[1:]
    down_full = gathered(down_weight[0], "dp")
    if fast:
        tiles = (rows_own, hidden // CHUNK, 1, CHUNK)
        both_own = jnp.concatenate(
            [gate_weight.reshape(tiles), up_weight.reshape(tiles)], axis=2
        ).reshape(rows_own, 2 * hidden)
        early = gathered(both_own[:, : READY * TILE], "dp")
    else:
        gate_full, up_full = (gathered(value[0], "dp") for value in (gate_weight, up_weight))

    beside = jnp.concatenate(
        [
            router_weight,
            first_gain[:, None],
            second_gain[:, None],
            jnp.pad(bias_table, (0, share - bias_share))[:, None],
            jnp.zeros((share, 128 - expert_count - 3), BF16),
        ],
        axis=1,
    )
    weights_own = jnp.concatenate([qkv_weight, out_weight, beside], axis=1)
    lane = np.arange(width)
    flat = lane // share * bias_share + lane % share
    in_table = lane % share < bias_share
    heads = np.arange(HEADS)[:, None] == np.where(in_table, flat // BUCKETS, -1)[None, :]
    heads = jnp.asarray(heads.astype(np.float32), BF16)
    ahead = np.arange(2 * slots)

    def hot(ahead):
        return jnp.asarray(
            np.where(in_table[:, None], diagonal_onehot(ahead)[flat % BUCKETS], 0.0), BF16
        )

    valid_rows = jnp.arange(slots, dtype=jnp.int32) < lengths[0, 0]
    meta_own = jnp.concatenate(
        [
            routes.T,
            priority,
            valid_rows.astype(jnp.int32)[None, :],
            jnp.zeros((4, slots), jnp.int32),
        ],
        axis=0,
    )

    weights = gather_weights(weights_own) if fast else gathered(weights_own, both)
    qkv, attended, probs, resid, normed_two, small, *spread = attention_forward(
        fast,
        expert_count,
        tokens,
        weights,
        heads,
        hot(np.where(ahead < slots, ahead, ahead - 2 * slots)),
        lengths,
        cotangent,
        meta_own,
    )
    if fast:
        rows, cots, meta = spread
    else:
        rows, cots, meta = (
            gathered(value, "expert", tiled=False) for value in (normed_two, cotangent, meta_own)
        )
    buffer, scaled, plain, select, gate_column = dispatch(rows, cots, meta, small, own)
    if fast:
        sums, rest, grad_down, mixed, returned, inner_rows = sweep(
            READY,
            SUMMED,
            buffer,
            scaled,
            plain,
            gate_column,
            select,
            both_own,
            early,
            down_full,
        )
        left = [rest, grad_down]
    else:
        expert_out, grad_buffer, inner, *grad_experts = experts(
            buffer, scaled, plain, gate_full, up_full, down_full
        )
        mixed, returned, inner_rows = (
            exchanged(value)
            for value in give_back(select, expert_out, grad_buffer, inner, gate_column)
        )
        grad_gate, grad_up, grad_down = (scattered(value, "dp")[None] for value in grad_experts)
        left = []
    output, grad_tokens, grad_weights, grad_small, *more = attention_backward(
        fast,
        expert_count,
        DOWN_EARLY,
        tokens,
        cotangent,
        weights,
        small,
        heads,
        hot(ahead - (slots - 1)),
        lengths,
        meta_own,
        own,
        returned,
        inner_rows,
        mixed,
        qkv,
        attended,
        probs,
        resid,
        normed_two,
        *left,
    )
    if fast:
        grad_qkv, grad_out, grad_small, down_late = add_up(
            DOWN_EARLY, grad_weights, grad_small, grad_down
        )
        rest_sums, down_early = more
        tiles = jnp.concatenate([sums, rest_sums], axis=0)
        grad_gate, grad_up = (
            jnp.transpose(tiles[:, :, i * CHUNK : (i + 1) * CHUNK], (1, 0, 2)).reshape(
                1, rows_own, hidden
            )
            for i in range(2)
        )
        tiles = jnp.concatenate([down_early, down_late], axis=0)
        grad_down = jnp.transpose(tiles, (1, 0, 2)).reshape((1,) + down_weight.shape[1:])
    else:
        grad_weights = scattered(grad_weights, both)
        grad_qkv, grad_out = grad_weights[:, : 3 * width], grad_weights[:, 3 * width :]
        grad_small = lax.psum(grad_small, both)
    grad_small = lax.dynamic_slice(grad_small, (0, device * share), (small_rows, share))
    return (
        output,
        grad_tokens,
        grad_qkv,
        grad_out,
        grad_small[:expert_count].T,
        grad_small[expert_count],
        grad_small[expert_count + 1],
        grad_small[expert_count + 2, :bias_share],
        grad_gate,
        grad_up,
        grad_down,
    )


def solution(mesh):
    fast = dict(mesh.shape) == {"dp": 8, "expert": 4}
    rows = P(("dp", "expert"), None)
    flat = P(("dp", "expert"))
    expert = P("expert", "dp", None)
    grid = P("dp", "expert")
    return jax.shard_map(
        functools.partial(on_device, fast),
        mesh=mesh,
        in_specs=(rows,) * 5 + (flat,) * 3 + (expert,) * 3 + (grid, rows, grid),
        out_specs=(rows,) * 5 + (flat,) * 3 + (expert,) * 3,
        check_vma=False,
    )
```

```python
import functools
import math

import jax
import jax.numpy as jnp
import numpy as np
from jax import lax
from jax.experimental import pallas as pl
from jax.experimental.pallas import tpu as pltpu
from jax.sharding import PartitionSpec as P

HEADS = 16
HD = 64
BUCKETS = 32
CAP = 480
PAIRS = HEADS // 2
LANES = 2 * HD

epsilon = 1e-06
masked_value = -1e30
max_distance = 128.0
SCALE = 1.0 / math.sqrt(HD)
MB = 1 << 20
F32 = jnp.float32
BF16 = jnp.bfloat16


def bucket_of(offset, bucket_count):
    halfway = bucket_count // 2
    exact_span = bucket_count // 4
    distance = np.abs(offset)
    log_part = np.log(np.maximum(distance, 1) / float(exact_span)) / np.log(
        max_distance / exact_span
    )
    far_bucket = np.minimum(
        exact_span + np.floor(log_part * exact_span).astype(np.int64), halfway - 1
    )
    inside = np.where(distance < exact_span, distance, far_bucket)
    return np.where(offset < 0, halfway, 0) + inside


def diagonal_onehot(ahead):
    return (bucket_of(-ahead, BUCKETS)[None, :] == np.arange(BUCKETS)[:, None]).astype(np.float32)


def dot(a, b):
    return jnp.dot(a, b, preferred_element_type=F32)


def dot_nt(a, b):
    return lax.dot_general(a, b, (((1,), (1,)), ((), ())), preferred_element_type=F32)


def dot_tn(a, b):
    return lax.dot_general(a, b, (((0,), (0,)), ((), ())), preferred_element_type=F32)


def two_halves(value):
    high = value.astype(BF16)
    return high, (value - high.astype(F32)).astype(BF16)


def columns(index, width):
    return pl.ds(pl.multiple_of(index * width, width), width)


VMEM_SPEC = pl.BlockSpec(memory_space=pltpu.VMEM)


ANY_SPEC = pl.BlockSpec(memory_space=pl.ANY)
MESH = pl.DeviceIdType.MESH
DMA = pltpu.SemaphoreType.DMA


def call(kernel, out_shape, scratch, vmem, flops, *args, stay=(), land=(), link=None, aliases=None):
    nbytes = sum(a.size * a.dtype.itemsize for a in args)
    params = dict(vmem_limit_bytes=vmem)
    if link is not None:
        params.update(collective_id=link, has_side_effects=True)
    return pl.pallas_call(
        kernel,
        out_shape=out_shape,
        in_specs=[ANY_SPEC if i in stay else VMEM_SPEC for i in range(len(args))],
        out_specs=tuple(ANY_SPEC if i in land else VMEM_SPEC for i in range(len(out_shape))),
        scratch_shapes=scratch,
        input_output_aliases=aliases or {},
        compiler_params=pltpu.CompilerParams(**params),
        cost_estimate=pl.CostEstimate(flops=flops, bytes_accessed=nbytes, transcendentals=0),
    )(*args)


def here():
    d, e = lax.axis_index("dp"), lax.axis_index("expert")
    return d, e, d // 2, lax.rem(d, 2)


def flipped(value, bits):
    low, high = lax.rem(value, 2), value // 2
    low = 1 - low if bits & 1 else low
    high = 1 - high if bits & 2 else high
    return 2 * high + low


def meet(partners):
    barrier = pltpu.get_barrier_semaphore()
    for partner in partners:
        pl.semaphore_signal(barrier, inc=1, device_id=partner, device_id_type=MESH)
    pl.semaphore_wait(barrier, len(partners))


def push(src, dst, send, recv, to):
    copy = pltpu.make_async_remote_copy(
        src_ref=src, dst_ref=dst, send_sem=send, recv_sem=recv, device_id=to, device_id_type=MESH
    )
    copy.start()
    return copy


def group(d, e):
    return [None] + [(d, flipped(e, q)) for q in (1, 2, 3)]


class Spread:
    def __init__(self, src, dst, send, recv, d, e):
        self.src, self.dst, self.send, self.recv = src, dst, send, recv
        self.to = group(d, e)
        self.half = src.shape[0] // 2
        self.copies = {}

    def part(self, ref, half):
        return ref.at[pl.ds(half * self.half, self.half)]

    def start(self):
        for turn in range(2):
            for q in (1, 2):
                half = turn if q == 1 else 1 - turn
                at = 2 * (q - 1) + half
                self.copies[q, half] = push(
                    self.part(self.src, half),
                    self.part(self.dst.at[q], half),
                    self.send.at[at],
                    self.recv.at[at],
                    self.to[q],
                )

    def forward(self):
        for q, half, across, at in ((1, 0, 2, 4), (2, 1, 1, 5)):
            self.copies[q, half].wait_recv()
            self.copies[3, half] = push(
                self.part(self.dst.at[q], half),
                self.part(self.dst.at[3], half),
                self.send.at[at],
                self.recv.at[at],
                self.to[across],
            )

    def arrived(self, q):
        for half in {1: (1,), 2: (0,), 3: (0, 1)}[q]:
            self.copies[q, half].wait_recv()

    def sent(self):
        for copy in self.copies.values():
            copy.wait_send()

    def finish(self):
        for q in (1, 2, 3):
            self.arrived(q)
        self.sent()


class Swap:
    def __init__(self, src, dst, send, recv, d, e):
        self.src, self.dst, self.send, self.recv = src, dst, send, recv
        self.to = group(d, e)
        self.copies = {}

    def start(self, q):
        self.copies[q] = push(
            self.src.at[q], self.dst.at[q], self.send.at[q], self.recv.at[q], self.to[q]
        )

    def finish(self):
        for copy in self.copies.values():
            copy.wait_recv()
        for copy in self.copies.values():
            copy.wait_send()


class DeviceGather:
    WAYS = 5

    def __init__(self, full, share, send, recv):
        self.full, self.share, self.send, self.recv = full, share, send, recv
        self.d, self.e, self.z, self.core = d, e, z, c = here()
        self.to_x, self.to_y = (d, flipped(e, 1)), (d, flipped(e, 2))
        self.other = (2 * z + 1 - c, e)
        self.to_z = [None] + [(2 * flipped(z, k) + c, e) for k in (1, 2, 3)]
        self.end = jnp.logical_or(z == 0, z == 3)
        self.middle = jnp.logical_not(self.end)

    def item(self, k, q, core=None):
        device = 2 * flipped(self.z, k) + (self.core if core is None else core)
        row = (device * 4 + flipped(self.e, q)) * self.share
        return self.full.at[pl.ds(pl.multiple_of(row, self.share), self.share)]

    def pass_on(self, k, q, way, at, to, into=None):
        piece = self.item(k, q)
        return pltpu.make_async_remote_copy(
            src_ref=piece,
            dst_ref=piece,
            send_sem=self.send.at[way, at],
            recv_sem=self.recv.at[way, at if into is None else into],
            device_id=to,
            device_id_type=MESH,
        )

    def along_z(self, k):
        return self.pass_on(0, 0, 0, k, self.to_z[k])

    def relay_z(self, k):
        return self.pass_on(k, 0, 0, 2 + k, self.to_z[1], 5 - k)

    def along_x(self, k):
        return self.pass_on(k, 0, 1, k, self.to_x)

    def along_y(self, k):
        return self.pass_on(k, 0, 2, k, self.to_y)

    def across(self, k):
        return self.pass_on(k, 1, 3, k, self.to_y) if k % 2 == 0 else self.pass_on(k, 2, 3, k, self.to_x)

    def over(self, k, q):
        return self.pass_on(k, q, 4, 4 * q + k, self.other)

    def start(self):
        self.along_z(1).start()

        @pl.when(self.middle)
        def _():
            self.along_z(3).start()

        @pl.when(self.end)
        def _():
            self.along_z(2).start()

        self.spread_out(0)

    def spread_out(self, k):
        self.along_x(k).start()
        self.along_y(k).start()
        self.over(k, 0).start()

    def from_z(self, k):
        self.along_z(k).wait_recv()
        if k > 1:

            @pl.when(self.middle)
            def _():
                self.relay_z(k).start()

        self.spread_out(k)

    def from_neighbours(self, k):
        self.along_x(k).wait_recv()
        if k % 2 == 0:
            self.across(k).start()
        self.over(k, 1).start()
        self.along_y(k).wait_recv()
        if k % 2 == 1:
            self.across(k).start()
        self.over(k, 2).start()

    def from_across(self, k):
        self.across(k).wait_recv()
        self.over(k, 3).start()

    def complete(self):
        for q in range(4):
            for k in range(4):
                self.over(k, q).wait_recv()

    def settle(self):
        self.along_z(1).wait_send()

        @pl.when(self.middle)
        def _():
            self.along_z(3).wait_send()
            self.relay_z(2).wait_send()
            self.relay_z(3).wait_send()

        @pl.when(self.end)
        def _():
            self.along_z(2).wait_send()

        for k in range(4):
            self.along_x(k).wait_send()
            self.along_y(k).wait_send()
            self.across(k).wait_send()
            for q in range(4):
                self.over(k, q).wait_send()


class LineSum:
    def __init__(self, count, source, scratch, load):
        self.count, self.source, self.load_first = count, source, load
        scratch = list(scratch)
        self.theirs, self.landed, self.send, self.recv = scratch[:4]
        if load:
            self.loads, self.loaded = scratch[4:]
        self.d, self.e, self.z, self.core = here()
        self.other = (2 * self.z + 1 - self.core, self.e)
        self.to = [None] + [(2 * flipped(self.z, k) + self.core, self.e) for k in (1, 2, 3)]
        self.end = jnp.logical_or(self.z == 0, self.z == 3)
        self.middle = jnp.logical_not(self.end)

    @staticmethod
    def scratch(count, rows, width, load):
        part = (rows, width)
        parts = [
            pltpu.VMEM((count, 4) + part, BF16),
            pltpu.VMEM((count, 5) + part, BF16),
            DMA((count, 3, 5)),
            DMA((count, 3, 5)),
        ]
        return parts + ([pltpu.VMEM((count, 4) + part, BF16), DMA((count, 4))] if load else [])

    def remote(self, i, src, dst, stage, out, into, to):
        return pltpu.make_async_remote_copy(
            src_ref=src,
            dst_ref=dst,
            send_sem=self.send.at[i, stage, out],
            recv_sem=self.recv.at[i, stage, into],
            device_id=to,
            device_id_type=MESH,
        )

    def load(self, i, k):
        return pltpu.make_async_copy(
            self.source(i, k, self.core), self.loads.at[i, k], self.loaded.at[i, k]
        )

    def swap(self, i, k):
        src = self.source(i, k, 1 - self.core)
        return self.remote(i, src, self.theirs.at[i, k], 0, k, k, self.other)

    def hand(self, i, k):
        at = 1 if k == 1 else 5 - k
        return self.remote(i, self.theirs.at[i, k], self.landed.at[i, at], 1, k, at, self.to[1])

    def handed(self, i, at):
        return self.remote(i, self.theirs.at[i, at], self.landed.at[i, at], 1, at, at, self.to[1])

    def deliver(self, i, k):
        at = 0 if k == 3 else 4
        return self.remote(i, self.theirs.at[i, k], self.landed.at[i, at], 2, k, at, self.to[3])

    def for_partner(self, i):
        return self.remote(i, self.theirs.at[i, 0], self.landed.at[i, 4], 2, 4, 4, self.to[3])

    def last(self, i):
        return self.remote(i, self.theirs.at[i, 1], self.landed.at[i, 0], 2, 0, 0, self.to[1])

    def add(self, i, k, more):
        self.theirs[i, k] = (self.theirs[i, k].astype(F32) + more[...].astype(F32)).astype(BF16)

    def begin(self, i):
        for k in (3, 2, 1, 0):
            self.swap(i, k).start()
            if self.load_first:
                self.load(i, k).start()

    def halve(self, i):
        for k in (3, 2, 1, 0):
            if self.load_first:
                self.load(i, k).wait()
            self.swap(i, k).wait_recv()
            self.add(i, k, self.loads.at[i, k] if self.load_first else self.source(i, k, self.core))
        self.hand_over(i)

    def hand_over(self, i):
        @pl.when(self.end)
        def _():
            for k in (3, 2, 1):
                self.hand(i, k).start()

    def relay(self, i):
        @pl.when(self.middle)
        def _():
            for k in (2, 3):
                self.handed(i, k).wait_recv()
                self.add(i, k, self.landed.at[i, k])
                self.deliver(i, k).start()

    def pass_on(self, i):
        @pl.when(self.middle)
        def _():
            self.for_partner(i).wait_recv()
            self.add(i, 1, self.landed.at[i, 4])
            self.last(i).start()

    def finish(self, i, out):
        self.last(i).wait_recv()
        out[...] = self.theirs[i, 0].astype(F32) + self.landed[i, 0].astype(F32)
        if self.source is not None:
            for k in range(4):
                self.swap(i, k).wait_send()

        @pl.when(self.end)
        def _():
            for k in (3, 2, 1):
                self.hand(i, k).wait_send()

        @pl.when(self.middle)
        def _():
            self.handed(i, 1).wait_recv()
            out[...] += self.landed[i, 1].astype(F32)
            self.deliver(i, 2).wait_send()
            self.deliver(i, 3).wait_send()
            self.last(i).wait_send()


class LineSpread:
    def __init__(self, halves, place, scratch):
        self.halves, self.place = halves, place
        self.copied, self.send, self.recv = scratch
        self.d, self.e, self.z, self.core = here()
        self.other = (2 * self.z + 1 - self.core, self.e)
        self.to = [None] + [(2 * flipped(self.z, k) + self.core, self.e) for k in (1, 2, 3)]
        self.end = jnp.logical_or(self.z == 0, self.z == 3)
        self.middle = jnp.logical_not(self.end)

    @staticmethod
    def scratch(count):
        return [DMA((count,)), DMA((count, 9)), DMA((count, 8))]

    def from_chip(self, j, k, core=None):
        return self.place(j, 2 * flipped(self.z, k) + (self.core if core is None else core))

    def remote(self, j, src, dst, out, into, to):
        return pltpu.make_async_remote_copy(
            src_ref=src,
            dst_ref=dst,
            send_sem=self.send.at[j, out],
            recv_sem=self.recv.at[j, into],
            device_id=to,
            device_id_type=MESH,
        )

    def parts(self, j):
        piece = self.place(j, self.d)
        width = piece.shape[1] // 2
        for i, half in enumerate(self.halves(j)):
            yield half, piece.at[:, i * width : (i + 1) * width]

    def keep(self, j):
        piece = self.place(j, self.d)
        return pltpu.make_async_copy(piece, piece, self.copied.at[j])

    def first(self, j, way):
        piece = self.place(j, self.d)
        return self.remote(j, piece, piece, *self.way(way))

    def way(self, way):
        return min(way, 2), 4 if way == 0 else way, self.to[way] if way else self.other

    def send_own(self, j, way):
        for src, dst in self.parts(j):
            self.remote(j, src, dst, *self.way(way)).start()

    def share(self, j, k):
        piece = self.from_chip(j, k)
        return self.remote(j, piece, piece, 2 + k, 4 + k, self.other)

    def pass_on(self, j, k):
        piece = self.from_chip(j, k)
        return self.remote(j, piece, piece, 4 + k, 5 - k, self.to[1])

    def arrival(self, j, k):
        piece = self.from_chip(j, k)
        return self.remote(j, piece, piece, k, k, self.to[1])

    def shared(self, j, k):
        piece = self.from_chip(j, k, 1 - self.core)
        return self.remote(j, piece, piece, 4 + k if k else 0, 4 + k, self.other)

    def across(self, j):
        piece = self.from_chip(j, 1)
        return self.remote(j, piece, piece, 8, 2, self.to[3])

    def start(self, j):
        self.send_own(j, 1)

        @pl.when(self.middle)
        def _():
            self.send_own(j, 3)

        self.send_own(j, 0)
        for src, dst in self.parts(j):
            pltpu.make_async_copy(src, dst, self.copied.at[j]).start()

    def relay_near(self, j):
        self.arrival(j, 1).wait_recv()

        @pl.when(self.middle)
        def _():
            self.across(j).start()

        self.share(j, 1).start()

    def relay_far(self, j):
        for k in (3, 2):
            self.arrival(j, k).wait_recv()

            @pl.when(self.middle)
            def _():
                self.pass_on(j, k).start()

            self.share(j, k).start()

    def complete(self, j):
        self.keep(j).wait()
        for k in range(4):
            self.shared(j, k).wait_recv()

    def settle(self, j):
        self.first(j, 0).wait_send()
        self.first(j, 1).wait_send()

        @pl.when(self.middle)
        def _():
            self.first(j, 3).wait_send()
            self.across(j).wait_send()
            self.pass_on(j, 2).wait_send()
            self.pass_on(j, 3).wait_send()

        for k in (1, 2, 3):
            self.share(j, k).wait_send()


def pair_gates(logits, route_zero, route_one):
    experts = logits.shape[0]
    which = lax.broadcasted_iota(jnp.int32, logits.shape, 0)
    zero = jnp.sum(jnp.where(which == route_zero, logits, 0.0), axis=0, keepdims=True)
    one = jnp.sum(jnp.where(which == route_one, logits, 0.0), axis=0, keepdims=True)
    top = jnp.maximum(zero, one)
    zero, one = jnp.exp(zero - top), jnp.exp(one - top)
    total = zero + one
    return zero / total, one / total


class Dispatch:
    def __init__(self, expert, meta, rank, places):
        self.expert, self.meta, self.rank, self.places = expert, meta, rank, places
        self.blocks, _, self.slots = meta.shape

    def names(self, block):
        info = self.meta[block]
        valid = info[3:4, :] > 0
        zero = jnp.logical_and(valid, info[0:1, :] == self.expert)
        one = jnp.logical_and(valid, info[1:2, :] == self.expert)
        return info, zero, one

    def find_places(self):
        row_of = lax.broadcasted_iota(jnp.int32, (16, self.slots), 0)
        total_zero = jnp.zeros((1, 1), F32)
        for block in range(self.blocks):
            _, zero, _ = self.names(block)
            total_zero = total_zero + jnp.sum(zero.astype(F32), axis=1, keepdims=True)
            self.rank[block] = jnp.transpose(self.meta[block].astype(F32))

        def block_places(block, _):
            info, zero, one = self.names(block)
            mine = info[2:3, :].astype(F32)

            def earlier(other, counts):
                _, other_zero, other_one = self.names(other)
                marks = jnp.where(row_of == 0, other_zero.astype(F32), 0.0) + jnp.where(
                    row_of == 1, other_one.astype(F32), 0.0
                )
                before = (self.rank[other][:, 2:3] < mine).astype(F32).astype(BF16)
                return counts + dot(marks.astype(BF16), before)

            counts = lax.fori_loop(0, self.blocks, earlier, jnp.zeros((16, self.slots), F32))
            place = jnp.where(
                zero, counts[0:1, :], jnp.where(one, counts[1:2, :] + total_zero, -1.0)
            ).astype(jnp.int32)
            self.places[block] = jnp.broadcast_to(place, self.places.shape[1:])
            return 0

        lax.fori_loop(0, self.blocks, block_places, 0)

    def hot(self, block):
        return lax.broadcasted_iota(jnp.int32, (CAP, self.slots), 0) == self.places[block][0:1, :]

    def gates(self, block, rows, router_t):
        info, zero, one = self.names(block)
        gate_zero, gate_one = pair_gates(dot_nt(router_t, rows), info[0:1, :], info[1:2, :])
        gate = jnp.where(zero, gate_zero, jnp.where(one, gate_one, 0.0))
        return jnp.sum(jnp.where(self.hot(block), gate, 0.0), axis=1, keepdims=True)


def attend_forward(experts, tokens, weights, heads, hot, length, out, between):
    qkv, attended, probs, resid, normed_two, small, normed, diagonals = out
    slots, width = tokens.shape
    small[...] = jnp.transpose(weights[:, 4 * width :].astype(F32))[: small.shape[0], :]
    x = tokens[...].astype(F32)
    inv_one = lax.rsqrt(jnp.mean(x * x, axis=1, keepdims=True) + epsilon)
    normed[...] = (x * inv_one * small[experts : experts + 1, :]).astype(BF16)
    spread_bias = heads[...].astype(F32) * small[experts + 2 : experts + 3, :]
    diagonals[...] = dot(spread_bias.astype(BF16), hot[...])

    @pl.loop(0, 3 * width // 512)
    def _(j):
        qkv[:, columns(j, 512)] = dot(normed[...], weights[:, columns(j, 512)]).astype(BF16)

    lane = lax.broadcasted_iota(jnp.int32, (slots, LANES), 1)
    first = lane < HD
    live = lax.broadcasted_iota(jnp.int32, (slots, slots), 1) < length[0, 0]

    def attend(pair):
        q = qkv[:, columns(pair, LANES)]
        k = qkv[:, columns(PAIRS + pair, LANES)]
        v = qkv[:, columns(2 * PAIRS + pair, LANES)]
        outs = []
        for half in range(2):
            head = 2 * pair + half
            own = first if half == 0 else jnp.logical_not(first)
            row = jnp.broadcast_to(diagonals[pl.ds(head, 1), :], (slots, 2 * slots))
            bias = pltpu.roll(row, 0, 1, stride=1, stride_axis=0)[:, :slots]
            scores = dot_nt(jnp.where(own, q, jnp.zeros_like(q)), k) * SCALE + bias
            scores = jnp.where(live, scores, masked_value)
            exponent = jnp.exp(scores - jnp.max(scores, axis=1, keepdims=True))
            low = (exponent / jnp.sum(exponent, axis=1, keepdims=True)).astype(BF16)
            probs[head] = low
            outs.append(dot(low, v))
        attended[:, columns(pair, LANES)] = jnp.where(first, outs[0], outs[1]).astype(BF16)

    pl.loop(0, PAIRS // 2)(attend)
    between()
    pl.loop(PAIRS // 2, PAIRS)(attend)

    @pl.loop(0, width // 512)
    def _(j):
        resid[:, columns(j, 512)] = tokens[:, columns(j, 512)].astype(F32) + dot(
            attended[...], weights[:, columns(3 * width // 512 + j, 512)]
        )

    r = resid[...]
    inv_two = lax.rsqrt(jnp.mean(r * r, axis=1, keepdims=True) + epsilon)
    normed_two[...] = (r * inv_two * small[experts + 1 : experts + 2, :]).astype(BF16)


def attention_forward_kernel(
    experts,
    tokens,
    weights,
    heads,
    hot,
    length,
    qkv,
    attended,
    probs,
    resid,
    normed_two,
    small,
    *scratch,
):
    out = (qkv, attended, probs, resid, normed_two, small) + scratch
    attend_forward(experts, tokens, weights, heads, hot, length, out, lambda: None)


def attention_shapes(experts, tokens):
    slots, width = tokens.shape
    return (
        jax.ShapeDtypeStruct((slots, 3 * width), BF16),
        jax.ShapeDtypeStruct((slots, width), BF16),
        jax.ShapeDtypeStruct((HEADS, slots, slots), BF16),
        jax.ShapeDtypeStruct((slots, width), F32),
        jax.ShapeDtypeStruct((slots, width), BF16),
        jax.ShapeDtypeStruct((-(-(experts + 3) // 8) * 8, width), F32),
    )


def attention_forward(experts, tokens, weights, heads, hot, length):
    slots, width = tokens.shape
    return call(
        functools.partial(attention_forward_kernel, experts),
        attention_shapes(experts, tokens),
        [pltpu.VMEM((slots, width), BF16), pltpu.VMEM((HEADS, 2 * slots), F32)],
        48 * MB,
        2 * slots * width * (4 * width + 2 * slots),
        tokens,
        weights,
        heads,
        hot,
        length,
    )


def dispatch_kernel(
    rows, cots, meta, small, own, buffer, scaled, plain, select, gate_column, acc, acc_cot, rank, places
):
    work = Dispatch(own[0, 0], meta, rank, places)
    work.find_places()
    acc[...] = jnp.zeros_like(acc)
    acc_cot[...] = jnp.zeros_like(acc_cot)
    gate_column[...] = jnp.zeros_like(gate_column)
    router_t = small[...].astype(BF16)
    for block in range(work.blocks):
        picked = work.hot(block).astype(F32).astype(BF16)
        select[block] = picked
        gate_column[...] += work.gates(block, rows[block], router_t)
        acc[...] += dot(picked, rows[block])
        acc_cot[...] += dot(picked, cots[block])
    buffer[...] = acc[...].astype(BF16)
    plain[...] = acc_cot[...].astype(BF16)
    scaled[...] = (acc_cot[...] * gate_column[:, 0:1]).astype(BF16)


def dispatch_shapes(blocks, slots, width):
    return (
        jax.ShapeDtypeStruct((CAP, width), BF16),
        jax.ShapeDtypeStruct((CAP, width), BF16),
        jax.ShapeDtypeStruct((CAP, width), BF16),
        jax.ShapeDtypeStruct((blocks, CAP, slots), BF16),
        jax.ShapeDtypeStruct((CAP, 128), F32),
    )


def dispatch_scratch(blocks, slots, width):
    return [
        pltpu.VMEM((CAP, width), F32),
        pltpu.VMEM((CAP, width), F32),
        pltpu.VMEM((blocks, slots, 8), F32),
        pltpu.VMEM((blocks, 8, slots), jnp.int32),
    ]


def dispatch(rows, cots, meta, small, own):
    blocks, slots, width = rows.shape
    return call(
        dispatch_kernel,
        dispatch_shapes(blocks, slots, width),
        dispatch_scratch(blocks, slots, width),
        60 * MB,
        4 * CAP * blocks * slots * width,
        rows,
        cots,
        meta,
        small,
        own,
    )


def forward_kernel(
    experts,
    tokens,
    heads,
    hot,
    length,
    cotangent,
    meta,
    qkv_own,
    out_own,
    beside,
    qkv,
    attended,
    probs,
    resid,
    normed_two,
    small,
    buffer,
    scaled,
    plain,
    select,
    gate_column,
    kept,
    acc,
    acc_cot,
    rank,
    places,
    weights,
    rows,
    cots,
    metas,
    normed,
    diagonals,
    local,
    send,
    recv,
    gather_send,
    gather_recv,
):
    d, e, z, c = here()
    slots, width = tokens.shape
    share = qkv_own.shape[0]
    gather = DeviceGather(weights, share, gather_send, gather_recv)
    rows_spread = Spread(normed_two, rows, send.at[0], recv.at[0], d, e)
    cots_spread = Spread(cotangent, cots, send.at[1], recv.at[1], d, e)
    work = Dispatch(e, metas, rank, places)

    mine = gather.item(0, 0)
    own_parts = [
        pltpu.make_async_copy(part, mine.at[:, start : start + part.shape[1]], local.at[i])
        for i, (part, start) in enumerate(((qkv_own, 0), (out_own, 3 * width), (beside, 4 * width)))
    ]
    own_cots = pltpu.make_async_copy(cotangent, cots.at[0], local.at[3])
    for copy in own_parts:
        copy.start()
    meet(group(d, e)[1:] + [gather.other] + gather.to_z[1:])
    meta_copies = [
        push(meta, metas.at[q], send.at[2, q], recv.at[2, q], group(d, e)[q]) for q in (1, 2, 3)
    ]
    for copy in own_parts:
        copy.wait()
    gather.start()
    own_cots.start()
    metas[0] = meta[...]
    for copy in meta_copies:
        copy.wait_recv()
    work.find_places()
    for k in (1, 3, 2):
        gather.from_z(k)
        if k == 3:
            gather.from_neighbours(0)
    for k in (1, 3, 2):
        gather.from_neighbours(k)
    cots_spread.start()
    for k in (0, 1, 3, 2):
        gather.from_across(k)
    gather.complete()
    keep = pltpu.make_async_copy(weights, kept, local.at[4])
    keep.start()

    out = (qkv, attended, probs, resid, normed_two, small, normed, diagonals)
    attend_forward(experts, tokens, weights, heads, hot, length, out, cots_spread.forward)

    rows_spread.start()
    own_cots.wait()
    cots_spread.finish()
    router_t = small[...].astype(BF16)

    def take_cots(block):
        picked = work.hot(block).astype(F32).astype(BF16)
        select[block] = picked
        more = dot(picked, cots[block])
        if block:
            acc_cot[...] += more
        else:
            acc_cot[...] = more

    def take_rows(block, ref):
        gate = work.gates(block, ref[...], router_t)
        more = dot(select[block], ref[...])
        if block:
            gate_column[...] += gate
            acc[...] += more
        else:
            gate_column[...] = jnp.broadcast_to(gate, gate_column.shape)
            acc[...] = more

    take_cots(0)
    take_cots(1)
    rows_spread.forward()
    take_cots(2)
    take_cots(3)
    plain[...] = acc_cot[...].astype(BF16)
    take_rows(0, normed_two)
    rows_spread.arrived(1)
    take_rows(1, rows.at[1])
    rows_spread.arrived(2)
    take_rows(2, rows.at[2])
    rows_spread.arrived(3)
    take_rows(3, rows.at[3])
    buffer[...] = acc[...].astype(BF16)
    scaled[...] = (acc_cot[...] * gate_column[:, 0:1]).astype(BF16)
    rows_spread.sent()
    gather.settle()
    for copy in meta_copies:
        copy.wait_send()
    keep.wait()


def forward(experts, tokens, heads, hot, length, cotangent, meta, qkv_own, out_own, beside):
    slots, width = tokens.shape
    full = (32 * qkv_own.shape[0], 4 * width + beside.shape[1])
    block = (experts, slots, width)
    scratch = dispatch_scratch(*block) + [
        pltpu.VMEM(full, BF16),
        pltpu.VMEM(block, BF16),
        pltpu.VMEM(block, BF16),
        pltpu.VMEM((experts,) + meta.shape, jnp.int32),
        pltpu.VMEM((slots, width), BF16),
        pltpu.VMEM((HEADS, 2 * slots), F32),
        DMA((5,)),
        DMA((3, 6)),
        DMA((3, 6)),
        DMA((5, 16)),
        DMA((5, 16)),
    ]
    shapes = attention_shapes(experts, tokens) + dispatch_shapes(*block)
    return call(
        functools.partial(forward_kernel, experts),
        shapes + (jax.ShapeDtypeStruct(full, BF16),),
        scratch,
        60 * MB,
        2 * slots * width * (4 * width + 2 * slots),
        tokens,
        heads,
        hot,
        length,
        cotangent,
        meta,
        qkv_own,
        out_own,
        beside,
        stay=(4, 6, 7, 8),
        land=(len(shapes),),
        link=0,
    )


CHUNK = 256
GELU_A = math.sqrt(2.0 / math.pi)
GELU_B = 0.044715


def expert_chunk(buffer, scaled, gate, up, down):
    gate_in, up_in = dot(buffer, gate), dot(buffer, up)
    square = gate_in * gate_in
    wave = jnp.tanh(GELU_A * gate_in * (1.0 + GELU_B * square))
    half = 0.5 * (1.0 + wave)
    activated = gate_in * half
    slope = half + (0.5 * GELU_A) * gate_in * (1.0 - wave * wave) * (1.0 + 3.0 * GELU_B * square)
    hidden = (activated * up_in).astype(BF16)
    grad_hidden = dot_nt(scaled, down)
    grad_gate_in = (grad_hidden * up_in * slope).astype(BF16)
    grad_up_in = (grad_hidden * activated).astype(BF16)
    grad_buffer = dot_nt(grad_gate_in, gate) + dot_nt(grad_up_in, up)
    return (
        dot(hidden, down),
        grad_buffer,
        dot_tn(buffer, grad_gate_in),
        dot_tn(buffer, grad_up_in),
        dot_tn(hidden, scaled),
    )


def expert_kernel(
    buffer,
    scaled,
    plain,
    gate,
    up,
    down,
    out,
    grad_buffer,
    inner,
    grad_gate,
    grad_up,
    grad_down,
    acc_out,
    acc_grad,
):
    step = pl.program_id(0)

    @pl.when(step == 0)
    def _():
        acc_out[...] = jnp.zeros_like(acc_out)
        acc_grad[...] = jnp.zeros_like(acc_grad)

    more_out, more_grad, d_gate, d_up, d_down = expert_chunk(
        buffer[...], scaled[...], gate[...], up[...], down[...]
    )
    acc_out[...] += more_out
    acc_grad[...] += more_grad
    grad_gate[...] = d_gate.astype(BF16)
    grad_up[...] = d_up.astype(BF16)
    grad_down[...] = d_down.astype(BF16)

    @pl.when(step == pl.num_programs(0) - 1)
    def _():
        low = acc_out[...].astype(BF16)
        out[...] = low
        grad_buffer[...] = acc_grad[...].astype(BF16)
        inner[...] = jnp.broadcast_to(
            jnp.sum(low.astype(F32) * plain[...].astype(F32), axis=1, keepdims=True), inner.shape
        )


def experts(buffer, scaled, plain, gate, up, down):
    rows, width = buffer.shape
    hidden = gate.shape[1]
    whole = pl.BlockSpec((rows, width), lambda j: (0, 0))
    tall = pl.BlockSpec((width, CHUNK), lambda j: (0, j))
    wide = pl.BlockSpec((CHUNK, width), lambda j: (j, 0))
    shapes = (
        jax.ShapeDtypeStruct((rows, width), BF16),
        jax.ShapeDtypeStruct((rows, width), BF16),
        jax.ShapeDtypeStruct((rows, 128), F32),
        jax.ShapeDtypeStruct((width, hidden), BF16),
        jax.ShapeDtypeStruct((width, hidden), BF16),
        jax.ShapeDtypeStruct((hidden, width), BF16),
    )
    return pl.pallas_call(
        expert_kernel,
        out_shape=shapes,
        grid=(hidden // CHUNK,),
        in_specs=[whole, whole, whole, tall, tall, wide],
        out_specs=(whole, whole, pl.BlockSpec((rows, 128), lambda j: (0, 0)), tall, tall, wide),
        scratch_shapes=[pltpu.VMEM((rows, width), F32), pltpu.VMEM((rows, width), F32)],
        compiler_params=pltpu.CompilerParams(
            vmem_limit_bytes=48 * MB, dimension_semantics=("arbitrary",)
        ),
        cost_estimate=pl.CostEstimate(
            flops=18 * rows * width * hidden,
            bytes_accessed=12 * width * hidden,
            transcendentals=rows * hidden,
        ),
    )(buffer, scaled, plain, gate, up, down)


def give_back_kernel(select, out, grad_buffer, inner, gate_column, mixed, grads, inner_rows):
    weighted = (out[...].astype(F32) * gate_column[:, 0:1]).astype(BF16)
    for block in range(select.shape[0]):
        row = jnp.sum(select[block].astype(F32) * inner[:, 0:1], axis=0, keepdims=True)
        inner_rows[block] = jnp.broadcast_to(row, inner_rows.shape[1:])
        grads[block] = dot_tn(select[block], grad_buffer[...]).astype(BF16)
        mixed[block] = dot_tn(select[block], weighted).astype(BF16)


def give_back(select, out, grad_buffer, inner, gate_column):
    blocks, rows, slots = select.shape
    width = out.shape[1]
    wide = (blocks, slots, width)
    return call(
        give_back_kernel,
        (
            jax.ShapeDtypeStruct(wide, BF16),
            jax.ShapeDtypeStruct(wide, BF16),
            jax.ShapeDtypeStruct((blocks, 8, slots), F32),
        ),
        [],
        56 * MB,
        4 * rows * blocks * slots * width,
        select,
        out,
        grad_buffer,
        inner,
        gate_column,
    )


TILE = 2 * CHUNK


def sweep_kernel(
    ready,
    buffer,
    scaled,
    plain,
    gate_column,
    select,
    gate_own,
    up_own,
    early,
    down_full,
    gate_sum,
    up_sum,
    grad_down,
    mixed,
    returned,
    inner_full,
    sums,
    both,
    down,
    acc_out,
    acc_grad,
    down_stage,
    grads,
    inner_rows,
    loaded,
    stored,
    local,
    swap_send,
    swap_recv,
    *scratch,
):
    tiles, width = both.shape[0], both.shape[1]
    share = gate_own.shape[0]
    coming = tiles - ready
    d, e, z, c = here()

    def columns_of(tile):
        return pl.ds(pl.multiple_of(tile * TILE, TILE), TILE)

    def rows_of(device):
        return pl.ds(pl.multiple_of(device * share, share), share)

    spread = LineSpread(
        lambda j: [own.at[:, columns(ready + j, CHUNK)] for own in (gate_own, up_own)],
        lambda j, device: both.at[ready + j, rows_of(device)],
        scratch[:3],
    )
    line = LineSum(
        tiles,
        lambda i, k, core: both.at[i, rows_of(2 * flipped(z, k) + core)],
        scratch[3:],
        load=False,
    )
    swap = Swap(grads, returned, swap_send.at[0], swap_recv.at[0], d, e)
    inner_swap = Swap(inner_rows, inner_full, swap_send.at[1], swap_recv.at[1], d, e)
    meet(group(d, e)[1:] + [line.other] + line.to[1:])

    def early_load(t):
        return pltpu.make_async_copy(early.at[:, columns_of(t)], both.at[t], loaded.at[t])

    down_load = pltpu.make_async_copy(down_full, down, loaded.at[tiles])
    for t in range(ready):
        early_load(t).start()
        if t == 0:
            down_load.start()
    for j in range(min(DEPTH, coming)):
        spread.start(j)
    acc_out[...] = jnp.zeros_like(acc_out)
    acc_grad[...] = jnp.zeros_like(acc_grad)
    down_load.wait()

    def down_rows(t):
        return pl.ds(pl.multiple_of(t * CHUNK, CHUNK), CHUNK)

    def down_store(t, slot):
        return pltpu.make_async_copy(
            down_stage.at[slot], grad_down.at[down_rows(t)], stored.at[slot]
        )

    def between(low, value, high):
        return jnp.logical_and(value >= low, value < high)

    def tile_step(t, _):
        @pl.when(t < ready)
        def _():
            early_load(t).wait()

        near = t - ready + NEAR

        @pl.when(between(0, near, coming))
        def _():
            spread.relay_near(near)

        @pl.when(between(0, near - 1, coming))
        def _():
            spread.relay_far(near - 1)

        @pl.when(between(DEPTH, near - 1 + DEPTH, coming))
        def _():
            spread.start(near - 1 + DEPTH)

        @pl.when(t >= ready)
        def _():
            spread.complete(t - ready)

        @pl.when(t >= 1)
        def _():
            line.halve(t - 1)

        @pl.when(t >= LAG)
        def _():
            line.relay(t - LAG)

        @pl.when(t >= LAG + 1)
        def _():
            line.pass_on(t - LAG - 1)

        more_out, more_grad, d_gate, d_up, d_down = expert_chunk(
            buffer[...], scaled[...], both[t, :, :CHUNK], both[t, :, CHUNK:], down[down_rows(t)]
        )
        acc_out[...] += more_out
        acc_grad[...] += more_grad

        @pl.when(t >= ready)
        def _():
            spread.settle(t - ready)

        both[t, :, :CHUNK] = d_gate.astype(BF16)
        both[t, :, CHUNK:] = d_up.astype(BF16)
        slot = lax.rem(t, 2)

        @pl.when(t >= 2)
        def _():
            down_store(t - 2, slot).wait()

        down_stage[slot] = d_down.astype(BF16)
        down_store(t, slot).start()
        line.begin(t)
        return 0

    lax.fori_loop(0, tiles, tile_step, 0)

    low = acc_out[...].astype(BF16)
    inner = jnp.sum(low.astype(F32) * plain[...].astype(F32), axis=1, keepdims=True)
    grad_low = acc_grad[...].astype(BF16)
    order = (3, 1, 2, 0)
    for block in order:
        row = jnp.sum(select[block].astype(F32) * inner, axis=0, keepdims=True)
        inner_rows[block] = jnp.broadcast_to(row, inner_rows.shape[1:])
        grads[block] = dot_tn(select[block], grad_low).astype(BF16)
        if block:
            inner_swap.start(block)
            swap.start(block)
    own_copies = [
        pltpu.make_async_copy(grads.at[0], returned.at[0], local.at[0]),
        pltpu.make_async_copy(inner_rows.at[0], inner_full.at[0], local.at[1]),
    ]
    for copy in own_copies:
        copy.start()
    line.halve(tiles - 1)
    weighted = (low.astype(F32) * gate_column[:, 0:1]).astype(BF16)
    for block in order:
        mixed[block] = dot_tn(select[block], weighted).astype(BF16)

    @pl.loop(tiles - LAG, tiles + 1)
    def _(i):
        @pl.when(i < tiles)
        def _():
            line.relay(i)

        line.pass_on(i - 1)

    @pl.loop(0, tiles)
    def _(i):
        line.finish(i, sums.at[i])
        for copy in result_stores(sums.at[i], gate_sum, up_sum, i, local.at[2]):
            copy.start()

    @pl.loop(0, tiles)
    def _(i):
        for copy in result_stores(sums.at[i], gate_sum, up_sum, i, local.at[2]):
            copy.wait()

    for t in range(tiles - 2, tiles):
        down_store(t, t % 2).wait()
    for copy in own_copies:
        copy.wait()
    inner_swap.finish()
    swap.finish()


def result_stores(value, gate_sum, up_sum, tile, sem):
    return [
        pltpu.make_async_copy(
            value.at[:, i * CHUNK : (i + 1) * CHUNK], array.at[:, columns(tile, CHUNK)], sem
        )
        for i, array in enumerate((gate_sum, up_sum))
    ]


LAG = 5

DEPTH = 6
NEAR = 2


def sweep(ready, buffer, scaled, plain, gate_column, select, gate_own, up_own, early, down_full):
    rows, width = buffer.shape
    tiles = gate_own.shape[1] // CHUNK
    share = gate_own.shape[0]
    block = (select.shape[0], select.shape[2], width)
    thin = (select.shape[0], 8, select.shape[2])
    hidden = tiles * CHUNK
    shapes = (
        jax.ShapeDtypeStruct(gate_own.shape, F32),
        jax.ShapeDtypeStruct(gate_own.shape, F32),
        jax.ShapeDtypeStruct(down_full.shape, BF16),
        jax.ShapeDtypeStruct(block, BF16),
        jax.ShapeDtypeStruct(block, BF16),
        jax.ShapeDtypeStruct(thin, F32),
    )
    scratch = [
        pltpu.VMEM((tiles, share, TILE), F32),
        pltpu.VMEM((tiles, width, TILE), BF16),
        pltpu.VMEM(down_full.shape, BF16),
        pltpu.VMEM((rows, width), F32),
        pltpu.VMEM((rows, width), F32),
        pltpu.VMEM((2, CHUNK, width), BF16),
        pltpu.VMEM(block, BF16),
        pltpu.VMEM(thin, F32),
        DMA((tiles + 1,)),
        DMA((2,)),
        DMA((3,)),
        DMA((2, 4)),
        DMA((2, 4)),
    ]
    scratch += LineSpread.scratch(tiles - ready) + LineSum.scratch(tiles, share, TILE, False)
    return call(
        functools.partial(sweep_kernel, ready),
        shapes,
        scratch,
        62 * MB,
        18 * rows * width * hidden,
        buffer,
        scaled,
        plain,
        gate_column,
        select,
        gate_own,
        up_own,
        early,
        down_full,
        stay=(5, 6, 7, 8),
        land=(0, 1, 2, 4, 5),
        link=2,
    )


PARTS = 4


def backward_layer(experts, relative, ins, outs, work, reached):
    tokens, cotangent, weights, small, heads, hot_back, length, meta, own = ins[:9]
    returned, inner_rows, qkv, attended, probs, resid, normed_two = ins[9:]
    grad_tokens, grad_small, grad_out, *grad_halves = outs
    grad_attended, grad_qkv, branch, normed, grad_resid, grad_diagonals = work
    slots, width = tokens.shape
    blocks = returned.shape[0]
    router_t = small[...].astype(BF16)
    keep_row = lax.broadcasted_iota(jnp.int32, (slots, 1), 0) < length[0, 0]
    logits = dot_nt(router_t, normed_two[...])
    zero_route, one_route = meta[0:1, :], meta[1:2, :]
    gate_zero, gate_one = pair_gates(logits, zero_route, one_route)
    which = lax.broadcasted_iota(jnp.int32, logits.shape, 0)
    grad_zero = jnp.zeros((1, slots), F32)
    grad_one = jnp.zeros((1, slots), F32)
    for block in range(blocks):
        row = inner_rows[block][0:1, :]
        expert = jnp.bitwise_xor(own[0, 0], block) if relative else block
        grad_zero = grad_zero + jnp.where(zero_route == expert, row, 0.0)
        grad_one = grad_one + jnp.where(one_route == expert, row, 0.0)
    shared = gate_zero * grad_zero + gate_one * grad_one
    grad_zero = gate_zero * (grad_zero - shared)
    grad_one = gate_one * (grad_one - shared)
    grad_logits = jnp.where(which == zero_route, grad_zero, 0.0) + jnp.where(
        which == one_route, grad_one, 0.0
    )
    high, low = two_halves(grad_logits)
    grad_small[...] = dot(high, normed_two[...]) + dot(low, normed_two[...])
    grad_normed_two = dot_tn(high, router_t) + dot_tn(low, router_t)
    for block in range(blocks):
        grad_normed_two = grad_normed_two + returned[block].astype(F32)
    r = resid[...]
    inv_two = lax.rsqrt(jnp.mean(r * r, axis=1, keepdims=True) + epsilon)
    unit_two = r * inv_two
    grad_small[experts + 1 : experts + 2, :] = jnp.sum(
        grad_normed_two * unit_two, axis=0, keepdims=True
    )
    scaled_two = small[experts + 1 : experts + 2, :] * grad_normed_two
    grad_resid[...] = jnp.where(keep_row, cotangent[...].astype(F32), 0.0) + inv_two * (
        scaled_two - unit_two * jnp.mean(scaled_two * unit_two, axis=1, keepdims=True)
    )
    branch[...] = grad_resid[...].astype(BF16)
    reached("branch")

    @pl.loop(0, width // 256)
    def _(j):
        grad_out[:, columns(j, 256)] = dot_tn(attended[...], branch[:, columns(j, 256)]).astype(
            BF16
        )

    reached("out")
    grad_attended[...] = dot_nt(branch[...], weights[:, 3 * width : 4 * width]).astype(BF16)
    x = tokens[...].astype(F32)
    inv_one = lax.rsqrt(jnp.mean(x * x, axis=1, keepdims=True) + epsilon)
    normed[...] = (x * inv_one * small[experts : experts + 1, :]).astype(BF16)
    reached("attended")

    lane = lax.broadcasted_iota(jnp.int32, (slots, LANES), 1)
    first = lane < HD
    square = (slots, slots)
    flip = (
        lax.broadcasted_iota(jnp.int32, square, 0) + lax.broadcasted_iota(jnp.int32, square, 1)
        == slots - 1
    )
    flip = flip.astype(F32).astype(BF16)

    def attend_back(pair):
        q = qkv[:, columns(pair, LANES)]
        k = qkv[:, columns(PAIRS + pair, LANES)]
        v = qkv[:, columns(2 * PAIRS + pair, LANES)]
        g = grad_attended[:, columns(pair, LANES)]
        dq, dk, dv = [], [], []
        for half in range(2):
            head = 2 * pair + half
            mine = first if half == 0 else jnp.logical_not(first)
            low = probs[head]
            p = low.astype(F32)
            grad_probs = dot_nt(jnp.where(mine, g, jnp.zeros_like(g)), v)
            ds = p * (grad_probs - jnp.sum(p * grad_probs, axis=1, keepdims=True))
            ds = ds.astype(BF16)
            wide = jnp.concatenate([dot(flip, ds), jnp.zeros((slots, slots), F32)], axis=1)
            skewed = pltpu.roll(wide, 0, 1, stride=1, stride_axis=0)
            grad_diagonals[pl.ds(head, 1), :] = jnp.sum(skewed, axis=0, keepdims=True)
            dq.append(dot(ds, k))
            dk.append(dot_tn(ds, q))
            dv.append(dot_tn(low, g))
        grad_qkv[:, columns(pair, LANES)] = (jnp.where(first, dq[0], dq[1]) * SCALE).astype(BF16)
        grad_qkv[:, columns(PAIRS + pair, LANES)] = (
            jnp.where(first, dk[0], dk[1]) * SCALE
        ).astype(BF16)
        grad_qkv[:, columns(2 * PAIRS + pair, LANES)] = jnp.where(first, dv[0], dv[1]).astype(BF16)

    for part in range(PARTS):
        pl.loop(part * PAIRS // PARTS, (part + 1) * PAIRS // PARTS)(attend_back)
        reached(f"part{part}")
        if part % 2 == 1:
            half, wide = part // 2, width // 2
            for i in range(3):
                for j in range(wide // 256):
                    source = i * width + half * wide + j * 256
                    at = i * wide + j * 256
                    grad_halves[half][:, at : at + 256] = dot_tn(
                        normed[...], grad_qkv[:, source : source + 256]
                    ).astype(BF16)
            reached(f"half{half}")

    high, low = two_halves(grad_diagonals[...])
    by_lane = dot_nt(high, hot_back[...]) + dot_nt(low, hot_back[...])
    grad_small[experts + 2 : experts + 3, :] = jnp.sum(
        by_lane * heads[...].astype(F32), axis=0, keepdims=True
    )
    grad_normed = dot_nt(grad_qkv[...], weights[:, : 3 * width])
    x = tokens[...].astype(F32)
    inv_one = lax.rsqrt(jnp.mean(x * x, axis=1, keepdims=True) + epsilon)
    unit_one = x * inv_one
    grad_small[experts : experts + 1, :] = jnp.sum(grad_normed * unit_one, axis=0, keepdims=True)
    scaled_one = small[experts : experts + 1, :] * grad_normed
    grad_tokens[...] = grad_resid[...] + inv_one * (
        scaled_one - unit_one * jnp.mean(scaled_one * unit_one, axis=1, keepdims=True)
    )
    reached("tokens")


def backward_scratch(slots, width):
    return [
        pltpu.VMEM((slots, width), BF16),
        pltpu.VMEM((slots, 3 * width), BF16),
        pltpu.VMEM((slots, width), BF16),
        pltpu.VMEM((slots, width), BF16),
        pltpu.VMEM((slots, width), F32),
        pltpu.VMEM((HEADS, 2 * slots), F32),
    ]


def add_mixed(output, resid, length, parts):
    keep_row = lax.broadcasted_iota(jnp.int32, (resid.shape[0], 1), 0) < length[0, 0]
    total = resid[...]
    for part in parts:
        total = total + part[...].astype(F32)
    output[...] = jnp.where(keep_row, total, 0.0).astype(BF16)


def local_backward_kernel(experts, *refs):
    ins, mixed, output, outs, work = refs[:16], refs[16], refs[17], refs[18:23], refs[23:]
    backward_layer(experts, False, ins, outs, work, lambda name: None)
    add_mixed(output, ins[14], ins[6], [mixed.at[block] for block in range(mixed.shape[0])])


def local_backward(experts, *args):
    tokens, small = args[0], args[3]
    slots, width = tokens.shape
    return call(
        functools.partial(local_backward_kernel, experts),
        (
            jax.ShapeDtypeStruct((slots, width), BF16),
            jax.ShapeDtypeStruct((slots, width), F32),
            jax.ShapeDtypeStruct(small.shape, F32),
            jax.ShapeDtypeStruct((width, width), BF16),
            jax.ShapeDtypeStruct((width, 3 * width // 2), BF16),
            jax.ShapeDtypeStruct((width, 3 * width // 2), BF16),
        ),
        backward_scratch(slots, width),
        62 * MB,
        4 * slots * width * (4 * width + 2 * slots),
        *args,
    )


class DeviceSum:
    @staticmethod
    def scratch(share, width):
        return [
            pltpu.VMEM((4, 4 * share, width), BF16),
            pltpu.VMEM((4, 2, share, width), BF16),
            pltpu.VMEM((4, share, width), BF16),
            DMA((4, 4)),
            DMA((4, 4)),
        ] + LineSum.scratch(1, share, width, False)

    def __init__(self, partial, scratch):
        self.partial = partial
        self.theirs, self.first_in, self.second_in, self.send, self.recv = scratch[:5]
        self.line = LineSum(1, None, scratch[5:], False)
        self.share = self.second_in.shape[1]
        self.d, self.e, self.z, self.core = here()
        self.other = (2 * self.z + 1 - self.core, self.e)
        self.to_x, self.to_y = (self.d, flipped(self.e, 1)), (self.d, flipped(self.e, 2))

    def rows(self, k, core, start, count):
        row = (2 * flipped(self.z, k) + core) * 4 * self.share + start
        return self.partial.at[pl.ds(pl.multiple_of(row, self.share), count)]

    def piece(self, k, q):
        return self.rows(k, self.core, flipped(self.e, q) * self.share, self.share)

    def remote(self, src, dst, stage, k, to):
        return pltpu.make_async_remote_copy(
            src_ref=src,
            dst_ref=dst,
            send_sem=self.send.at[stage, k],
            recv_sem=self.recv.at[stage, k],
            device_id=to,
            device_id_type=MESH,
        )

    def swap(self, k):
        src = self.rows(k, 1 - self.core, 0, 4 * self.share)
        return self.remote(src, self.theirs.at[k], 0, k, self.other)

    def first(self, k, slot):
        near, to = (1, self.to_x) if k % 2 == 0 else (2, self.to_y)
        return self.remote(
            self.piece(k, 3 if slot else near), self.first_in.at[k, slot], 1 + slot, k, to
        )

    def far(self, k):
        return 2 if k % 2 == 0 else 1

    def second(self, k):
        to = self.to_y if k % 2 == 0 else self.to_x
        return self.remote(self.piece(k, self.far(k)), self.second_in.at[k], 3, k, to)

    def begin(self):
        for k in (3, 2, 1, 0):
            self.swap(k).start()

    def stage_one(self):
        for k in (3, 2, 1, 0):
            self.swap(k).wait_recv()

            @pl.loop(0, 4)
            def _(j):
                start = pl.multiple_of(j * self.share, self.share)
                mine = self.rows(k, self.core, start, self.share)
                mine[...] = (
                    mine[...].astype(F32) + self.theirs[k, pl.ds(start, self.share)].astype(F32)
                ).astype(BF16)

            self.first(k, 1).start()
            self.first(k, 0).start()

    def stage_two(self):
        for k in (3, 2, 1, 0):
            self.first(k, 1).wait_recv()
            source = self.piece(k, self.far(k))
            source[...] = (source[...].astype(F32) + self.first_in[k, 1].astype(F32)).astype(BF16)
            self.second(k).start()

    def stage_three(self):
        for k in (3, 2, 1, 0):
            self.first(k, 0).wait_recv()
            self.second(k).wait_recv()
            total = self.piece(k, 0)[...].astype(F32) + self.first_in[k, 0].astype(F32)
            self.line.theirs[0, k] = (total + self.second_in[k].astype(F32)).astype(BF16)
        self.line.hand_over(0)

    def settle(self):
        for k in range(4):
            self.swap(k).wait_send()
            self.first(k, 0).wait_send()
            self.first(k, 1).wait_send()
            self.second(k).wait_send()


class EverySum:
    @staticmethod
    def scratch(shape):
        return [
            pltpu.VMEM((6,) + shape, F32),
            pltpu.VMEM((5,) + shape, F32),
            DMA((5,)),
            DMA((5,)),
        ]

    def __init__(self, scratch):
        self.sums, self.landed, self.send, self.recv = scratch
        d, e, z, c = here()
        near = [(2 * flipped(z, k) + c, e) for k in (1, 2)]
        self.to = [(2 * z + 1 - c, e), (d, flipped(e, 1)), (d, flipped(e, 2))] + near

    def copy(self, at):
        return pltpu.make_async_remote_copy(
            src_ref=self.sums.at[at],
            dst_ref=self.landed.at[at],
            send_sem=self.send.at[at],
            recv_sem=self.recv.at[at],
            device_id=self.to[at],
            device_id_type=MESH,
        )

    def start(self, value):
        self.sums[0] = value
        self.copy(0).start()

    def step(self, at):
        self.copy(at).wait_recv()
        self.sums[at + 1] = self.sums[at] + self.landed[at]
        if at + 1 < len(self.to):
            self.copy(at + 1).start()

    def settle(self):
        for at in range(len(self.to)):
            self.copy(at).wait_send()


def down_source(array, z, share):
    def source(i, k, core):
        row = pl.multiple_of((2 * flipped(z, k) + core) * share, share)
        return array.at[pl.ds(row, share), pl.ds(pl.multiple_of(i * CHUNK, CHUNK), CHUNK)]

    return source


def backward_kernel(experts, *refs):
    refs = list(refs)

    def take(count):
        taken, refs[:] = refs[:count], refs[count:]
        return taken

    ins = take(16)
    mixed, grad_down = take(2)
    output, grad_tokens, qkv_sum, out_sum, small_sum, down_sum = take(6)
    grad_small, grad_out, *grad_halves = take(4)
    work = take(6)
    (half_sums,) = take(1)
    mixed_full, mixed_send, mixed_recv = take(3)
    d, e, z, _ = here()
    width = out_sum.shape[1]
    down = LineSum(width // CHUNK, down_source(grad_down, z, down_sum.shape[0]), take(6), True)
    out = DeviceSum(grad_out, take(9))
    halves = [DeviceSum(grad_half, take(9)) for grad_half in grad_halves]
    every = EverySum(take(4))
    swap = Swap(mixed, mixed_full, mixed_send, mixed_recv, d, e)
    meet(group(d, e)[1:] + [down.other] + down.to[1:])
    for i in range(down.count):
        down.begin(i)
    down.halve(0)

    def reached(name):
        if name == "branch":
            down.halve(1)
        elif name == "out":
            out.begin()
        elif name == "attended":
            down.halve(2)
        elif name == "part0":
            out.stage_one()
            down.relay(0)
        elif name == "part1":
            out.stage_two()
        elif name == "half0":
            halves[0].begin()
            down.pass_on(0)
            down.relay(1)
        elif name == "part2":
            halves[0].stage_one()
            out.stage_three()
            down.halve(3)
        elif name == "part3":
            halves[0].stage_two()
            down.pass_on(1)
        elif name == "half1":
            halves[1].begin()
            down.relay(2)
        elif name == "tokens":
            every.start(grad_small[...])
            halves[1].stage_one()
            for block in (3, 1, 2):
                swap.start(block)

    outs = [grad_tokens, grad_small, grad_out] + grad_halves
    backward_layer(experts, True, ins, outs, work, reached)
    halves[0].stage_three()
    every.step(0)
    halves[1].stage_two()
    out.line.relay(0)
    every.step(1)
    down.pass_on(2)
    down.relay(3)
    out.line.pass_on(0)
    halves[1].stage_three()
    every.step(2)
    halves[0].line.relay(0)
    down.pass_on(3)
    every.step(3)
    halves[0].line.pass_on(0)
    halves[1].line.relay(0)
    every.step(4)
    small_sum[...] = every.sums[5]
    for i in range(down.count):
        down.finish(i, down_sum.at[:, i * CHUNK : (i + 1) * CHUNK])
    halves[1].line.pass_on(0)
    swap.finish()
    add_mixed(output, ins[14], ins[6], [mixed.at[0]] + [mixed_full.at[q] for q in (1, 2, 3)])
    out.line.finish(0, out_sum)
    wide = width // 2
    for half, sums in enumerate(halves):
        sums.line.finish(0, half_sums.at[half])
        for i in range(3):
            at = i * width + half * wide
            qkv_sum[:, at : at + wide] = half_sums[half, :, i * wide : (i + 1) * wide]
    for sums in [out] + halves:
        sums.settle()
    every.settle()


def backward(experts, *args):
    tokens, small, mixed, grad_down = args[0], args[3], args[16], args[17]
    slots, width = tokens.shape
    share, down_share = width // 32, grad_down.shape[0] // 8
    half = 3 * width // 2
    scratch = [
        pltpu.VMEM(small.shape, F32),
        pltpu.VMEM((width, width), BF16),
        pltpu.VMEM((width, half), BF16),
        pltpu.VMEM((width, half), BF16),
        *backward_scratch(slots, width),
        pltpu.VMEM((2, share, half), F32),
        pltpu.VMEM(mixed.shape, BF16),
        DMA((4,)),
        DMA((4,)),
        *LineSum.scratch(width // CHUNK, down_share, CHUNK, True),
        *DeviceSum.scratch(share, width),
        *DeviceSum.scratch(share, half),
        *DeviceSum.scratch(share, half),
        *EverySum.scratch(small.shape),
    ]
    return call(
        functools.partial(backward_kernel, experts),
        (
            jax.ShapeDtypeStruct((slots, width), BF16),
            jax.ShapeDtypeStruct((slots, width), F32),
            jax.ShapeDtypeStruct((share, 3 * width), F32),
            jax.ShapeDtypeStruct((share, width), F32),
            jax.ShapeDtypeStruct(small.shape, F32),
            jax.ShapeDtypeStruct((down_share, width), F32),
        ),
        scratch,
        63 * MB,
        4 * slots * width * (4 * width + 2 * slots),
        *args,
        stay=(17,),
        link=3,
    )


READY = 2


def on_device(
    fast,
    tokens,
    cotangent,
    qkv_weight,
    out_weight,
    router_weight,
    first_gain,
    second_gain,
    bias_table,
    gate_weight,
    up_weight,
    down_weight,
    lengths,
    routes,
    priority,
):
    both = ("dp", "expert")
    slots, width = tokens.shape
    expert_count = lax.axis_size("expert")
    device_count = lax.axis_size("dp") * expert_count
    share, bias_share = first_gain.shape[0], bias_table.shape[0]
    device = lax.axis_index("dp") * expert_count + lax.axis_index("expert")
    own = lax.axis_index("expert").astype(jnp.int32).reshape(1, 1)
    small_rows = -(-(expert_count + 3) // 8) * 8

    def gathered(value, axes, axis=0, tiled=True):
        return lax.all_gather(value, axes, axis=axis, tiled=tiled)

    def scattered(value, axes):
        return lax.psum_scatter(value, axes, scatter_dimension=0, tiled=True).astype(F32)

    def exchanged(value):
        return lax.all_to_all(value, "expert", split_axis=0, concat_axis=0, tiled=True)

    rows_own, hidden = gate_weight.shape[1:]
    down_full = gathered(down_weight[0], "dp")
    if fast:
        cut = (rows_own, READY, 1, CHUNK)
        early = jnp.concatenate(
            [value[0, :, : READY * CHUNK].reshape(cut) for value in (gate_weight, up_weight)],
            axis=2,
        ).reshape(rows_own, READY * TILE)
        early = gathered(early, "dp")
    else:
        gate_full, up_full = (gathered(value[0], "dp") for value in (gate_weight, up_weight))

    beside = jnp.concatenate(
        [
            router_weight,
            first_gain[:, None],
            second_gain[:, None],
            jnp.pad(bias_table, (0, share - bias_share))[:, None],
            jnp.zeros((share, 128 - expert_count - 3), BF16),
        ],
        axis=1,
    )
    lane = np.arange(width)
    flat = lane // share * bias_share + lane % share
    in_table = lane % share < bias_share
    heads = np.arange(HEADS)[:, None] == np.where(in_table, flat // BUCKETS, -1)[None, :]
    heads = jnp.asarray(heads.astype(np.float32), BF16)
    ahead = np.arange(2 * slots)

    def hot(ahead):
        return jnp.asarray(
            np.where(in_table[:, None], diagonal_onehot(ahead)[flat % BUCKETS], 0.0), BF16
        )

    valid_rows = jnp.arange(slots, dtype=jnp.int32) < lengths[0, 0]
    meta_own = jnp.concatenate(
        [
            routes.T,
            priority,
            valid_rows.astype(jnp.int32)[None, :],
            jnp.zeros((4, slots), jnp.int32),
        ],
        axis=0,
    )

    diagonals_hot = hot(np.where(ahead < slots, ahead, ahead - 2 * slots))
    if fast:
        *kept, buffer, scaled, plain, select, gate_column, weights = forward(
            expert_count,
            tokens,
            heads,
            diagonals_hot,
            lengths,
            cotangent,
            meta_own,
            qkv_weight,
            out_weight,
            beside,
        )
    else:
        weights = gathered(jnp.concatenate([qkv_weight, out_weight, beside], axis=1), both)
        kept = attention_forward(expert_count, tokens, weights, heads, diagonals_hot, lengths)
        rows, cots, meta = (
            gathered(value, "expert", tiled=False) for value in (kept[4], cotangent, meta_own)
        )
        buffer, scaled, plain, select, gate_column = dispatch(rows, cots, meta, kept[5], own)
    qkv, attended, probs, resid, normed_two, small = kept
    if fast:
        grad_gate, grad_up, grad_down, mixed, returned, inner_rows = sweep(
            READY,
            buffer,
            scaled,
            plain,
            gate_column,
            select,
            gate_weight[0],
            up_weight[0],
            early,
            down_full,
        )
    else:
        expert_out, grad_buffer, inner, *grad_experts = experts(
            buffer, scaled, plain, gate_full, up_full, down_full
        )
        mixed, returned, inner_rows = (
            exchanged(value)
            for value in give_back(select, expert_out, grad_buffer, inner, gate_column)
        )
        grad_gate, grad_up, grad_down = (scattered(value, "dp")[None] for value in grad_experts)
    layer = (
        tokens,
        cotangent,
        weights,
        small,
        heads,
        hot(ahead - (slots - 1)),
        lengths,
        meta_own,
        own,
        returned,
        inner_rows,
        qkv,
        attended,
        probs,
        resid,
        normed_two,
        mixed,
    )
    if fast:
        output, grad_tokens, grad_qkv, grad_out, grad_small, grad_down = backward(
            expert_count, *layer, grad_down
        )
        grad_gate, grad_up, grad_down = grad_gate[None], grad_up[None], grad_down[None]
    else:
        output, grad_tokens, grad_small, *grad_weights = local_backward(expert_count, *layer)
        grad_out, *halves = (scattered(value, both) for value in grad_weights)
        grad_qkv = jnp.stack([half.reshape(share, 3, width // 2) for half in halves], axis=2)
        grad_qkv = grad_qkv.reshape(share, 3 * width)
        grad_small = lax.psum(grad_small, both)
    grad_small = lax.dynamic_slice(grad_small, (0, device * share), (small_rows, share))
    return (
        output,
        grad_tokens,
        grad_qkv,
        grad_out,
        grad_small[:expert_count].T,
        grad_small[expert_count],
        grad_small[expert_count + 1],
        grad_small[expert_count + 2, :bias_share],
        grad_gate,
        grad_up,
        grad_down,
    )


def solution(mesh):
    fast = dict(mesh.shape) == {"dp": 8, "expert": 4}
    rows = P(("dp", "expert"), None)
    flat = P(("dp", "expert"))
    expert = P("expert", "dp", None)
    grid = P("dp", "expert")
    return jax.shard_map(
        functools.partial(on_device, fast),
        mesh=mesh,
        in_specs=(rows,) * 5 + (flat,) * 3 + (expert,) * 3 + (grid, rows, grid),
        out_specs=(rows,) * 5 + (flat,) * 3 + (expert,) * 3,
        check_vma=False,
    )
```

```python
import functools
import math

import jax
import jax.numpy as jnp
import numpy as np
from jax import lax
from jax.experimental import pallas as pl
from jax.experimental.pallas import tpu as pltpu
from jax.sharding import PartitionSpec as P

HEADS = 16
HD = 64
BUCKETS = 32
CAP = 480
PAIRS = HEADS // 2
LANES = 2 * HD
PARTS = 4

epsilon = 1e-06
masked_value = -1e30
max_distance = 128.0
SCALE = 1.0 / math.sqrt(HD)
MB = 1 << 20
F32 = jnp.float32
BF16 = jnp.bfloat16


def bucket_of(offset, bucket_count):
    halfway = bucket_count // 2
    exact_span = bucket_count // 4
    distance = np.abs(offset)
    log_part = np.log(np.maximum(distance, 1) / float(exact_span)) / np.log(
        max_distance / exact_span
    )
    far_bucket = np.minimum(
        exact_span + np.floor(log_part * exact_span).astype(np.int64), halfway - 1
    )
    inside = np.where(distance < exact_span, distance, far_bucket)
    return np.where(offset < 0, halfway, 0) + inside


def diagonal_onehot(ahead):
    return (bucket_of(-ahead, BUCKETS)[None, :] == np.arange(BUCKETS)[:, None]).astype(np.float32)


def dot(a, b):
    return jnp.dot(a, b, preferred_element_type=F32)


def dot_nt(a, b):
    return lax.dot_general(a, b, (((1,), (1,)), ((), ())), preferred_element_type=F32)


def dot_tn(a, b):
    return lax.dot_general(a, b, (((0,), (0,)), ((), ())), preferred_element_type=F32)


def two_halves(value):
    high = value.astype(BF16)
    return high, (value - high.astype(F32)).astype(BF16)


def columns(index, width):
    return pl.ds(pl.multiple_of(index * width, width), width)


VMEM_SPEC = pl.BlockSpec(memory_space=pltpu.VMEM)


ANY_SPEC = pl.BlockSpec(memory_space=pl.ANY)
MESH = pl.DeviceIdType.MESH
DMA = pltpu.SemaphoreType.DMA


def call(kernel, out_shape, scratch, vmem, flops, *args, stay=(), land=(), link=None, aliases=None):
    nbytes = sum(a.size * a.dtype.itemsize for a in args)
    params = dict(vmem_limit_bytes=vmem)
    if link is not None:
        params.update(collective_id=link, has_side_effects=True)
    return pl.pallas_call(
        kernel,
        out_shape=out_shape,
        in_specs=[ANY_SPEC if i in stay else VMEM_SPEC for i in range(len(args))],
        out_specs=tuple(ANY_SPEC if i in land else VMEM_SPEC for i in range(len(out_shape))),
        scratch_shapes=scratch,
        input_output_aliases=aliases or {},
        compiler_params=pltpu.CompilerParams(**params),
        cost_estimate=pl.CostEstimate(flops=flops, bytes_accessed=nbytes, transcendentals=0),
    )(*args)


def here():
    d, e = lax.axis_index("dp"), lax.axis_index("expert")
    return d, e, d // 2, lax.rem(d, 2)


def flipped(value, bits):
    low, high = lax.rem(value, 2), value // 2
    low = 1 - low if bits & 1 else low
    high = 1 - high if bits & 2 else high
    return 2 * high + low


def meet(partners):
    barrier = pltpu.get_barrier_semaphore()
    for partner in partners:
        pl.semaphore_signal(barrier, inc=1, device_id=partner, device_id_type=MESH)
    pl.semaphore_wait(barrier, len(partners))


def push(src, dst, send, recv, to):
    copy = pltpu.make_async_remote_copy(
        src_ref=src, dst_ref=dst, send_sem=send, recv_sem=recv, device_id=to, device_id_type=MESH
    )
    copy.start()
    return copy


def group(d, e):
    return [None] + [(d, flipped(e, q)) for q in (1, 2, 3)]


class Spread:
    def __init__(self, src, dst, send, recv, d, e):
        self.src, self.dst, self.send, self.recv = src, dst, send, recv
        self.to = group(d, e)
        self.half = src.shape[0] // 2
        self.copies = {}

    def part(self, ref, half):
        return ref.at[pl.ds(half * self.half, self.half)]

    def start(self):
        for turn in range(2):
            for q in (1, 2):
                half = turn if q == 1 else 1 - turn
                at = 2 * (q - 1) + half
                self.copies[q, half] = push(
                    self.part(self.src, half),
                    self.part(self.dst.at[q], half),
                    self.send.at[at],
                    self.recv.at[at],
                    self.to[q],
                )

    def forward(self):
        for q, half, across, at in ((1, 0, 2, 4), (2, 1, 1, 5)):
            self.copies[q, half].wait_recv()
            self.copies[3, half] = push(
                self.part(self.dst.at[q], half),
                self.part(self.dst.at[3], half),
                self.send.at[at],
                self.recv.at[at],
                self.to[across],
            )

    def arrived(self, q):
        for half in {1: (1,), 2: (0,), 3: (0, 1)}[q]:
            self.copies[q, half].wait_recv()

    def sent(self):
        for copy in self.copies.values():
            copy.wait_send()

    def finish(self):
        for q in (1, 2, 3):
            self.arrived(q)
        self.sent()


class Swap:
    def __init__(self, src, dst, send, recv, d, e):
        self.src, self.dst, self.send, self.recv = src, dst, send, recv
        self.to = group(d, e)
        self.copies = {}

    def start(self, q):
        self.copies[q] = push(
            self.src.at[q], self.dst.at[q], self.send.at[q], self.recv.at[q], self.to[q]
        )

    def finish(self):
        for copy in self.copies.values():
            copy.wait_recv()
        for copy in self.copies.values():
            copy.wait_send()


class DeviceGather:
    WAYS = 5

    def __init__(self, full, share, send, recv):
        self.full, self.share, self.send, self.recv = full, share, send, recv
        self.d, self.e, self.z, self.core = d, e, z, c = here()
        self.to_x, self.to_y = (d, flipped(e, 1)), (d, flipped(e, 2))
        self.other = (2 * z + 1 - c, e)
        self.to_z = [None] + [(2 * flipped(z, k) + c, e) for k in (1, 2, 3)]
        self.end = jnp.logical_or(z == 0, z == 3)
        self.middle = jnp.logical_not(self.end)

    def item(self, k, q, core=None):
        device = 2 * flipped(self.z, k) + (self.core if core is None else core)
        row = (device * 4 + flipped(self.e, q)) * self.share
        return self.full.at[pl.ds(pl.multiple_of(row, self.share), self.share)]

    def pass_on(self, k, q, way, at, to, into=None):
        piece = self.item(k, q)
        return pltpu.make_async_remote_copy(
            src_ref=piece,
            dst_ref=piece,
            send_sem=self.send.at[way, at],
            recv_sem=self.recv.at[way, at if into is None else into],
            device_id=to,
            device_id_type=MESH,
        )

    def along_z(self, k):
        return self.pass_on(0, 0, 0, k, self.to_z[k])

    def relay_z(self, k):
        return self.pass_on(k, 0, 0, 2 + k, self.to_z[1], 5 - k)

    def along_x(self, k):
        return self.pass_on(k, 0, 1, k, self.to_x)

    def along_y(self, k):
        return self.pass_on(k, 0, 2, k, self.to_y)

    def across(self, k):
        return self.pass_on(k, 1, 3, k, self.to_y) if k % 2 == 0 else self.pass_on(k, 2, 3, k, self.to_x)

    def over(self, k, q):
        return self.pass_on(k, q, 4, 4 * q + k, self.other)

    def start(self):
        self.along_z(1).start()

        @pl.when(self.middle)
        def _():
            self.along_z(3).start()

        @pl.when(self.end)
        def _():
            self.along_z(2).start()

    def spread_out(self, k):
        self.along_x(k).start()
        self.along_y(k).start()
        self.over(k, 0).start()

    def from_z(self, k):
        self.along_z(k).wait_recv()
        if k > 1:

            @pl.when(self.middle)
            def _():
                self.relay_z(k).start()

        self.spread_out(k)

    def from_neighbours(self, k):
        self.along_x(k).wait_recv()
        if k % 2 == 0:
            self.across(k).start()
        self.over(k, 1).start()
        self.along_y(k).wait_recv()
        if k % 2 == 1:
            self.across(k).start()
        self.over(k, 2).start()

    def from_across(self, k):
        self.across(k).wait_recv()
        self.over(k, 3).start()

    def complete(self):
        for q in range(4):
            for k in range(4):
                self.over(k, q).wait_recv()

    def settle(self):
        self.along_z(1).wait_send()

        @pl.when(self.middle)
        def _():
            self.along_z(3).wait_send()
            self.relay_z(2).wait_send()
            self.relay_z(3).wait_send()

        @pl.when(self.end)
        def _():
            self.along_z(2).wait_send()

        for k in range(4):
            self.along_x(k).wait_send()
            self.along_y(k).wait_send()
            self.across(k).wait_send()
            for q in range(4):
                self.over(k, q).wait_send()


class LineSum:
    def __init__(self, count, source, scratch, load):
        self.count, self.source, self.load_first = count, source, load
        scratch = list(scratch)
        self.theirs, self.landed, self.send, self.recv = scratch[:4]
        if load:
            self.loads, self.loaded = scratch[4:]
        self.d, self.e, self.z, self.core = here()
        self.other = (2 * self.z + 1 - self.core, self.e)
        self.to = [None] + [(2 * flipped(self.z, k) + self.core, self.e) for k in (1, 2, 3)]
        self.end = jnp.logical_or(self.z == 0, self.z == 3)
        self.middle = jnp.logical_not(self.end)

    @staticmethod
    def scratch(count, rows, width, load):
        part = (rows, width)
        parts = [
            pltpu.VMEM((count, 4) + part, BF16),
            pltpu.VMEM((count, 5) + part, BF16),
            DMA((count, 3, 5)),
            DMA((count, 3, 5)),
        ]
        return parts + ([pltpu.VMEM((count, 4) + part, BF16), DMA((count, 4))] if load else [])

    def remote(self, i, src, dst, stage, out, into, to):
        return pltpu.make_async_remote_copy(
            src_ref=src,
            dst_ref=dst,
            send_sem=self.send.at[i, stage, out],
            recv_sem=self.recv.at[i, stage, into],
            device_id=to,
            device_id_type=MESH,
        )

    def load(self, i, k):
        return pltpu.make_async_copy(
            self.source(i, k, self.core), self.loads.at[i, k], self.loaded.at[i, k]
        )

    def swap(self, i, k):
        src = self.source(i, k, 1 - self.core)
        return self.remote(i, src, self.theirs.at[i, k], 0, k, k, self.other)

    def hand(self, i, k):
        at = 1 if k == 1 else 5 - k
        return self.remote(i, self.theirs.at[i, k], self.landed.at[i, at], 1, k, at, self.to[1])

    def handed(self, i, at):
        return self.remote(i, self.theirs.at[i, at], self.landed.at[i, at], 1, at, at, self.to[1])

    def deliver(self, i, k):
        at = 0 if k == 3 else 4
        return self.remote(i, self.theirs.at[i, k], self.landed.at[i, at], 2, k, at, self.to[3])

    def for_partner(self, i):
        return self.remote(i, self.theirs.at[i, 0], self.landed.at[i, 4], 2, 4, 4, self.to[3])

    def last(self, i):
        return self.remote(i, self.theirs.at[i, 1], self.landed.at[i, 0], 2, 0, 0, self.to[1])

    def add(self, i, k, more):
        self.theirs[i, k] = (self.theirs[i, k].astype(F32) + more[...].astype(F32)).astype(BF16)

    def begin(self, i):
        for k in (3, 2, 1, 0):
            self.swap(i, k).start()
            if self.load_first:
                self.load(i, k).start()

    def halve(self, i):
        for k in (3, 2, 1, 0):
            if self.load_first:
                self.load(i, k).wait()
            self.swap(i, k).wait_recv()
            self.add(i, k, self.loads.at[i, k] if self.load_first else self.source(i, k, self.core))
        self.hand_over(i)

    def hand_over(self, i):
        @pl.when(self.end)
        def _():
            for k in (3, 2, 1):
                self.hand(i, k).start()

    def relay(self, i):
        @pl.when(self.middle)
        def _():
            for k in (2, 3):
                self.handed(i, k).wait_recv()
                self.add(i, k, self.landed.at[i, k])
                self.deliver(i, k).start()

    def pass_on(self, i):
        @pl.when(self.middle)
        def _():
            self.for_partner(i).wait_recv()
            self.add(i, 1, self.landed.at[i, 4])
            self.last(i).start()

    def finish(self, i, out):
        self.last(i).wait_recv()
        out[...] = self.theirs[i, 0].astype(F32) + self.landed[i, 0].astype(F32)
        if self.source is not None:
            for k in range(4):
                self.swap(i, k).wait_send()

        @pl.when(self.end)
        def _():
            for k in (3, 2, 1):
                self.hand(i, k).wait_send()

        @pl.when(self.middle)
        def _():
            self.handed(i, 1).wait_recv()
            out[...] += self.landed[i, 1].astype(F32)
            self.deliver(i, 2).wait_send()
            self.deliver(i, 3).wait_send()
            self.last(i).wait_send()


class LineSpread:
    def __init__(self, halves, place, scratch):
        self.halves, self.place = halves, place
        self.copied, self.send, self.recv = scratch
        self.d, self.e, self.z, self.core = here()
        self.other = (2 * self.z + 1 - self.core, self.e)
        self.to = [None] + [(2 * flipped(self.z, k) + self.core, self.e) for k in (1, 2, 3)]
        self.end = jnp.logical_or(self.z == 0, self.z == 3)
        self.middle = jnp.logical_not(self.end)

    @staticmethod
    def scratch(count):
        return [DMA((count,)), DMA((count, 9)), DMA((count, 8))]

    def from_chip(self, j, k, core=None):
        return self.place(j, 2 * flipped(self.z, k) + (self.core if core is None else core))

    def remote(self, j, src, dst, out, into, to):
        return pltpu.make_async_remote_copy(
            src_ref=src,
            dst_ref=dst,
            send_sem=self.send.at[j, out],
            recv_sem=self.recv.at[j, into],
            device_id=to,
            device_id_type=MESH,
        )

    def parts(self, j):
        piece = self.place(j, self.d)
        width = piece.shape[1] // 2
        for i, half in enumerate(self.halves(j)):
            yield half, piece.at[:, i * width : (i + 1) * width]

    def keep(self, j):
        piece = self.place(j, self.d)
        return pltpu.make_async_copy(piece, piece, self.copied.at[j])

    def first(self, j, way):
        piece = self.place(j, self.d)
        return self.remote(j, piece, piece, *self.way(way))

    def way(self, way):
        return min(way, 2), 4 if way == 0 else way, self.to[way] if way else self.other

    def send_own(self, j, way):
        for src, dst in self.parts(j):
            self.remote(j, src, dst, *self.way(way)).start()

    def share(self, j, k):
        piece = self.from_chip(j, k)
        return self.remote(j, piece, piece, 2 + k, 4 + k, self.other)

    def pass_on(self, j, k):
        piece = self.from_chip(j, k)
        return self.remote(j, piece, piece, 4 + k, 5 - k, self.to[1])

    def arrival(self, j, k):
        piece = self.from_chip(j, k)
        return self.remote(j, piece, piece, k, k, self.to[1])

    def shared(self, j, k):
        piece = self.from_chip(j, k, 1 - self.core)
        return self.remote(j, piece, piece, 4 + k if k else 0, 4 + k, self.other)

    def across(self, j):
        piece = self.from_chip(j, 1)
        return self.remote(j, piece, piece, 8, 2, self.to[3])

    def start(self, j):
        self.send_own(j, 1)

        @pl.when(self.middle)
        def _():
            self.send_own(j, 3)

        self.send_own(j, 0)
        for src, dst in self.parts(j):
            pltpu.make_async_copy(src, dst, self.copied.at[j]).start()

    def relay_near(self, j):
        self.arrival(j, 1).wait_recv()

        @pl.when(self.middle)
        def _():
            self.across(j).start()

        self.share(j, 1).start()

    def relay_far(self, j):
        for k in (3, 2):
            self.arrival(j, k).wait_recv()

            @pl.when(self.middle)
            def _():
                self.pass_on(j, k).start()

            self.share(j, k).start()

    def complete(self, j):
        self.keep(j).wait()
        for k in range(4):
            self.shared(j, k).wait_recv()

    def settle(self, j):
        self.first(j, 0).wait_send()
        self.first(j, 1).wait_send()

        @pl.when(self.middle)
        def _():
            self.first(j, 3).wait_send()
            self.across(j).wait_send()
            self.pass_on(j, 2).wait_send()
            self.pass_on(j, 3).wait_send()

        for k in (1, 2, 3):
            self.share(j, k).wait_send()


def pair_gates(logits, route_zero, route_one):
    experts = logits.shape[0]
    which = lax.broadcasted_iota(jnp.int32, logits.shape, 0)
    zero = jnp.sum(jnp.where(which == route_zero, logits, 0.0), axis=0, keepdims=True)
    one = jnp.sum(jnp.where(which == route_one, logits, 0.0), axis=0, keepdims=True)
    top = jnp.maximum(zero, one)
    zero, one = jnp.exp(zero - top), jnp.exp(one - top)
    total = zero + one
    return zero / total, one / total


class Dispatch:
    def __init__(self, expert, meta, rank, places):
        self.expert, self.meta, self.rank, self.places = expert, meta, rank, places
        self.blocks, _, self.slots = meta.shape

    def names(self, block):
        info = self.meta[block]
        valid = info[3:4, :] > 0
        zero = jnp.logical_and(valid, info[0:1, :] == self.expert)
        one = jnp.logical_and(valid, info[1:2, :] == self.expert)
        return info, zero, one

    def find_places(self):
        row_of = lax.broadcasted_iota(jnp.int32, (16, self.slots), 0)
        total_zero = jnp.zeros((1, 1), F32)
        for block in range(self.blocks):
            _, zero, _ = self.names(block)
            total_zero = total_zero + jnp.sum(zero.astype(F32), axis=1, keepdims=True)
            self.rank[block] = jnp.transpose(self.meta[block].astype(F32))

        def block_places(block, _):
            info, zero, one = self.names(block)
            mine = info[2:3, :].astype(F32)

            def earlier(other, counts):
                _, other_zero, other_one = self.names(other)
                marks = jnp.where(row_of == 0, other_zero.astype(F32), 0.0) + jnp.where(
                    row_of == 1, other_one.astype(F32), 0.0
                )
                before = (self.rank[other][:, 2:3] < mine).astype(F32).astype(BF16)
                return counts + dot(marks.astype(BF16), before)

            counts = lax.fori_loop(0, self.blocks, earlier, jnp.zeros((16, self.slots), F32))
            place = jnp.where(
                zero, counts[0:1, :], jnp.where(one, counts[1:2, :] + total_zero, -1.0)
            ).astype(jnp.int32)
            self.places[block] = jnp.broadcast_to(place, self.places.shape[1:])
            return 0

        lax.fori_loop(0, self.blocks, block_places, 0)

    def hot(self, block):
        return lax.broadcasted_iota(jnp.int32, (CAP, self.slots), 0) == self.places[block][0:1, :]

    def gates(self, block, rows, router_t):
        info, zero, one = self.names(block)
        gate_zero, gate_one = pair_gates(dot_nt(router_t, rows), info[0:1, :], info[1:2, :])
        gate = jnp.where(zero, gate_zero, jnp.where(one, gate_one, 0.0))
        return jnp.sum(jnp.where(self.hot(block), gate, 0.0), axis=1, keepdims=True)


def attend_forward(experts, tokens, weights, out_weight, heads, hot, length, out, between):
    qkv, attended, probs, resid, normed_two, small, normed, diagonals = out
    slots, width = tokens.shape
    small[...] = jnp.transpose(weights[:, 3 * width :].astype(F32))[: small.shape[0], :]
    x = tokens[...].astype(F32)
    inv_one = lax.rsqrt(jnp.mean(x * x, axis=1, keepdims=True) + epsilon)
    normed[...] = (x * inv_one * small[experts : experts + 1, :]).astype(BF16)
    spread_bias = heads[...].astype(F32) * small[experts + 2 : experts + 3, :]
    diagonals[...] = dot(spread_bias.astype(BF16), hot[...])

    @pl.loop(0, 3 * width // 512)
    def _(j):
        qkv[:, columns(j, 512)] = dot(normed[...], weights[:, columns(j, 512)]).astype(BF16)

    lane = lax.broadcasted_iota(jnp.int32, (slots, LANES), 1)
    first = lane < HD
    live = lax.broadcasted_iota(jnp.int32, (slots, slots), 1) < length[0, 0]

    def attend(pair):
        q = qkv[:, columns(pair, LANES)]
        k = qkv[:, columns(PAIRS + pair, LANES)]
        v = qkv[:, columns(2 * PAIRS + pair, LANES)]
        outs = []
        for half in range(2):
            head = 2 * pair + half
            own = first if half == 0 else jnp.logical_not(first)
            row = jnp.broadcast_to(diagonals[pl.ds(head, 1), :], (slots, 2 * slots))
            bias = pltpu.roll(row, 0, 1, stride=1, stride_axis=0)[:, :slots]
            scores = dot_nt(jnp.where(own, q, jnp.zeros_like(q)), k) * SCALE + bias
            scores = jnp.where(live, scores, masked_value)
            exponent = jnp.exp(scores - jnp.max(scores, axis=1, keepdims=True))
            low = (exponent / jnp.sum(exponent, axis=1, keepdims=True)).astype(BF16)
            probs[head] = low
            outs.append(dot(low, v))
        attended[:, columns(pair, LANES)] = jnp.where(first, outs[0], outs[1]).astype(BF16)

    for part in range(PARTS):
        pl.loop(part * PAIRS // PARTS, (part + 1) * PAIRS // PARTS)(attend)
        between(part)

    @pl.loop(0, width // 512)
    def _(j):
        resid[:, columns(j, 512)] = tokens[:, columns(j, 512)].astype(F32) + dot(
            attended[...], out_weight[:, columns(j, 512)]
        )

    r = resid[...]
    inv_two = lax.rsqrt(jnp.mean(r * r, axis=1, keepdims=True) + epsilon)
    normed_two[...] = (r * inv_two * small[experts + 1 : experts + 2, :]).astype(BF16)


def attention_forward_kernel(
    experts,
    tokens,
    weights,
    out_weight,
    heads,
    hot,
    length,
    qkv,
    attended,
    probs,
    resid,
    normed_two,
    small,
    *scratch,
):
    out = (qkv, attended, probs, resid, normed_two, small) + scratch
    attend_forward(
        experts, tokens, weights, out_weight, heads, hot, length, out, lambda part: None
    )


def attention_shapes(experts, tokens):
    slots, width = tokens.shape
    return (
        jax.ShapeDtypeStruct((slots, 3 * width), BF16),
        jax.ShapeDtypeStruct((slots, width), BF16),
        jax.ShapeDtypeStruct((HEADS, slots, slots), BF16),
        jax.ShapeDtypeStruct((slots, width), F32),
        jax.ShapeDtypeStruct((slots, width), BF16),
        jax.ShapeDtypeStruct((-(-(experts + 3) // 8) * 8, width), F32),
    )


def attention_forward(experts, tokens, weights, out_weight, heads, hot, length):
    slots, width = tokens.shape
    return call(
        functools.partial(attention_forward_kernel, experts),
        attention_shapes(experts, tokens),
        [pltpu.VMEM((slots, width), BF16), pltpu.VMEM((HEADS, 2 * slots), F32)],
        48 * MB,
        2 * slots * width * (4 * width + 2 * slots),
        tokens,
        weights,
        out_weight,
        heads,
        hot,
        length,
    )


def dispatch_kernel(
    rows, cots, meta, small, own, buffer, scaled, plain, select, gate_column, acc, acc_cot, rank, places
):
    work = Dispatch(own[0, 0], meta, rank, places)
    work.find_places()
    acc[...] = jnp.zeros_like(acc)
    acc_cot[...] = jnp.zeros_like(acc_cot)
    gate_column[...] = jnp.zeros_like(gate_column)
    router_t = small[...].astype(BF16)
    for block in range(work.blocks):
        picked = work.hot(block).astype(F32).astype(BF16)
        select[block] = picked
        gate_column[...] += work.gates(block, rows[block], router_t)
        acc[...] += dot(picked, rows[block])
        acc_cot[...] += dot(picked, cots[block])
    buffer[...] = acc[...].astype(BF16)
    plain[...] = acc_cot[...].astype(BF16)
    scaled[...] = (acc_cot[...] * gate_column[:, 0:1]).astype(BF16)


def dispatch_shapes(blocks, slots, width):
    return (
        jax.ShapeDtypeStruct((CAP, width), BF16),
        jax.ShapeDtypeStruct((CAP, width), BF16),
        jax.ShapeDtypeStruct((CAP, width), BF16),
        jax.ShapeDtypeStruct((blocks, CAP, slots), BF16),
        jax.ShapeDtypeStruct((CAP, 128), F32),
    )


def dispatch_scratch(blocks, slots, width):
    return [
        pltpu.VMEM((CAP, width), F32),
        pltpu.VMEM((CAP, width), F32),
        pltpu.VMEM((blocks, slots, 8), F32),
        pltpu.VMEM((blocks, 8, slots), jnp.int32),
    ]


def dispatch(rows, cots, meta, small, own):
    blocks, slots, width = rows.shape
    return call(
        dispatch_kernel,
        dispatch_shapes(blocks, slots, width),
        dispatch_scratch(blocks, slots, width),
        60 * MB,
        4 * CAP * blocks * slots * width,
        rows,
        cots,
        meta,
        small,
        own,
    )


def forward_kernel(
    experts,
    tokens,
    heads,
    hot,
    length,
    cotangent,
    meta,
    qkv_own,
    out_own,
    beside,
    qkv,
    attended,
    probs,
    resid,
    normed_two,
    small,
    buffer,
    scaled,
    plain,
    select,
    gate_column,
    kept,
    acc,
    acc_cot,
    rank,
    places,
    weights,
    rows,
    cots,
    metas,
    normed,
    diagonals,
    local,
    send,
    recv,
    gather_send,
    gather_recv,
):
    d, e, z, c = here()
    slots, width = tokens.shape
    share = qkv_own.shape[0]
    gather = DeviceGather(weights, share, gather_send, gather_recv)
    rows_spread = Spread(normed_two, rows, send.at[0], recv.at[0], d, e)
    cots_spread = Spread(cotangent, cots, send.at[1], recv.at[1], d, e)
    work = Dispatch(e, metas, rank, places)

    cut = 3 * width + beside.shape[1]
    mine = gather.item(0, 0)
    own_parts = [
        pltpu.make_async_copy(qkv_own, mine.at[:, : 3 * width], local.at[0]),
        pltpu.make_async_copy(beside, mine.at[:, 3 * width : cut], local.at[1]),
        pltpu.make_async_copy(out_own, mine.at[:, cut:], local.at[2]),
    ]
    own_cots = pltpu.make_async_copy(cotangent, cots.at[0], local.at[3])
    for copy in own_parts:
        copy.start()
    meet(group(d, e)[1:] + [gather.other] + gather.to_z[1:])
    meta_copies = [
        push(meta, metas.at[q], send.at[2, q], recv.at[2, q], group(d, e)[q]) for q in (1, 2, 3)
    ]
    for copy in own_parts:
        copy.wait()
    gather.start()
    gather.spread_out(0)
    own_cots.start()
    metas[0] = meta[...]
    for copy in meta_copies:
        copy.wait_recv()
    work.find_places()
    gather.from_z(1)
    gather.from_neighbours(0)
    gather.from_z(3)
    gather.from_z(2)
    for k in (1, 3, 2):
        gather.from_neighbours(k)
    cots_spread.start()
    for k in (0, 1, 3, 2):
        gather.from_across(k)
    gather.complete()
    keep = pltpu.make_async_copy(weights, kept, local.at[4])
    keep.start()

    def between(part):
        if part == 1:
            cots_spread.forward()

    out = (qkv, attended, probs, resid, normed_two, small, normed, diagonals)
    projections, out_weight = weights.at[:, :cut], weights.at[:, cut:]
    attend_forward(experts, tokens, projections, out_weight, heads, hot, length, out, between)

    rows_spread.start()
    own_cots.wait()
    cots_spread.finish()
    router_t = small[...].astype(BF16)

    def take_cots(block):
        picked = work.hot(block).astype(F32).astype(BF16)
        select[block] = picked
        more = dot(picked, cots[block])
        if block:
            acc_cot[...] += more
        else:
            acc_cot[...] = more

    def take_rows(block, ref):
        gate = work.gates(block, ref[...], router_t)
        more = dot(select[block], ref[...])
        if block:
            gate_column[...] += gate
            acc[...] += more
        else:
            gate_column[...] = jnp.broadcast_to(gate, gate_column.shape)
            acc[...] = more

    take_cots(0)
    take_cots(1)
    rows_spread.forward()
    take_cots(2)
    take_cots(3)
    plain[...] = acc_cot[...].astype(BF16)
    take_rows(0, normed_two)
    rows_spread.arrived(1)
    take_rows(1, rows.at[1])
    rows_spread.arrived(2)
    take_rows(2, rows.at[2])
    rows_spread.arrived(3)
    take_rows(3, rows.at[3])
    buffer[...] = acc[...].astype(BF16)
    scaled[...] = (acc_cot[...] * gate_column[:, 0:1]).astype(BF16)
    rows_spread.sent()
    gather.settle()
    for copy in meta_copies:
        copy.wait_send()
    keep.wait()


def forward(experts, tokens, heads, hot, length, cotangent, meta, qkv_own, out_own, beside):
    slots, width = tokens.shape
    full = (32 * qkv_own.shape[0], 4 * width + beside.shape[1])
    block = (experts, slots, width)
    scratch = dispatch_scratch(*block) + [
        pltpu.VMEM(full, BF16),
        pltpu.VMEM(block, BF16),
        pltpu.VMEM(block, BF16),
        pltpu.VMEM((experts,) + meta.shape, jnp.int32),
        pltpu.VMEM((slots, width), BF16),
        pltpu.VMEM((HEADS, 2 * slots), F32),
        DMA((5,)),
        DMA((3, 6)),
        DMA((3, 6)),
        DMA((5, 16)),
        DMA((5, 16)),
    ]
    shapes = attention_shapes(experts, tokens) + dispatch_shapes(*block)
    return call(
        functools.partial(forward_kernel, experts),
        shapes + (jax.ShapeDtypeStruct(full, BF16),),
        scratch,
        60 * MB,
        2 * slots * width * (4 * width + 2 * slots),
        tokens,
        heads,
        hot,
        length,
        cotangent,
        meta,
        qkv_own,
        out_own,
        beside,
        stay=(4, 6, 7, 8),
        land=(len(shapes),),
        link=0,
    )


CHUNK = 256
GELU_A = math.sqrt(2.0 / math.pi)
GELU_B = 0.044715


def expert_chunk(buffer, scaled, gate, up, down):
    gate_in, up_in = dot(buffer, gate), dot(buffer, up)
    square = gate_in * gate_in
    wave = jnp.tanh(GELU_A * gate_in * (1.0 + GELU_B * square))
    half = 0.5 * (1.0 + wave)
    activated = gate_in * half
    slope = half + (0.5 * GELU_A) * gate_in * (1.0 - wave * wave) * (1.0 + 3.0 * GELU_B * square)
    hidden = (activated * up_in).astype(BF16)
    grad_hidden = dot_nt(scaled, down)
    grad_gate_in = (grad_hidden * up_in * slope).astype(BF16)
    grad_up_in = (grad_hidden * activated).astype(BF16)
    grad_buffer = dot_nt(grad_gate_in, gate) + dot_nt(grad_up_in, up)
    return (
        dot(hidden, down),
        grad_buffer,
        dot_tn(buffer, grad_gate_in),
        dot_tn(buffer, grad_up_in),
        dot_tn(hidden, scaled),
    )


def expert_kernel(
    buffer,
    scaled,
    plain,
    gate,
    up,
    down,
    out,
    grad_buffer,
    inner,
    grad_gate,
    grad_up,
    grad_down,
    acc_out,
    acc_grad,
):
    step = pl.program_id(0)

    @pl.when(step == 0)
    def _():
        acc_out[...] = jnp.zeros_like(acc_out)
        acc_grad[...] = jnp.zeros_like(acc_grad)

    more_out, more_grad, d_gate, d_up, d_down = expert_chunk(
        buffer[...], scaled[...], gate[...], up[...], down[...]
    )
    acc_out[...] += more_out
    acc_grad[...] += more_grad
    grad_gate[...] = d_gate.astype(BF16)
    grad_up[...] = d_up.astype(BF16)
    grad_down[...] = d_down.astype(BF16)

    @pl.when(step == pl.num_programs(0) - 1)
    def _():
        low = acc_out[...].astype(BF16)
        out[...] = low
        grad_buffer[...] = acc_grad[...].astype(BF16)
        inner[...] = jnp.broadcast_to(
            jnp.sum(low.astype(F32) * plain[...].astype(F32), axis=1, keepdims=True), inner.shape
        )


def experts(buffer, scaled, plain, gate, up, down):
    rows, width = buffer.shape
    hidden = gate.shape[1]
    whole = pl.BlockSpec((rows, width), lambda j: (0, 0))
    tall = pl.BlockSpec((width, CHUNK), lambda j: (0, j))
    wide = pl.BlockSpec((CHUNK, width), lambda j: (j, 0))
    shapes = (
        jax.ShapeDtypeStruct((rows, width), BF16),
        jax.ShapeDtypeStruct((rows, width), BF16),
        jax.ShapeDtypeStruct((rows, 128), F32),
        jax.ShapeDtypeStruct((width, hidden), BF16),
        jax.ShapeDtypeStruct((width, hidden), BF16),
        jax.ShapeDtypeStruct((hidden, width), BF16),
    )
    return pl.pallas_call(
        expert_kernel,
        out_shape=shapes,
        grid=(hidden // CHUNK,),
        in_specs=[whole, whole, whole, tall, tall, wide],
        out_specs=(whole, whole, pl.BlockSpec((rows, 128), lambda j: (0, 0)), tall, tall, wide),
        scratch_shapes=[pltpu.VMEM((rows, width), F32), pltpu.VMEM((rows, width), F32)],
        compiler_params=pltpu.CompilerParams(
            vmem_limit_bytes=48 * MB, dimension_semantics=("arbitrary",)
        ),
        cost_estimate=pl.CostEstimate(
            flops=18 * rows * width * hidden,
            bytes_accessed=12 * width * hidden,
            transcendentals=rows * hidden,
        ),
    )(buffer, scaled, plain, gate, up, down)


def give_back_kernel(select, out, grad_buffer, inner, gate_column, mixed, grads, inner_rows):
    weighted = (out[...].astype(F32) * gate_column[:, 0:1]).astype(BF16)
    for block in range(select.shape[0]):
        row = jnp.sum(select[block].astype(F32) * inner[:, 0:1], axis=0, keepdims=True)
        inner_rows[block] = jnp.broadcast_to(row, inner_rows.shape[1:])
        grads[block] = dot_tn(select[block], grad_buffer[...]).astype(BF16)
        mixed[block] = dot_tn(select[block], weighted).astype(BF16)


def give_back(select, out, grad_buffer, inner, gate_column):
    blocks, rows, slots = select.shape
    width = out.shape[1]
    wide = (blocks, slots, width)
    return call(
        give_back_kernel,
        (
            jax.ShapeDtypeStruct(wide, BF16),
            jax.ShapeDtypeStruct(wide, BF16),
            jax.ShapeDtypeStruct((blocks, 8, slots), F32),
        ),
        [],
        56 * MB,
        4 * rows * blocks * slots * width,
        select,
        out,
        grad_buffer,
        inner,
        gate_column,
    )


TILE = 2 * CHUNK


def sweep_kernel(
    ready,
    buffer,
    scaled,
    plain,
    gate_column,
    select,
    gate_own,
    up_own,
    early,
    down_full,
    gate_sum,
    up_sum,
    grad_down,
    mixed,
    returned,
    inner_full,
    sums,
    both,
    down,
    acc_out,
    acc_grad,
    down_stage,
    grads,
    inner_rows,
    loaded,
    stored,
    local,
    swap_send,
    swap_recv,
    *scratch,
):
    tiles, width = both.shape[0], both.shape[1]
    share = gate_own.shape[0]
    coming = tiles - ready
    d, e, z, c = here()

    def columns_of(tile):
        return pl.ds(pl.multiple_of(tile * TILE, TILE), TILE)

    def rows_of(device):
        return pl.ds(pl.multiple_of(device * share, share), share)

    spread = LineSpread(
        lambda j: [own.at[:, columns(ready + j, CHUNK)] for own in (gate_own, up_own)],
        lambda j, device: both.at[ready + j, rows_of(device)],
        scratch[:3],
    )
    line = LineSum(
        tiles,
        lambda i, k, core: both.at[i, rows_of(2 * flipped(z, k) + core)],
        scratch[3:],
        load=False,
    )
    swap = Swap(grads, returned, swap_send.at[0], swap_recv.at[0], d, e)
    inner_swap = Swap(inner_rows, inner_full, swap_send.at[1], swap_recv.at[1], d, e)
    meet(group(d, e)[1:] + [line.other] + line.to[1:])

    def early_load(t):
        return pltpu.make_async_copy(early.at[:, columns_of(t)], both.at[t], loaded.at[t])

    down_load = pltpu.make_async_copy(down_full, down, loaded.at[tiles])
    for t in range(ready):
        early_load(t).start()
        if t == 0:
            down_load.start()
    for j in range(min(DEPTH, coming)):
        spread.start(j)
    acc_out[...] = jnp.zeros_like(acc_out)
    acc_grad[...] = jnp.zeros_like(acc_grad)
    down_load.wait()

    def down_rows(t):
        return pl.ds(pl.multiple_of(t * CHUNK, CHUNK), CHUNK)

    def down_store(t, slot):
        return pltpu.make_async_copy(
            down_stage.at[slot], grad_down.at[down_rows(t)], stored.at[slot]
        )

    def between(low, value, high):
        return jnp.logical_and(value >= low, value < high)

    def tile_step(t, _):
        @pl.when(t < ready)
        def _():
            early_load(t).wait()

        near = t - ready + NEAR

        @pl.when(between(0, near, coming))
        def _():
            spread.relay_near(near)

        @pl.when(between(0, near - 1, coming))
        def _():
            spread.relay_far(near - 1)

        @pl.when(between(DEPTH, near - 1 + DEPTH, coming))
        def _():
            spread.start(near - 1 + DEPTH)

        @pl.when(t >= ready)
        def _():
            spread.complete(t - ready)

        @pl.when(t >= 1)
        def _():
            line.halve(t - 1)

        @pl.when(t >= LAG)
        def _():
            line.relay(t - LAG)

        @pl.when(t >= LAG + 1)
        def _():
            line.pass_on(t - LAG - 1)

        more_out, more_grad, d_gate, d_up, d_down = expert_chunk(
            buffer[...], scaled[...], both[t, :, :CHUNK], both[t, :, CHUNK:], down[down_rows(t)]
        )
        acc_out[...] += more_out
        acc_grad[...] += more_grad

        @pl.when(t >= ready)
        def _():
            spread.settle(t - ready)

        both[t, :, :CHUNK] = d_gate.astype(BF16)
        both[t, :, CHUNK:] = d_up.astype(BF16)
        slot = lax.rem(t, 2)

        @pl.when(t >= 2)
        def _():
            down_store(t - 2, slot).wait()

        down_stage[slot] = d_down.astype(BF16)
        down_store(t, slot).start()
        line.begin(t)
        return 0

    lax.fori_loop(0, tiles, tile_step, 0)

    low = acc_out[...].astype(BF16)
    inner = jnp.sum(low.astype(F32) * plain[...].astype(F32), axis=1, keepdims=True)
    grad_low = acc_grad[...].astype(BF16)
    order = (3, 1, 2, 0)
    for block in order:
        row = jnp.sum(select[block].astype(F32) * inner, axis=0, keepdims=True)
        inner_rows[block] = jnp.broadcast_to(row, inner_rows.shape[1:])
        grads[block] = dot_tn(select[block], grad_low).astype(BF16)
        if block:
            inner_swap.start(block)
            swap.start(block)
    own_copies = [
        pltpu.make_async_copy(grads.at[0], returned.at[0], local.at[0]),
        pltpu.make_async_copy(inner_rows.at[0], inner_full.at[0], local.at[1]),
    ]
    for copy in own_copies:
        copy.start()
    line.halve(tiles - 1)
    weighted = (low.astype(F32) * gate_column[:, 0:1]).astype(BF16)
    for block in order:
        mixed[block] = dot_tn(select[block], weighted).astype(BF16)

    @pl.loop(tiles - LAG, tiles + 1)
    def _(i):
        @pl.when(i < tiles)
        def _():
            line.relay(i)

        line.pass_on(i - 1)

    @pl.loop(0, tiles)
    def _(i):
        line.finish(i, sums.at[i])
        for copy in result_stores(sums.at[i], gate_sum, up_sum, i, local.at[2]):
            copy.start()

    @pl.loop(0, tiles)
    def _(i):
        for copy in result_stores(sums.at[i], gate_sum, up_sum, i, local.at[2]):
            copy.wait()

    for t in range(tiles - 2, tiles):
        down_store(t, t % 2).wait()
    for copy in own_copies:
        copy.wait()
    inner_swap.finish()
    swap.finish()


def result_stores(value, gate_sum, up_sum, tile, sem):
    return [
        pltpu.make_async_copy(
            value.at[:, i * CHUNK : (i + 1) * CHUNK], array.at[:, columns(tile, CHUNK)], sem
        )
        for i, array in enumerate((gate_sum, up_sum))
    ]


LAG = 5

DEPTH = 6
NEAR = 2


def sweep(ready, buffer, scaled, plain, gate_column, select, gate_own, up_own, early, down_full):
    rows, width = buffer.shape
    tiles = gate_own.shape[1] // CHUNK
    share = gate_own.shape[0]
    block = (select.shape[0], select.shape[2], width)
    thin = (select.shape[0], 8, select.shape[2])
    hidden = tiles * CHUNK
    shapes = (
        jax.ShapeDtypeStruct(gate_own.shape, F32),
        jax.ShapeDtypeStruct(gate_own.shape, F32),
        jax.ShapeDtypeStruct(down_full.shape, BF16),
        jax.ShapeDtypeStruct(block, BF16),
        jax.ShapeDtypeStruct(block, BF16),
        jax.ShapeDtypeStruct(thin, F32),
    )
    scratch = [
        pltpu.VMEM((tiles, share, TILE), F32),
        pltpu.VMEM((tiles, width, TILE), BF16),
        pltpu.VMEM(down_full.shape, BF16),
        pltpu.VMEM((rows, width), F32),
        pltpu.VMEM((rows, width), F32),
        pltpu.VMEM((2, CHUNK, width), BF16),
        pltpu.VMEM(block, BF16),
        pltpu.VMEM(thin, F32),
        DMA((tiles + 1,)),
        DMA((2,)),
        DMA((3,)),
        DMA((2, 4)),
        DMA((2, 4)),
    ]
    scratch += LineSpread.scratch(tiles - ready) + LineSum.scratch(tiles, share, TILE, False)
    return call(
        functools.partial(sweep_kernel, ready),
        shapes,
        scratch,
        62 * MB,
        18 * rows * width * hidden,
        buffer,
        scaled,
        plain,
        gate_column,
        select,
        gate_own,
        up_own,
        early,
        down_full,
        stay=(5, 6, 7, 8),
        land=(0, 1, 2, 4, 5),
        link=2,
    )


def backward_layer(experts, relative, ins, outs, work, reached):
    tokens, cotangent, weights, out_weight, small, heads, hot_back, length, meta, own = ins[:10]
    returned, inner_rows, qkv, attended, probs, resid, normed_two = ins[10:]
    grad_tokens, grad_small, grad_out, *grad_halves = outs
    grad_attended, grad_qkv, branch, normed, grad_resid, grad_diagonals = work
    slots, width = tokens.shape
    blocks = returned.shape[0]
    router_t = small[...].astype(BF16)
    keep_row = lax.broadcasted_iota(jnp.int32, (slots, 1), 0) < length[0, 0]
    logits = dot_nt(router_t, normed_two[...])
    zero_route, one_route = meta[0:1, :], meta[1:2, :]
    gate_zero, gate_one = pair_gates(logits, zero_route, one_route)
    which = lax.broadcasted_iota(jnp.int32, logits.shape, 0)
    grad_zero = jnp.zeros((1, slots), F32)
    grad_one = jnp.zeros((1, slots), F32)
    for block in range(blocks):
        row = inner_rows[block][0:1, :]
        expert = jnp.bitwise_xor(own[0, 0], block) if relative else block
        grad_zero = grad_zero + jnp.where(zero_route == expert, row, 0.0)
        grad_one = grad_one + jnp.where(one_route == expert, row, 0.0)
    shared = gate_zero * grad_zero + gate_one * grad_one
    grad_zero = gate_zero * (grad_zero - shared)
    grad_one = gate_one * (grad_one - shared)
    grad_logits = jnp.where(which == zero_route, grad_zero, 0.0) + jnp.where(
        which == one_route, grad_one, 0.0
    )
    high, low = two_halves(grad_logits)
    grad_small[...] = dot(high, normed_two[...]) + dot(low, normed_two[...])
    grad_normed_two = dot_tn(high, router_t) + dot_tn(low, router_t)
    for block in range(blocks):
        grad_normed_two = grad_normed_two + returned[block].astype(F32)
    r = resid[...]
    inv_two = lax.rsqrt(jnp.mean(r * r, axis=1, keepdims=True) + epsilon)
    unit_two = r * inv_two
    grad_small[experts + 1 : experts + 2, :] = jnp.sum(
        grad_normed_two * unit_two, axis=0, keepdims=True
    )
    scaled_two = small[experts + 1 : experts + 2, :] * grad_normed_two
    grad_resid[...] = jnp.where(keep_row, cotangent[...].astype(F32), 0.0) + inv_two * (
        scaled_two - unit_two * jnp.mean(scaled_two * unit_two, axis=1, keepdims=True)
    )
    branch[...] = grad_resid[...].astype(BF16)
    reached("branch")

    @pl.loop(0, width // 256)
    def _(j):
        grad_out[:, columns(j, 256)] = dot_tn(attended[...], branch[:, columns(j, 256)]).astype(
            BF16
        )

    reached("out")
    grad_attended[...] = dot_nt(branch[...], out_weight[...]).astype(BF16)
    x = tokens[...].astype(F32)
    inv_one = lax.rsqrt(jnp.mean(x * x, axis=1, keepdims=True) + epsilon)
    normed[...] = (x * inv_one * small[experts : experts + 1, :]).astype(BF16)
    reached("attended")

    lane = lax.broadcasted_iota(jnp.int32, (slots, LANES), 1)
    first = lane < HD
    square = (slots, slots)
    flip = (
        lax.broadcasted_iota(jnp.int32, square, 0) + lax.broadcasted_iota(jnp.int32, square, 1)
        == slots - 1
    )
    flip = flip.astype(F32).astype(BF16)

    def attend_back(pair):
        q = qkv[:, columns(pair, LANES)]
        k = qkv[:, columns(PAIRS + pair, LANES)]
        v = qkv[:, columns(2 * PAIRS + pair, LANES)]
        g = grad_attended[:, columns(pair, LANES)]
        dq, dk, dv = [], [], []
        for half in range(2):
            head = 2 * pair + half
            mine = first if half == 0 else jnp.logical_not(first)
            low = probs[head]
            p = low.astype(F32)
            grad_probs = dot_nt(jnp.where(mine, g, jnp.zeros_like(g)), v)
            ds = p * (grad_probs - jnp.sum(p * grad_probs, axis=1, keepdims=True))
            ds = ds.astype(BF16)
            wide = jnp.concatenate([dot(flip, ds), jnp.zeros((slots, slots), F32)], axis=1)
            skewed = pltpu.roll(wide, 0, 1, stride=1, stride_axis=0)
            grad_diagonals[pl.ds(head, 1), :] = jnp.sum(skewed, axis=0, keepdims=True)
            dq.append(dot(ds, k))
            dk.append(dot_tn(ds, q))
            dv.append(dot_tn(low, g))
        grad_qkv[:, columns(pair, LANES)] = (jnp.where(first, dq[0], dq[1]) * SCALE).astype(BF16)
        grad_qkv[:, columns(PAIRS + pair, LANES)] = (
            jnp.where(first, dk[0], dk[1]) * SCALE
        ).astype(BF16)
        grad_qkv[:, columns(2 * PAIRS + pair, LANES)] = jnp.where(first, dv[0], dv[1]).astype(BF16)

    for part in range(PARTS):
        pl.loop(part * PAIRS // PARTS, (part + 1) * PAIRS // PARTS)(attend_back)
        reached(f"part{part}")
        if part % 2 == 1:
            half, wide = part // 2, width // 2
            for i in range(3):
                for j in range(wide // 256):
                    source = i * width + half * wide + j * 256
                    at = i * wide + j * 256
                    grad_halves[half][:, at : at + 256] = dot_tn(
                        normed[...], grad_qkv[:, source : source + 256]
                    ).astype(BF16)
            reached(f"half{half}")

    high, low = two_halves(grad_diagonals[...])
    by_lane = dot_nt(high, hot_back[...]) + dot_nt(low, hot_back[...])
    grad_small[experts + 2 : experts + 3, :] = jnp.sum(
        by_lane * heads[...].astype(F32), axis=0, keepdims=True
    )
    grad_normed = dot_nt(grad_qkv[...], weights[:, : 3 * width])
    x = tokens[...].astype(F32)
    inv_one = lax.rsqrt(jnp.mean(x * x, axis=1, keepdims=True) + epsilon)
    unit_one = x * inv_one
    grad_small[experts : experts + 1, :] = jnp.sum(grad_normed * unit_one, axis=0, keepdims=True)
    scaled_one = small[experts : experts + 1, :] * grad_normed
    grad_tokens[...] = grad_resid[...] + inv_one * (
        scaled_one - unit_one * jnp.mean(scaled_one * unit_one, axis=1, keepdims=True)
    )
    reached("tokens")


def backward_scratch(slots, width):
    return [
        pltpu.VMEM((slots, width), BF16),
        pltpu.VMEM((slots, 3 * width), BF16),
        pltpu.VMEM((slots, width), BF16),
        pltpu.VMEM((slots, width), BF16),
        pltpu.VMEM((slots, width), F32),
        pltpu.VMEM((HEADS, 2 * slots), F32),
    ]


def add_mixed(output, resid, length, parts):
    keep_row = lax.broadcasted_iota(jnp.int32, (resid.shape[0], 1), 0) < length[0, 0]
    total = resid[...]
    for part in parts:
        total = total + part[...].astype(F32)
    output[...] = jnp.where(keep_row, total, 0.0).astype(BF16)


def local_backward_kernel(experts, *refs):
    ins, mixed, output, outs, work = refs[:17], refs[17], refs[18], refs[19:24], refs[24:]
    backward_layer(experts, False, ins, outs, work, lambda name: None)
    add_mixed(output, ins[15], ins[7], [mixed.at[block] for block in range(mixed.shape[0])])


def local_backward(experts, *args):
    tokens, small = args[0], args[4]
    slots, width = tokens.shape
    return call(
        functools.partial(local_backward_kernel, experts),
        (
            jax.ShapeDtypeStruct((slots, width), BF16),
            jax.ShapeDtypeStruct((slots, width), F32),
            jax.ShapeDtypeStruct(small.shape, F32),
            jax.ShapeDtypeStruct((width, width), BF16),
            jax.ShapeDtypeStruct((width, 3 * width // 2), BF16),
            jax.ShapeDtypeStruct((width, 3 * width // 2), BF16),
        ),
        backward_scratch(slots, width),
        62 * MB,
        4 * slots * width * (4 * width + 2 * slots),
        *args,
    )


class DeviceSum:
    @staticmethod
    def scratch(share, width):
        return [
            pltpu.VMEM((4, 4 * share, width), BF16),
            pltpu.VMEM((4, 2, share, width), BF16),
            pltpu.VMEM((4, share, width), BF16),
            DMA((4, 4)),
            DMA((4, 4)),
        ] + LineSum.scratch(1, share, width, False)

    def __init__(self, partial, scratch):
        self.partial = partial
        self.theirs, self.first_in, self.second_in, self.send, self.recv = scratch[:5]
        self.line = LineSum(1, None, scratch[5:], False)
        self.share = self.second_in.shape[1]
        self.d, self.e, self.z, self.core = here()
        self.other = (2 * self.z + 1 - self.core, self.e)
        self.to_x, self.to_y = (self.d, flipped(self.e, 1)), (self.d, flipped(self.e, 2))

    def rows(self, k, core, start, count):
        row = (2 * flipped(self.z, k) + core) * 4 * self.share + start
        return self.partial.at[pl.ds(pl.multiple_of(row, self.share), count)]

    def piece(self, k, q):
        return self.rows(k, self.core, flipped(self.e, q) * self.share, self.share)

    def remote(self, src, dst, stage, k, to):
        return pltpu.make_async_remote_copy(
            src_ref=src,
            dst_ref=dst,
            send_sem=self.send.at[stage, k],
            recv_sem=self.recv.at[stage, k],
            device_id=to,
            device_id_type=MESH,
        )

    def swap(self, k):
        src = self.rows(k, 1 - self.core, 0, 4 * self.share)
        return self.remote(src, self.theirs.at[k], 0, k, self.other)

    def first(self, k, slot):
        near, to = (1, self.to_x) if k % 2 == 0 else (2, self.to_y)
        return self.remote(
            self.piece(k, 3 if slot else near), self.first_in.at[k, slot], 1 + slot, k, to
        )

    def far(self, k):
        return 2 if k % 2 == 0 else 1

    def second(self, k):
        to = self.to_y if k % 2 == 0 else self.to_x
        return self.remote(self.piece(k, self.far(k)), self.second_in.at[k], 3, k, to)

    def begin(self):
        for k in (3, 2, 1, 0):
            self.swap(k).start()

    def stage_one(self):
        for k in (3, 2, 1, 0):
            self.swap(k).wait_recv()

            @pl.loop(0, 4)
            def _(j):
                start = pl.multiple_of(j * self.share, self.share)
                mine = self.rows(k, self.core, start, self.share)
                mine[...] = (
                    mine[...].astype(F32) + self.theirs[k, pl.ds(start, self.share)].astype(F32)
                ).astype(BF16)

            self.first(k, 1).start()
            self.first(k, 0).start()

    def stage_two(self):
        for k in (3, 2, 1, 0):
            self.first(k, 1).wait_recv()
            source = self.piece(k, self.far(k))
            source[...] = (source[...].astype(F32) + self.first_in[k, 1].astype(F32)).astype(BF16)
            self.second(k).start()

    def stage_three(self):
        for k in (3, 2, 1, 0):
            self.first(k, 0).wait_recv()
            self.second(k).wait_recv()
            total = self.piece(k, 0)[...].astype(F32) + self.first_in[k, 0].astype(F32)
            self.line.theirs[0, k] = (total + self.second_in[k].astype(F32)).astype(BF16)
        self.line.hand_over(0)

    def settle(self):
        for k in range(4):
            self.swap(k).wait_send()
            self.first(k, 0).wait_send()
            self.first(k, 1).wait_send()
            self.second(k).wait_send()


class EverySum:
    @staticmethod
    def scratch(shape):
        return [
            pltpu.VMEM((6,) + shape, F32),
            pltpu.VMEM((5,) + shape, F32),
            DMA((5,)),
            DMA((5,)),
        ]

    def __init__(self, scratch):
        self.sums, self.landed, self.send, self.recv = scratch
        d, e, z, c = here()
        near = [(2 * flipped(z, k) + c, e) for k in (1, 2)]
        self.to = [(2 * z + 1 - c, e), (d, flipped(e, 1)), (d, flipped(e, 2))] + near

    def copy(self, at):
        return pltpu.make_async_remote_copy(
            src_ref=self.sums.at[at],
            dst_ref=self.landed.at[at],
            send_sem=self.send.at[at],
            recv_sem=self.recv.at[at],
            device_id=self.to[at],
            device_id_type=MESH,
        )

    def start(self, value):
        self.sums[0] = value
        self.copy(0).start()

    def step(self, at):
        self.copy(at).wait_recv()
        self.sums[at + 1] = self.sums[at] + self.landed[at]
        if at + 1 < len(self.to):
            self.copy(at + 1).start()

    def settle(self):
        for at in range(len(self.to)):
            self.copy(at).wait_send()


def down_source(array, z, share):
    def source(i, k, core):
        row = pl.multiple_of((2 * flipped(z, k) + core) * share, share)
        return array.at[pl.ds(row, share), pl.ds(pl.multiple_of(i * CHUNK, CHUNK), CHUNK)]

    return source


def backward_kernel(experts, *refs):
    refs = list(refs)

    def take(count):
        taken, refs[:] = refs[:count], refs[count:]
        return taken

    ins = take(17)
    mixed, grad_down = take(2)
    output, grad_tokens, qkv_sum, out_sum, small_sum, down_sum = take(6)
    grad_small, grad_out, *grad_halves = take(4)
    work = take(6)
    half_sums, *brought, fetched = take(6)
    cut = brought[0].shape[1]
    ins[2], ins[3] = ins[2].at[:, :cut], ins[3].at[:, cut:]
    fetches = []
    for i, (at, ref) in enumerate(zip(FETCHED, brought)):
        fetches.append(pltpu.make_async_copy(ins[at], ref, fetched.at[i]))
        fetches[-1].start()
        ins[at] = ref
    mixed_full, mixed_send, mixed_recv = take(3)
    d, e, z, _ = here()
    width = out_sum.shape[1]
    down = LineSum(width // CHUNK, down_source(grad_down, z, down_sum.shape[0]), take(6), True)
    out = DeviceSum(grad_out, take(9))
    halves = [DeviceSum(grad_half, take(9)) for grad_half in grad_halves]
    every = EverySum(take(4))
    swap = Swap(mixed, mixed_full, mixed_send, mixed_recv, d, e)
    meet(group(d, e)[1:] + [down.other] + down.to[1:])
    for block in (3, 1, 2):
        swap.start(block)
    for i in range(down.count):
        down.begin(i)
    down.halve(0)

    def reached(name):
        if name == "branch":
            down.halve(1)
        elif name == "out":
            out.begin()
            for copy in fetches:
                copy.wait()
        elif name == "attended":
            down.halve(2)
        elif name == "part0":
            out.stage_one()
            down.relay(0)
        elif name == "part1":
            out.stage_two()
        elif name == "half0":
            halves[0].begin()
            down.pass_on(0)
            down.relay(1)
        elif name == "part2":
            halves[0].stage_one()
            out.stage_three()
            down.halve(3)
        elif name == "part3":
            halves[0].stage_two()
            down.pass_on(1)
        elif name == "half1":
            halves[1].begin()
            down.relay(2)
        elif name == "tokens":
            every.start(grad_small[...])
            halves[1].stage_one()

    outs = [grad_tokens, grad_small, grad_out] + grad_halves
    backward_layer(experts, True, ins, outs, work, reached)
    halves[0].stage_three()
    every.step(0)
    halves[1].stage_two()
    out.line.relay(0)
    every.step(1)
    down.pass_on(2)
    down.relay(3)
    out.line.pass_on(0)
    halves[1].stage_three()
    every.step(2)
    halves[0].line.relay(0)
    down.pass_on(3)
    every.step(3)
    halves[0].line.pass_on(0)
    halves[1].line.relay(0)
    every.step(4)
    small_sum[...] = every.sums[5]
    for i in range(down.count):
        down.finish(i, down_sum.at[:, i * CHUNK : (i + 1) * CHUNK])
    halves[1].line.pass_on(0)
    swap.finish()
    add_mixed(output, ins[15], ins[7], [mixed.at[0]] + [mixed_full.at[q] for q in (1, 2, 3)])
    out.line.finish(0, out_sum)
    wide = width // 2
    for half, sums in enumerate(halves):
        sums.line.finish(0, half_sums.at[half])
        for i in range(3):
            at = i * width + half * wide
            qkv_sum[:, at : at + wide] = half_sums[half, :, i * wide : (i + 1) * wide]
    for sums in [out] + halves:
        sums.settle()
    every.settle()


FETCHED = (2, 3, 12, 14)


def backward(experts, *args):
    tokens, small, mixed, grad_down = args[0], args[4], args[17], args[18]
    slots, width = tokens.shape
    share, down_share = width // 32, grad_down.shape[0] // 8
    half = 3 * width // 2
    scratch = [
        pltpu.VMEM(small.shape, F32),
        pltpu.VMEM((width, width), BF16),
        pltpu.VMEM((width, half), BF16),
        pltpu.VMEM((width, half), BF16),
        *backward_scratch(slots, width),
        pltpu.VMEM((2, share, half), F32),
        pltpu.VMEM((width, args[2].shape[1] - width), BF16),
        pltpu.VMEM((width, width), BF16),
        *[pltpu.VMEM(args[i].shape, BF16) for i in FETCHED[2:]],
        DMA((len(FETCHED),)),
        pltpu.VMEM(mixed.shape, BF16),
        DMA((4,)),
        DMA((4,)),
        *LineSum.scratch(width // CHUNK, down_share, CHUNK, True),
        *DeviceSum.scratch(share, width),
        *DeviceSum.scratch(share, half),
        *DeviceSum.scratch(share, half),
        *EverySum.scratch(small.shape),
    ]
    return call(
        functools.partial(backward_kernel, experts),
        (
            jax.ShapeDtypeStruct((slots, width), BF16),
            jax.ShapeDtypeStruct((slots, width), F32),
            jax.ShapeDtypeStruct((share, 3 * width), F32),
            jax.ShapeDtypeStruct((share, width), F32),
            jax.ShapeDtypeStruct(small.shape, F32),
            jax.ShapeDtypeStruct((down_share, width), F32),
        ),
        scratch,
        63 * MB,
        4 * slots * width * (4 * width + 2 * slots),
        *args,
        stay=(18,) + FETCHED,
        link=3,
    )


def publish_kernel(*refs):
    count = (len(refs) - 2) // 3
    ins, outs, held = refs[:count], refs[count : 2 * count], refs[2 * count : 3 * count]
    loads = [pltpu.make_async_copy(ins[i], held[i], refs[-2].at[i]) for i in range(count)]
    stores = [pltpu.make_async_copy(held[i], outs[i], refs[-1].at[i]) for i in range(count)]
    for copy in loads:
        copy.start()
    for load, store in zip(loads, stores):
        load.wait()
        store.start()
    for copy in stores:
        copy.wait()


def publish(*values):
    count = len(values)
    return call(
        publish_kernel,
        tuple(jax.ShapeDtypeStruct(value.shape, value.dtype) for value in values),
        [pltpu.VMEM(value.shape, value.dtype) for value in values] + [DMA((count,)), DMA((count,))],
        60 * MB,
        0,
        *values,
        stay=tuple(range(count)),
        land=tuple(range(count)),
    )


READY = 3


def on_device(
    fast,
    tokens,
    cotangent,
    qkv_weight,
    out_weight,
    router_weight,
    first_gain,
    second_gain,
    bias_table,
    gate_weight,
    up_weight,
    down_weight,
    lengths,
    routes,
    priority,
):
    both = ("dp", "expert")
    slots, width = tokens.shape
    expert_count = lax.axis_size("expert")
    device_count = lax.axis_size("dp") * expert_count
    share, bias_share = first_gain.shape[0], bias_table.shape[0]
    device = lax.axis_index("dp") * expert_count + lax.axis_index("expert")
    own = lax.axis_index("expert").astype(jnp.int32).reshape(1, 1)
    small_rows = -(-(expert_count + 3) // 8) * 8

    def gathered(value, axes, axis=0, tiled=True):
        return lax.all_gather(value, axes, axis=axis, tiled=tiled)

    def scattered(value, axes):
        return lax.psum_scatter(value, axes, scatter_dimension=0, tiled=True).astype(F32)

    def exchanged(value):
        return lax.all_to_all(value, "expert", split_axis=0, concat_axis=0, tiled=True)

    rows_own, hidden = gate_weight.shape[1:]
    down_full = gathered(down_weight[0], "dp")
    if fast:
        cut = (rows_own, READY, 1, CHUNK)
        early = jnp.concatenate(
            [value[0, :, : READY * CHUNK].reshape(cut) for value in (gate_weight, up_weight)],
            axis=2,
        ).reshape(rows_own, READY * TILE)
        early = gathered(early, "dp")
    else:
        gate_full, up_full = (gathered(value[0], "dp") for value in (gate_weight, up_weight))

    beside = jnp.concatenate(
        [
            router_weight,
            first_gain[:, None],
            second_gain[:, None],
            jnp.pad(bias_table, (0, share - bias_share))[:, None],
            jnp.zeros((share, 128 - expert_count - 3), BF16),
        ],
        axis=1,
    )
    lane = np.arange(width)
    flat = lane // share * bias_share + lane % share
    in_table = lane % share < bias_share
    heads = np.arange(HEADS)[:, None] == np.where(in_table, flat // BUCKETS, -1)[None, :]
    heads = jnp.asarray(heads.astype(np.float32), BF16)
    ahead = np.arange(2 * slots)

    def hot(ahead):
        return jnp.asarray(
            np.where(in_table[:, None], diagonal_onehot(ahead)[flat % BUCKETS], 0.0), BF16
        )

    valid_rows = jnp.arange(slots, dtype=jnp.int32) < lengths[0, 0]
    meta_own = jnp.concatenate(
        [
            routes.T,
            priority,
            valid_rows.astype(jnp.int32)[None, :],
            jnp.zeros((4, slots), jnp.int32),
        ],
        axis=0,
    )

    diagonals_hot = hot(np.where(ahead < slots, ahead, ahead - 2 * slots))
    if fast:
        *kept, buffer, scaled, plain, select, gate_column, weights = forward(
            expert_count,
            tokens,
            heads,
            diagonals_hot,
            lengths,
            cotangent,
            meta_own,
            qkv_weight,
            out_weight,
            beside,
        )
        out_full = weights
    else:
        weights = gathered(jnp.concatenate([qkv_weight, beside], axis=1), both)
        out_full = gathered(out_weight, both)
        kept = attention_forward(
            expert_count, tokens, weights, out_full, heads, diagonals_hot, lengths
        )
        rows, cots, meta = (
            gathered(value, "expert", tiled=False) for value in (kept[4], cotangent, meta_own)
        )
        buffer, scaled, plain, select, gate_column = dispatch(rows, cots, meta, kept[5], own)
    qkv, attended, probs, resid, normed_two, small = kept
    if fast:
        grad_gate, grad_up, grad_down, mixed, returned, inner_rows = sweep(
            READY,
            buffer,
            scaled,
            plain,
            gate_column,
            select,
            gate_weight[0],
            up_weight[0],
            early,
            down_full,
        )
    else:
        expert_out, grad_buffer, inner, *grad_experts = experts(
            buffer, scaled, plain, gate_full, up_full, down_full
        )
        mixed, returned, inner_rows = (
            exchanged(value)
            for value in give_back(select, expert_out, grad_buffer, inner, gate_column)
        )
        grad_gate, grad_up, grad_down = (scattered(value, "dp")[None] for value in grad_experts)
    layer = (
        tokens,
        cotangent,
        weights,
        out_full,
        small,
        heads,
        hot(ahead - (slots - 1)),
        lengths,
        meta_own,
        own,
        returned,
        inner_rows,
        qkv,
        attended,
        probs,
        resid,
        normed_two,
        mixed,
    )
    if fast:
        output, grad_tokens, grad_qkv, grad_out, grad_small, grad_down = backward(
            expert_count, *layer, grad_down
        )
        output, grad_tokens, grad_qkv, grad_out, grad_gate, grad_up, grad_down = publish(
            output, grad_tokens, grad_qkv, grad_out, grad_gate, grad_up, grad_down
        )
        grad_gate, grad_up, grad_down = grad_gate[None], grad_up[None], grad_down[None]
    else:
        output, grad_tokens, grad_small, *grad_weights = local_backward(expert_count, *layer)
        grad_out, *halves = (scattered(value, both) for value in grad_weights)
        grad_qkv = jnp.stack([half.reshape(share, 3, width // 2) for half in halves], axis=2)
        grad_qkv = grad_qkv.reshape(share, 3 * width)
        grad_small = lax.psum(grad_small, both)
    grad_small = lax.dynamic_slice(grad_small, (0, device * share), (small_rows, share))
    return (
        output,
        grad_tokens,
        grad_qkv,
        grad_out,
        grad_small[:expert_count].T,
        grad_small[expert_count],
        grad_small[expert_count + 1],
        grad_small[expert_count + 2, :bias_share],
        grad_gate,
        grad_up,
        grad_down,
    )


def solution(mesh):
    fast = dict(mesh.shape) == {"dp": 8, "expert": 4}
    rows = P(("dp", "expert"), None)
    flat = P(("dp", "expert"))
    expert = P("expert", "dp", None)
    grid = P("dp", "expert")
    return jax.shard_map(
        functools.partial(on_device, fast),
        mesh=mesh,
        in_specs=(rows,) * 5 + (flat,) * 3 + (expert,) * 3 + (grid, rows, grid),
        out_specs=(rows,) * 5 + (flat,) * 3 + (expert,) * 3,
        check_vma=False,
    )
```

```python
import functools
import math

import jax
import jax.numpy as jnp
import numpy as np
from jax import lax
from jax.experimental import pallas as pl
from jax.experimental.pallas import tpu as pltpu
from jax.sharding import PartitionSpec as P

HEADS = 16
HD = 64
BUCKETS = 32
CAP = 480
PAIRS = HEADS // 2
LANES = 2 * HD
PARTS = 4
CHUNK = 256
TILE = 2 * CHUNK

epsilon = 1e-06
masked_value = -1e30
max_distance = 128.0
SCALE = 1.0 / math.sqrt(HD)
MB = 1 << 20
F32 = jnp.float32
BF16 = jnp.bfloat16


def bucket_of(offset, bucket_count):
    halfway = bucket_count // 2
    exact_span = bucket_count // 4
    distance = np.abs(offset)
    log_part = np.log(np.maximum(distance, 1) / float(exact_span)) / np.log(
        max_distance / exact_span
    )
    far_bucket = np.minimum(
        exact_span + np.floor(log_part * exact_span).astype(np.int64), halfway - 1
    )
    inside = np.where(distance < exact_span, distance, far_bucket)
    return np.where(offset < 0, halfway, 0) + inside


def diagonal_onehot(ahead):
    return (bucket_of(-ahead, BUCKETS)[None, :] == np.arange(BUCKETS)[:, None]).astype(np.float32)


def dot(a, b):
    return jnp.dot(a, b, preferred_element_type=F32)


def dot_nt(a, b):
    return lax.dot_general(a, b, (((1,), (1,)), ((), ())), preferred_element_type=F32)


def dot_tn(a, b):
    return lax.dot_general(a, b, (((0,), (0,)), ((), ())), preferred_element_type=F32)


def two_halves(value):
    high = value.astype(BF16)
    return high, (value - high.astype(F32)).astype(BF16)


def columns(index, width):
    return pl.ds(pl.multiple_of(index * width, width), width)


VMEM_SPEC = pl.BlockSpec(memory_space=pltpu.VMEM)


ANY_SPEC = pl.BlockSpec(memory_space=pl.ANY)
MESH = pl.DeviceIdType.MESH
DMA = pltpu.SemaphoreType.DMA


def call(kernel, out_shape, scratch, vmem, flops, *args, stay=(), land=(), link=None, aliases=None):
    nbytes = sum(a.size * a.dtype.itemsize for a in args)
    params = dict(vmem_limit_bytes=vmem)
    if link is not None:
        params.update(collective_id=link, has_side_effects=True)
    return pl.pallas_call(
        kernel,
        out_shape=out_shape,
        in_specs=[ANY_SPEC if i in stay else VMEM_SPEC for i in range(len(args))],
        out_specs=tuple(ANY_SPEC if i in land else VMEM_SPEC for i in range(len(out_shape))),
        scratch_shapes=scratch,
        input_output_aliases=aliases or {},
        compiler_params=pltpu.CompilerParams(**params),
        cost_estimate=pl.CostEstimate(flops=flops, bytes_accessed=nbytes, transcendentals=0),
    )(*args)


def here():
    d, e = lax.axis_index("dp"), lax.axis_index("expert")
    return d, e, d // 2, lax.rem(d, 2)


def flipped(value, bits):
    low, high = lax.rem(value, 2), value // 2
    low = 1 - low if bits & 1 else low
    high = 1 - high if bits & 2 else high
    return 2 * high + low


def meet(partners):
    barrier = pltpu.get_barrier_semaphore()
    for partner in partners:
        pl.semaphore_signal(barrier, inc=1, device_id=partner, device_id_type=MESH)
    pl.semaphore_wait(barrier, len(partners))


def push(src, dst, send, recv, to):
    copy = pltpu.make_async_remote_copy(
        src_ref=src, dst_ref=dst, send_sem=send, recv_sem=recv, device_id=to, device_id_type=MESH
    )
    copy.start()
    return copy


def group(d, e):
    return [None] + [(d, flipped(e, q)) for q in (1, 2, 3)]


class Spread:
    def __init__(self, src, dst, send, recv, d, e):
        self.src, self.dst, self.send, self.recv = src, dst, send, recv
        self.to = group(d, e)
        self.half = src.shape[0] // 2
        self.copies = {}

    def part(self, ref, half):
        return ref.at[pl.ds(half * self.half, self.half)]

    def start(self):
        for turn in range(2):
            for q in (1, 2):
                half = turn if q == 1 else 1 - turn
                at = 2 * (q - 1) + half
                self.copies[q, half] = push(
                    self.part(self.src, half),
                    self.part(self.dst.at[q], half),
                    self.send.at[at],
                    self.recv.at[at],
                    self.to[q],
                )

    def forward(self):
        for q, half, across, at in ((1, 0, 2, 4), (2, 1, 1, 5)):
            self.copies[q, half].wait_recv()
            self.copies[3, half] = push(
                self.part(self.dst.at[q], half),
                self.part(self.dst.at[3], half),
                self.send.at[at],
                self.recv.at[at],
                self.to[across],
            )

    def arrived(self, q):
        for half in {1: (1,), 2: (0,), 3: (0, 1)}[q]:
            self.copies[q, half].wait_recv()

    def sent(self):
        for copy in self.copies.values():
            copy.wait_send()

    def finish(self):
        for q in (1, 2, 3):
            self.arrived(q)
        self.sent()


class Swap:
    def __init__(self, src, dst, send, recv, d, e):
        self.src, self.dst, self.send, self.recv = src, dst, send, recv
        self.to = group(d, e)
        self.copies = {}

    def start(self, q):
        self.copies[q] = push(
            self.src.at[q], self.dst.at[q], self.send.at[q], self.recv.at[q], self.to[q]
        )

    def finish(self):
        for copy in self.copies.values():
            copy.wait_recv()
        for copy in self.copies.values():
            copy.wait_send()


class DeviceGather:
    WAYS = 5

    def __init__(self, full, share, send, recv):
        self.full, self.share, self.send, self.recv = full, share, send, recv
        self.d, self.e, self.z, self.core = d, e, z, c = here()
        self.to_x, self.to_y = (d, flipped(e, 1)), (d, flipped(e, 2))
        self.other = (2 * z + 1 - c, e)
        self.to_z = [None] + [(2 * flipped(z, k) + c, e) for k in (1, 2, 3)]
        self.end = jnp.logical_or(z == 0, z == 3)
        self.middle = jnp.logical_not(self.end)

    def item(self, k, q, core=None):
        device = 2 * flipped(self.z, k) + (self.core if core is None else core)
        row = (device * 4 + flipped(self.e, q)) * self.share
        return self.full.at[pl.ds(pl.multiple_of(row, self.share), self.share)]

    def pass_on(self, k, q, way, at, to, into=None):
        piece = self.item(k, q)
        return pltpu.make_async_remote_copy(
            src_ref=piece,
            dst_ref=piece,
            send_sem=self.send.at[way, at],
            recv_sem=self.recv.at[way, at if into is None else into],
            device_id=to,
            device_id_type=MESH,
        )

    def along_z(self, k):
        return self.pass_on(0, 0, 0, k, self.to_z[k])

    def relay_z(self, k):
        return self.pass_on(k, 0, 0, 2 + k, self.to_z[1], 5 - k)

    def along_x(self, k):
        return self.pass_on(k, 0, 1, k, self.to_x)

    def along_y(self, k):
        return self.pass_on(k, 0, 2, k, self.to_y)

    def across(self, k):
        return self.pass_on(k, 1, 3, k, self.to_y) if k % 2 == 0 else self.pass_on(k, 2, 3, k, self.to_x)

    def over(self, k, q):
        return self.pass_on(k, q, 4, 4 * q + k, self.other)

    def start(self):
        self.along_z(1).start()

        @pl.when(self.middle)
        def _():
            self.along_z(3).start()

        @pl.when(self.end)
        def _():
            self.along_z(2).start()

    def spread_out(self, k):
        self.along_x(k).start()
        self.along_y(k).start()
        self.over(k, 0).start()

    def from_z(self, k):
        self.along_z(k).wait_recv()
        if k > 1:

            @pl.when(self.middle)
            def _():
                self.relay_z(k).start()

        self.spread_out(k)

    def from_neighbours(self, k):
        self.along_x(k).wait_recv()
        if k % 2 == 0:
            self.across(k).start()
        self.over(k, 1).start()
        self.along_y(k).wait_recv()
        if k % 2 == 1:
            self.across(k).start()
        self.over(k, 2).start()

    def from_across(self, k):
        self.across(k).wait_recv()
        self.over(k, 3).start()

    def complete(self):
        for q in range(4):
            for k in range(4):
                self.over(k, q).wait_recv()

    def settle(self):
        self.along_z(1).wait_send()

        @pl.when(self.middle)
        def _():
            self.along_z(3).wait_send()
            self.relay_z(2).wait_send()
            self.relay_z(3).wait_send()

        @pl.when(self.end)
        def _():
            self.along_z(2).wait_send()

        for k in range(4):
            self.along_x(k).wait_send()
            self.along_y(k).wait_send()
            self.across(k).wait_send()
            for q in range(4):
                self.over(k, q).wait_send()


class LineSum:
    def __init__(self, count, source, scratch, load):
        self.count, self.source, self.load_first = count, source, load
        scratch = list(scratch)
        self.theirs, self.landed, self.send, self.recv = scratch[:4]
        if load:
            self.loads, self.loaded = scratch[4:]
        self.d, self.e, self.z, self.core = here()
        self.other = (2 * self.z + 1 - self.core, self.e)
        self.to = [None] + [(2 * flipped(self.z, k) + self.core, self.e) for k in (1, 2, 3)]
        self.end = jnp.logical_or(self.z == 0, self.z == 3)
        self.middle = jnp.logical_not(self.end)

    @staticmethod
    def scratch(count, rows, width, load):
        part = (rows, width)
        parts = [
            pltpu.VMEM((count, 4) + part, BF16),
            pltpu.VMEM((count, 5) + part, BF16),
            DMA((count, 3, 5)),
            DMA((count, 3, 5)),
        ]
        return parts + ([pltpu.VMEM((count, 4) + part, BF16), DMA((count, 4))] if load else [])

    def remote(self, i, src, dst, stage, out, into, to):
        return pltpu.make_async_remote_copy(
            src_ref=src,
            dst_ref=dst,
            send_sem=self.send.at[i, stage, out],
            recv_sem=self.recv.at[i, stage, into],
            device_id=to,
            device_id_type=MESH,
        )

    def load(self, i, k):
        return pltpu.make_async_copy(
            self.source(i, k, self.core), self.loads.at[i, k], self.loaded.at[i, k]
        )

    def swap(self, i, k):
        src = self.source(i, k, 1 - self.core)
        return self.remote(i, src, self.theirs.at[i, k], 0, k, k, self.other)

    def hand(self, i, k):
        at = 1 if k == 1 else 5 - k
        return self.remote(i, self.theirs.at[i, k], self.landed.at[i, at], 1, k, at, self.to[1])

    def handed(self, i, at):
        return self.remote(i, self.theirs.at[i, at], self.landed.at[i, at], 1, at, at, self.to[1])

    def deliver(self, i, k):
        at = 0 if k == 3 else 4
        return self.remote(i, self.theirs.at[i, k], self.landed.at[i, at], 2, k, at, self.to[3])

    def for_partner(self, i):
        return self.remote(i, self.theirs.at[i, 0], self.landed.at[i, 4], 2, 4, 4, self.to[3])

    def last(self, i):
        return self.remote(i, self.theirs.at[i, 1], self.landed.at[i, 0], 2, 0, 0, self.to[1])

    def add(self, i, k, more):
        self.theirs[i, k] = (self.theirs[i, k].astype(F32) + more[...].astype(F32)).astype(BF16)

    def begin(self, i):
        for k in (3, 2, 1, 0):
            self.swap(i, k).start()
            if self.load_first:
                self.load(i, k).start()

    def halve(self, i):
        for k in (3, 2, 1, 0):
            if self.load_first:
                self.load(i, k).wait()
            self.swap(i, k).wait_recv()
            self.add(i, k, self.loads.at[i, k] if self.load_first else self.source(i, k, self.core))
        self.hand_over(i)

    def hand_over(self, i):
        @pl.when(self.end)
        def _():
            for k in (3, 2, 1):
                self.hand(i, k).start()

    def relay(self, i):
        @pl.when(self.middle)
        def _():
            for k in (2, 3):
                self.handed(i, k).wait_recv()
                self.add(i, k, self.landed.at[i, k])
                self.deliver(i, k).start()

    def pass_on(self, i):
        @pl.when(self.middle)
        def _():
            self.for_partner(i).wait_recv()
            self.add(i, 1, self.landed.at[i, 4])
            self.last(i).start()

    def finish(self, i, out):
        self.last(i).wait_recv()
        out[...] = self.theirs[i, 0].astype(F32) + self.landed[i, 0].astype(F32)
        if self.source is not None:
            for k in range(4):
                self.swap(i, k).wait_send()

        @pl.when(self.end)
        def _():
            for k in (3, 2, 1):
                self.hand(i, k).wait_send()

        @pl.when(self.middle)
        def _():
            self.handed(i, 1).wait_recv()
            out[...] += self.landed[i, 1].astype(F32)
            self.deliver(i, 2).wait_send()
            self.deliver(i, 3).wait_send()
            self.last(i).wait_send()


class LineSpread:
    def __init__(self, halves, place, scratch):
        self.halves, self.place = halves, place
        self.copied, self.send, self.recv = scratch
        self.d, self.e, self.z, self.core = here()
        self.other = (2 * self.z + 1 - self.core, self.e)
        self.to = [None] + [(2 * flipped(self.z, k) + self.core, self.e) for k in (1, 2, 3)]
        self.end = jnp.logical_or(self.z == 0, self.z == 3)
        self.middle = jnp.logical_not(self.end)

    @staticmethod
    def scratch(count):
        return [DMA((count,)), DMA((count, 9)), DMA((count, 8))]

    def from_chip(self, j, k, core=None):
        return self.place(j, 2 * flipped(self.z, k) + (self.core if core is None else core))

    def remote(self, j, src, dst, out, into, to):
        return pltpu.make_async_remote_copy(
            src_ref=src,
            dst_ref=dst,
            send_sem=self.send.at[j, out],
            recv_sem=self.recv.at[j, into],
            device_id=to,
            device_id_type=MESH,
        )

    def parts(self, j):
        piece, halves = self.place(j, self.d), self.halves(j)
        width = piece.shape[1] // len(halves)
        for i, half in enumerate(halves):
            yield half, piece.at[:, i * width : (i + 1) * width]

    def keep(self, j):
        piece = self.place(j, self.d)
        return pltpu.make_async_copy(piece, piece, self.copied.at[j])

    def first(self, j, way):
        piece = self.place(j, self.d)
        return self.remote(j, piece, piece, *self.way(way))

    def way(self, way):
        return min(way, 2), 4 if way == 0 else way, self.to[way] if way else self.other

    def send_own(self, j, way):
        for src, dst in self.parts(j):
            self.remote(j, src, dst, *self.way(way)).start()

    def share(self, j, k):
        piece = self.from_chip(j, k)
        return self.remote(j, piece, piece, 2 + k, 4 + k, self.other)

    def pass_on(self, j, k):
        piece = self.from_chip(j, k)
        return self.remote(j, piece, piece, 4 + k, 5 - k, self.to[1])

    def arrival(self, j, k):
        piece = self.from_chip(j, k)
        return self.remote(j, piece, piece, k, k, self.to[1])

    def shared(self, j, k):
        piece = self.from_chip(j, k, 1 - self.core)
        return self.remote(j, piece, piece, 4 + k if k else 0, 4 + k, self.other)

    def across(self, j):
        piece = self.from_chip(j, 1)
        return self.remote(j, piece, piece, 8, 2, self.to[3])

    def start(self, j):
        self.send_own(j, 1)

        @pl.when(self.middle)
        def _():
            self.send_own(j, 3)

        self.send_own(j, 0)
        for src, dst in self.parts(j):
            pltpu.make_async_copy(src, dst, self.copied.at[j]).start()

    def relay_near(self, j):
        self.arrival(j, 1).wait_recv()

        @pl.when(self.middle)
        def _():
            self.across(j).start()

        self.share(j, 1).start()

    def relay_far(self, j):
        for k in (3, 2):
            self.arrival(j, k).wait_recv()

            @pl.when(self.middle)
            def _():
                self.pass_on(j, k).start()

            self.share(j, k).start()

    def complete(self, j):
        self.keep(j).wait()
        for k in range(4):
            self.shared(j, k).wait_recv()

    def settle(self, j):
        self.first(j, 0).wait_send()
        self.first(j, 1).wait_send()

        @pl.when(self.middle)
        def _():
            self.first(j, 3).wait_send()
            self.across(j).wait_send()
            self.pass_on(j, 2).wait_send()
            self.pass_on(j, 3).wait_send()

        for k in (1, 2, 3):
            self.share(j, k).wait_send()


def pair_gates(logits, route_zero, route_one):
    experts = logits.shape[0]
    which = lax.broadcasted_iota(jnp.int32, logits.shape, 0)
    zero = jnp.sum(jnp.where(which == route_zero, logits, 0.0), axis=0, keepdims=True)
    one = jnp.sum(jnp.where(which == route_one, logits, 0.0), axis=0, keepdims=True)
    top = jnp.maximum(zero, one)
    zero, one = jnp.exp(zero - top), jnp.exp(one - top)
    total = zero + one
    return zero / total, one / total


class Dispatch:
    def __init__(self, expert, meta, rank, places):
        self.expert, self.meta, self.rank, self.places = expert, meta, rank, places
        self.blocks, _, self.slots = meta.shape

    def names(self, block):
        info = self.meta[block]
        valid = info[3:4, :] > 0
        zero = jnp.logical_and(valid, info[0:1, :] == self.expert)
        one = jnp.logical_and(valid, info[1:2, :] == self.expert)
        return info, zero, one

    def find_places(self):
        row_of = lax.broadcasted_iota(jnp.int32, (16, self.slots), 0)
        total_zero = jnp.zeros((1, 1), F32)
        for block in range(self.blocks):
            _, zero, _ = self.names(block)
            total_zero = total_zero + jnp.sum(zero.astype(F32), axis=1, keepdims=True)
            self.rank[block] = jnp.transpose(self.meta[block].astype(F32))

        def block_places(block, _):
            info, zero, one = self.names(block)
            mine = info[2:3, :].astype(F32)

            def earlier(other, counts):
                _, other_zero, other_one = self.names(other)
                marks = jnp.where(row_of == 0, other_zero.astype(F32), 0.0) + jnp.where(
                    row_of == 1, other_one.astype(F32), 0.0
                )
                before = (self.rank[other][:, 2:3] < mine).astype(F32).astype(BF16)
                return counts + dot(marks.astype(BF16), before)

            counts = lax.fori_loop(0, self.blocks, earlier, jnp.zeros((16, self.slots), F32))
            place = jnp.where(
                zero, counts[0:1, :], jnp.where(one, counts[1:2, :] + total_zero, -1.0)
            ).astype(jnp.int32)
            self.places[block] = jnp.broadcast_to(place, self.places.shape[1:])
            return 0

        lax.fori_loop(0, self.blocks, block_places, 0)

    def hot(self, block):
        return lax.broadcasted_iota(jnp.int32, (CAP, self.slots), 0) == self.places[block][0:1, :]

    def gates(self, block, rows, router_t):
        info, zero, one = self.names(block)
        gate_zero, gate_one = pair_gates(dot_nt(router_t, rows), info[0:1, :], info[1:2, :])
        gate = jnp.where(zero, gate_zero, jnp.where(one, gate_one, 0.0))
        return jnp.sum(jnp.where(self.hot(block), gate, 0.0), axis=1, keepdims=True)


def attend_forward(experts, tokens, weights, out_weight, heads, hot, length, out, between):
    qkv, attended, probs, resid, normed_two, small, normed, diagonals = out
    slots, width = tokens.shape
    small[...] = jnp.transpose(weights[:, 3 * width :].astype(F32))[: small.shape[0], :]
    x = tokens[...].astype(F32)
    inv_one = lax.rsqrt(jnp.mean(x * x, axis=1, keepdims=True) + epsilon)
    normed[...] = (x * inv_one * small[experts : experts + 1, :]).astype(BF16)
    spread_bias = heads[...].astype(F32) * small[experts + 2 : experts + 3, :]
    diagonals[...] = dot(spread_bias.astype(BF16), hot[...])

    @pl.loop(0, 3 * width // 512)
    def _(j):
        qkv[:, columns(j, 512)] = dot(normed[...], weights[:, columns(j, 512)]).astype(BF16)

    lane = lax.broadcasted_iota(jnp.int32, (slots, LANES), 1)
    first = lane < HD
    live = lax.broadcasted_iota(jnp.int32, (slots, slots), 1) < length[0, 0]

    def attend(pair):
        q = qkv[:, columns(pair, LANES)]
        k = qkv[:, columns(PAIRS + pair, LANES)]
        v = qkv[:, columns(2 * PAIRS + pair, LANES)]
        outs = []
        for half in range(2):
            head = 2 * pair + half
            own = first if half == 0 else jnp.logical_not(first)
            row = jnp.broadcast_to(diagonals[pl.ds(head, 1), :], (slots, 2 * slots))
            bias = pltpu.roll(row, 0, 1, stride=1, stride_axis=0)[:, :slots]
            scores = dot_nt(jnp.where(own, q, jnp.zeros_like(q)), k) * SCALE + bias
            scores = jnp.where(live, scores, masked_value)
            exponent = jnp.exp(scores - jnp.max(scores, axis=1, keepdims=True))
            low = (exponent / jnp.sum(exponent, axis=1, keepdims=True)).astype(BF16)
            probs[head] = low
            outs.append(dot(low, v))
        attended[:, columns(pair, LANES)] = jnp.where(first, outs[0], outs[1]).astype(BF16)

    for part in range(PARTS):
        pl.loop(part * PAIRS // PARTS, (part + 1) * PAIRS // PARTS)(attend)
        between(part)

    @pl.loop(0, width // 512)
    def _(j):
        resid[:, columns(j, 512)] = tokens[:, columns(j, 512)].astype(F32) + dot(
            attended[...], out_weight[:, columns(j, 512)]
        )

    r = resid[...]
    inv_two = lax.rsqrt(jnp.mean(r * r, axis=1, keepdims=True) + epsilon)
    normed_two[...] = (r * inv_two * small[experts + 1 : experts + 2, :]).astype(BF16)


def attention_forward_kernel(
    experts,
    tokens,
    weights,
    out_weight,
    heads,
    hot,
    length,
    qkv,
    attended,
    probs,
    resid,
    normed_two,
    small,
    *scratch,
):
    out = (qkv, attended, probs, resid, normed_two, small) + scratch
    attend_forward(
        experts, tokens, weights, out_weight, heads, hot, length, out, lambda part: None
    )


def attention_shapes(experts, tokens):
    slots, width = tokens.shape
    return (
        jax.ShapeDtypeStruct((slots, 3 * width), BF16),
        jax.ShapeDtypeStruct((slots, width), BF16),
        jax.ShapeDtypeStruct((HEADS, slots, slots), BF16),
        jax.ShapeDtypeStruct((slots, width), F32),
        jax.ShapeDtypeStruct((slots, width), BF16),
        jax.ShapeDtypeStruct((-(-(experts + 3) // 8) * 8, width), F32),
    )


def attention_forward(experts, tokens, weights, out_weight, heads, hot, length):
    slots, width = tokens.shape
    return call(
        functools.partial(attention_forward_kernel, experts),
        attention_shapes(experts, tokens),
        [pltpu.VMEM((slots, width), BF16), pltpu.VMEM((HEADS, 2 * slots), F32)],
        48 * MB,
        2 * slots * width * (4 * width + 2 * slots),
        tokens,
        weights,
        out_weight,
        heads,
        hot,
        length,
    )


def dispatch_kernel(
    rows, cots, meta, small, own, buffer, scaled, plain, select, gate_column, acc, acc_cot, rank, places
):
    work = Dispatch(own[0, 0], meta, rank, places)
    work.find_places()
    acc[...] = jnp.zeros_like(acc)
    acc_cot[...] = jnp.zeros_like(acc_cot)
    gate_column[...] = jnp.zeros_like(gate_column)
    router_t = small[...].astype(BF16)
    for block in range(work.blocks):
        picked = work.hot(block).astype(F32).astype(BF16)
        select[block] = picked
        gate_column[...] += work.gates(block, rows[block], router_t)
        acc[...] += dot(picked, rows[block])
        acc_cot[...] += dot(picked, cots[block])
    buffer[...] = acc[...].astype(BF16)
    plain[...] = acc_cot[...].astype(BF16)
    scaled[...] = (acc_cot[...] * gate_column[:, 0:1]).astype(BF16)


def dispatch_shapes(blocks, slots, width):
    return (
        jax.ShapeDtypeStruct((CAP, width), BF16),
        jax.ShapeDtypeStruct((CAP, width), BF16),
        jax.ShapeDtypeStruct((CAP, width), BF16),
        jax.ShapeDtypeStruct((blocks, CAP, slots), BF16),
        jax.ShapeDtypeStruct((CAP, 128), F32),
    )


def dispatch_scratch(blocks, slots, width):
    return [
        pltpu.VMEM((CAP, width), F32),
        pltpu.VMEM((CAP, width), F32),
        pltpu.VMEM((blocks, slots, 8), F32),
        pltpu.VMEM((blocks, 8, slots), jnp.int32),
    ]


def dispatch(rows, cots, meta, small, own):
    blocks, slots, width = rows.shape
    return call(
        dispatch_kernel,
        dispatch_shapes(blocks, slots, width),
        dispatch_scratch(blocks, slots, width),
        60 * MB,
        4 * CAP * blocks * slots * width,
        rows,
        cots,
        meta,
        small,
        own,
    )


def forward_kernel(
    experts,
    tokens,
    heads,
    hot,
    length,
    cotangent,
    routes,
    priority,
    router,
    first_gain,
    second_gain,
    bias,
    qkv_own,
    out_own,
    gate_own,
    up_own,
    down_own,
    qkv,
    attended,
    probs,
    resid,
    normed_two,
    small,
    buffer,
    scaled,
    plain,
    select,
    gate_column,
    meta,
    kept,
    early_kept,
    down_kept,
    early,
    down,
    acc,
    acc_cot,
    rank,
    places,
    weights,
    rows,
    cots,
    metas,
    normed,
    diagonals,
    local,
    send,
    recv,
    gather_send,
    gather_recv,
    piece_stored,
    own_small,
    *scratch,
):
    d, e, z, c = here()
    slots, width = tokens.shape
    share = qkv_own.shape[0]
    gather = DeviceGather(weights, share, gather_send, gather_recv)
    rows_spread = Spread(normed_two, rows, send.at[0], recv.at[0], d, e)
    cots_spread = Spread(cotangent, cots, send.at[1], recv.at[1], d, e)
    work = Dispatch(e, metas, rank, places)
    tile_share, down_share = gate_own.shape[0], down_own.shape[0]
    tile_spread = LineSpread(
        lambda j: [own.at[:, j * CHUNK : (j + 1) * CHUNK] for own in (gate_own, up_own)],
        lambda j, device: early.at[
            j, pl.ds(pl.multiple_of(device * tile_share, tile_share), tile_share)
        ],
        scratch[:3],
    )
    down_spread = LineSpread(
        lambda j: [down_own.at[:, j * CHUNK : (j + 1) * CHUNK]],
        lambda j, device: down.at[
            pl.ds(pl.multiple_of(device * down_share, down_share), down_share),
            j * CHUNK : (j + 1) * CHUNK,
        ],
        scratch[3:],
    )
    pieces = [(tile_spread, j) for j in range(early.shape[0])]
    pieces += [(down_spread, j) for j in range(width // CHUNK)]

    def near(i):
        if 0 <= i < len(pieces):
            pieces[i][0].relay_near(pieces[i][1])

    def far(i):
        if 0 <= i < len(pieces):
            pieces[i][0].relay_far(pieces[i][1])
        begin(i + AHEAD)

    def begin(i):
        if i < len(pieces):
            pieces[i][0].start(pieces[i][1])

    def store(i):
        spread, j = pieces[i]
        if spread is tile_spread:
            src, dst = early.at[j], early_kept.at[j]
        else:
            at = slice(j * CHUNK, (j + 1) * CHUNK)
            src, dst = down.at[:, at], down_kept.at[:, at]
        return pltpu.make_async_copy(src, dst, piece_stored.at[i])

    cut = weights.shape[1] - width
    mine = gather.item(0, 0)
    own_parts = [
        pltpu.make_async_copy(qkv_own, mine.at[:, : 3 * width], local.at[0]),
        pltpu.make_async_copy(out_own, mine.at[:, cut:], local.at[1]),
    ]
    own_cots = pltpu.make_async_copy(cotangent, cots.at[0], local.at[3])
    for copy in own_parts:
        copy.start()
    meta[0:2, :] = routes[...]
    meta[2:3, :] = priority[...]
    slot = lax.broadcasted_iota(jnp.int32, (1, slots), 1)
    meta[3:4, :] = (slot < length[0, 0]).astype(jnp.int32)
    meta[4:8, :] = jnp.zeros((4, slots), jnp.int32)
    own_small[...] = jnp.zeros_like(own_small)
    row = 0
    for part in (router, first_gain, second_gain, bias):
        own_small[row : row + part.shape[0], : part.shape[1]] = part[...].astype(F32)
        row += part.shape[0]
    mine[:, 3 * width : cut] = jnp.zeros((share, cut - 3 * width), BF16)
    mine[:, 3 * width : 3 * width + own_small.shape[0]] = jnp.transpose(own_small[...])[
        :share, :
    ].astype(BF16)
    meet(group(d, e)[1:] + [gather.other] + gather.to_z[1:])
    meta_copies = [
        push(meta, metas.at[q], send.at[2, q], recv.at[2, q], group(d, e)[q]) for q in (1, 2, 3)
    ]
    for copy in own_parts:
        copy.wait()
    gather.start()
    gather.spread_out(0)
    own_cots.start()
    metas[0] = meta[...]
    for copy in meta_copies:
        copy.wait_recv()
    work.find_places()
    gather.from_z(1)
    gather.from_neighbours(0)
    gather.from_z(3)
    gather.from_z(2)
    for i in range(AHEAD):
        begin(i)
    gather.from_neighbours(1)
    near(0)
    gather.from_neighbours(3)
    near(1)
    far(0)
    gather.from_neighbours(2)
    cots_spread.start()
    far(1)
    for k in (0, 1, 3, 2):
        gather.from_across(k)
    near(2)
    gather.complete()
    far(2)
    keep = pltpu.make_async_copy(weights, kept, local.at[4])
    keep.start()

    def between(part):
        if part == 0:
            near(3)
        elif part == 1:
            cots_spread.forward()
            far(3)
        elif part == 2:
            near(4)
        else:
            far(4)

    out = (qkv, attended, probs, resid, normed_two, small, normed, diagonals)
    projections, out_weight = weights.at[:, :cut], weights.at[:, cut:]
    attend_forward(experts, tokens, projections, out_weight, heads, hot, length, out, between)

    rows_spread.start()
    own_cots.wait()
    cots_spread.finish()
    router_t = small[...].astype(BF16)

    def take_cots(block):
        picked = work.hot(block).astype(F32).astype(BF16)
        select[block] = picked
        more = dot(picked, cots[block])
        if block:
            acc_cot[...] += more
        else:
            acc_cot[...] = more

    def take_rows(block, ref):
        gate = work.gates(block, ref[...], router_t)
        more = dot(select[block], ref[...])
        if block:
            gate_column[...] += gate
            acc[...] += more
        else:
            gate_column[...] = jnp.broadcast_to(gate, gate_column.shape)
            acc[...] = more

    take_cots(0)
    take_cots(1)
    rows_spread.forward()
    take_cots(2)
    near(5)
    take_cots(3)
    plain[...] = acc_cot[...].astype(BF16)
    take_rows(0, normed_two)
    far(5)
    near(6)
    rows_spread.arrived(1)
    take_rows(1, rows.at[1])
    rows_spread.arrived(2)
    take_rows(2, rows.at[2])
    rows_spread.arrived(3)
    take_rows(3, rows.at[3])
    buffer[...] = acc[...].astype(BF16)
    scaled[...] = (acc_cot[...] * gate_column[:, 0:1]).astype(BF16)
    far(6)
    for i, (spread, j) in enumerate(pieces):
        spread.complete(j)
        store(i).start()
    rows_spread.sent()
    gather.settle()
    for i, (spread, j) in enumerate(pieces):
        spread.settle(j)
        store(i).wait()
    for copy in meta_copies:
        copy.wait_send()
    keep.wait()


AHEAD = 3


def forward(ready, experts, *args):
    tokens, cotangent, qkv_own, gate_own, down_own = args[0], args[4], args[11], args[13], args[15]
    slots, width = tokens.shape
    full = (32 * qkv_own.shape[0], 4 * width + 128)
    meta = jax.ShapeDtypeStruct((8, slots), jnp.int32)
    block = (experts, slots, width)
    tiles, down_full = (ready, width, TILE), (8 * down_own.shape[0], width)
    pieces = ready + width // CHUNK
    scratch = [pltpu.VMEM(tiles, BF16), pltpu.VMEM(down_full, BF16)]
    scratch += dispatch_scratch(*block) + [
        pltpu.VMEM(full, BF16),
        pltpu.VMEM(block, BF16),
        pltpu.VMEM(block, BF16),
        pltpu.VMEM((experts,) + meta.shape, meta.dtype),
        pltpu.VMEM((slots, width), BF16),
        pltpu.VMEM((HEADS, 2 * slots), F32),
        DMA((5,)),
        DMA((3, 6)),
        DMA((3, 6)),
        DMA((5, 16)),
        DMA((5, 16)),
        DMA((pieces,)),
        pltpu.VMEM((8, 128), F32),
        *LineSpread.scratch(ready),
        *LineSpread.scratch(width // CHUNK),
    ]
    shapes = attention_shapes(experts, tokens) + dispatch_shapes(*block) + (meta,)
    return call(
        functools.partial(forward_kernel, experts),
        shapes
        + tuple(jax.ShapeDtypeStruct(shape, BF16) for shape in (full, tiles, down_full)),
        scratch,
        62 * MB,
        2 * slots * width * (4 * width + 2 * slots),
        *args,
        stay=(4, 11, 12, 13, 14, 15),
        land=tuple(len(shapes) + i for i in range(3)),
        link=0,
    )


GELU_A = math.sqrt(2.0 / math.pi)
GELU_B = 0.044715


def expert_chunk(buffer, scaled, gate, up, down):
    gate_in, up_in = dot(buffer, gate), dot(buffer, up)
    square = gate_in * gate_in
    wave = jnp.tanh(GELU_A * gate_in * (1.0 + GELU_B * square))
    half = 0.5 * (1.0 + wave)
    activated = gate_in * half
    slope = half + (0.5 * GELU_A) * gate_in * (1.0 - wave * wave) * (1.0 + 3.0 * GELU_B * square)
    hidden = (activated * up_in).astype(BF16)
    grad_hidden = dot_nt(scaled, down)
    grad_gate_in = (grad_hidden * up_in * slope).astype(BF16)
    grad_up_in = (grad_hidden * activated).astype(BF16)
    grad_buffer = dot_nt(grad_gate_in, gate) + dot_nt(grad_up_in, up)
    return (
        dot(hidden, down),
        grad_buffer,
        dot_tn(buffer, grad_gate_in),
        dot_tn(buffer, grad_up_in),
        dot_tn(hidden, scaled),
    )


def expert_kernel(
    buffer,
    scaled,
    plain,
    gate,
    up,
    down,
    out,
    grad_buffer,
    inner,
    grad_gate,
    grad_up,
    grad_down,
    acc_out,
    acc_grad,
):
    step = pl.program_id(0)

    @pl.when(step == 0)
    def _():
        acc_out[...] = jnp.zeros_like(acc_out)
        acc_grad[...] = jnp.zeros_like(acc_grad)

    more_out, more_grad, d_gate, d_up, d_down = expert_chunk(
        buffer[...], scaled[...], gate[...], up[...], down[...]
    )
    acc_out[...] += more_out
    acc_grad[...] += more_grad
    grad_gate[...] = d_gate.astype(BF16)
    grad_up[...] = d_up.astype(BF16)
    grad_down[...] = d_down.astype(BF16)

    @pl.when(step == pl.num_programs(0) - 1)
    def _():
        low = acc_out[...].astype(BF16)
        out[...] = low
        grad_buffer[...] = acc_grad[...].astype(BF16)
        inner[...] = jnp.broadcast_to(
            jnp.sum(low.astype(F32) * plain[...].astype(F32), axis=1, keepdims=True), inner.shape
        )


def experts(buffer, scaled, plain, gate, up, down):
    rows, width = buffer.shape
    hidden = gate.shape[1]
    whole = pl.BlockSpec((rows, width), lambda j: (0, 0))
    tall = pl.BlockSpec((width, CHUNK), lambda j: (0, j))
    wide = pl.BlockSpec((CHUNK, width), lambda j: (j, 0))
    shapes = (
        jax.ShapeDtypeStruct((rows, width), BF16),
        jax.ShapeDtypeStruct((rows, width), BF16),
        jax.ShapeDtypeStruct((rows, 128), F32),
        jax.ShapeDtypeStruct((width, hidden), BF16),
        jax.ShapeDtypeStruct((width, hidden), BF16),
        jax.ShapeDtypeStruct((hidden, width), BF16),
    )
    return pl.pallas_call(
        expert_kernel,
        out_shape=shapes,
        grid=(hidden // CHUNK,),
        in_specs=[whole, whole, whole, tall, tall, wide],
        out_specs=(whole, whole, pl.BlockSpec((rows, 128), lambda j: (0, 0)), tall, tall, wide),
        scratch_shapes=[pltpu.VMEM((rows, width), F32), pltpu.VMEM((rows, width), F32)],
        compiler_params=pltpu.CompilerParams(
            vmem_limit_bytes=48 * MB, dimension_semantics=("arbitrary",)
        ),
        cost_estimate=pl.CostEstimate(
            flops=18 * rows * width * hidden,
            bytes_accessed=12 * width * hidden,
            transcendentals=rows * hidden,
        ),
    )(buffer, scaled, plain, gate, up, down)


def give_back_kernel(select, out, grad_buffer, inner, gate_column, mixed, grads, inner_rows):
    weighted = (out[...].astype(F32) * gate_column[:, 0:1]).astype(BF16)
    for block in range(select.shape[0]):
        row = jnp.sum(select[block].astype(F32) * inner[:, 0:1], axis=0, keepdims=True)
        inner_rows[block] = jnp.broadcast_to(row, inner_rows.shape[1:])
        grads[block] = dot_tn(select[block], grad_buffer[...]).astype(BF16)
        mixed[block] = dot_tn(select[block], weighted).astype(BF16)


def give_back(select, out, grad_buffer, inner, gate_column):
    blocks, rows, slots = select.shape
    width = out.shape[1]
    wide = (blocks, slots, width)
    return call(
        give_back_kernel,
        (
            jax.ShapeDtypeStruct(wide, BF16),
            jax.ShapeDtypeStruct(wide, BF16),
            jax.ShapeDtypeStruct((blocks, 8, slots), F32),
        ),
        [],
        56 * MB,
        4 * rows * blocks * slots * width,
        select,
        out,
        grad_buffer,
        inner,
        gate_column,
    )


def sweep_kernel(
    ready,
    buffer,
    scaled,
    plain,
    gate_column,
    select,
    gate_own,
    up_own,
    early,
    down_full,
    gate_sum,
    up_sum,
    grad_down,
    mixed,
    returned,
    inner_full,
    sums,
    both,
    down,
    acc_out,
    acc_grad,
    down_stage,
    grads,
    inner_rows,
    loaded,
    stored,
    local,
    swap_send,
    swap_recv,
    *scratch,
):
    tiles, width = both.shape[0], both.shape[1]
    share = gate_own.shape[0]
    coming = tiles - ready
    d, e, z, c = here()

    def rows_of(device):
        return pl.ds(pl.multiple_of(device * share, share), share)

    spread = LineSpread(
        lambda j: [own.at[:, columns(ready + j, CHUNK)] for own in (gate_own, up_own)],
        lambda j, device: both.at[ready + j, rows_of(device)],
        scratch[:3],
    )
    line = LineSum(
        tiles,
        lambda i, k, core: both.at[i, rows_of(2 * flipped(z, k) + core)],
        scratch[3:],
        load=False,
    )
    swap = Swap(grads, returned, swap_send.at[0], swap_recv.at[0], d, e)
    inner_swap = Swap(inner_rows, inner_full, swap_send.at[1], swap_recv.at[1], d, e)
    meet(group(d, e)[1:] + [line.other] + line.to[1:])

    def early_load(t):
        return pltpu.make_async_copy(early.at[t], both.at[t], loaded.at[t])

    down_load = pltpu.make_async_copy(down_full, down, loaded.at[tiles])
    for t in range(ready):
        early_load(t).start()
        if t == 0:
            down_load.start()
    for j in range(min(DEPTH, coming)):
        spread.start(j)
    acc_out[...] = jnp.zeros_like(acc_out)
    acc_grad[...] = jnp.zeros_like(acc_grad)
    down_load.wait()

    def down_rows(t):
        return pl.ds(pl.multiple_of(t * CHUNK, CHUNK), CHUNK)

    def down_store(t, slot):
        return pltpu.make_async_copy(
            down_stage.at[slot], grad_down.at[down_rows(t)], stored.at[slot]
        )

    def between(low, value, high):
        return jnp.logical_and(value >= low, value < high)

    def tile_step(t, _):
        @pl.when(t < ready)
        def _():
            early_load(t).wait()

        near = t - ready + NEAR

        @pl.when(between(0, near, coming))
        def _():
            spread.relay_near(near)

        @pl.when(between(0, near - 1, coming))
        def _():
            spread.relay_far(near - 1)

        @pl.when(between(DEPTH, near - 1 + DEPTH, coming))
        def _():
            spread.start(near - 1 + DEPTH)

        @pl.when(t >= ready)
        def _():
            spread.complete(t - ready)

        @pl.when(t >= 1)
        def _():
            line.halve(t - 1)

        @pl.when(t >= LAG)
        def _():
            line.relay(t - LAG)

        @pl.when(t >= LAG + 1)
        def _():
            line.pass_on(t - LAG - 1)

        more_out, more_grad, d_gate, d_up, d_down = expert_chunk(
            buffer[...], scaled[...], both[t, :, :CHUNK], both[t, :, CHUNK:], down[down_rows(t)]
        )
        acc_out[...] += more_out
        acc_grad[...] += more_grad

        @pl.when(t >= ready)
        def _():
            spread.settle(t - ready)

        both[t, :, :CHUNK] = d_gate.astype(BF16)
        both[t, :, CHUNK:] = d_up.astype(BF16)
        slot = lax.rem(t, 2)

        @pl.when(t >= 2)
        def _():
            down_store(t - 2, slot).wait()

        down_stage[slot] = d_down.astype(BF16)
        down_store(t, slot).start()
        line.begin(t)
        return 0

    lax.fori_loop(0, tiles, tile_step, 0)

    low = acc_out[...].astype(BF16)
    inner = jnp.sum(low.astype(F32) * plain[...].astype(F32), axis=1, keepdims=True)
    grad_low = acc_grad[...].astype(BF16)
    order = (3, 1, 2, 0)
    for block in order:
        row = jnp.sum(select[block].astype(F32) * inner, axis=0, keepdims=True)
        inner_rows[block] = jnp.broadcast_to(row, inner_rows.shape[1:])
        grads[block] = dot_tn(select[block], grad_low).astype(BF16)
        if block:
            inner_swap.start(block)
            swap.start(block)
    own_copies = [
        pltpu.make_async_copy(grads.at[0], returned.at[0], local.at[0]),
        pltpu.make_async_copy(inner_rows.at[0], inner_full.at[0], local.at[1]),
    ]
    for copy in own_copies:
        copy.start()
    line.halve(tiles - 1)
    weighted = (low.astype(F32) * gate_column[:, 0:1]).astype(BF16)
    for block in order:
        mixed[block] = dot_tn(select[block], weighted).astype(BF16)

    @pl.loop(tiles - LAG, tiles + 1)
    def _(i):
        @pl.when(i < tiles)
        def _():
            line.relay(i)

        line.pass_on(i - 1)

    @pl.loop(0, tiles)
    def _(i):
        line.finish(i, sums.at[i])
        for copy in result_stores(sums.at[i], gate_sum, up_sum, i, local.at[2]):
            copy.start()

    @pl.loop(0, tiles)
    def _(i):
        for copy in result_stores(sums.at[i], gate_sum, up_sum, i, local.at[2]):
            copy.wait()

    for t in range(tiles - 2, tiles):
        down_store(t, t % 2).wait()
    for copy in own_copies:
        copy.wait()
    inner_swap.finish()
    swap.finish()


def result_stores(value, gate_sum, up_sum, tile, sem):
    return [
        pltpu.make_async_copy(
            value.at[:, i * CHUNK : (i + 1) * CHUNK], array.at[:, columns(tile, CHUNK)], sem
        )
        for i, array in enumerate((gate_sum, up_sum))
    ]


LAG = 5

DEPTH = 6
NEAR = 2


def sweep(ready, buffer, scaled, plain, gate_column, select, gate_own, up_own, early, down_full):
    rows, width = buffer.shape
    tiles = gate_own.shape[1] // CHUNK
    share = gate_own.shape[0]
    block = (select.shape[0], select.shape[2], width)
    thin = (select.shape[0], 8, select.shape[2])
    hidden = tiles * CHUNK
    shapes = (
        jax.ShapeDtypeStruct(gate_own.shape, F32),
        jax.ShapeDtypeStruct(gate_own.shape, F32),
        jax.ShapeDtypeStruct(down_full.shape, BF16),
        jax.ShapeDtypeStruct(block, BF16),
        jax.ShapeDtypeStruct(block, BF16),
        jax.ShapeDtypeStruct(thin, F32),
    )
    scratch = [
        pltpu.VMEM((tiles, share, TILE), F32),
        pltpu.VMEM((tiles, width, TILE), BF16),
        pltpu.VMEM(down_full.shape, BF16),
        pltpu.VMEM((rows, width), F32),
        pltpu.VMEM((rows, width), F32),
        pltpu.VMEM((2, CHUNK, width), BF16),
        pltpu.VMEM(block, BF16),
        pltpu.VMEM(thin, F32),
        DMA((tiles + 1,)),
        DMA((2,)),
        DMA((3,)),
        DMA((2, 4)),
        DMA((2, 4)),
    ]
    scratch += LineSpread.scratch(tiles - ready) + LineSum.scratch(tiles, share, TILE, False)
    return call(
        functools.partial(sweep_kernel, ready),
        shapes,
        scratch,
        62 * MB,
        18 * rows * width * hidden,
        buffer,
        scaled,
        plain,
        gate_column,
        select,
        gate_own,
        up_own,
        early,
        down_full,
        stay=(5, 6, 7, 8),
        land=(0, 1, 2, 4, 5),
        link=2,
    )


def backward_layer(experts, relative, ins, outs, work, reached):
    tokens, cotangent, weights, out_weight, small, heads, hot_back, length, meta, own = ins[:10]
    returned, inner_rows, qkv, attended, probs, resid, normed_two = ins[10:]
    grad_tokens, grad_small, grad_out, *grad_halves = outs
    grad_attended, grad_qkv, branch, normed, grad_resid, grad_diagonals = work
    slots, width = tokens.shape
    blocks = returned.shape[0]
    router_t = small[...].astype(BF16)
    keep_row = lax.broadcasted_iota(jnp.int32, (slots, 1), 0) < length[0, 0]
    logits = dot_nt(router_t, normed_two[...])
    zero_route, one_route = meta[0:1, :], meta[1:2, :]
    gate_zero, gate_one = pair_gates(logits, zero_route, one_route)
    which = lax.broadcasted_iota(jnp.int32, logits.shape, 0)
    grad_zero = jnp.zeros((1, slots), F32)
    grad_one = jnp.zeros((1, slots), F32)
    for block in range(blocks):
        row = inner_rows[block][0:1, :]
        expert = jnp.bitwise_xor(own[0, 0], block) if relative else block
        grad_zero = grad_zero + jnp.where(zero_route == expert, row, 0.0)
        grad_one = grad_one + jnp.where(one_route == expert, row, 0.0)
    shared = gate_zero * grad_zero + gate_one * grad_one
    grad_zero = gate_zero * (grad_zero - shared)
    grad_one = gate_one * (grad_one - shared)
    grad_logits = jnp.where(which == zero_route, grad_zero, 0.0) + jnp.where(
        which == one_route, grad_one, 0.0
    )
    high, low = two_halves(grad_logits)
    grad_small[...] = dot(high, normed_two[...]) + dot(low, normed_two[...])
    grad_normed_two = dot_tn(high, router_t) + dot_tn(low, router_t)
    for block in range(blocks):
        grad_normed_two = grad_normed_two + returned[block].astype(F32)
    r = resid[...]
    inv_two = lax.rsqrt(jnp.mean(r * r, axis=1, keepdims=True) + epsilon)
    unit_two = r * inv_two
    grad_small[experts + 1 : experts + 2, :] = jnp.sum(
        grad_normed_two * unit_two, axis=0, keepdims=True
    )
    scaled_two = small[experts + 1 : experts + 2, :] * grad_normed_two
    grad_resid[...] = jnp.where(keep_row, cotangent[...].astype(F32), 0.0) + inv_two * (
        scaled_two - unit_two * jnp.mean(scaled_two * unit_two, axis=1, keepdims=True)
    )
    branch[...] = grad_resid[...].astype(BF16)
    reached("branch")

    @pl.loop(0, width // 256)
    def _(j):
        grad_out[:, columns(j, 256)] = dot_tn(attended[...], branch[:, columns(j, 256)]).astype(
            BF16
        )

    reached("out")
    grad_attended[...] = dot_nt(branch[...], out_weight[...]).astype(BF16)
    x = tokens[...].astype(F32)
    inv_one = lax.rsqrt(jnp.mean(x * x, axis=1, keepdims=True) + epsilon)
    normed[...] = (x * inv_one * small[experts : experts + 1, :]).astype(BF16)
    reached("attended")

    lane = lax.broadcasted_iota(jnp.int32, (slots, LANES), 1)
    first = lane < HD
    square = (slots, slots)
    flip = (
        lax.broadcasted_iota(jnp.int32, square, 0) + lax.broadcasted_iota(jnp.int32, square, 1)
        == slots - 1
    )
    flip = flip.astype(F32).astype(BF16)

    def attend_back(pair):
        q = qkv[:, columns(pair, LANES)]
        k = qkv[:, columns(PAIRS + pair, LANES)]
        v = qkv[:, columns(2 * PAIRS + pair, LANES)]
        g = grad_attended[:, columns(pair, LANES)]
        dq, dk, dv = [], [], []
        for half in range(2):
            head = 2 * pair + half
            mine = first if half == 0 else jnp.logical_not(first)
            low = probs[head]
            p = low.astype(F32)
            grad_probs = dot_nt(jnp.where(mine, g, jnp.zeros_like(g)), v)
            ds = p * (grad_probs - jnp.sum(p * grad_probs, axis=1, keepdims=True))
            ds = ds.astype(BF16)
            wide = jnp.concatenate([dot(flip, ds), jnp.zeros((slots, slots), F32)], axis=1)
            skewed = pltpu.roll(wide, 0, 1, stride=1, stride_axis=0)
            grad_diagonals[pl.ds(head, 1), :] = jnp.sum(skewed, axis=0, keepdims=True)
            dq.append(dot(ds, k))
            dk.append(dot_tn(ds, q))
            dv.append(dot_tn(low, g))
        grad_qkv[:, columns(pair, LANES)] = (jnp.where(first, dq[0], dq[1]) * SCALE).astype(BF16)
        grad_qkv[:, columns(PAIRS + pair, LANES)] = (
            jnp.where(first, dk[0], dk[1]) * SCALE
        ).astype(BF16)
        grad_qkv[:, columns(2 * PAIRS + pair, LANES)] = jnp.where(first, dv[0], dv[1]).astype(BF16)

    for part in range(PARTS):
        pl.loop(part * PAIRS // PARTS, (part + 1) * PAIRS // PARTS)(attend_back)
        reached(f"part{part}")
        if part % 2 == 1:
            half, wide = part // 2, width // 2
            for i in range(3):
                for j in range(wide // 256):
                    source = i * width + half * wide + j * 256
                    at = i * wide + j * 256
                    grad_halves[half][:, at : at + 256] = dot_tn(
                        normed[...], grad_qkv[:, source : source + 256]
                    ).astype(BF16)
            reached(f"half{half}")

    high, low = two_halves(grad_diagonals[...])
    by_lane = dot_nt(high, hot_back[...]) + dot_nt(low, hot_back[...])
    grad_small[experts + 2 : experts + 3, :] = jnp.sum(
        by_lane * heads[...].astype(F32), axis=0, keepdims=True
    )
    grad_normed = dot_nt(grad_qkv[...], weights[:, : 3 * width])
    x = tokens[...].astype(F32)
    inv_one = lax.rsqrt(jnp.mean(x * x, axis=1, keepdims=True) + epsilon)
    unit_one = x * inv_one
    grad_small[experts : experts + 1, :] = jnp.sum(grad_normed * unit_one, axis=0, keepdims=True)
    scaled_one = small[experts : experts + 1, :] * grad_normed
    grad_tokens[...] = grad_resid[...] + inv_one * (
        scaled_one - unit_one * jnp.mean(scaled_one * unit_one, axis=1, keepdims=True)
    )
    reached("tokens")


def backward_scratch(slots, width):
    return [
        pltpu.VMEM((slots, width), BF16),
        pltpu.VMEM((slots, 3 * width), BF16),
        pltpu.VMEM((slots, width), BF16),
        pltpu.VMEM((slots, width), BF16),
        pltpu.VMEM((slots, width), F32),
        pltpu.VMEM((HEADS, 2 * slots), F32),
    ]


def add_mixed(output, resid, length, parts):
    keep_row = lax.broadcasted_iota(jnp.int32, (resid.shape[0], 1), 0) < length[0, 0]
    total = resid[...]
    for part in parts:
        total = total + part[...].astype(F32)
    output[...] = jnp.where(keep_row, total, 0.0).astype(BF16)


def local_backward_kernel(experts, *refs):
    ins, mixed, output, outs, work = refs[:17], refs[17], refs[18], refs[19:24], refs[24:]
    backward_layer(experts, False, ins, outs, work, lambda name: None)
    add_mixed(output, ins[15], ins[7], [mixed.at[block] for block in range(mixed.shape[0])])


def local_backward(experts, *args):
    tokens, small = args[0], args[4]
    slots, width = tokens.shape
    return call(
        functools.partial(local_backward_kernel, experts),
        (
            jax.ShapeDtypeStruct((slots, width), BF16),
            jax.ShapeDtypeStruct((slots, width), F32),
            jax.ShapeDtypeStruct(small.shape, F32),
            jax.ShapeDtypeStruct((width, width), BF16),
            jax.ShapeDtypeStruct((width, 3 * width // 2), BF16),
            jax.ShapeDtypeStruct((width, 3 * width // 2), BF16),
        ),
        backward_scratch(slots, width),
        62 * MB,
        4 * slots * width * (4 * width + 2 * slots),
        *args,
    )


class DeviceSum:
    @staticmethod
    def scratch(share, width):
        return [
            pltpu.VMEM((4, 4 * share, width), BF16),
            pltpu.VMEM((4, 2, share, width), BF16),
            pltpu.VMEM((4, share, width), BF16),
            DMA((4, 4)),
            DMA((4, 4)),
        ] + LineSum.scratch(1, share, width, False)

    def __init__(self, partial, scratch):
        self.partial = partial
        self.theirs, self.first_in, self.second_in, self.send, self.recv = scratch[:5]
        self.line = LineSum(1, None, scratch[5:], False)
        self.share = self.second_in.shape[1]
        self.d, self.e, self.z, self.core = here()
        self.other = (2 * self.z + 1 - self.core, self.e)
        self.to_x, self.to_y = (self.d, flipped(self.e, 1)), (self.d, flipped(self.e, 2))

    def rows(self, k, core, start, count):
        row = (2 * flipped(self.z, k) + core) * 4 * self.share + start
        return self.partial.at[pl.ds(pl.multiple_of(row, self.share), count)]

    def piece(self, k, q):
        return self.rows(k, self.core, flipped(self.e, q) * self.share, self.share)

    def remote(self, src, dst, stage, k, to):
        return pltpu.make_async_remote_copy(
            src_ref=src,
            dst_ref=dst,
            send_sem=self.send.at[stage, k],
            recv_sem=self.recv.at[stage, k],
            device_id=to,
            device_id_type=MESH,
        )

    def swap(self, k):
        src = self.rows(k, 1 - self.core, 0, 4 * self.share)
        return self.remote(src, self.theirs.at[k], 0, k, self.other)

    def first(self, k, slot):
        near, to = (1, self.to_x) if k % 2 == 0 else (2, self.to_y)
        return self.remote(
            self.piece(k, 3 if slot else near), self.first_in.at[k, slot], 1 + slot, k, to
        )

    def far(self, k):
        return 2 if k % 2 == 0 else 1

    def second(self, k):
        to = self.to_y if k % 2 == 0 else self.to_x
        return self.remote(self.piece(k, self.far(k)), self.second_in.at[k], 3, k, to)

    def begin(self):
        for k in (3, 2, 1, 0):
            self.swap(k).start()

    def stage_one(self):
        for k in (3, 2, 1, 0):
            self.swap(k).wait_recv()

            @pl.loop(0, 4)
            def _(j):
                start = pl.multiple_of(j * self.share, self.share)
                mine = self.rows(k, self.core, start, self.share)
                mine[...] = (
                    mine[...].astype(F32) + self.theirs[k, pl.ds(start, self.share)].astype(F32)
                ).astype(BF16)

            self.first(k, 1).start()
            self.first(k, 0).start()

    def stage_two(self):
        for k in (3, 2, 1, 0):
            self.first(k, 1).wait_recv()
            source = self.piece(k, self.far(k))
            source[...] = (source[...].astype(F32) + self.first_in[k, 1].astype(F32)).astype(BF16)
            self.second(k).start()

    def stage_three(self):
        for k in (3, 2, 1, 0):
            self.first(k, 0).wait_recv()
            self.second(k).wait_recv()
            total = self.piece(k, 0)[...].astype(F32) + self.first_in[k, 0].astype(F32)
            self.line.theirs[0, k] = (total + self.second_in[k].astype(F32)).astype(BF16)
        self.line.hand_over(0)

    def settle(self):
        for k in range(4):
            self.swap(k).wait_send()
            self.first(k, 0).wait_send()
            self.first(k, 1).wait_send()
            self.second(k).wait_send()


class EverySum:
    @staticmethod
    def scratch(shape):
        return [
            pltpu.VMEM((6,) + shape, F32),
            pltpu.VMEM((5,) + shape, F32),
            DMA((5,)),
            DMA((5,)),
        ]

    def __init__(self, scratch):
        self.sums, self.landed, self.send, self.recv = scratch
        d, e, z, c = here()
        near = [(2 * flipped(z, k) + c, e) for k in (1, 2)]
        self.to = [(2 * z + 1 - c, e), (d, flipped(e, 1)), (d, flipped(e, 2))] + near

    def copy(self, at):
        return pltpu.make_async_remote_copy(
            src_ref=self.sums.at[at],
            dst_ref=self.landed.at[at],
            send_sem=self.send.at[at],
            recv_sem=self.recv.at[at],
            device_id=self.to[at],
            device_id_type=MESH,
        )

    def start(self, value):
        self.sums[0] = value
        self.copy(0).start()

    def step(self, at):
        self.copy(at).wait_recv()
        self.sums[at + 1] = self.sums[at] + self.landed[at]
        if at + 1 < len(self.to):
            self.copy(at + 1).start()

    def settle(self):
        for at in range(len(self.to)):
            self.copy(at).wait_send()


def down_source(array, z, share):
    def source(i, k, core):
        row = pl.multiple_of((2 * flipped(z, k) + core) * share, share)
        return array.at[pl.ds(row, share), pl.ds(pl.multiple_of(i * CHUNK, CHUNK), CHUNK)]

    return source


def backward_kernel(experts, *refs):
    refs = list(refs)

    def take(count):
        taken, refs[:] = refs[:count], refs[count:]
        return taken

    ins = take(17)
    mixed, grad_down = take(2)
    output, grad_tokens, qkv_sum, out_sum, small_sum, down_sum = take(6)
    grad_small, grad_out, *grad_halves = take(4)
    work = take(6)
    half_sums, *brought, fetched = take(6)
    cut = brought[0].shape[1]
    ins[2], ins[3] = ins[2].at[:, :cut], ins[3].at[:, cut:]
    fetches = []
    for i, (at, ref) in enumerate(zip(FETCHED, brought)):
        fetches.append(pltpu.make_async_copy(ins[at], ref, fetched.at[i]))
        fetches[-1].start()
        ins[at] = ref
    mixed_full, mixed_send, mixed_recv = take(3)
    d, e, z, _ = here()
    width = out_sum.shape[1]
    down = LineSum(width // CHUNK, down_source(grad_down, z, down_sum.shape[0]), take(6), True)
    out = DeviceSum(grad_out, take(9))
    halves = [DeviceSum(grad_half, take(9)) for grad_half in grad_halves]
    every = EverySum(take(4))
    swap = Swap(mixed, mixed_full, mixed_send, mixed_recv, d, e)
    meet(group(d, e)[1:] + [down.other] + down.to[1:])
    for block in (3, 1, 2):
        swap.start(block)
    for i in range(down.count):
        down.begin(i)
    down.halve(0)

    def reached(name):
        if name == "branch":
            down.halve(1)
        elif name == "out":
            out.begin()
            for copy in fetches:
                copy.wait()
        elif name == "attended":
            down.halve(2)
        elif name == "part0":
            out.stage_one()
            down.relay(0)
        elif name == "part1":
            out.stage_two()
        elif name == "half0":
            halves[0].begin()
            down.pass_on(0)
            down.relay(1)
        elif name == "part2":
            halves[0].stage_one()
            out.stage_three()
            down.halve(3)
        elif name == "part3":
            halves[0].stage_two()
            down.pass_on(1)
        elif name == "half1":
            halves[1].begin()
            down.relay(2)
        elif name == "tokens":
            every.start(grad_small[...])
            halves[1].stage_one()

    outs = [grad_tokens, grad_small, grad_out] + grad_halves
    backward_layer(experts, True, ins, outs, work, reached)
    halves[0].stage_three()
    every.step(0)
    halves[1].stage_two()
    out.line.relay(0)
    every.step(1)
    down.pass_on(2)
    down.relay(3)
    out.line.pass_on(0)
    halves[1].stage_three()
    every.step(2)
    halves[0].line.relay(0)
    down.pass_on(3)
    every.step(3)
    halves[0].line.pass_on(0)
    halves[1].line.relay(0)
    every.step(4)
    small_sum[...] = every.sums[5]
    for i in range(down.count):
        down.finish(i, down_sum.at[:, i * CHUNK : (i + 1) * CHUNK])
    halves[1].line.pass_on(0)
    swap.finish()
    add_mixed(output, ins[15], ins[7], [mixed.at[0]] + [mixed_full.at[q] for q in (1, 2, 3)])
    out.line.finish(0, out_sum)
    wide = width // 2
    for half, sums in enumerate(halves):
        sums.line.finish(0, half_sums.at[half])
        for i in range(3):
            at = i * width + half * wide
            qkv_sum[:, at : at + wide] = half_sums[half, :, i * wide : (i + 1) * wide]
    for sums in [out] + halves:
        sums.settle()
    every.settle()


FETCHED = (2, 3, 12, 14)


def backward(experts, *args):
    tokens, small, mixed, grad_down = args[0], args[4], args[17], args[18]
    slots, width = tokens.shape
    share, down_share = width // 32, grad_down.shape[0] // 8
    half = 3 * width // 2
    scratch = [
        pltpu.VMEM(small.shape, F32),
        pltpu.VMEM((width, width), BF16),
        pltpu.VMEM((width, half), BF16),
        pltpu.VMEM((width, half), BF16),
        *backward_scratch(slots, width),
        pltpu.VMEM((2, share, half), F32),
        pltpu.VMEM((width, args[2].shape[1] - width), BF16),
        pltpu.VMEM((width, width), BF16),
        *[pltpu.VMEM(args[i].shape, BF16) for i in FETCHED[2:]],
        DMA((len(FETCHED),)),
        pltpu.VMEM(mixed.shape, BF16),
        DMA((4,)),
        DMA((4,)),
        *LineSum.scratch(width // CHUNK, down_share, CHUNK, True),
        *DeviceSum.scratch(share, width),
        *DeviceSum.scratch(share, half),
        *DeviceSum.scratch(share, half),
        *EverySum.scratch(small.shape),
    ]
    return call(
        functools.partial(backward_kernel, experts),
        (
            jax.ShapeDtypeStruct((slots, width), BF16),
            jax.ShapeDtypeStruct((slots, width), F32),
            jax.ShapeDtypeStruct((share, 3 * width), F32),
            jax.ShapeDtypeStruct((share, width), F32),
            jax.ShapeDtypeStruct(small.shape, F32),
            jax.ShapeDtypeStruct((down_share, width), F32),
        ),
        scratch,
        63 * MB,
        4 * slots * width * (4 * width + 2 * slots),
        *args,
        stay=(18,) + FETCHED,
        link=3,
    )


def publish_kernel(experts, small, *refs):
    count = (len(refs) - 6) // 3
    ins, refs = refs[:count], refs[count:]
    router, first, second, bias, *refs = refs
    outs, held = refs[:count], refs[count : 2 * count]
    loads = [pltpu.make_async_copy(ins[i], held[i], refs[-2].at[i]) for i in range(count)]
    stores = [pltpu.make_async_copy(held[i], outs[i], refs[-1].at[i]) for i in range(count)]
    for copy in loads:
        copy.start()
    width, share = small.shape[1], first.shape[1]
    device = lax.axis_index("dp") * experts + lax.axis_index("expert")
    turned = pltpu.roll(small[...], lax.rem(width - device * share, width), 1)
    router[...] = turned[:experts, :share]
    first[...] = turned[experts : experts + 1, :share]
    second[...] = turned[experts + 1 : experts + 2, :share]
    bias[...] = turned[experts + 2 : experts + 3, : bias.shape[1]]
    for load, store in zip(loads, stores):
        load.wait()
        store.start()
    for copy in stores:
        copy.wait()


def publish(experts, small, bias_share, *values):
    count = len(values)
    share = small.shape[1] // 32
    return call(
        functools.partial(publish_kernel, experts),
        tuple(
            jax.ShapeDtypeStruct(shape, F32)
            for shape in ((experts, share), (1, share), (1, share), (1, bias_share))
        )
        + tuple(jax.ShapeDtypeStruct(value.shape, value.dtype) for value in values),
        [pltpu.VMEM(value.shape, value.dtype) for value in values] + [DMA((count,)), DMA((count,))],
        60 * MB,
        0,
        small,
        *values,
        stay=tuple(range(1, count + 1)),
        land=tuple(range(4, count + 4)),
    )


READY = 2


def on_device(
    fast,
    tokens,
    cotangent,
    qkv_weight,
    out_weight,
    router_weight,
    first_gain,
    second_gain,
    bias_table,
    gate_weight,
    up_weight,
    down_weight,
    lengths,
    routes,
    priority,
):
    both = ("dp", "expert")
    slots, width = tokens.shape
    expert_count = lax.axis_size("expert")
    device_count = lax.axis_size("dp") * expert_count
    share, bias_share = first_gain.shape[0], bias_table.shape[0]
    device = lax.axis_index("dp") * expert_count + lax.axis_index("expert")
    own = lax.axis_index("expert").astype(jnp.int32).reshape(1, 1)
    small_rows = -(-(expert_count + 3) // 8) * 8

    def gathered(value, axes, axis=0, tiled=True):
        return lax.all_gather(value, axes, axis=axis, tiled=tiled)

    def scattered(value, axes):
        return lax.psum_scatter(value, axes, scatter_dimension=0, tiled=True).astype(F32)

    def exchanged(value):
        return lax.all_to_all(value, "expert", split_axis=0, concat_axis=0, tiled=True)

    rows_own, hidden = gate_weight.shape[1:]
    if not fast:
        gate_full, up_full, down_full = (
            gathered(value[0], "dp") for value in (gate_weight, up_weight, down_weight)
        )

    lane = np.arange(width)
    flat = lane // share * bias_share + lane % share
    in_table = lane % share < bias_share
    heads = np.arange(HEADS)[:, None] == np.where(in_table, flat // BUCKETS, -1)[None, :]
    heads = jnp.asarray(heads.astype(np.float32), BF16)
    ahead = np.arange(2 * slots)

    def hot(ahead):
        return jnp.asarray(
            np.where(in_table[:, None], diagonal_onehot(ahead)[flat % BUCKETS], 0.0), BF16
        )

    diagonals_hot = hot(np.where(ahead < slots, ahead, ahead - 2 * slots))
    if fast:
        *kept, buffer, scaled, plain, select, gate_column, meta_own, weights, early, down_full = forward(
            READY,
            expert_count,
            tokens,
            heads,
            diagonals_hot,
            lengths,
            cotangent,
            routes.T,
            priority,
            router_weight.T,
            first_gain[None],
            second_gain[None],
            bias_table[None],
            qkv_weight,
            out_weight,
            gate_weight[0],
            up_weight[0],
            down_weight[0],
        )
        out_full = weights
    else:
        beside = jnp.concatenate(
            [
                router_weight,
                first_gain[:, None],
                second_gain[:, None],
                jnp.pad(bias_table, (0, share - bias_share))[:, None],
                jnp.zeros((share, 128 - expert_count - 3), BF16),
            ],
            axis=1,
        )
        valid_rows = jnp.arange(slots, dtype=jnp.int32) < lengths[0, 0]
        meta_own = jnp.concatenate(
            [
                routes.T,
                priority,
                valid_rows.astype(jnp.int32)[None, :],
                jnp.zeros((4, slots), jnp.int32),
            ],
            axis=0,
        )
        weights = gathered(jnp.concatenate([qkv_weight, beside], axis=1), both)
        out_full = gathered(out_weight, both)
        kept = attention_forward(
            expert_count, tokens, weights, out_full, heads, diagonals_hot, lengths
        )
        rows, cots, meta = (
            gathered(value, "expert", tiled=False) for value in (kept[4], cotangent, meta_own)
        )
        buffer, scaled, plain, select, gate_column = dispatch(rows, cots, meta, kept[5], own)
    qkv, attended, probs, resid, normed_two, small = kept
    if fast:
        grad_gate, grad_up, grad_down, mixed, returned, inner_rows = sweep(
            READY,
            buffer,
            scaled,
            plain,
            gate_column,
            select,
            gate_weight[0],
            up_weight[0],
            early,
            down_full,
        )
    else:
        expert_out, grad_buffer, inner, *grad_experts = experts(
            buffer, scaled, plain, gate_full, up_full, down_full
        )
        mixed, returned, inner_rows = (
            exchanged(value)
            for value in give_back(select, expert_out, grad_buffer, inner, gate_column)
        )
        grad_gate, grad_up, grad_down = (scattered(value, "dp")[None] for value in grad_experts)
    layer = (
        tokens,
        cotangent,
        weights,
        out_full,
        small,
        heads,
        hot(ahead - (slots - 1)),
        lengths,
        meta_own,
        own,
        returned,
        inner_rows,
        qkv,
        attended,
        probs,
        resid,
        normed_two,
        mixed,
    )
    if fast:
        output, grad_tokens, grad_qkv, grad_out, grad_small, grad_down = backward(
            expert_count, *layer, grad_down
        )
        grad_router, grad_first, grad_second, grad_bias, *large = publish(
            expert_count,
            grad_small,
            bias_share,
            output,
            grad_tokens,
            grad_qkv,
            grad_out,
            grad_gate,
            grad_up,
            grad_down,
        )
        output, grad_tokens, grad_qkv, grad_out, grad_gate, grad_up, grad_down = large
        grad_gate, grad_up, grad_down = grad_gate[None], grad_up[None], grad_down[None]
    else:
        output, grad_tokens, grad_small, *grad_weights = local_backward(expert_count, *layer)
        grad_out, *halves = (scattered(value, both) for value in grad_weights)
        grad_qkv = jnp.stack([half.reshape(share, 3, width // 2) for half in halves], axis=2)
        grad_qkv = grad_qkv.reshape(share, 3 * width)
        grad_small = lax.psum(grad_small, both)
        grad_small = lax.dynamic_slice(grad_small, (0, device * share), (small_rows, share))
        grad_router, grad_first, grad_second, grad_bias = (
            grad_small[:expert_count],
            grad_small[expert_count : expert_count + 1],
            grad_small[expert_count + 1 : expert_count + 2],
            grad_small[expert_count + 2 : expert_count + 3, :bias_share],
        )
    return (
        output,
        grad_tokens,
        grad_qkv,
        grad_out,
        grad_router.T,
        grad_first[0],
        grad_second[0],
        grad_bias[0],
        grad_gate,
        grad_up,
        grad_down,
    )


def solution(mesh):
    fast = dict(mesh.shape) == {"dp": 8, "expert": 4}
    rows = P(("dp", "expert"), None)
    flat = P(("dp", "expert"))
    expert = P("expert", "dp", None)
    grid = P("dp", "expert")
    return jax.shard_map(
        functools.partial(on_device, fast),
        mesh=mesh,
        in_specs=(rows,) * 5 + (flat,) * 3 + (expert,) * 3 + (grid, rows, grid),
        out_specs=(rows,) * 5 + (flat,) * 3 + (expert,) * 3,
        check_vma=False,
    )
```

```python
import functools
import math

import jax
import jax.numpy as jnp
import numpy as np
from jax import lax
from jax.experimental import pallas as pl
from jax.experimental.pallas import tpu as pltpu
from jax.sharding import PartitionSpec as P

HEADS = 16
HD = 64
BUCKETS = 32
CAP = 480
PAIRS = HEADS // 2
LANES = 2 * HD
PARTS = 4
CHUNK = 256
TILE = 2 * CHUNK

epsilon = 1e-06
masked_value = -1e30
max_distance = 128.0
SCALE = 1.0 / math.sqrt(HD)
MB = 1 << 20
F32 = jnp.float32
BF16 = jnp.bfloat16


def bucket_of(offset, bucket_count):
    halfway = bucket_count // 2
    exact_span = bucket_count // 4
    distance = np.abs(offset)
    log_part = np.log(np.maximum(distance, 1) / float(exact_span)) / np.log(
        max_distance / exact_span
    )
    far_bucket = np.minimum(
        exact_span + np.floor(log_part * exact_span).astype(np.int64), halfway - 1
    )
    inside = np.where(distance < exact_span, distance, far_bucket)
    return np.where(offset < 0, halfway, 0) + inside


def diagonal_onehot(ahead):
    return (bucket_of(-ahead, BUCKETS)[None, :] == np.arange(BUCKETS)[:, None]).astype(np.float32)


def dot(a, b):
    return jnp.dot(a, b, preferred_element_type=F32)


def dot_nt(a, b):
    return lax.dot_general(a, b, (((1,), (1,)), ((), ())), preferred_element_type=F32)


def dot_tn(a, b):
    return lax.dot_general(a, b, (((0,), (0,)), ((), ())), preferred_element_type=F32)


def two_halves(value):
    high = value.astype(BF16)
    return high, (value - high.astype(F32)).astype(BF16)


def columns(index, width):
    return pl.ds(pl.multiple_of(index * width, width), width)


VMEM_SPEC = pl.BlockSpec(memory_space=pltpu.VMEM)


ANY_SPEC = pl.BlockSpec(memory_space=pl.ANY)
MESH = pl.DeviceIdType.MESH
DMA = pltpu.SemaphoreType.DMA


def call(kernel, out_shape, scratch, vmem, flops, *args, stay=(), land=(), link=None, aliases=None):
    nbytes = sum(a.size * a.dtype.itemsize for a in args)
    params = dict(vmem_limit_bytes=vmem)
    if link is not None:
        params.update(collective_id=link, has_side_effects=True)
    return pl.pallas_call(
        kernel,
        out_shape=out_shape,
        in_specs=[ANY_SPEC if i in stay else VMEM_SPEC for i in range(len(args))],
        out_specs=tuple(ANY_SPEC if i in land else VMEM_SPEC for i in range(len(out_shape))),
        scratch_shapes=scratch,
        input_output_aliases=aliases or {},
        compiler_params=pltpu.CompilerParams(**params),
        cost_estimate=pl.CostEstimate(flops=flops, bytes_accessed=nbytes, transcendentals=0),
    )(*args)


def here():
    d, e = lax.axis_index("dp"), lax.axis_index("expert")
    return d, e, d // 2, lax.rem(d, 2)


def flipped(value, bits):
    low, high = lax.rem(value, 2), value // 2
    low = 1 - low if bits & 1 else low
    high = 1 - high if bits & 2 else high
    return 2 * high + low


def meet(partners):
    barrier = pltpu.get_barrier_semaphore()
    for partner in partners:
        pl.semaphore_signal(barrier, inc=1, device_id=partner, device_id_type=MESH)
    pl.semaphore_wait(barrier, len(partners))


def push(src, dst, send, recv, to):
    copy = pltpu.make_async_remote_copy(
        src_ref=src, dst_ref=dst, send_sem=send, recv_sem=recv, device_id=to, device_id_type=MESH
    )
    copy.start()
    return copy


def group(d, e):
    return [None] + [(d, flipped(e, q)) for q in (1, 2, 3)]


class Spread:
    def __init__(self, src, dst, send, recv, d, e):
        self.src, self.dst, self.send, self.recv = src, dst, send, recv
        self.to = group(d, e)
        self.half = src.shape[0] // 2
        self.copies = {}

    def part(self, ref, half):
        return ref.at[pl.ds(half * self.half, self.half)]

    def start(self):
        for turn in range(2):
            for q in (1, 2):
                half = turn if q == 1 else 1 - turn
                at = 2 * (q - 1) + half
                self.copies[q, half] = push(
                    self.part(self.src, half),
                    self.part(self.dst.at[q], half),
                    self.send.at[at],
                    self.recv.at[at],
                    self.to[q],
                )

    def forward(self):
        for q, half, across, at in ((1, 0, 2, 4), (2, 1, 1, 5)):
            self.copies[q, half].wait_recv()
            self.copies[3, half] = push(
                self.part(self.dst.at[q], half),
                self.part(self.dst.at[3], half),
                self.send.at[at],
                self.recv.at[at],
                self.to[across],
            )

    def arrived(self, q):
        for half in {1: (1,), 2: (0,), 3: (0, 1)}[q]:
            self.copies[q, half].wait_recv()

    def sent(self):
        for copy in self.copies.values():
            copy.wait_send()

    def finish(self):
        for q in (1, 2, 3):
            self.arrived(q)
        self.sent()


class Swap:
    def __init__(self, src, dst, send, recv, d, e):
        self.src, self.dst, self.send, self.recv = src, dst, send, recv
        self.to = group(d, e)
        self.copies = {}

    def start(self, q):
        self.copies[q] = push(
            self.src.at[q], self.dst.at[q], self.send.at[q], self.recv.at[q], self.to[q]
        )

    def finish(self):
        for copy in self.copies.values():
            copy.wait_recv()
        for copy in self.copies.values():
            copy.wait_send()


class DeviceGather:
    WAYS = 5

    def __init__(self, full, share, send, recv):
        self.full, self.share, self.send, self.recv = full, share, send, recv
        self.d, self.e, self.z, self.core = d, e, z, c = here()
        self.to_x, self.to_y = (d, flipped(e, 1)), (d, flipped(e, 2))
        self.other = (2 * z + 1 - c, e)
        self.to_z = [None] + [(2 * flipped(z, k) + c, e) for k in (1, 2, 3)]
        self.end = jnp.logical_or(z == 0, z == 3)
        self.middle = jnp.logical_not(self.end)

    def item(self, k, q, core=None):
        device = 2 * flipped(self.z, k) + (self.core if core is None else core)
        row = (device * 4 + flipped(self.e, q)) * self.share
        return self.full.at[pl.ds(pl.multiple_of(row, self.share), self.share)]

    def pass_on(self, k, q, way, at, to, into=None):
        piece = self.item(k, q)
        return pltpu.make_async_remote_copy(
            src_ref=piece,
            dst_ref=piece,
            send_sem=self.send.at[way, at],
            recv_sem=self.recv.at[way, at if into is None else into],
            device_id=to,
            device_id_type=MESH,
        )

    def along_z(self, k):
        return self.pass_on(0, 0, 0, k, self.to_z[k])

    def relay_z(self, k):
        return self.pass_on(k, 0, 0, 2 + k, self.to_z[1], 5 - k)

    def along_x(self, k):
        return self.pass_on(k, 0, 1, k, self.to_x)

    def along_y(self, k):
        return self.pass_on(k, 0, 2, k, self.to_y)

    def across(self, k):
        return self.pass_on(k, 1, 3, k, self.to_y) if k % 2 == 0 else self.pass_on(k, 2, 3, k, self.to_x)

    def over(self, k, q):
        return self.pass_on(k, q, 4, 4 * q + k, self.other)

    def start(self):
        self.along_z(1).start()

        @pl.when(self.middle)
        def _():
            self.along_z(3).start()

        @pl.when(self.end)
        def _():
            self.along_z(2).start()

    def spread_out(self, k):
        self.along_x(k).start()
        self.along_y(k).start()
        self.over(k, 0).start()

    def from_z(self, k):
        self.along_z(k).wait_recv()
        if k > 1:

            @pl.when(self.middle)
            def _():
                self.relay_z(k).start()

        self.spread_out(k)

    def from_neighbours(self, k):
        self.along_x(k).wait_recv()
        if k % 2 == 0:
            self.across(k).start()
        self.over(k, 1).start()
        self.along_y(k).wait_recv()
        if k % 2 == 1:
            self.across(k).start()
        self.over(k, 2).start()

    def from_across(self, k):
        self.across(k).wait_recv()
        self.over(k, 3).start()

    def complete(self):
        for q in range(4):
            for k in range(4):
                self.over(k, q).wait_recv()

    def settle(self):
        self.along_z(1).wait_send()

        @pl.when(self.middle)
        def _():
            self.along_z(3).wait_send()
            self.relay_z(2).wait_send()
            self.relay_z(3).wait_send()

        @pl.when(self.end)
        def _():
            self.along_z(2).wait_send()

        for k in range(4):
            self.along_x(k).wait_send()
            self.along_y(k).wait_send()
            self.across(k).wait_send()
            for q in range(4):
                self.over(k, q).wait_send()


class LineSum:
    def __init__(self, count, source, scratch, load):
        self.count, self.source, self.load_first = count, source, load
        scratch = list(scratch)
        self.theirs, self.landed, self.send, self.recv = scratch[:4]
        if load:
            self.loads, self.loaded = scratch[4:]
        self.d, self.e, self.z, self.core = here()
        self.other = (2 * self.z + 1 - self.core, self.e)
        self.to = [None] + [(2 * flipped(self.z, k) + self.core, self.e) for k in (1, 2, 3)]
        self.end = jnp.logical_or(self.z == 0, self.z == 3)
        self.middle = jnp.logical_not(self.end)

    @staticmethod
    def scratch(count, rows, width, load):
        part = (rows, width)
        parts = [
            pltpu.VMEM((count, 4) + part, BF16),
            pltpu.VMEM((count, 5) + part, BF16),
            DMA((count, 3, 5)),
            DMA((count, 3, 5)),
        ]
        return parts + ([pltpu.VMEM((count, 4) + part, BF16), DMA((count, 4))] if load else [])

    def remote(self, i, src, dst, stage, out, into, to):
        return pltpu.make_async_remote_copy(
            src_ref=src,
            dst_ref=dst,
            send_sem=self.send.at[i, stage, out],
            recv_sem=self.recv.at[i, stage, into],
            device_id=to,
            device_id_type=MESH,
        )

    def load(self, i, k):
        return pltpu.make_async_copy(
            self.source(i, k, self.core), self.loads.at[i, k], self.loaded.at[i, k]
        )

    def swap(self, i, k):
        src = self.source(i, k, 1 - self.core)
        return self.remote(i, src, self.theirs.at[i, k], 0, k, k, self.other)

    def hand(self, i, k):
        at = 1 if k == 1 else 5 - k
        return self.remote(i, self.theirs.at[i, k], self.landed.at[i, at], 1, k, at, self.to[1])

    def handed(self, i, at):
        return self.remote(i, self.theirs.at[i, at], self.landed.at[i, at], 1, at, at, self.to[1])

    def deliver(self, i, k):
        at = 0 if k == 3 else 4
        return self.remote(i, self.theirs.at[i, k], self.landed.at[i, at], 2, k, at, self.to[3])

    def for_partner(self, i):
        return self.remote(i, self.theirs.at[i, 0], self.landed.at[i, 4], 2, 4, 4, self.to[3])

    def last(self, i):
        return self.remote(i, self.theirs.at[i, 1], self.landed.at[i, 0], 2, 0, 0, self.to[1])

    def add(self, i, k, more):
        self.theirs[i, k] = (self.theirs[i, k].astype(F32) + more[...].astype(F32)).astype(BF16)

    def begin(self, i):
        for k in (3, 2, 1, 0):
            self.swap(i, k).start()
            if self.load_first:
                self.load(i, k).start()

    def halve(self, i):
        for k in (3, 2, 1, 0):
            if self.load_first:
                self.load(i, k).wait()
            self.swap(i, k).wait_recv()
            self.add(i, k, self.loads.at[i, k] if self.load_first else self.source(i, k, self.core))
        self.hand_over(i)

    def hand_over(self, i):
        @pl.when(self.end)
        def _():
            for k in (3, 2, 1):
                self.hand(i, k).start()

    def relay(self, i):
        @pl.when(self.middle)
        def _():
            for k in (2, 3):
                self.handed(i, k).wait_recv()
                self.add(i, k, self.landed.at[i, k])
                self.deliver(i, k).start()

    def pass_on(self, i):
        @pl.when(self.middle)
        def _():
            self.for_partner(i).wait_recv()
            self.add(i, 1, self.landed.at[i, 4])
            self.last(i).start()

    def finish(self, i, out):
        self.last(i).wait_recv()
        out[...] = self.theirs[i, 0].astype(F32) + self.landed[i, 0].astype(F32)
        if self.source is not None:
            for k in range(4):
                self.swap(i, k).wait_send()

        @pl.when(self.end)
        def _():
            for k in (3, 2, 1):
                self.hand(i, k).wait_send()

        @pl.when(self.middle)
        def _():
            self.handed(i, 1).wait_recv()
            out[...] += self.landed[i, 1].astype(F32)
            self.deliver(i, 2).wait_send()
            self.deliver(i, 3).wait_send()
            self.last(i).wait_send()


class LineSpread:
    def __init__(self, halves, place, scratch):
        self.halves, self.place = halves, place
        self.copied, self.send, self.recv = scratch
        self.d, self.e, self.z, self.core = here()
        self.other = (2 * self.z + 1 - self.core, self.e)
        self.to = [None] + [(2 * flipped(self.z, k) + self.core, self.e) for k in (1, 2, 3)]
        self.end = jnp.logical_or(self.z == 0, self.z == 3)
        self.middle = jnp.logical_not(self.end)

    @staticmethod
    def scratch(count):
        return [DMA((count,)), DMA((count, 9)), DMA((count, 8))]

    def from_chip(self, j, k, core=None):
        return self.place(j, 2 * flipped(self.z, k) + (self.core if core is None else core))

    def remote(self, j, src, dst, out, into, to):
        return pltpu.make_async_remote_copy(
            src_ref=src,
            dst_ref=dst,
            send_sem=self.send.at[j, out],
            recv_sem=self.recv.at[j, into],
            device_id=to,
            device_id_type=MESH,
        )

    def parts(self, j):
        piece, halves = self.place(j, self.d), self.halves(j)
        width = piece.shape[1] // len(halves)
        for i, half in enumerate(halves):
            yield half, piece.at[:, i * width : (i + 1) * width]

    def keep(self, j):
        piece = self.place(j, self.d)
        return pltpu.make_async_copy(piece, piece, self.copied.at[j])

    def first(self, j, way):
        piece = self.place(j, self.d)
        return self.remote(j, piece, piece, *self.way(way))

    def way(self, way):
        return min(way, 2), 4 if way == 0 else way, self.to[way] if way else self.other

    def send_own(self, j, way):
        for src, dst in self.parts(j):
            self.remote(j, src, dst, *self.way(way)).start()

    def share(self, j, k):
        piece = self.from_chip(j, k)
        return self.remote(j, piece, piece, 2 + k, 4 + k, self.other)

    def pass_on(self, j, k):
        piece = self.from_chip(j, k)
        return self.remote(j, piece, piece, 4 + k, 5 - k, self.to[1])

    def arrival(self, j, k):
        piece = self.from_chip(j, k)
        return self.remote(j, piece, piece, k, k, self.to[1])

    def shared(self, j, k):
        piece = self.from_chip(j, k, 1 - self.core)
        return self.remote(j, piece, piece, 4 + k if k else 0, 4 + k, self.other)

    def across(self, j):
        piece = self.from_chip(j, 1)
        return self.remote(j, piece, piece, 8, 2, self.to[3])

    def start(self, j):
        self.send_own(j, 1)

        @pl.when(self.middle)
        def _():
            self.send_own(j, 3)

        self.send_own(j, 0)
        for src, dst in self.parts(j):
            pltpu.make_async_copy(src, dst, self.copied.at[j]).start()

    def relay_near(self, j):
        self.arrival(j, 1).wait_recv()

        @pl.when(self.middle)
        def _():
            self.across(j).start()

        self.share(j, 1).start()

    def relay_far(self, j):
        for k in (3, 2):
            self.arrival(j, k).wait_recv()

            @pl.when(self.middle)
            def _():
                self.pass_on(j, k).start()

            self.share(j, k).start()

    def complete(self, j):
        self.keep(j).wait()
        for k in range(4):
            self.shared(j, k).wait_recv()

    def settle(self, j):
        self.first(j, 0).wait_send()
        self.first(j, 1).wait_send()

        @pl.when(self.middle)
        def _():
            self.first(j, 3).wait_send()
            self.across(j).wait_send()
            self.pass_on(j, 2).wait_send()
            self.pass_on(j, 3).wait_send()

        for k in (1, 2, 3):
            self.share(j, k).wait_send()


def pair_gates(logits, route_zero, route_one):
    experts = logits.shape[0]
    which = lax.broadcasted_iota(jnp.int32, logits.shape, 0)
    zero = jnp.sum(jnp.where(which == route_zero, logits, 0.0), axis=0, keepdims=True)
    one = jnp.sum(jnp.where(which == route_one, logits, 0.0), axis=0, keepdims=True)
    top = jnp.maximum(zero, one)
    zero, one = jnp.exp(zero - top), jnp.exp(one - top)
    total = zero + one
    return zero / total, one / total


class Dispatch:
    def __init__(self, expert, meta, rank, places):
        self.expert, self.meta, self.rank, self.places = expert, meta, rank, places
        self.blocks, _, self.slots = meta.shape

    def names(self, block):
        info = self.meta[block]
        valid = info[3:4, :] > 0
        zero = jnp.logical_and(valid, info[0:1, :] == self.expert)
        one = jnp.logical_and(valid, info[1:2, :] == self.expert)
        return info, zero, one

    def find_places(self):
        row_of = lax.broadcasted_iota(jnp.int32, (16, self.slots), 0)
        total_zero = jnp.zeros((1, 1), F32)
        for block in range(self.blocks):
            _, zero, _ = self.names(block)
            total_zero = total_zero + jnp.sum(zero.astype(F32), axis=1, keepdims=True)
            self.rank[block] = jnp.transpose(self.meta[block].astype(F32))

        def block_places(block, _):
            info, zero, one = self.names(block)
            mine = info[2:3, :].astype(F32)

            def earlier(other, counts):
                _, other_zero, other_one = self.names(other)
                marks = jnp.where(row_of == 0, other_zero.astype(F32), 0.0) + jnp.where(
                    row_of == 1, other_one.astype(F32), 0.0
                )
                before = (self.rank[other][:, 2:3] < mine).astype(F32).astype(BF16)
                return counts + dot(marks.astype(BF16), before)

            counts = lax.fori_loop(0, self.blocks, earlier, jnp.zeros((16, self.slots), F32))
            place = jnp.where(
                zero, counts[0:1, :], jnp.where(one, counts[1:2, :] + total_zero, -1.0)
            ).astype(jnp.int32)
            self.places[block] = jnp.broadcast_to(place, self.places.shape[1:])
            return 0

        lax.fori_loop(0, self.blocks, block_places, 0)

    def hot(self, block):
        return lax.broadcasted_iota(jnp.int32, (CAP, self.slots), 0) == self.places[block][0:1, :]

    def gates(self, block, rows, router_t):
        info, zero, one = self.names(block)
        gate_zero, gate_one = pair_gates(dot_nt(router_t, rows), info[0:1, :], info[1:2, :])
        gate = jnp.where(zero, gate_zero, jnp.where(one, gate_one, 0.0))
        return jnp.sum(jnp.where(self.hot(block), gate, 0.0), axis=1, keepdims=True)


def attend_forward(experts, tokens, weights, out_weight, heads, hot, length, out, between):
    qkv, attended, probs, resid, normed_two, small, normed, diagonals = out
    slots, width = tokens.shape
    small[...] = jnp.transpose(weights[:, 3 * width :].astype(F32))[: small.shape[0], :]
    x = tokens[...].astype(F32)
    inv_one = lax.rsqrt(jnp.mean(x * x, axis=1, keepdims=True) + epsilon)
    normed[...] = (x * inv_one * small[experts : experts + 1, :]).astype(BF16)
    spread_bias = heads[...].astype(F32) * small[experts + 2 : experts + 3, :]
    diagonals[...] = dot(spread_bias.astype(BF16), hot[...])

    @pl.loop(0, 3 * width // 512)
    def _(j):
        qkv[:, columns(j, 512)] = dot(normed[...], weights[:, columns(j, 512)]).astype(BF16)

    lane = lax.broadcasted_iota(jnp.int32, (slots, LANES), 1)
    first = lane < HD
    live = lax.broadcasted_iota(jnp.int32, (slots, slots), 1) < length[0, 0]

    def attend(pair):
        q = qkv[:, columns(pair, LANES)]
        k = qkv[:, columns(PAIRS + pair, LANES)]
        v = qkv[:, columns(2 * PAIRS + pair, LANES)]
        outs = []
        for half in range(2):
            head = 2 * pair + half
            own = first if half == 0 else jnp.logical_not(first)
            row = jnp.broadcast_to(diagonals[pl.ds(head, 1), :], (slots, 2 * slots))
            bias = pltpu.roll(row, 0, 1, stride=1, stride_axis=0)[:, :slots]
            scores = dot_nt(jnp.where(own, q, jnp.zeros_like(q)), k) * SCALE + bias
            scores = jnp.where(live, scores, masked_value)
            exponent = jnp.exp(scores - jnp.max(scores, axis=1, keepdims=True))
            low = (exponent / jnp.sum(exponent, axis=1, keepdims=True)).astype(BF16)
            probs[head] = low
            outs.append(dot(low, v))
        attended[:, columns(pair, LANES)] = jnp.where(first, outs[0], outs[1]).astype(BF16)

    for part in range(PARTS):
        pl.loop(part * PAIRS // PARTS, (part + 1) * PAIRS // PARTS)(attend)
        between(part)

    @pl.loop(0, width // 512)
    def _(j):
        resid[:, columns(j, 512)] = tokens[:, columns(j, 512)].astype(F32) + dot(
            attended[...], out_weight[:, columns(j, 512)]
        )

    r = resid[...]
    inv_two = lax.rsqrt(jnp.mean(r * r, axis=1, keepdims=True) + epsilon)
    normed_two[...] = (r * inv_two * small[experts + 1 : experts + 2, :]).astype(BF16)


def attention_forward_kernel(
    experts,
    tokens,
    weights,
    out_weight,
    heads,
    hot,
    length,
    qkv,
    attended,
    probs,
    resid,
    normed_two,
    small,
    *scratch,
):
    out = (qkv, attended, probs, resid, normed_two, small) + scratch
    attend_forward(
        experts, tokens, weights, out_weight, heads, hot, length, out, lambda part: None
    )


def attention_shapes(experts, tokens):
    slots, width = tokens.shape
    return (
        jax.ShapeDtypeStruct((slots, 3 * width), BF16),
        jax.ShapeDtypeStruct((slots, width), BF16),
        jax.ShapeDtypeStruct((HEADS, slots, slots), BF16),
        jax.ShapeDtypeStruct((slots, width), F32),
        jax.ShapeDtypeStruct((slots, width), BF16),
        jax.ShapeDtypeStruct((-(-(experts + 3) // 8) * 8, width), F32),
    )


def attention_forward(experts, tokens, weights, out_weight, heads, hot, length):
    slots, width = tokens.shape
    return call(
        functools.partial(attention_forward_kernel, experts),
        attention_shapes(experts, tokens),
        [pltpu.VMEM((slots, width), BF16), pltpu.VMEM((HEADS, 2 * slots), F32)],
        48 * MB,
        2 * slots * width * (4 * width + 2 * slots),
        tokens,
        weights,
        out_weight,
        heads,
        hot,
        length,
    )


def dispatch_kernel(
    rows, cots, meta, small, own, buffer, scaled, plain, select, gate_column, acc, acc_cot, rank, places
):
    work = Dispatch(own[0, 0], meta, rank, places)
    work.find_places()
    acc[...] = jnp.zeros_like(acc)
    acc_cot[...] = jnp.zeros_like(acc_cot)
    gate_column[...] = jnp.zeros_like(gate_column)
    router_t = small[...].astype(BF16)
    for block in range(work.blocks):
        picked = work.hot(block).astype(F32).astype(BF16)
        select[block] = picked
        gate_column[...] += work.gates(block, rows[block], router_t)
        acc[...] += dot(picked, rows[block])
        acc_cot[...] += dot(picked, cots[block])
    buffer[...] = acc[...].astype(BF16)
    plain[...] = acc_cot[...].astype(BF16)
    scaled[...] = (acc_cot[...] * gate_column[:, 0:1]).astype(BF16)


def dispatch_shapes(blocks, slots, width):
    return (
        jax.ShapeDtypeStruct((CAP, width), BF16),
        jax.ShapeDtypeStruct((CAP, width), BF16),
        jax.ShapeDtypeStruct((CAP, width), BF16),
        jax.ShapeDtypeStruct((blocks, CAP, slots), BF16),
        jax.ShapeDtypeStruct((CAP, 128), F32),
    )


def dispatch_scratch(blocks, slots, width):
    return [
        pltpu.VMEM((CAP, width), F32),
        pltpu.VMEM((CAP, width), F32),
        pltpu.VMEM((blocks, slots, 8), F32),
        pltpu.VMEM((blocks, 8, slots), jnp.int32),
    ]


def dispatch(rows, cots, meta, small, own):
    blocks, slots, width = rows.shape
    return call(
        dispatch_kernel,
        dispatch_shapes(blocks, slots, width),
        dispatch_scratch(blocks, slots, width),
        60 * MB,
        4 * CAP * blocks * slots * width,
        rows,
        cots,
        meta,
        small,
        own,
    )


def forward_kernel(
    experts,
    tokens,
    heads,
    hot,
    length,
    cotangent,
    routes,
    priority,
    router,
    first_gain,
    second_gain,
    bias,
    qkv_own,
    out_own,
    gate_own,
    up_own,
    down_own,
    qkv_kept,
    attended_kept,
    probs_kept,
    resid_kept,
    normed_kept,
    small,
    buffer,
    scaled,
    plain,
    select,
    gate_column,
    meta,
    kept,
    early_kept,
    down_kept,
    early,
    down,
    acc,
    acc_cot,
    rank,
    places,
    weights,
    rows,
    cots,
    metas,
    normed,
    diagonals,
    local,
    send,
    recv,
    gather_send,
    gather_recv,
    piece_stored,
    own_small,
    qkv,
    attended,
    probs,
    resid,
    normed_two,
    result_stored,
    *scratch,
):
    d, e, z, c = here()
    slots, width = tokens.shape
    share = qkv_own.shape[0]
    gather = DeviceGather(weights, share, gather_send, gather_recv)
    rows_spread = Spread(normed_two, rows, send.at[0], recv.at[0], d, e)
    cots_spread = Spread(cotangent, cots, send.at[1], recv.at[1], d, e)
    work = Dispatch(e, metas, rank, places)
    tile_share, down_share = gate_own.shape[0], down_own.shape[0]
    tile_spread = LineSpread(
        lambda j: [own.at[:, j * CHUNK : (j + 1) * CHUNK] for own in (gate_own, up_own)],
        lambda j, device: early.at[
            j, pl.ds(pl.multiple_of(device * tile_share, tile_share), tile_share)
        ],
        scratch[:3],
    )
    down_spread = LineSpread(
        lambda j: [down_own.at[:, j * CHUNK : (j + 1) * CHUNK]],
        lambda j, device: down.at[
            pl.ds(pl.multiple_of(device * down_share, down_share), down_share),
            j * CHUNK : (j + 1) * CHUNK,
        ],
        scratch[3:],
    )
    pieces = [(tile_spread, j) for j in range(early.shape[0])]
    pieces += [(down_spread, j) for j in range(width // CHUNK)]

    def near(i):
        if 0 <= i < len(pieces):
            pieces[i][0].relay_near(pieces[i][1])

    def far(i):
        if 0 <= i < len(pieces):
            pieces[i][0].relay_far(pieces[i][1])
        begin(i + AHEAD)

    def begin(i):
        if i < len(pieces):
            pieces[i][0].start(pieces[i][1])

    def store(i):
        spread, j = pieces[i]
        if spread is tile_spread:
            src, dst = early.at[j], early_kept.at[j]
        else:
            at = slice(j * CHUNK, (j + 1) * CHUNK)
            src, dst = down.at[:, at], down_kept.at[:, at]
        return pltpu.make_async_copy(src, dst, piece_stored.at[i])

    cut = weights.shape[1] - width
    mine = gather.item(0, 0)
    own_parts = [
        pltpu.make_async_copy(qkv_own, mine.at[:, : 3 * width], local.at[0]),
        pltpu.make_async_copy(out_own, mine.at[:, cut:], local.at[1]),
    ]
    own_cots = pltpu.make_async_copy(cotangent, cots.at[0], local.at[3])
    for copy in own_parts:
        copy.start()
    meta[0:2, :] = routes[...]
    meta[2:3, :] = priority[...]
    slot = lax.broadcasted_iota(jnp.int32, (1, slots), 1)
    meta[3:4, :] = (slot < length[0, 0]).astype(jnp.int32)
    meta[4:8, :] = jnp.zeros((4, slots), jnp.int32)
    own_small[...] = jnp.zeros_like(own_small)
    row = 0
    for part in (router, first_gain, second_gain, bias):
        own_small[row : row + part.shape[0], : part.shape[1]] = part[...].astype(F32)
        row += part.shape[0]
    mine[:, 3 * width : cut] = jnp.zeros((share, cut - 3 * width), BF16)
    mine[:, 3 * width : 3 * width + own_small.shape[0]] = jnp.transpose(own_small[...])[
        :share, :
    ].astype(BF16)
    meet(group(d, e)[1:] + [gather.other] + gather.to_z[1:])
    meta_copies = [
        push(meta, metas.at[q], send.at[2, q], recv.at[2, q], group(d, e)[q]) for q in (1, 2, 3)
    ]
    for copy in own_parts:
        copy.wait()
    gather.start()
    gather.spread_out(0)
    own_cots.start()
    metas[0] = meta[...]
    for copy in meta_copies:
        copy.wait_recv()
    work.find_places()
    gather.from_z(1)
    gather.from_neighbours(0)
    gather.from_z(3)
    gather.from_z(2)
    for i in range(AHEAD):
        begin(i)
    gather.from_neighbours(1)
    near(0)
    gather.from_neighbours(3)
    near(1)
    far(0)
    gather.from_neighbours(2)
    cots_spread.start()
    far(1)
    for k in (0, 1, 3, 2):
        gather.from_across(k)
    near(2)
    gather.complete()
    far(2)
    keep = pltpu.make_async_copy(weights, kept, local.at[4])
    keep.start()

    def between(part):
        if part == 0:
            near(3)
        elif part == 1:
            cots_spread.forward()
            far(3)
        elif part == 2:
            near(4)
        else:
            far(4)

    out = (qkv, attended, probs, resid, normed_two, small, normed, diagonals)
    projections, out_weight = weights.at[:, :cut], weights.at[:, cut:]
    attend_forward(experts, tokens, projections, out_weight, heads, hot, length, out, between)

    rows_spread.start()
    results = [
        pltpu.make_async_copy(src, dst, result_stored.at[i])
        for i, (src, dst) in enumerate(
            (
                (qkv, qkv_kept),
                (attended, attended_kept),
                (probs, probs_kept),
                (resid, resid_kept),
                (normed_two, normed_kept),
            )
        )
    ]
    for copy in results:
        copy.start()
    own_cots.wait()
    cots_spread.finish()
    router_t = small[...].astype(BF16)

    def take_cots(block):
        picked = work.hot(block).astype(F32).astype(BF16)
        select[block] = picked
        more = dot(picked, cots[block])
        if block:
            acc_cot[...] += more
        else:
            acc_cot[...] = more

    def take_rows(block, ref):
        gate = work.gates(block, ref[...], router_t)
        more = dot(select[block], ref[...])
        if block:
            gate_column[...] += gate
            acc[...] += more
        else:
            gate_column[...] = jnp.broadcast_to(gate, gate_column.shape)
            acc[...] = more

    take_cots(0)
    take_cots(1)
    rows_spread.forward()
    take_cots(2)
    near(5)
    take_cots(3)
    plain[...] = acc_cot[...].astype(BF16)
    take_rows(0, normed_two)
    far(5)
    near(6)
    rows_spread.arrived(1)
    take_rows(1, rows.at[1])
    rows_spread.arrived(2)
    take_rows(2, rows.at[2])
    rows_spread.arrived(3)
    take_rows(3, rows.at[3])
    buffer[...] = acc[...].astype(BF16)
    scaled[...] = (acc_cot[...] * gate_column[:, 0:1]).astype(BF16)
    far(6)
    for i, (spread, j) in enumerate(pieces):
        spread.complete(j)
        store(i).start()
    rows_spread.sent()
    for copy in results:
        copy.wait()
    gather.settle()
    for i, (spread, j) in enumerate(pieces):
        spread.settle(j)
        store(i).wait()
    for copy in meta_copies:
        copy.wait_send()
    keep.wait()


AHEAD = 3


def forward(ready, experts, *args):
    tokens, cotangent, qkv_own, gate_own, down_own = args[0], args[4], args[11], args[13], args[15]
    slots, width = tokens.shape
    full = (32 * qkv_own.shape[0], 4 * width + 128)
    meta = jax.ShapeDtypeStruct((8, slots), jnp.int32)
    block = (experts, slots, width)
    tiles, down_full = (ready, width, TILE), (8 * down_own.shape[0], width)
    pieces = ready + width // CHUNK
    scratch = [pltpu.VMEM(tiles, BF16), pltpu.VMEM(down_full, BF16)]
    scratch += dispatch_scratch(*block) + [
        pltpu.VMEM(full, BF16),
        pltpu.VMEM(block, BF16),
        pltpu.VMEM(block, BF16),
        pltpu.VMEM((experts,) + meta.shape, meta.dtype),
        pltpu.VMEM((slots, width), BF16),
        pltpu.VMEM((HEADS, 2 * slots), F32),
        DMA((5,)),
        DMA((3, 6)),
        DMA((3, 6)),
        DMA((5, 16)),
        DMA((5, 16)),
        DMA((pieces,)),
        pltpu.VMEM((8, 128), F32),
        *[pltpu.VMEM(value.shape, value.dtype) for value in attention_shapes(experts, tokens)[:5]],
        DMA((5,)),
        *LineSpread.scratch(ready),
        *LineSpread.scratch(width // CHUNK),
    ]
    shapes = attention_shapes(experts, tokens) + dispatch_shapes(*block) + (meta,)
    return call(
        functools.partial(forward_kernel, experts),
        shapes
        + tuple(jax.ShapeDtypeStruct(shape, BF16) for shape in (full, tiles, down_full)),
        scratch,
        62 * MB,
        2 * slots * width * (4 * width + 2 * slots),
        *args,
        stay=(4, 11, 12, 13, 14, 15),
        land=tuple(range(5)) + tuple(len(shapes) + i for i in range(3)),
        link=0,
    )


GELU_A = math.sqrt(2.0 / math.pi)
GELU_B = 0.044715


def expert_chunk(buffer, scaled, gate, up, down):
    gate_in, up_in = dot(buffer, gate), dot(buffer, up)
    square = gate_in * gate_in
    wave = jnp.tanh(GELU_A * gate_in * (1.0 + GELU_B * square))
    half = 0.5 * (1.0 + wave)
    activated = gate_in * half
    slope = half + (0.5 * GELU_A) * gate_in * (1.0 - wave * wave) * (1.0 + 3.0 * GELU_B * square)
    hidden = (activated * up_in).astype(BF16)
    grad_hidden = dot_nt(scaled, down)
    grad_gate_in = (grad_hidden * up_in * slope).astype(BF16)
    grad_up_in = (grad_hidden * activated).astype(BF16)
    grad_buffer = dot_nt(grad_gate_in, gate) + dot_nt(grad_up_in, up)
    return (
        dot(hidden, down),
        grad_buffer,
        dot_tn(buffer, grad_gate_in),
        dot_tn(buffer, grad_up_in),
        dot_tn(hidden, scaled),
    )


def expert_kernel(
    buffer,
    scaled,
    plain,
    gate,
    up,
    down,
    out,
    grad_buffer,
    inner,
    grad_gate,
    grad_up,
    grad_down,
    acc_out,
    acc_grad,
):
    step = pl.program_id(0)

    @pl.when(step == 0)
    def _():
        acc_out[...] = jnp.zeros_like(acc_out)
        acc_grad[...] = jnp.zeros_like(acc_grad)

    more_out, more_grad, d_gate, d_up, d_down = expert_chunk(
        buffer[...], scaled[...], gate[...], up[...], down[...]
    )
    acc_out[...] += more_out
    acc_grad[...] += more_grad
    grad_gate[...] = d_gate.astype(BF16)
    grad_up[...] = d_up.astype(BF16)
    grad_down[...] = d_down.astype(BF16)

    @pl.when(step == pl.num_programs(0) - 1)
    def _():
        low = acc_out[...].astype(BF16)
        out[...] = low
        grad_buffer[...] = acc_grad[...].astype(BF16)
        inner[...] = jnp.broadcast_to(
            jnp.sum(low.astype(F32) * plain[...].astype(F32), axis=1, keepdims=True), inner.shape
        )


def experts(buffer, scaled, plain, gate, up, down):
    rows, width = buffer.shape
    hidden = gate.shape[1]
    whole = pl.BlockSpec((rows, width), lambda j: (0, 0))
    tall = pl.BlockSpec((width, CHUNK), lambda j: (0, j))
    wide = pl.BlockSpec((CHUNK, width), lambda j: (j, 0))
    shapes = (
        jax.ShapeDtypeStruct((rows, width), BF16),
        jax.ShapeDtypeStruct((rows, width), BF16),
        jax.ShapeDtypeStruct((rows, 128), F32),
        jax.ShapeDtypeStruct((width, hidden), BF16),
        jax.ShapeDtypeStruct((width, hidden), BF16),
        jax.ShapeDtypeStruct((hidden, width), BF16),
    )
    return pl.pallas_call(
        expert_kernel,
        out_shape=shapes,
        grid=(hidden // CHUNK,),
        in_specs=[whole, whole, whole, tall, tall, wide],
        out_specs=(whole, whole, pl.BlockSpec((rows, 128), lambda j: (0, 0)), tall, tall, wide),
        scratch_shapes=[pltpu.VMEM((rows, width), F32), pltpu.VMEM((rows, width), F32)],
        compiler_params=pltpu.CompilerParams(
            vmem_limit_bytes=48 * MB, dimension_semantics=("arbitrary",)
        ),
        cost_estimate=pl.CostEstimate(
            flops=18 * rows * width * hidden,
            bytes_accessed=12 * width * hidden,
            transcendentals=rows * hidden,
        ),
    )(buffer, scaled, plain, gate, up, down)


def give_back_kernel(select, out, grad_buffer, inner, gate_column, mixed, grads, inner_rows):
    weighted = (out[...].astype(F32) * gate_column[:, 0:1]).astype(BF16)
    for block in range(select.shape[0]):
        row = jnp.sum(select[block].astype(F32) * inner[:, 0:1], axis=0, keepdims=True)
        inner_rows[block] = jnp.broadcast_to(row, inner_rows.shape[1:])
        grads[block] = dot_tn(select[block], grad_buffer[...]).astype(BF16)
        mixed[block] = dot_tn(select[block], weighted).astype(BF16)


def give_back(select, out, grad_buffer, inner, gate_column):
    blocks, rows, slots = select.shape
    width = out.shape[1]
    wide = (blocks, slots, width)
    return call(
        give_back_kernel,
        (
            jax.ShapeDtypeStruct(wide, BF16),
            jax.ShapeDtypeStruct(wide, BF16),
            jax.ShapeDtypeStruct((blocks, 8, slots), F32),
        ),
        [],
        56 * MB,
        4 * rows * blocks * slots * width,
        select,
        out,
        grad_buffer,
        inner,
        gate_column,
    )


def sweep_kernel(
    ready,
    buffer,
    scaled,
    plain,
    gate_column,
    select,
    gate_own,
    up_own,
    early,
    down_full,
    gate_sum,
    up_sum,
    grad_down,
    mixed,
    returned,
    inner_full,
    sums,
    both,
    down,
    acc_out,
    acc_grad,
    down_stage,
    grads,
    inner_rows,
    buffer_in,
    scaled_in,
    plain_in,
    column_in,
    select_in,
    fetched,
    loaded,
    stored,
    local,
    swap_send,
    swap_recv,
    *scratch,
):
    tiles, width = both.shape[0], both.shape[1]
    share = gate_own.shape[0]
    coming = tiles - ready
    d, e, z, c = here()

    def rows_of(device):
        return pl.ds(pl.multiple_of(device * share, share), share)

    spread = LineSpread(
        lambda j: [own.at[:, columns(ready + j, CHUNK)] for own in (gate_own, up_own)],
        lambda j, device: both.at[ready + j, rows_of(device)],
        scratch[:3],
    )
    line = LineSum(
        tiles,
        lambda i, k, core: both.at[i, rows_of(2 * flipped(z, k) + core)],
        scratch[3:],
        load=False,
    )
    swap = Swap(grads, returned, swap_send.at[0], swap_recv.at[0], d, e)
    inner_swap = Swap(inner_rows, inner_full, swap_send.at[1], swap_recv.at[1], d, e)
    meet(group(d, e)[1:] + [line.other] + line.to[1:])

    def early_load(t):
        return pltpu.make_async_copy(early.at[t], both.at[t], loaded.at[t])

    for j in range(min(DEPTH, coming)):
        spread.start(j)
    fetches = []
    for i, (src, dst) in enumerate(
        (
            (buffer, buffer_in),
            (scaled, scaled_in),
            (plain, plain_in),
            (gate_column, column_in),
            (select, select_in),
        )
    ):
        fetches.append(pltpu.make_async_copy(src, dst, fetched.at[i]))
        fetches[-1].start()
    buffer, scaled, plain, gate_column, select = buffer_in, scaled_in, plain_in, column_in, select_in
    down_load = pltpu.make_async_copy(down_full, down, loaded.at[tiles])
    for t in range(ready):
        early_load(t).start()
        if t == 0:
            down_load.start()
    acc_out[...] = jnp.zeros_like(acc_out)
    acc_grad[...] = jnp.zeros_like(acc_grad)
    for copy in fetches:
        copy.wait()
    down_load.wait()

    def down_rows(t):
        return pl.ds(pl.multiple_of(t * CHUNK, CHUNK), CHUNK)

    def down_store(t, slot):
        return pltpu.make_async_copy(
            down_stage.at[slot], grad_down.at[down_rows(t)], stored.at[slot]
        )

    def between(low, value, high):
        return jnp.logical_and(value >= low, value < high)

    def tile_step(t, _):
        @pl.when(t < ready)
        def _():
            early_load(t).wait()

        near = t - ready + NEAR

        @pl.when(between(0, near, coming))
        def _():
            spread.relay_near(near)

        @pl.when(between(0, near - 1, coming))
        def _():
            spread.relay_far(near - 1)

        @pl.when(between(DEPTH, near - 1 + DEPTH, coming))
        def _():
            spread.start(near - 1 + DEPTH)

        @pl.when(t >= ready)
        def _():
            spread.complete(t - ready)

        @pl.when(t >= 1)
        def _():
            line.halve(t - 1)

        @pl.when(t >= LAG)
        def _():
            line.relay(t - LAG)

        @pl.when(t >= LAG + 1)
        def _():
            line.pass_on(t - LAG - 1)

        more_out, more_grad, d_gate, d_up, d_down = expert_chunk(
            buffer[...], scaled[...], both[t, :, :CHUNK], both[t, :, CHUNK:], down[down_rows(t)]
        )
        acc_out[...] += more_out
        acc_grad[...] += more_grad

        @pl.when(t >= ready)
        def _():
            spread.settle(t - ready)

        both[t, :, :CHUNK] = d_gate.astype(BF16)
        both[t, :, CHUNK:] = d_up.astype(BF16)
        slot = lax.rem(t, 2)

        @pl.when(t >= 2)
        def _():
            down_store(t - 2, slot).wait()

        down_stage[slot] = d_down.astype(BF16)
        down_store(t, slot).start()
        line.begin(t)
        return 0

    lax.fori_loop(0, tiles, tile_step, 0)

    low = acc_out[...].astype(BF16)
    inner = jnp.sum(low.astype(F32) * plain[...].astype(F32), axis=1, keepdims=True)
    grad_low = acc_grad[...].astype(BF16)
    order = (3, 1, 2, 0)
    for block in order:
        row = jnp.sum(select[block].astype(F32) * inner, axis=0, keepdims=True)
        inner_rows[block] = jnp.broadcast_to(row, inner_rows.shape[1:])
        grads[block] = dot_tn(select[block], grad_low).astype(BF16)
        if block:
            inner_swap.start(block)
            swap.start(block)
    own_copies = [
        pltpu.make_async_copy(grads.at[0], returned.at[0], local.at[0]),
        pltpu.make_async_copy(inner_rows.at[0], inner_full.at[0], local.at[1]),
    ]
    for copy in own_copies:
        copy.start()
    line.halve(tiles - 1)
    weighted = (low.astype(F32) * gate_column[:, 0:1]).astype(BF16)
    for block in order:
        mixed[block] = dot_tn(select[block], weighted).astype(BF16)

    @pl.loop(tiles - LAG, tiles + 1)
    def _(i):
        @pl.when(i < tiles)
        def _():
            line.relay(i)

        line.pass_on(i - 1)

    @pl.loop(0, tiles)
    def _(i):
        line.finish(i, sums.at[i])
        for copy in result_stores(sums.at[i], gate_sum, up_sum, i, local.at[2]):
            copy.start()

    @pl.loop(0, tiles)
    def _(i):
        for copy in result_stores(sums.at[i], gate_sum, up_sum, i, local.at[2]):
            copy.wait()

    for t in range(tiles - 2, tiles):
        down_store(t, t % 2).wait()
    for copy in own_copies:
        copy.wait()
    inner_swap.finish()
    swap.finish()


def result_stores(value, gate_sum, up_sum, tile, sem):
    return [
        pltpu.make_async_copy(
            value.at[:, i * CHUNK : (i + 1) * CHUNK], array.at[:, columns(tile, CHUNK)], sem
        )
        for i, array in enumerate((gate_sum, up_sum))
    ]


LAG = 5

DEPTH = 6
NEAR = 2


def sweep(ready, buffer, scaled, plain, gate_column, select, gate_own, up_own, early, down_full):
    rows, width = buffer.shape
    tiles = gate_own.shape[1] // CHUNK
    share = gate_own.shape[0]
    block = (select.shape[0], select.shape[2], width)
    thin = (select.shape[0], 8, select.shape[2])
    hidden = tiles * CHUNK
    shapes = (
        jax.ShapeDtypeStruct(gate_own.shape, F32),
        jax.ShapeDtypeStruct(gate_own.shape, F32),
        jax.ShapeDtypeStruct(down_full.shape, BF16),
        jax.ShapeDtypeStruct(block, BF16),
        jax.ShapeDtypeStruct(block, BF16),
        jax.ShapeDtypeStruct(thin, F32),
    )
    scratch = [
        pltpu.VMEM((tiles, share, TILE), F32),
        pltpu.VMEM((tiles, width, TILE), BF16),
        pltpu.VMEM(down_full.shape, BF16),
        pltpu.VMEM((rows, width), F32),
        pltpu.VMEM((rows, width), F32),
        pltpu.VMEM((2, CHUNK, width), BF16),
        pltpu.VMEM(block, BF16),
        pltpu.VMEM(thin, F32),
        *[
            pltpu.VMEM(value.shape, value.dtype)
            for value in (buffer, scaled, plain, gate_column, select)
        ],
        DMA((5,)),
        DMA((tiles + 1,)),
        DMA((2,)),
        DMA((3,)),
        DMA((2, 4)),
        DMA((2, 4)),
    ]
    scratch += LineSpread.scratch(tiles - ready) + LineSum.scratch(tiles, share, TILE, False)
    return call(
        functools.partial(sweep_kernel, ready),
        shapes,
        scratch,
        62 * MB,
        18 * rows * width * hidden,
        buffer,
        scaled,
        plain,
        gate_column,
        select,
        gate_own,
        up_own,
        early,
        down_full,
        stay=tuple(range(9)),
        land=(0, 1, 2, 4, 5),
        link=2,
    )


def backward_layer(experts, relative, ins, outs, work, reached):
    tokens, cotangent, weights, out_weight, small, heads, hot_back, length, meta, own = ins[:10]
    returned, inner_rows, qkv, attended, probs, resid, normed_two = ins[10:]
    grad_tokens, grad_small, grad_out, *grad_halves = outs
    grad_attended, grad_qkv, branch, normed, grad_resid, grad_diagonals = work
    slots, width = tokens.shape
    blocks = returned.shape[0]
    router_t = small[...].astype(BF16)
    keep_row = lax.broadcasted_iota(jnp.int32, (slots, 1), 0) < length[0, 0]
    logits = dot_nt(router_t, normed_two[...])
    zero_route, one_route = meta[0:1, :], meta[1:2, :]
    gate_zero, gate_one = pair_gates(logits, zero_route, one_route)
    which = lax.broadcasted_iota(jnp.int32, logits.shape, 0)
    grad_zero = jnp.zeros((1, slots), F32)
    grad_one = jnp.zeros((1, slots), F32)
    for block in range(blocks):
        row = inner_rows[block][0:1, :]
        expert = jnp.bitwise_xor(own[0, 0], block) if relative else block
        grad_zero = grad_zero + jnp.where(zero_route == expert, row, 0.0)
        grad_one = grad_one + jnp.where(one_route == expert, row, 0.0)
    shared = gate_zero * grad_zero + gate_one * grad_one
    grad_zero = gate_zero * (grad_zero - shared)
    grad_one = gate_one * (grad_one - shared)
    grad_logits = jnp.where(which == zero_route, grad_zero, 0.0) + jnp.where(
        which == one_route, grad_one, 0.0
    )
    high, low = two_halves(grad_logits)
    grad_small[...] = dot(high, normed_two[...]) + dot(low, normed_two[...])
    grad_normed_two = dot_tn(high, router_t) + dot_tn(low, router_t)
    for block in range(blocks):
        grad_normed_two = grad_normed_two + returned[block].astype(F32)
    r = resid[...]
    inv_two = lax.rsqrt(jnp.mean(r * r, axis=1, keepdims=True) + epsilon)
    unit_two = r * inv_two
    grad_small[experts + 1 : experts + 2, :] = jnp.sum(
        grad_normed_two * unit_two, axis=0, keepdims=True
    )
    scaled_two = small[experts + 1 : experts + 2, :] * grad_normed_two
    grad_resid[...] = jnp.where(keep_row, cotangent[...].astype(F32), 0.0) + inv_two * (
        scaled_two - unit_two * jnp.mean(scaled_two * unit_two, axis=1, keepdims=True)
    )
    branch[...] = grad_resid[...].astype(BF16)
    reached("branch")

    @pl.loop(0, width // 256)
    def _(j):
        grad_out[:, columns(j, 256)] = dot_tn(attended[...], branch[:, columns(j, 256)]).astype(
            BF16
        )

    reached("out")
    grad_attended[...] = dot_nt(branch[...], out_weight[...]).astype(BF16)
    x = tokens[...].astype(F32)
    inv_one = lax.rsqrt(jnp.mean(x * x, axis=1, keepdims=True) + epsilon)
    normed[...] = (x * inv_one * small[experts : experts + 1, :]).astype(BF16)
    reached("attended")

    lane = lax.broadcasted_iota(jnp.int32, (slots, LANES), 1)
    first = lane < HD
    square = (slots, slots)
    flip = (
        lax.broadcasted_iota(jnp.int32, square, 0) + lax.broadcasted_iota(jnp.int32, square, 1)
        == slots - 1
    )
    flip = flip.astype(F32).astype(BF16)

    def attend_back(pair):
        q = qkv[:, columns(pair, LANES)]
        k = qkv[:, columns(PAIRS + pair, LANES)]
        v = qkv[:, columns(2 * PAIRS + pair, LANES)]
        g = grad_attended[:, columns(pair, LANES)]
        dq, dk, dv = [], [], []
        for half in range(2):
            head = 2 * pair + half
            mine = first if half == 0 else jnp.logical_not(first)
            low = probs[head]
            p = low.astype(F32)
            grad_probs = dot_nt(jnp.where(mine, g, jnp.zeros_like(g)), v)
            ds = p * (grad_probs - jnp.sum(p * grad_probs, axis=1, keepdims=True))
            ds = ds.astype(BF16)
            wide = jnp.concatenate([dot(flip, ds), jnp.zeros((slots, slots), F32)], axis=1)
            skewed = pltpu.roll(wide, 0, 1, stride=1, stride_axis=0)
            grad_diagonals[pl.ds(head, 1), :] = jnp.sum(skewed, axis=0, keepdims=True)
            dq.append(dot(ds, k))
            dk.append(dot_tn(ds, q))
            dv.append(dot_tn(low, g))
        grad_qkv[:, columns(pair, LANES)] = (jnp.where(first, dq[0], dq[1]) * SCALE).astype(BF16)
        grad_qkv[:, columns(PAIRS + pair, LANES)] = (
            jnp.where(first, dk[0], dk[1]) * SCALE
        ).astype(BF16)
        grad_qkv[:, columns(2 * PAIRS + pair, LANES)] = jnp.where(first, dv[0], dv[1]).astype(BF16)

    for part in range(PARTS):
        pl.loop(part * PAIRS // PARTS, (part + 1) * PAIRS // PARTS)(attend_back)
        reached(f"part{part}")
        if part % 2 == 1:
            half, wide = part // 2, width // 2
            for i in range(3):
                for j in range(wide // 256):
                    source = i * width + half * wide + j * 256
                    at = i * wide + j * 256
                    grad_halves[half][:, at : at + 256] = dot_tn(
                        normed[...], grad_qkv[:, source : source + 256]
                    ).astype(BF16)
            reached(f"half{half}")

    high, low = two_halves(grad_diagonals[...])
    by_lane = dot_nt(high, hot_back[...]) + dot_nt(low, hot_back[...])
    grad_small[experts + 2 : experts + 3, :] = jnp.sum(
        by_lane * heads[...].astype(F32), axis=0, keepdims=True
    )
    grad_normed = dot_nt(grad_qkv[...], weights[:, : 3 * width])
    x = tokens[...].astype(F32)
    inv_one = lax.rsqrt(jnp.mean(x * x, axis=1, keepdims=True) + epsilon)
    unit_one = x * inv_one
    grad_small[experts : experts + 1, :] = jnp.sum(grad_normed * unit_one, axis=0, keepdims=True)
    scaled_one = small[experts : experts + 1, :] * grad_normed
    grad_tokens[...] = grad_resid[...] + inv_one * (
        scaled_one - unit_one * jnp.mean(scaled_one * unit_one, axis=1, keepdims=True)
    )
    reached("tokens")


def backward_scratch(slots, width):
    return [
        pltpu.VMEM((slots, width), BF16),
        pltpu.VMEM((slots, 3 * width), BF16),
        pltpu.VMEM((slots, width), BF16),
        pltpu.VMEM((slots, width), BF16),
        pltpu.VMEM((slots, width), F32),
        pltpu.VMEM((HEADS, 2 * slots), F32),
    ]


def add_mixed(output, resid, length, parts):
    keep_row = lax.broadcasted_iota(jnp.int32, (resid.shape[0], 1), 0) < length[0, 0]
    total = resid[...]
    for part in parts:
        total = total + part[...].astype(F32)
    output[...] = jnp.where(keep_row, total, 0.0).astype(BF16)


def local_backward_kernel(experts, *refs):
    ins, mixed, output, outs, work = refs[:17], refs[17], refs[18], refs[19:24], refs[24:]
    backward_layer(experts, False, ins, outs, work, lambda name: None)
    add_mixed(output, ins[15], ins[7], [mixed.at[block] for block in range(mixed.shape[0])])


def local_backward(experts, *args):
    tokens, small = args[0], args[4]
    slots, width = tokens.shape
    return call(
        functools.partial(local_backward_kernel, experts),
        (
            jax.ShapeDtypeStruct((slots, width), BF16),
            jax.ShapeDtypeStruct((slots, width), F32),
            jax.ShapeDtypeStruct(small.shape, F32),
            jax.ShapeDtypeStruct((width, width), BF16),
            jax.ShapeDtypeStruct((width, 3 * width // 2), BF16),
            jax.ShapeDtypeStruct((width, 3 * width // 2), BF16),
        ),
        backward_scratch(slots, width),
        62 * MB,
        4 * slots * width * (4 * width + 2 * slots),
        *args,
    )


class DeviceSum:
    @staticmethod
    def scratch(share, width):
        return [
            pltpu.VMEM((4, 4 * share, width), BF16),
            pltpu.VMEM((4, 2, share, width), BF16),
            pltpu.VMEM((4, share, width), BF16),
            DMA((4, 4)),
            DMA((4, 4)),
        ] + LineSum.scratch(1, share, width, False)

    def __init__(self, partial, scratch):
        self.partial = partial
        self.theirs, self.first_in, self.second_in, self.send, self.recv = scratch[:5]
        self.line = LineSum(1, None, scratch[5:], False)
        self.share = self.second_in.shape[1]
        self.d, self.e, self.z, self.core = here()
        self.other = (2 * self.z + 1 - self.core, self.e)
        self.to_x, self.to_y = (self.d, flipped(self.e, 1)), (self.d, flipped(self.e, 2))

    def rows(self, k, core, start, count):
        row = (2 * flipped(self.z, k) + core) * 4 * self.share + start
        return self.partial.at[pl.ds(pl.multiple_of(row, self.share), count)]

    def piece(self, k, q):
        return self.rows(k, self.core, flipped(self.e, q) * self.share, self.share)

    def remote(self, src, dst, stage, k, to):
        return pltpu.make_async_remote_copy(
            src_ref=src,
            dst_ref=dst,
            send_sem=self.send.at[stage, k],
            recv_sem=self.recv.at[stage, k],
            device_id=to,
            device_id_type=MESH,
        )

    def swap(self, k):
        src = self.rows(k, 1 - self.core, 0, 4 * self.share)
        return self.remote(src, self.theirs.at[k], 0, k, self.other)

    def first(self, k, slot):
        near, to = (1, self.to_x) if k % 2 == 0 else (2, self.to_y)
        return self.remote(
            self.piece(k, 3 if slot else near), self.first_in.at[k, slot], 1 + slot, k, to
        )

    def far(self, k):
        return 2 if k % 2 == 0 else 1

    def second(self, k):
        to = self.to_y if k % 2 == 0 else self.to_x
        return self.remote(self.piece(k, self.far(k)), self.second_in.at[k], 3, k, to)

    def begin(self):
        for k in (3, 2, 1, 0):
            self.swap(k).start()

    def stage_one(self):
        for k in (3, 2, 1, 0):
            self.swap(k).wait_recv()

            @pl.loop(0, 4)
            def _(j):
                start = pl.multiple_of(j * self.share, self.share)
                mine = self.rows(k, self.core, start, self.share)
                mine[...] = (
                    mine[...].astype(F32) + self.theirs[k, pl.ds(start, self.share)].astype(F32)
                ).astype(BF16)

            self.first(k, 1).start()
            self.first(k, 0).start()

    def stage_two(self):
        for k in (3, 2, 1, 0):
            self.first(k, 1).wait_recv()
            source = self.piece(k, self.far(k))
            source[...] = (source[...].astype(F32) + self.first_in[k, 1].astype(F32)).astype(BF16)
            self.second(k).start()

    def stage_three(self):
        for k in (3, 2, 1, 0):
            self.first(k, 0).wait_recv()
            self.second(k).wait_recv()
            total = self.piece(k, 0)[...].astype(F32) + self.first_in[k, 0].astype(F32)
            self.line.theirs[0, k] = (total + self.second_in[k].astype(F32)).astype(BF16)
        self.line.hand_over(0)

    def settle(self):
        for k in range(4):
            self.swap(k).wait_send()
            self.first(k, 0).wait_send()
            self.first(k, 1).wait_send()
            self.second(k).wait_send()


class EverySum:
    @staticmethod
    def scratch(shape):
        return [
            pltpu.VMEM((6,) + shape, F32),
            pltpu.VMEM((5,) + shape, F32),
            DMA((5,)),
            DMA((5,)),
        ]

    def __init__(self, scratch):
        self.sums, self.landed, self.send, self.recv = scratch
        d, e, z, c = here()
        near = [(2 * flipped(z, k) + c, e) for k in (1, 2)]
        self.to = [(2 * z + 1 - c, e), (d, flipped(e, 1)), (d, flipped(e, 2))] + near

    def copy(self, at):
        return pltpu.make_async_remote_copy(
            src_ref=self.sums.at[at],
            dst_ref=self.landed.at[at],
            send_sem=self.send.at[at],
            recv_sem=self.recv.at[at],
            device_id=self.to[at],
            device_id_type=MESH,
        )

    def start(self, value):
        self.sums[0] = value
        self.copy(0).start()

    def step(self, at):
        self.copy(at).wait_recv()
        self.sums[at + 1] = self.sums[at] + self.landed[at]
        if at + 1 < len(self.to):
            self.copy(at + 1).start()

    def settle(self):
        for at in range(len(self.to)):
            self.copy(at).wait_send()


def down_source(array, z, share):
    def source(i, k, core):
        row = pl.multiple_of((2 * flipped(z, k) + core) * share, share)
        return array.at[pl.ds(row, share), pl.ds(pl.multiple_of(i * CHUNK, CHUNK), CHUNK)]

    return source


def backward_kernel(experts, *refs):
    refs = list(refs)

    def take(count):
        taken, refs[:] = refs[:count], refs[count:]
        return taken

    ins = take(17)
    mixed, grad_down = take(2)
    output, grad_tokens, qkv_sum, out_sum, small_sum, down_sum = take(6)
    grad_small, grad_out, *grad_halves = take(4)
    work = take(6)
    (half_sums,) = take(1)
    brought, (own_mixed, fetched) = take(len(FETCHED)), take(2)
    cut = brought[FETCHED.index(2)].shape[1]
    ins[2], ins[3] = ins[2].at[:, :cut], ins[3].at[:, cut:]
    fetches = {}
    for i, (at, ref) in enumerate(zip(FETCHED, brought)):
        fetches[at] = pltpu.make_async_copy(ins[at], ref, fetched.at[i])
        fetches[at].start()
        ins[at] = ref
    fetches["mixed"] = pltpu.make_async_copy(mixed.at[0], own_mixed, fetched.at[len(FETCHED)])
    fetches["mixed"].start()

    def bring(names):
        for name in names:
            fetches.pop(name).wait()

    mixed_full, mixed_send, mixed_recv = take(3)
    d, e, z, _ = here()
    width = out_sum.shape[1]
    down = LineSum(width // CHUNK, down_source(grad_down, z, down_sum.shape[0]), take(6), True)
    out = DeviceSum(grad_out, take(9))
    halves = [DeviceSum(grad_half, take(9)) for grad_half in grad_halves]
    every = EverySum(take(4))
    swap = Swap(mixed, mixed_full, mixed_send, mixed_recv, d, e)
    meet(group(d, e)[1:] + [down.other] + down.to[1:])
    for block in (3, 1, 2):
        swap.start(block)
    for i in range(down.count):
        down.begin(i)
    down.halve(0)

    def reached(name):
        if name == "branch":
            bring(tuple(fetches))
            down.halve(1)
        elif name == "out":
            out.begin()
        elif name == "attended":
            down.halve(2)
        elif name == "part0":
            out.stage_one()
            down.relay(0)
        elif name == "part1":
            out.stage_two()
        elif name == "half0":
            halves[0].begin()
            down.pass_on(0)
            down.relay(1)
        elif name == "part2":
            halves[0].stage_one()
            out.stage_three()
            down.halve(3)
        elif name == "part3":
            halves[0].stage_two()
            down.pass_on(1)
        elif name == "half1":
            halves[1].begin()
            down.relay(2)
        elif name == "tokens":
            every.start(grad_small[...])
            halves[1].stage_one()

    outs = [grad_tokens, grad_small, grad_out] + grad_halves
    bring((16, 10, 15, 1))
    backward_layer(experts, True, ins, outs, work, reached)
    halves[0].stage_three()
    every.step(0)
    halves[1].stage_two()
    out.line.relay(0)
    every.step(1)
    down.pass_on(2)
    down.relay(3)
    out.line.pass_on(0)
    halves[1].stage_three()
    every.step(2)
    halves[0].line.relay(0)
    down.pass_on(3)
    every.step(3)
    halves[0].line.pass_on(0)
    halves[1].line.relay(0)
    every.step(4)
    small_sum[...] = every.sums[5]
    for i in range(down.count):
        down.finish(i, down_sum.at[:, i * CHUNK : (i + 1) * CHUNK])
    halves[1].line.pass_on(0)
    swap.finish()
    add_mixed(output, ins[15], ins[7], [own_mixed] + [mixed_full.at[q] for q in (1, 2, 3)])
    out.line.finish(0, out_sum)
    wide = width // 2
    for half, sums in enumerate(halves):
        sums.line.finish(0, half_sums.at[half])
        for i in range(3):
            at = i * width + half * wide
            qkv_sum[:, at : at + wide] = half_sums[half, :, i * wide : (i + 1) * wide]
    for sums in [out] + halves:
        sums.settle()
    every.settle()


FETCHED = (16, 10, 15, 1, 13, 3, 0, 12, 14, 2, 6)


def fetched_shape(args, at):
    width = args[0].shape[1]
    if at in (2, 3):
        return (width, args[2].shape[1] - width if at == 2 else width)
    return args[at].shape


def backward(experts, *args):
    tokens, small, mixed, grad_down = args[0], args[4], args[17], args[18]
    slots, width = tokens.shape
    share, down_share = width // 32, grad_down.shape[0] // 8
    half = 3 * width // 2
    scratch = [
        pltpu.VMEM(small.shape, F32),
        pltpu.VMEM((width, width), BF16),
        pltpu.VMEM((width, half), BF16),
        pltpu.VMEM((width, half), BF16),
        *backward_scratch(slots, width),
        pltpu.VMEM((2, share, half), F32),
        *[pltpu.VMEM(fetched_shape(args, i), args[i].dtype) for i in FETCHED],
        pltpu.VMEM(mixed.shape[1:], BF16),
        DMA((len(FETCHED) + 1,)),
        pltpu.VMEM(mixed.shape, BF16),
        DMA((4,)),
        DMA((4,)),
        *LineSum.scratch(width // CHUNK, down_share, CHUNK, True),
        *DeviceSum.scratch(share, width),
        *DeviceSum.scratch(share, half),
        *DeviceSum.scratch(share, half),
        *EverySum.scratch(small.shape),
    ]
    return call(
        functools.partial(backward_kernel, experts),
        (
            jax.ShapeDtypeStruct((slots, width), BF16),
            jax.ShapeDtypeStruct((slots, width), F32),
            jax.ShapeDtypeStruct((share, 3 * width), F32),
            jax.ShapeDtypeStruct((share, width), F32),
            jax.ShapeDtypeStruct(small.shape, F32),
            jax.ShapeDtypeStruct((down_share, width), F32),
        ),
        scratch,
        63 * MB,
        4 * slots * width * (4 * width + 2 * slots),
        *args,
        stay=(17, 18) + FETCHED,
        link=3,
    )


def publish_kernel(experts, small, *refs):
    count = (len(refs) - 6) // 3
    ins, refs = refs[:count], refs[count:]
    router, first, second, bias, *refs = refs
    outs, held = refs[:count], refs[count : 2 * count]
    loads = [pltpu.make_async_copy(ins[i], held[i], refs[-2].at[i]) for i in range(count)]
    stores = [pltpu.make_async_copy(held[i], outs[i], refs[-1].at[i]) for i in range(count)]
    for copy in loads:
        copy.start()
    width, share = small.shape[1], first.shape[1]
    device = lax.axis_index("dp") * experts + lax.axis_index("expert")
    turned = pltpu.roll(small[...], lax.rem(width - device * share, width), 1)
    router[...] = turned[:experts, :share]
    first[...] = turned[experts : experts + 1, :share]
    second[...] = turned[experts + 1 : experts + 2, :share]
    bias[...] = turned[experts + 2 : experts + 3, : bias.shape[1]]
    for load, store in zip(loads, stores):
        load.wait()
        store.start()
    for copy in stores:
        copy.wait()


def publish(experts, small, bias_share, *values):
    count = len(values)
    share = small.shape[1] // 32
    return call(
        functools.partial(publish_kernel, experts),
        tuple(
            jax.ShapeDtypeStruct(shape, F32)
            for shape in ((experts, share), (1, share), (1, share), (1, bias_share))
        )
        + tuple(jax.ShapeDtypeStruct(value.shape, value.dtype) for value in values),
        [pltpu.VMEM(value.shape, value.dtype) for value in values] + [DMA((count,)), DMA((count,))],
        60 * MB,
        0,
        small,
        *values,
        stay=tuple(range(1, count + 1)),
        land=tuple(range(4, count + 4)),
    )


READY = 2


def on_device(
    fast,
    tokens,
    cotangent,
    qkv_weight,
    out_weight,
    router_weight,
    first_gain,
    second_gain,
    bias_table,
    gate_weight,
    up_weight,
    down_weight,
    lengths,
    routes,
    priority,
):
    both = ("dp", "expert")
    slots, width = tokens.shape
    expert_count = lax.axis_size("expert")
    device_count = lax.axis_size("dp") * expert_count
    share, bias_share = first_gain.shape[0], bias_table.shape[0]
    device = lax.axis_index("dp") * expert_count + lax.axis_index("expert")
    own = lax.axis_index("expert").astype(jnp.int32).reshape(1, 1)
    small_rows = -(-(expert_count + 3) // 8) * 8

    def gathered(value, axes, axis=0, tiled=True):
        return lax.all_gather(value, axes, axis=axis, tiled=tiled)

    def scattered(value, axes):
        return lax.psum_scatter(value, axes, scatter_dimension=0, tiled=True).astype(F32)

    def exchanged(value):
        return lax.all_to_all(value, "expert", split_axis=0, concat_axis=0, tiled=True)

    rows_own, hidden = gate_weight.shape[1:]
    if not fast:
        gate_full, up_full, down_full = (
            gathered(value[0], "dp") for value in (gate_weight, up_weight, down_weight)
        )

    lane = np.arange(width)
    flat = lane // share * bias_share + lane % share
    in_table = lane % share < bias_share
    heads = np.arange(HEADS)[:, None] == np.where(in_table, flat // BUCKETS, -1)[None, :]
    heads = jnp.asarray(heads.astype(np.float32), BF16)
    ahead = np.arange(2 * slots)

    def hot(ahead):
        return jnp.asarray(
            np.where(in_table[:, None], diagonal_onehot(ahead)[flat % BUCKETS], 0.0), BF16
        )

    diagonals_hot = hot(np.where(ahead < slots, ahead, ahead - 2 * slots))
    if fast:
        *kept, buffer, scaled, plain, select, gate_column, meta_own, weights, early, down_full = forward(
            READY,
            expert_count,
            tokens,
            heads,
            diagonals_hot,
            lengths,
            cotangent,
            routes.T,
            priority,
            router_weight.T,
            first_gain[None],
            second_gain[None],
            bias_table[None],
            qkv_weight,
            out_weight,
            gate_weight[0],
            up_weight[0],
            down_weight[0],
        )
        out_full = weights
    else:
        beside = jnp.concatenate(
            [
                router_weight,
                first_gain[:, None],
                second_gain[:, None],
                jnp.pad(bias_table, (0, share - bias_share))[:, None],
                jnp.zeros((share, 128 - expert_count - 3), BF16),
            ],
            axis=1,
        )
        valid_rows = jnp.arange(slots, dtype=jnp.int32) < lengths[0, 0]
        meta_own = jnp.concatenate(
            [
                routes.T,
                priority,
                valid_rows.astype(jnp.int32)[None, :],
                jnp.zeros((4, slots), jnp.int32),
            ],
            axis=0,
        )
        weights = gathered(jnp.concatenate([qkv_weight, beside], axis=1), both)
        out_full = gathered(out_weight, both)
        kept = attention_forward(
            expert_count, tokens, weights, out_full, heads, diagonals_hot, lengths
        )
        rows, cots, meta = (
            gathered(value, "expert", tiled=False) for value in (kept[4], cotangent, meta_own)
        )
        buffer, scaled, plain, select, gate_column = dispatch(rows, cots, meta, kept[5], own)
    qkv, attended, probs, resid, normed_two, small = kept
    if fast:
        grad_gate, grad_up, grad_down, mixed, returned, inner_rows = sweep(
            READY,
            buffer,
            scaled,
            plain,
            gate_column,
            select,
            gate_weight[0],
            up_weight[0],
            early,
            down_full,
        )
    else:
        expert_out, grad_buffer, inner, *grad_experts = experts(
            buffer, scaled, plain, gate_full, up_full, down_full
        )
        mixed, returned, inner_rows = (
            exchanged(value)
            for value in give_back(select, expert_out, grad_buffer, inner, gate_column)
        )
        grad_gate, grad_up, grad_down = (scattered(value, "dp")[None] for value in grad_experts)
    layer = (
        tokens,
        cotangent,
        weights,
        out_full,
        small,
        heads,
        hot(ahead - (slots - 1)),
        lengths,
        meta_own,
        own,
        returned,
        inner_rows,
        qkv,
        attended,
        probs,
        resid,
        normed_two,
        mixed,
    )
    if fast:
        output, grad_tokens, grad_qkv, grad_out, grad_small, grad_down = backward(
            expert_count, *layer, grad_down
        )
        grad_router, grad_first, grad_second, grad_bias, *large = publish(
            expert_count,
            grad_small,
            bias_share,
            output,
            grad_tokens,
            grad_qkv,
            grad_out,
            grad_gate,
            grad_up,
            grad_down,
        )
        output, grad_tokens, grad_qkv, grad_out, grad_gate, grad_up, grad_down = large
        grad_gate, grad_up, grad_down = grad_gate[None], grad_up[None], grad_down[None]
    else:
        output, grad_tokens, grad_small, *grad_weights = local_backward(expert_count, *layer)
        grad_out, *halves = (scattered(value, both) for value in grad_weights)
        grad_qkv = jnp.stack([half.reshape(share, 3, width // 2) for half in halves], axis=2)
        grad_qkv = grad_qkv.reshape(share, 3 * width)
        grad_small = lax.psum(grad_small, both)
        grad_small = lax.dynamic_slice(grad_small, (0, device * share), (small_rows, share))
        grad_router, grad_first, grad_second, grad_bias = (
            grad_small[:expert_count],
            grad_small[expert_count : expert_count + 1],
            grad_small[expert_count + 1 : expert_count + 2],
            grad_small[expert_count + 2 : expert_count + 3, :bias_share],
        )
    return (
        output,
        grad_tokens,
        grad_qkv,
        grad_out,
        grad_router.T,
        grad_first[0],
        grad_second[0],
        grad_bias[0],
        grad_gate,
        grad_up,
        grad_down,
    )


def solution(mesh):
    fast = dict(mesh.shape) == {"dp": 8, "expert": 4}
    rows = P(("dp", "expert"), None)
    flat = P(("dp", "expert"))
    expert = P("expert", "dp", None)
    grid = P("dp", "expert")
    return jax.shard_map(
        functools.partial(on_device, fast),
        mesh=mesh,
        in_specs=(rows,) * 5 + (flat,) * 3 + (expert,) * 3 + (grid, rows, grid),
        out_specs=(rows,) * 5 + (flat,) * 3 + (expert,) * 3,
        check_vma=False,
    )
```

```python
import functools
import math

import jax
import jax.numpy as jnp
import numpy as np
from jax import lax
from jax.experimental import pallas as pl
from jax.experimental.pallas import tpu as pltpu
from jax.sharding import PartitionSpec as P

HEADS = 16
HD = 64
BUCKETS = 32
CAP = 480
PAIRS = HEADS // 2
LANES = 2 * HD
PARTS = 4
CHUNK = 256
TILE = 2 * CHUNK

epsilon = 1e-06
masked_value = -1e30
max_distance = 128.0
SCALE = 1.0 / math.sqrt(HD)
MB = 1 << 20
F32 = jnp.float32
BF16 = jnp.bfloat16


def bucket_of(offset, bucket_count):
    halfway = bucket_count // 2
    exact_span = bucket_count // 4
    distance = np.abs(offset)
    log_part = np.log(np.maximum(distance, 1) / float(exact_span)) / np.log(
        max_distance / exact_span
    )
    far_bucket = np.minimum(
        exact_span + np.floor(log_part * exact_span).astype(np.int64), halfway - 1
    )
    inside = np.where(distance < exact_span, distance, far_bucket)
    return np.where(offset < 0, halfway, 0) + inside


def diagonal_onehot(ahead):
    return (bucket_of(-ahead, BUCKETS)[None, :] == np.arange(BUCKETS)[:, None]).astype(np.float32)


def dot(a, b):
    return jnp.dot(a, b, preferred_element_type=F32)


def dot_nt(a, b):
    return lax.dot_general(a, b, (((1,), (1,)), ((), ())), preferred_element_type=F32)


def dot_tn(a, b):
    return lax.dot_general(a, b, (((0,), (0,)), ((), ())), preferred_element_type=F32)


def two_halves(value):
    high = value.astype(BF16)
    return high, (value - high.astype(F32)).astype(BF16)


def columns(index, width):
    return pl.ds(pl.multiple_of(index * width, width), width)


VMEM_SPEC = pl.BlockSpec(memory_space=pltpu.VMEM)


ANY_SPEC = pl.BlockSpec(memory_space=pl.ANY)
MESH = pl.DeviceIdType.MESH
DMA = pltpu.SemaphoreType.DMA


def call(kernel, out_shape, scratch, vmem, flops, *args, stay=(), land=(), link=None, aliases=None):
    nbytes = sum(a.size * a.dtype.itemsize for a in args)
    params = dict(vmem_limit_bytes=vmem)
    if link is not None:
        params.update(collective_id=link, has_side_effects=True)
    return pl.pallas_call(
        kernel,
        out_shape=out_shape,
        in_specs=[ANY_SPEC if i in stay else VMEM_SPEC for i in range(len(args))],
        out_specs=tuple(ANY_SPEC if i in land else VMEM_SPEC for i in range(len(out_shape))),
        scratch_shapes=scratch,
        input_output_aliases=aliases or {},
        compiler_params=pltpu.CompilerParams(**params),
        cost_estimate=pl.CostEstimate(flops=flops, bytes_accessed=nbytes, transcendentals=0),
    )(*args)


def here():
    d, e = lax.axis_index("dp"), lax.axis_index("expert")
    return d, e, d // 2, lax.rem(d, 2)


def flipped(value, bits):
    low, high = lax.rem(value, 2), value // 2
    low = 1 - low if bits & 1 else low
    high = 1 - high if bits & 2 else high
    return 2 * high + low


def meet(partners):
    barrier = pltpu.get_barrier_semaphore()
    for partner in partners:
        pl.semaphore_signal(barrier, inc=1, device_id=partner, device_id_type=MESH)
    pl.semaphore_wait(barrier, len(partners))


def push(src, dst, send, recv, to):
    copy = pltpu.make_async_remote_copy(
        src_ref=src, dst_ref=dst, send_sem=send, recv_sem=recv, device_id=to, device_id_type=MESH
    )
    copy.start()
    return copy


def group(d, e):
    return [None] + [(d, flipped(e, q)) for q in (1, 2, 3)]


class Spread:
    def __init__(self, src, dst, send, recv, d, e):
        self.src, self.dst, self.send, self.recv = src, dst, send, recv
        self.to = group(d, e)
        self.half = src.shape[0] // 2
        self.copies = {}

    def part(self, ref, half):
        return ref.at[pl.ds(half * self.half, self.half)]

    def start(self):
        for turn in range(2):
            for q in (1, 2):
                half = turn if q == 1 else 1 - turn
                at = 2 * (q - 1) + half
                self.copies[q, half] = push(
                    self.part(self.src, half),
                    self.part(self.dst.at[q], half),
                    self.send.at[at],
                    self.recv.at[at],
                    self.to[q],
                )

    def forward(self):
        for q, half, across, at in ((1, 0, 2, 4), (2, 1, 1, 5)):
            self.copies[q, half].wait_recv()
            self.copies[3, half] = push(
                self.part(self.dst.at[q], half),
                self.part(self.dst.at[3], half),
                self.send.at[at],
                self.recv.at[at],
                self.to[across],
            )

    def arrived(self, q):
        for half in {1: (1,), 2: (0,), 3: (0, 1)}[q]:
            self.copies[q, half].wait_recv()

    def sent(self):
        for copy in self.copies.values():
            copy.wait_send()

    def finish(self):
        for q in (1, 2, 3):
            self.arrived(q)
        self.sent()


class Swap:
    def __init__(self, src, dst, send, recv, d, e):
        self.src, self.dst, self.send, self.recv = src, dst, send, recv
        self.to = group(d, e)
        self.copies = {}

    def start(self, q):
        self.copies[q] = push(
            self.src.at[q], self.dst.at[q], self.send.at[q], self.recv.at[q], self.to[q]
        )

    def finish(self):
        for copy in self.copies.values():
            copy.wait_recv()
        for copy in self.copies.values():
            copy.wait_send()


class DeviceGather:
    WAYS = 5

    def __init__(self, full, share, send, recv):
        self.full, self.share, self.send, self.recv = full, share, send, recv
        self.d, self.e, self.z, self.core = d, e, z, c = here()
        self.to_x, self.to_y = (d, flipped(e, 1)), (d, flipped(e, 2))
        self.other = (2 * z + 1 - c, e)
        self.to_z = [None] + [(2 * flipped(z, k) + c, e) for k in (1, 2, 3)]
        self.end = jnp.logical_or(z == 0, z == 3)
        self.middle = jnp.logical_not(self.end)

    def item(self, k, q, core=None):
        device = 2 * flipped(self.z, k) + (self.core if core is None else core)
        row = (device * 4 + flipped(self.e, q)) * self.share
        return self.full.at[pl.ds(pl.multiple_of(row, self.share), self.share)]

    def pass_on(self, k, q, way, at, to, into=None):
        piece = self.item(k, q)
        return pltpu.make_async_remote_copy(
            src_ref=piece,
            dst_ref=piece,
            send_sem=self.send.at[way, at],
            recv_sem=self.recv.at[way, at if into is None else into],
            device_id=to,
            device_id_type=MESH,
        )

    def along_z(self, k):
        return self.pass_on(0, 0, 0, k, self.to_z[k])

    def relay_z(self, k):
        return self.pass_on(k, 0, 0, 2 + k, self.to_z[1], 5 - k)

    def along_x(self, k):
        return self.pass_on(k, 0, 1, k, self.to_x)

    def along_y(self, k):
        return self.pass_on(k, 0, 2, k, self.to_y)

    def across(self, k):
        return self.pass_on(k, 1, 3, k, self.to_y) if k % 2 == 0 else self.pass_on(k, 2, 3, k, self.to_x)

    def over(self, k, q):
        return self.pass_on(k, q, 4, 4 * q + k, self.other)

    def start(self):
        self.along_z(1).start()

        @pl.when(self.middle)
        def _():
            self.along_z(3).start()

        @pl.when(self.end)
        def _():
            self.along_z(2).start()

    def spread_out(self, k):
        self.along_x(k).start()
        self.along_y(k).start()
        self.over(k, 0).start()

    def from_z(self, k):
        self.along_z(k).wait_recv()
        if k > 1:

            @pl.when(self.middle)
            def _():
                self.relay_z(k).start()

        self.spread_out(k)

    def from_neighbours(self, k):
        self.along_x(k).wait_recv()
        if k % 2 == 0:
            self.across(k).start()
        self.over(k, 1).start()
        self.along_y(k).wait_recv()
        if k % 2 == 1:
            self.across(k).start()
        self.over(k, 2).start()

    def from_across(self, k):
        self.across(k).wait_recv()
        self.over(k, 3).start()

    def complete(self):
        for q in range(4):
            for k in range(4):
                self.over(k, q).wait_recv()

    def settle(self):
        self.along_z(1).wait_send()

        @pl.when(self.middle)
        def _():
            self.along_z(3).wait_send()
            self.relay_z(2).wait_send()
            self.relay_z(3).wait_send()

        @pl.when(self.end)
        def _():
            self.along_z(2).wait_send()

        for k in range(4):
            self.along_x(k).wait_send()
            self.along_y(k).wait_send()
            self.across(k).wait_send()
            for q in range(4):
                self.over(k, q).wait_send()


class LineSum:
    def __init__(self, count, source, scratch, load):
        self.count, self.source, self.load_first = count, source, load
        scratch = list(scratch)
        self.theirs, self.landed, self.send, self.recv = scratch[:4]
        if load:
            self.loads, self.loaded = scratch[4:]
        self.d, self.e, self.z, self.core = here()
        self.other = (2 * self.z + 1 - self.core, self.e)
        self.to = [None] + [(2 * flipped(self.z, k) + self.core, self.e) for k in (1, 2, 3)]
        self.end = jnp.logical_or(self.z == 0, self.z == 3)
        self.middle = jnp.logical_not(self.end)

    @staticmethod
    def scratch(count, rows, width, load):
        part = (rows, width)
        parts = [
            pltpu.VMEM((count, 4) + part, BF16),
            pltpu.VMEM((count, 5) + part, BF16),
            DMA((count, 3, 5)),
            DMA((count, 3, 5)),
        ]
        return parts + ([pltpu.VMEM((count, 4) + part, BF16), DMA((count, 4))] if load else [])

    def remote(self, i, src, dst, stage, out, into, to):
        return pltpu.make_async_remote_copy(
            src_ref=src,
            dst_ref=dst,
            send_sem=self.send.at[i, stage, out],
            recv_sem=self.recv.at[i, stage, into],
            device_id=to,
            device_id_type=MESH,
        )

    def load(self, i, k):
        return pltpu.make_async_copy(
            self.source(i, k, self.core), self.loads.at[i, k], self.loaded.at[i, k]
        )

    def swap(self, i, k):
        src = self.source(i, k, 1 - self.core)
        return self.remote(i, src, self.theirs.at[i, k], 0, k, k, self.other)

    def hand(self, i, k):
        at = 1 if k == 1 else 5 - k
        return self.remote(i, self.theirs.at[i, k], self.landed.at[i, at], 1, k, at, self.to[1])

    def handed(self, i, at):
        return self.remote(i, self.theirs.at[i, at], self.landed.at[i, at], 1, at, at, self.to[1])

    def deliver(self, i, k):
        at = 0 if k == 3 else 4
        return self.remote(i, self.theirs.at[i, k], self.landed.at[i, at], 2, k, at, self.to[3])

    def for_partner(self, i):
        return self.remote(i, self.theirs.at[i, 0], self.landed.at[i, 4], 2, 4, 4, self.to[3])

    def last(self, i):
        return self.remote(i, self.theirs.at[i, 1], self.landed.at[i, 0], 2, 0, 0, self.to[1])

    def add(self, i, k, more):
        self.theirs[i, k] = (self.theirs[i, k].astype(F32) + more[...].astype(F32)).astype(BF16)

    def begin(self, i):
        for k in (3, 2, 1, 0):
            self.swap(i, k).start()
            if self.load_first:
                self.load(i, k).start()

    def halve(self, i):
        for k in (3, 2, 1, 0):
            if self.load_first:
                self.load(i, k).wait()
            self.swap(i, k).wait_recv()
            self.add(i, k, self.loads.at[i, k] if self.load_first else self.source(i, k, self.core))
        self.hand_over(i)

    def hand_over(self, i):
        @pl.when(self.end)
        def _():
            for k in (3, 2, 1):
                self.hand(i, k).start()

    def relay(self, i):
        @pl.when(self.middle)
        def _():
            for k in (2, 3):
                self.handed(i, k).wait_recv()
                self.add(i, k, self.landed.at[i, k])
                self.deliver(i, k).start()

    def pass_on(self, i):
        @pl.when(self.middle)
        def _():
            self.for_partner(i).wait_recv()
            self.add(i, 1, self.landed.at[i, 4])
            self.last(i).start()

    def finish(self, i, out):
        self.last(i).wait_recv()
        out[...] = self.theirs[i, 0].astype(F32) + self.landed[i, 0].astype(F32)
        if self.source is not None:
            for k in range(4):
                self.swap(i, k).wait_send()

        @pl.when(self.end)
        def _():
            for k in (3, 2, 1):
                self.hand(i, k).wait_send()

        @pl.when(self.middle)
        def _():
            self.handed(i, 1).wait_recv()
            out[...] += self.landed[i, 1].astype(F32)
            self.deliver(i, 2).wait_send()
            self.deliver(i, 3).wait_send()
            self.last(i).wait_send()


class LineSpread:
    def __init__(self, halves, place, scratch):
        self.halves, self.place = halves, place
        self.copied, self.send, self.recv = scratch
        self.d, self.e, self.z, self.core = here()
        self.other = (2 * self.z + 1 - self.core, self.e)
        self.to = [None] + [(2 * flipped(self.z, k) + self.core, self.e) for k in (1, 2, 3)]
        self.end = jnp.logical_or(self.z == 0, self.z == 3)
        self.middle = jnp.logical_not(self.end)

    @staticmethod
    def scratch(count):
        return [DMA((count,)), DMA((count, 9)), DMA((count, 8))]

    def from_chip(self, j, k, core=None):
        return self.place(j, 2 * flipped(self.z, k) + (self.core if core is None else core))

    def remote(self, j, src, dst, out, into, to):
        return pltpu.make_async_remote_copy(
            src_ref=src,
            dst_ref=dst,
            send_sem=self.send.at[j, out],
            recv_sem=self.recv.at[j, into],
            device_id=to,
            device_id_type=MESH,
        )

    def parts(self, j):
        piece, halves = self.place(j, self.d), self.halves(j)
        width = piece.shape[1] // len(halves)
        for i, half in enumerate(halves):
            yield half, piece.at[:, i * width : (i + 1) * width]

    def keep(self, j):
        piece = self.place(j, self.d)
        return pltpu.make_async_copy(piece, piece, self.copied.at[j])

    def first(self, j, way):
        piece = self.place(j, self.d)
        return self.remote(j, piece, piece, *self.way(way))

    def way(self, way):
        return min(way, 2), 4 if way == 0 else way, self.to[way] if way else self.other

    def send_own(self, j, way):
        for src, dst in self.parts(j):
            self.remote(j, src, dst, *self.way(way)).start()

    def share(self, j, k):
        piece = self.from_chip(j, k)
        return self.remote(j, piece, piece, 2 + k, 4 + k, self.other)

    def pass_on(self, j, k):
        piece = self.from_chip(j, k)
        return self.remote(j, piece, piece, 4 + k, 5 - k, self.to[1])

    def arrival(self, j, k):
        piece = self.from_chip(j, k)
        return self.remote(j, piece, piece, k, k, self.to[1])

    def shared(self, j, k):
        piece = self.from_chip(j, k, 1 - self.core)
        return self.remote(j, piece, piece, 4 + k if k else 0, 4 + k, self.other)

    def across(self, j):
        piece = self.from_chip(j, 1)
        return self.remote(j, piece, piece, 8, 2, self.to[3])

    def start(self, j):
        self.send_own(j, 1)

        @pl.when(self.middle)
        def _():
            self.send_own(j, 3)

        self.send_own(j, 0)
        for src, dst in self.parts(j):
            pltpu.make_async_copy(src, dst, self.copied.at[j]).start()

    def relay_near(self, j):
        self.arrival(j, 1).wait_recv()

        @pl.when(self.middle)
        def _():
            self.across(j).start()

        self.share(j, 1).start()

    def relay_far(self, j):
        for k in (3, 2):
            self.arrival(j, k).wait_recv()

            @pl.when(self.middle)
            def _():
                self.pass_on(j, k).start()

            self.share(j, k).start()

    def complete(self, j):
        self.keep(j).wait()
        for k in range(4):
            self.shared(j, k).wait_recv()

    def settle(self, j):
        self.first(j, 0).wait_send()
        self.first(j, 1).wait_send()

        @pl.when(self.middle)
        def _():
            self.first(j, 3).wait_send()
            self.across(j).wait_send()
            self.pass_on(j, 2).wait_send()
            self.pass_on(j, 3).wait_send()

        for k in (1, 2, 3):
            self.share(j, k).wait_send()


def pair_gates(logits, route_zero, route_one):
    experts = logits.shape[0]
    which = lax.broadcasted_iota(jnp.int32, logits.shape, 0)
    zero = jnp.sum(jnp.where(which == route_zero, logits, 0.0), axis=0, keepdims=True)
    one = jnp.sum(jnp.where(which == route_one, logits, 0.0), axis=0, keepdims=True)
    top = jnp.maximum(zero, one)
    zero, one = jnp.exp(zero - top), jnp.exp(one - top)
    total = zero + one
    return zero / total, one / total


class Dispatch:
    def __init__(self, expert, meta, rank, places):
        self.expert, self.meta, self.rank, self.places = expert, meta, rank, places
        self.blocks, _, self.slots = meta.shape

    def names(self, block):
        info = self.meta[block]
        valid = info[3:4, :] > 0
        zero = jnp.logical_and(valid, info[0:1, :] == self.expert)
        one = jnp.logical_and(valid, info[1:2, :] == self.expert)
        return info, zero, one

    def find_places(self):
        row_of = lax.broadcasted_iota(jnp.int32, (16, self.slots), 0)
        total_zero = jnp.zeros((1, 1), F32)
        for block in range(self.blocks):
            _, zero, _ = self.names(block)
            total_zero = total_zero + jnp.sum(zero.astype(F32), axis=1, keepdims=True)
            self.rank[block] = jnp.transpose(self.meta[block].astype(F32))

        def block_places(block, _):
            info, zero, one = self.names(block)
            mine = info[2:3, :].astype(F32)

            def earlier(other, counts):
                _, other_zero, other_one = self.names(other)
                marks = jnp.where(row_of == 0, other_zero.astype(F32), 0.0) + jnp.where(
                    row_of == 1, other_one.astype(F32), 0.0
                )
                before = (self.rank[other][:, 2:3] < mine).astype(F32).astype(BF16)
                return counts + dot(marks.astype(BF16), before)

            counts = lax.fori_loop(0, self.blocks, earlier, jnp.zeros((16, self.slots), F32))
            place = jnp.where(
                zero, counts[0:1, :], jnp.where(one, counts[1:2, :] + total_zero, -1.0)
            ).astype(jnp.int32)
            self.places[block] = jnp.broadcast_to(place, self.places.shape[1:])
            return 0

        lax.fori_loop(0, self.blocks, block_places, 0)

    def hot(self, block):
        return lax.broadcasted_iota(jnp.int32, (CAP, self.slots), 0) == self.places[block][0:1, :]

    def gates(self, block, rows, router_t):
        info, zero, one = self.names(block)
        gate_zero, gate_one = pair_gates(dot_nt(router_t, rows), info[0:1, :], info[1:2, :])
        gate = jnp.where(zero, gate_zero, jnp.where(one, gate_one, 0.0))
        return jnp.sum(jnp.where(self.hot(block), gate, 0.0), axis=1, keepdims=True)


def attend_forward(experts, tokens, weights, out_weight, heads, hot, length, out, between):
    qkv, attended, probs, resid, normed_two, small, normed, diagonals = out
    slots, width = tokens.shape
    small[...] = jnp.transpose(weights[:, 3 * width :].astype(F32))[: small.shape[0], :]
    x = tokens[...].astype(F32)
    inv_one = lax.rsqrt(jnp.mean(x * x, axis=1, keepdims=True) + epsilon)
    normed[...] = (x * inv_one * small[experts : experts + 1, :]).astype(BF16)
    spread_bias = heads[...].astype(F32) * small[experts + 2 : experts + 3, :]
    diagonals[...] = dot(spread_bias.astype(BF16), hot[...])

    @pl.loop(0, 3 * width // 512)
    def _(j):
        qkv[:, columns(j, 512)] = dot(normed[...], weights[:, columns(j, 512)]).astype(BF16)

    lane = lax.broadcasted_iota(jnp.int32, (slots, LANES), 1)
    first = lane < HD
    live = lax.broadcasted_iota(jnp.int32, (slots, slots), 1) < length[0, 0]

    def attend(pair):
        q = qkv[:, columns(pair, LANES)]
        k = qkv[:, columns(PAIRS + pair, LANES)]
        v = qkv[:, columns(2 * PAIRS + pair, LANES)]
        outs = []
        for half in range(2):
            head = 2 * pair + half
            own = first if half == 0 else jnp.logical_not(first)
            row = jnp.broadcast_to(diagonals[pl.ds(head, 1), :], (slots, 2 * slots))
            bias = pltpu.roll(row, 0, 1, stride=1, stride_axis=0)[:, :slots]
            scores = dot_nt(jnp.where(own, q, jnp.zeros_like(q)), k) * SCALE + bias
            scores = jnp.where(live, scores, masked_value)
            exponent = jnp.exp(scores - jnp.max(scores, axis=1, keepdims=True))
            low = (exponent / jnp.sum(exponent, axis=1, keepdims=True)).astype(BF16)
            probs[head] = low
            outs.append(dot(low, v))
        attended[:, columns(pair, LANES)] = jnp.where(first, outs[0], outs[1]).astype(BF16)

    for part in range(PARTS):
        pl.loop(part * PAIRS // PARTS, (part + 1) * PAIRS // PARTS)(attend)
        between(part)

    @pl.loop(0, width // 512)
    def _(j):
        resid[:, columns(j, 512)] = tokens[:, columns(j, 512)].astype(F32) + dot(
            attended[...], out_weight[:, columns(j, 512)]
        )

    r = resid[...]
    inv_two = lax.rsqrt(jnp.mean(r * r, axis=1, keepdims=True) + epsilon)
    normed_two[...] = (r * inv_two * small[experts + 1 : experts + 2, :]).astype(BF16)


def attention_forward_kernel(
    experts,
    tokens,
    weights,
    out_weight,
    heads,
    hot,
    length,
    qkv,
    attended,
    probs,
    resid,
    normed_two,
    small,
    *scratch,
):
    out = (qkv, attended, probs, resid, normed_two, small) + scratch
    attend_forward(
        experts, tokens, weights, out_weight, heads, hot, length, out, lambda part: None
    )


def attention_shapes(experts, tokens):
    slots, width = tokens.shape
    return (
        jax.ShapeDtypeStruct((slots, 3 * width), BF16),
        jax.ShapeDtypeStruct((slots, width), BF16),
        jax.ShapeDtypeStruct((HEADS, slots, slots), BF16),
        jax.ShapeDtypeStruct((slots, width), F32),
        jax.ShapeDtypeStruct((slots, width), BF16),
        jax.ShapeDtypeStruct((-(-(experts + 3) // 8) * 8, width), F32),
    )


def attention_forward(experts, tokens, weights, out_weight, heads, hot, length):
    slots, width = tokens.shape
    return call(
        functools.partial(attention_forward_kernel, experts),
        attention_shapes(experts, tokens),
        [pltpu.VMEM((slots, width), BF16), pltpu.VMEM((HEADS, 2 * slots), F32)],
        48 * MB,
        2 * slots * width * (4 * width + 2 * slots),
        tokens,
        weights,
        out_weight,
        heads,
        hot,
        length,
    )


def dispatch_kernel(
    rows, cots, meta, small, own, buffer, scaled, plain, select, gate_column, acc, acc_cot, rank, places
):
    work = Dispatch(own[0, 0], meta, rank, places)
    work.find_places()
    acc[...] = jnp.zeros_like(acc)
    acc_cot[...] = jnp.zeros_like(acc_cot)
    gate_column[...] = jnp.zeros_like(gate_column)
    router_t = small[...].astype(BF16)
    for block in range(work.blocks):
        picked = work.hot(block).astype(F32).astype(BF16)
        select[block] = picked
        gate_column[...] += work.gates(block, rows[block], router_t)
        acc[...] += dot(picked, rows[block])
        acc_cot[...] += dot(picked, cots[block])
    buffer[...] = acc[...].astype(BF16)
    plain[...] = acc_cot[...].astype(BF16)
    scaled[...] = (acc_cot[...] * gate_column[:, 0:1]).astype(BF16)


def dispatch_shapes(blocks, slots, width):
    return (
        jax.ShapeDtypeStruct((CAP, width), BF16),
        jax.ShapeDtypeStruct((CAP, width), BF16),
        jax.ShapeDtypeStruct((CAP, width), BF16),
        jax.ShapeDtypeStruct((blocks, CAP, slots), BF16),
        jax.ShapeDtypeStruct((CAP, 128), F32),
    )


def dispatch_scratch(blocks, slots, width):
    return [
        pltpu.VMEM((CAP, width), F32),
        pltpu.VMEM((CAP, width), F32),
        pltpu.VMEM((blocks, slots, 8), F32),
        pltpu.VMEM((blocks, 8, slots), jnp.int32),
    ]


def dispatch(rows, cots, meta, small, own):
    blocks, slots, width = rows.shape
    return call(
        dispatch_kernel,
        dispatch_shapes(blocks, slots, width),
        dispatch_scratch(blocks, slots, width),
        60 * MB,
        4 * CAP * blocks * slots * width,
        rows,
        cots,
        meta,
        small,
        own,
    )


def forward_kernel(
    experts,
    tokens,
    heads,
    hot,
    length,
    cotangent,
    routes,
    priority,
    router,
    first_gain,
    second_gain,
    bias,
    qkv_own,
    out_own,
    gate_own,
    up_own,
    down_own,
    qkv_kept,
    attended_kept,
    probs_kept,
    resid_kept,
    normed_kept,
    small,
    buffer,
    scaled,
    plain,
    select,
    gate_column,
    meta,
    kept,
    early_kept,
    down_kept,
    early,
    down,
    acc,
    acc_cot,
    rank,
    places,
    weights,
    rows,
    cots,
    metas,
    normed,
    diagonals,
    local,
    send,
    recv,
    gather_send,
    gather_recv,
    piece_stored,
    own_small,
    qkv,
    attended,
    probs,
    resid,
    normed_two,
    result_stored,
    *scratch,
):
    d, e, z, c = here()
    slots, width = tokens.shape
    share = qkv_own.shape[0]
    gather = DeviceGather(weights, share, gather_send, gather_recv)
    rows_spread = Spread(normed_two, rows, send.at[0], recv.at[0], d, e)
    cots_spread = Spread(cotangent, cots, send.at[1], recv.at[1], d, e)
    work = Dispatch(e, metas, rank, places)
    tile_share, down_share = gate_own.shape[0], down_own.shape[0]
    tile_spread = LineSpread(
        lambda j: [own.at[:, j * CHUNK : (j + 1) * CHUNK] for own in (gate_own, up_own)],
        lambda j, device: early.at[
            j, pl.ds(pl.multiple_of(device * tile_share, tile_share), tile_share)
        ],
        scratch[:3],
    )
    down_spread = LineSpread(
        lambda j: [down_own.at[:, j * CHUNK : (j + 1) * CHUNK]],
        lambda j, device: down.at[
            pl.ds(pl.multiple_of(device * down_share, down_share), down_share),
            j * CHUNK : (j + 1) * CHUNK,
        ],
        scratch[3:],
    )
    pieces = [(tile_spread, j) for j in range(early.shape[0])]
    pieces += [(down_spread, j) for j in range(width // CHUNK)]

    def near(i):
        if 0 <= i < len(pieces):
            pieces[i][0].relay_near(pieces[i][1])

    def far(i):
        if 0 <= i < len(pieces):
            pieces[i][0].relay_far(pieces[i][1])
        begin(i + AHEAD)

    def begin(i):
        if i < len(pieces):
            pieces[i][0].start(pieces[i][1])

    def store(i):
        spread, j = pieces[i]
        if spread is tile_spread:
            src, dst = early.at[j], early_kept.at[j]
        else:
            at = slice(j * CHUNK, (j + 1) * CHUNK)
            src, dst = down.at[:, at], down_kept.at[:, at]
        return pltpu.make_async_copy(src, dst, piece_stored.at[i])

    cut = weights.shape[1] - width
    mine = gather.item(0, 0)
    own_parts = [
        pltpu.make_async_copy(qkv_own, mine.at[:, : 3 * width], local.at[0]),
        pltpu.make_async_copy(out_own, mine.at[:, cut:], local.at[1]),
    ]
    own_cots = pltpu.make_async_copy(cotangent, cots.at[0], local.at[3])
    for copy in own_parts:
        copy.start()
    meta[0:2, :] = routes[...]
    meta[2:3, :] = priority[...]
    slot = lax.broadcasted_iota(jnp.int32, (1, slots), 1)
    meta[3:4, :] = (slot < length[0, 0]).astype(jnp.int32)
    meta[4:8, :] = jnp.zeros((4, slots), jnp.int32)
    own_small[...] = jnp.zeros_like(own_small)
    row = 0
    for part in (router, first_gain, second_gain, bias):
        own_small[row : row + part.shape[0], : part.shape[1]] = part[...].astype(F32)
        row += part.shape[0]
    mine[:, 3 * width : cut] = jnp.zeros((share, cut - 3 * width), BF16)
    mine[:, 3 * width : 3 * width + own_small.shape[0]] = jnp.transpose(own_small[...])[
        :share, :
    ].astype(BF16)
    meet(group(d, e)[1:] + [gather.other] + gather.to_z[1:])
    meta_copies = [
        push(meta, metas.at[q], send.at[2, q], recv.at[2, q], group(d, e)[q]) for q in (1, 2, 3)
    ]
    for copy in own_parts:
        copy.wait()
    gather.start()
    gather.spread_out(0)
    own_cots.start()
    metas[0] = meta[...]
    for copy in meta_copies:
        copy.wait_recv()
    work.find_places()
    gather.from_z(1)
    gather.from_neighbours(0)
    gather.from_z(3)
    gather.from_z(2)
    for i in range(AHEAD):
        begin(i)
    gather.from_neighbours(1)
    near(0)
    gather.from_neighbours(3)
    near(1)
    far(0)
    gather.from_neighbours(2)
    cots_spread.start()
    far(1)
    for k in (0, 1, 3, 2):
        gather.from_across(k)
    near(2)
    gather.complete()
    far(2)
    keep = pltpu.make_async_copy(weights, kept, local.at[4])
    keep.start()

    def between(part):
        if part == 0:
            near(3)
        elif part == 1:
            cots_spread.forward()
            far(3)
        elif part == 2:
            near(4)
        else:
            far(4)

    out = (qkv, attended, probs, resid, normed_two, small, normed, diagonals)
    projections, out_weight = weights.at[:, :cut], weights.at[:, cut:]
    attend_forward(experts, tokens, projections, out_weight, heads, hot, length, out, between)

    rows_spread.start()
    results = [
        pltpu.make_async_copy(src, dst, result_stored.at[i])
        for i, (src, dst) in enumerate(
            (
                (qkv, qkv_kept),
                (attended, attended_kept),
                (probs, probs_kept),
                (resid, resid_kept),
                (normed_two, normed_kept),
            )
        )
    ]
    for copy in results:
        copy.start()
    own_cots.wait()
    cots_spread.finish()
    router_t = small[...].astype(BF16)

    def take_cots(block):
        picked = work.hot(block).astype(F32).astype(BF16)
        select[block] = picked
        more = dot(picked, cots[block])
        if block:
            acc_cot[...] += more
        else:
            acc_cot[...] = more

    def take_rows(block, ref):
        gate = work.gates(block, ref[...], router_t)
        more = dot(select[block], ref[...])
        if block:
            gate_column[...] += gate
            acc[...] += more
        else:
            gate_column[...] = jnp.broadcast_to(gate, gate_column.shape)
            acc[...] = more

    take_cots(0)
    take_cots(1)
    rows_spread.forward()
    take_cots(2)
    near(5)
    take_cots(3)
    plain[...] = acc_cot[...].astype(BF16)
    take_rows(0, normed_two)
    far(5)
    near(6)
    rows_spread.arrived(1)
    take_rows(1, rows.at[1])
    rows_spread.arrived(2)
    take_rows(2, rows.at[2])
    rows_spread.arrived(3)
    take_rows(3, rows.at[3])
    buffer[...] = acc[...].astype(BF16)
    scaled[...] = (acc_cot[...] * gate_column[:, 0:1]).astype(BF16)
    far(6)
    for i, (spread, j) in enumerate(pieces):
        spread.complete(j)
        store(i).start()
    rows_spread.sent()
    for copy in results:
        copy.wait()
    gather.settle()
    for i, (spread, j) in enumerate(pieces):
        spread.settle(j)
        store(i).wait()
    for copy in meta_copies:
        copy.wait_send()
    keep.wait()


AHEAD = 3


def forward(ready, experts, *args):
    tokens, cotangent, qkv_own, gate_own, down_own = args[0], args[4], args[11], args[13], args[15]
    slots, width = tokens.shape
    full = (32 * qkv_own.shape[0], 4 * width + 128)
    meta = jax.ShapeDtypeStruct((8, slots), jnp.int32)
    block = (experts, slots, width)
    tiles, down_full = (ready, width, TILE), (8 * down_own.shape[0], width)
    pieces = ready + width // CHUNK
    scratch = [pltpu.VMEM(tiles, BF16), pltpu.VMEM(down_full, BF16)]
    scratch += dispatch_scratch(*block) + [
        pltpu.VMEM(full, BF16),
        pltpu.VMEM(block, BF16),
        pltpu.VMEM(block, BF16),
        pltpu.VMEM((experts,) + meta.shape, meta.dtype),
        pltpu.VMEM((slots, width), BF16),
        pltpu.VMEM((HEADS, 2 * slots), F32),
        DMA((5,)),
        DMA((3, 6)),
        DMA((3, 6)),
        DMA((5, 16)),
        DMA((5, 16)),
        DMA((pieces,)),
        pltpu.VMEM((8, 128), F32),
        *[pltpu.VMEM(value.shape, value.dtype) for value in attention_shapes(experts, tokens)[:5]],
        DMA((5,)),
        *LineSpread.scratch(ready),
        *LineSpread.scratch(width // CHUNK),
    ]
    shapes = attention_shapes(experts, tokens) + dispatch_shapes(*block) + (meta,)
    return call(
        functools.partial(forward_kernel, experts),
        shapes
        + tuple(jax.ShapeDtypeStruct(shape, BF16) for shape in (full, tiles, down_full)),
        scratch,
        62 * MB,
        2 * slots * width * (4 * width + 2 * slots),
        *args,
        stay=(4, 11, 12, 13, 14, 15),
        land=tuple(range(5)) + tuple(len(shapes) + i for i in range(3)),
        link=0,
    )


GELU_A = math.sqrt(2.0 / math.pi)
GELU_B = 0.044715


def expert_chunk(buffer, scaled, gate, up, down):
    gate_in, up_in = dot(buffer, gate), dot(buffer, up)
    square = gate_in * gate_in
    wave = jnp.tanh(GELU_A * gate_in * (1.0 + GELU_B * square))
    half = 0.5 * (1.0 + wave)
    activated = gate_in * half
    slope = half + (0.5 * GELU_A) * gate_in * (1.0 - wave * wave) * (1.0 + 3.0 * GELU_B * square)
    hidden = (activated * up_in).astype(BF16)
    grad_hidden = dot_nt(scaled, down)
    grad_gate_in = (grad_hidden * up_in * slope).astype(BF16)
    grad_up_in = (grad_hidden * activated).astype(BF16)
    grad_buffer = dot_nt(grad_gate_in, gate) + dot_nt(grad_up_in, up)
    return (
        dot(hidden, down),
        grad_buffer,
        dot_tn(buffer, grad_gate_in),
        dot_tn(buffer, grad_up_in),
        dot_tn(hidden, scaled),
    )


def expert_kernel(
    buffer,
    scaled,
    plain,
    gate,
    up,
    down,
    out,
    grad_buffer,
    inner,
    grad_gate,
    grad_up,
    grad_down,
    acc_out,
    acc_grad,
):
    step = pl.program_id(0)

    @pl.when(step == 0)
    def _():
        acc_out[...] = jnp.zeros_like(acc_out)
        acc_grad[...] = jnp.zeros_like(acc_grad)

    more_out, more_grad, d_gate, d_up, d_down = expert_chunk(
        buffer[...], scaled[...], gate[...], up[...], down[...]
    )
    acc_out[...] += more_out
    acc_grad[...] += more_grad
    grad_gate[...] = d_gate.astype(BF16)
    grad_up[...] = d_up.astype(BF16)
    grad_down[...] = d_down.astype(BF16)

    @pl.when(step == pl.num_programs(0) - 1)
    def _():
        low = acc_out[...].astype(BF16)
        out[...] = low
        grad_buffer[...] = acc_grad[...].astype(BF16)
        inner[...] = jnp.broadcast_to(
            jnp.sum(low.astype(F32) * plain[...].astype(F32), axis=1, keepdims=True), inner.shape
        )


def experts(buffer, scaled, plain, gate, up, down):
    rows, width = buffer.shape
    hidden = gate.shape[1]
    whole = pl.BlockSpec((rows, width), lambda j: (0, 0))
    tall = pl.BlockSpec((width, CHUNK), lambda j: (0, j))
    wide = pl.BlockSpec((CHUNK, width), lambda j: (j, 0))
    shapes = (
        jax.ShapeDtypeStruct((rows, width), BF16),
        jax.ShapeDtypeStruct((rows, width), BF16),
        jax.ShapeDtypeStruct((rows, 128), F32),
        jax.ShapeDtypeStruct((width, hidden), BF16),
        jax.ShapeDtypeStruct((width, hidden), BF16),
        jax.ShapeDtypeStruct((hidden, width), BF16),
    )
    return pl.pallas_call(
        expert_kernel,
        out_shape=shapes,
        grid=(hidden // CHUNK,),
        in_specs=[whole, whole, whole, tall, tall, wide],
        out_specs=(whole, whole, pl.BlockSpec((rows, 128), lambda j: (0, 0)), tall, tall, wide),
        scratch_shapes=[pltpu.VMEM((rows, width), F32), pltpu.VMEM((rows, width), F32)],
        compiler_params=pltpu.CompilerParams(
            vmem_limit_bytes=48 * MB, dimension_semantics=("arbitrary",)
        ),
        cost_estimate=pl.CostEstimate(
            flops=18 * rows * width * hidden,
            bytes_accessed=12 * width * hidden,
            transcendentals=rows * hidden,
        ),
    )(buffer, scaled, plain, gate, up, down)


def give_back_kernel(select, out, grad_buffer, inner, gate_column, mixed, grads, inner_rows):
    weighted = (out[...].astype(F32) * gate_column[:, 0:1]).astype(BF16)
    for block in range(select.shape[0]):
        row = jnp.sum(select[block].astype(F32) * inner[:, 0:1], axis=0, keepdims=True)
        inner_rows[block] = jnp.broadcast_to(row, inner_rows.shape[1:])
        grads[block] = dot_tn(select[block], grad_buffer[...]).astype(BF16)
        mixed[block] = dot_tn(select[block], weighted).astype(BF16)


def give_back(select, out, grad_buffer, inner, gate_column):
    blocks, rows, slots = select.shape
    width = out.shape[1]
    wide = (blocks, slots, width)
    return call(
        give_back_kernel,
        (
            jax.ShapeDtypeStruct(wide, BF16),
            jax.ShapeDtypeStruct(wide, BF16),
            jax.ShapeDtypeStruct((blocks, 8, slots), F32),
        ),
        [],
        56 * MB,
        4 * rows * blocks * slots * width,
        select,
        out,
        grad_buffer,
        inner,
        gate_column,
    )


def sweep_kernel(
    ready,
    buffer,
    scaled,
    plain,
    gate_column,
    select,
    gate_own,
    up_own,
    early,
    down_full,
    gate_sum,
    up_sum,
    grad_down,
    mixed,
    returned,
    inner_full,
    sums,
    both,
    down,
    acc_out,
    acc_grad,
    down_stage,
    grads,
    inner_rows,
    buffer_in,
    scaled_in,
    plain_in,
    column_in,
    select_in,
    fetched,
    loaded,
    stored,
    local,
    swap_send,
    swap_recv,
    *scratch,
):
    tiles, width = both.shape[0], both.shape[1]
    share = gate_own.shape[0]
    coming = tiles - ready
    d, e, z, c = here()

    def rows_of(device):
        return pl.ds(pl.multiple_of(device * share, share), share)

    spread = LineSpread(
        lambda j: [own.at[:, columns(ready + j, CHUNK)] for own in (gate_own, up_own)],
        lambda j, device: both.at[ready + j, rows_of(device)],
        scratch[:3],
    )
    line = LineSum(
        tiles,
        lambda i, k, core: both.at[i, rows_of(2 * flipped(z, k) + core)],
        scratch[3:],
        load=False,
    )
    swap = Swap(grads, returned, swap_send.at[0], swap_recv.at[0], d, e)
    inner_swap = Swap(inner_rows, inner_full, swap_send.at[1], swap_recv.at[1], d, e)
    meet(group(d, e)[1:] + [line.other] + line.to[1:])

    def early_load(t):
        return pltpu.make_async_copy(early.at[t], both.at[t], loaded.at[t])

    for j in range(min(DEPTH, coming)):
        spread.start(j)
    fetches = []
    for i, (src, dst) in enumerate(
        (
            (buffer, buffer_in),
            (scaled, scaled_in),
            (plain, plain_in),
            (gate_column, column_in),
            (select, select_in),
        )
    ):
        fetches.append(pltpu.make_async_copy(src, dst, fetched.at[i]))
        fetches[-1].start()
    buffer, scaled, plain, gate_column, select = buffer_in, scaled_in, plain_in, column_in, select_in
    down_load = pltpu.make_async_copy(down_full, down, loaded.at[tiles])
    for t in range(ready):
        early_load(t).start()
        if t == 0:
            down_load.start()
    acc_out[...] = jnp.zeros_like(acc_out)
    acc_grad[...] = jnp.zeros_like(acc_grad)
    for copy in fetches:
        copy.wait()
    down_load.wait()

    def down_rows(t):
        return pl.ds(pl.multiple_of(t * CHUNK, CHUNK), CHUNK)

    def down_store(t, slot):
        return pltpu.make_async_copy(
            down_stage.at[slot], grad_down.at[down_rows(t)], stored.at[slot]
        )

    def between(low, value, high):
        return jnp.logical_and(value >= low, value < high)

    def tile_step(t, _):
        @pl.when(t < ready)
        def _():
            early_load(t).wait()

        near = t - ready + NEAR

        @pl.when(between(0, near, coming))
        def _():
            spread.relay_near(near)

        @pl.when(between(0, near - 1, coming))
        def _():
            spread.relay_far(near - 1)

        @pl.when(between(DEPTH, near - 1 + DEPTH, coming))
        def _():
            spread.start(near - 1 + DEPTH)

        @pl.when(t >= ready)
        def _():
            spread.complete(t - ready)

        @pl.when(t >= 1)
        def _():
            line.halve(t - 1)

        @pl.when(t >= LAG)
        def _():
            line.relay(t - LAG)

        @pl.when(t >= LAG + 1)
        def _():
            line.pass_on(t - LAG - 1)

        more_out, more_grad, d_gate, d_up, d_down = expert_chunk(
            buffer[...], scaled[...], both[t, :, :CHUNK], both[t, :, CHUNK:], down[down_rows(t)]
        )
        acc_out[...] += more_out
        acc_grad[...] += more_grad

        @pl.when(t >= ready)
        def _():
            spread.settle(t - ready)

        both[t, :, :CHUNK] = d_gate.astype(BF16)
        both[t, :, CHUNK:] = d_up.astype(BF16)
        slot = lax.rem(t, 2)

        @pl.when(t >= 2)
        def _():
            down_store(t - 2, slot).wait()

        down_stage[slot] = d_down.astype(BF16)
        down_store(t, slot).start()
        line.begin(t)
        return 0

    lax.fori_loop(0, tiles, tile_step, 0)

    low = acc_out[...].astype(BF16)
    inner = jnp.sum(low.astype(F32) * plain[...].astype(F32), axis=1, keepdims=True)
    grad_low = acc_grad[...].astype(BF16)
    order = (3, 1, 2, 0)
    for block in order:
        row = jnp.sum(select[block].astype(F32) * inner, axis=0, keepdims=True)
        inner_rows[block] = jnp.broadcast_to(row, inner_rows.shape[1:])
        grads[block] = dot_tn(select[block], grad_low).astype(BF16)
        if block:
            inner_swap.start(block)
            swap.start(block)
    own_copies = [
        pltpu.make_async_copy(grads.at[0], returned.at[0], local.at[0]),
        pltpu.make_async_copy(inner_rows.at[0], inner_full.at[0], local.at[1]),
    ]
    for copy in own_copies:
        copy.start()
    line.halve(tiles - 1)
    weighted = (low.astype(F32) * gate_column[:, 0:1]).astype(BF16)
    for block in order:
        mixed[block] = dot_tn(select[block], weighted).astype(BF16)

    @pl.loop(tiles - LAG, tiles + 1)
    def _(i):
        @pl.when(i < tiles)
        def _():
            line.relay(i)

        line.pass_on(i - 1)

    @pl.loop(0, tiles)
    def _(i):
        line.finish(i, sums.at[i])
        for copy in result_stores(sums.at[i], gate_sum, up_sum, i, local.at[2]):
            copy.start()

    @pl.loop(0, tiles)
    def _(i):
        for copy in result_stores(sums.at[i], gate_sum, up_sum, i, local.at[2]):
            copy.wait()

    for t in range(tiles - 2, tiles):
        down_store(t, t % 2).wait()
    for copy in own_copies:
        copy.wait()
    inner_swap.finish()
    swap.finish()


def result_stores(value, gate_sum, up_sum, tile, sem):
    return [
        pltpu.make_async_copy(
            value.at[:, i * CHUNK : (i + 1) * CHUNK], array.at[:, columns(tile, CHUNK)], sem
        )
        for i, array in enumerate((gate_sum, up_sum))
    ]


LAG = 5

DEPTH = 6
NEAR = 2


def sweep(ready, buffer, scaled, plain, gate_column, select, gate_own, up_own, early, down_full):
    rows, width = buffer.shape
    tiles = gate_own.shape[1] // CHUNK
    share = gate_own.shape[0]
    block = (select.shape[0], select.shape[2], width)
    thin = (select.shape[0], 8, select.shape[2])
    hidden = tiles * CHUNK
    shapes = (
        jax.ShapeDtypeStruct(gate_own.shape, F32),
        jax.ShapeDtypeStruct(gate_own.shape, F32),
        jax.ShapeDtypeStruct(down_full.shape, BF16),
        jax.ShapeDtypeStruct(block, BF16),
        jax.ShapeDtypeStruct(block, BF16),
        jax.ShapeDtypeStruct(thin, F32),
    )
    scratch = [
        pltpu.VMEM((tiles, share, TILE), F32),
        pltpu.VMEM((tiles, width, TILE), BF16),
        pltpu.VMEM(down_full.shape, BF16),
        pltpu.VMEM((rows, width), F32),
        pltpu.VMEM((rows, width), F32),
        pltpu.VMEM((2, CHUNK, width), BF16),
        pltpu.VMEM(block, BF16),
        pltpu.VMEM(thin, F32),
        *[
            pltpu.VMEM(value.shape, value.dtype)
            for value in (buffer, scaled, plain, gate_column, select)
        ],
        DMA((5,)),
        DMA((tiles + 1,)),
        DMA((2,)),
        DMA((3,)),
        DMA((2, 4)),
        DMA((2, 4)),
    ]
    scratch += LineSpread.scratch(tiles - ready) + LineSum.scratch(tiles, share, TILE, False)
    return call(
        functools.partial(sweep_kernel, ready),
        shapes,
        scratch,
        62 * MB,
        18 * rows * width * hidden,
        buffer,
        scaled,
        plain,
        gate_column,
        select,
        gate_own,
        up_own,
        early,
        down_full,
        stay=tuple(range(9)),
        land=(0, 1, 2, 4, 5),
        link=2,
    )


def backward_layer(experts, relative, ins, outs, work, reached):
    tokens, cotangent, weights, out_weight, small, heads, hot_back, length, meta, own = ins[:10]
    returned, inner_rows, qkv, attended, probs, resid, normed_two = ins[10:]
    grad_tokens, grad_small, grad_out, *grad_halves = outs
    grad_attended, grad_qkv, branch, normed, grad_resid, grad_diagonals = work
    slots, width = tokens.shape
    blocks = returned.shape[0]
    router_t = small[...].astype(BF16)
    keep_row = lax.broadcasted_iota(jnp.int32, (slots, 1), 0) < length[0, 0]
    logits = dot_nt(router_t, normed_two[...])
    zero_route, one_route = meta[0:1, :], meta[1:2, :]
    gate_zero, gate_one = pair_gates(logits, zero_route, one_route)
    which = lax.broadcasted_iota(jnp.int32, logits.shape, 0)
    grad_zero = jnp.zeros((1, slots), F32)
    grad_one = jnp.zeros((1, slots), F32)
    for block in range(blocks):
        row = inner_rows[block][0:1, :]
        expert = jnp.bitwise_xor(own[0, 0], block) if relative else block
        grad_zero = grad_zero + jnp.where(zero_route == expert, row, 0.0)
        grad_one = grad_one + jnp.where(one_route == expert, row, 0.0)
    shared = gate_zero * grad_zero + gate_one * grad_one
    grad_zero = gate_zero * (grad_zero - shared)
    grad_one = gate_one * (grad_one - shared)
    grad_logits = jnp.where(which == zero_route, grad_zero, 0.0) + jnp.where(
        which == one_route, grad_one, 0.0
    )
    high, low = two_halves(grad_logits)
    grad_small[...] = dot(high, normed_two[...]) + dot(low, normed_two[...])
    grad_normed_two = dot_tn(high, router_t) + dot_tn(low, router_t)
    for block in range(blocks):
        grad_normed_two = grad_normed_two + returned[block].astype(F32)
    r = resid[...]
    inv_two = lax.rsqrt(jnp.mean(r * r, axis=1, keepdims=True) + epsilon)
    unit_two = r * inv_two
    grad_small[experts + 1 : experts + 2, :] = jnp.sum(
        grad_normed_two * unit_two, axis=0, keepdims=True
    )
    scaled_two = small[experts + 1 : experts + 2, :] * grad_normed_two
    grad_resid[...] = jnp.where(keep_row, cotangent[...].astype(F32), 0.0) + inv_two * (
        scaled_two - unit_two * jnp.mean(scaled_two * unit_two, axis=1, keepdims=True)
    )
    branch[...] = grad_resid[...].astype(BF16)
    reached("branch")

    @pl.loop(0, width // 256)
    def _(j):
        grad_out[:, columns(j, 256)] = dot_tn(attended[...], branch[:, columns(j, 256)]).astype(
            BF16
        )

    reached("out")
    grad_attended[...] = dot_nt(branch[...], out_weight[...]).astype(BF16)
    x = tokens[...].astype(F32)
    inv_one = lax.rsqrt(jnp.mean(x * x, axis=1, keepdims=True) + epsilon)
    normed[...] = (x * inv_one * small[experts : experts + 1, :]).astype(BF16)
    reached("attended")

    lane = lax.broadcasted_iota(jnp.int32, (slots, LANES), 1)
    first = lane < HD
    square = (slots, slots)
    flip = (
        lax.broadcasted_iota(jnp.int32, square, 0) + lax.broadcasted_iota(jnp.int32, square, 1)
        == slots - 1
    )
    flip = flip.astype(F32).astype(BF16)

    def attend_back(pair):
        q = qkv[:, columns(pair, LANES)]
        k = qkv[:, columns(PAIRS + pair, LANES)]
        v = qkv[:, columns(2 * PAIRS + pair, LANES)]
        g = grad_attended[:, columns(pair, LANES)]
        dq, dk, dv = [], [], []
        for half in range(2):
            head = 2 * pair + half
            mine = first if half == 0 else jnp.logical_not(first)
            low = probs[head]
            p = low.astype(F32)
            grad_probs = dot_nt(jnp.where(mine, g, jnp.zeros_like(g)), v)
            ds = p * (grad_probs - jnp.sum(p * grad_probs, axis=1, keepdims=True))
            ds = ds.astype(BF16)
            wide = jnp.concatenate([dot(flip, ds), jnp.zeros((slots, slots), F32)], axis=1)
            skewed = pltpu.roll(wide, 0, 1, stride=1, stride_axis=0)
            grad_diagonals[pl.ds(head, 1), :] = jnp.sum(skewed, axis=0, keepdims=True)
            dq.append(dot(ds, k))
            dk.append(dot_tn(ds, q))
            dv.append(dot_tn(low, g))
        grad_qkv[:, columns(pair, LANES)] = (jnp.where(first, dq[0], dq[1]) * SCALE).astype(BF16)
        grad_qkv[:, columns(PAIRS + pair, LANES)] = (
            jnp.where(first, dk[0], dk[1]) * SCALE
        ).astype(BF16)
        grad_qkv[:, columns(2 * PAIRS + pair, LANES)] = jnp.where(first, dv[0], dv[1]).astype(BF16)

    for part in range(PARTS):
        pl.loop(part * PAIRS // PARTS, (part + 1) * PAIRS // PARTS)(attend_back)
        reached(f"part{part}")
        if part % 2 == 1:
            half, wide = part // 2, width // 2
            for i in range(3):
                for j in range(wide // 256):
                    source = i * width + half * wide + j * 256
                    at = i * wide + j * 256
                    grad_halves[half][:, at : at + 256] = dot_tn(
                        normed[...], grad_qkv[:, source : source + 256]
                    ).astype(BF16)
            reached(f"half{half}")

    high, low = two_halves(grad_diagonals[...])
    by_lane = dot_nt(high, hot_back[...]) + dot_nt(low, hot_back[...])
    grad_small[experts + 2 : experts + 3, :] = jnp.sum(
        by_lane * heads[...].astype(F32), axis=0, keepdims=True
    )
    grad_normed = dot_nt(grad_qkv[...], weights[:, : 3 * width])
    x = tokens[...].astype(F32)
    inv_one = lax.rsqrt(jnp.mean(x * x, axis=1, keepdims=True) + epsilon)
    unit_one = x * inv_one
    grad_small[experts : experts + 1, :] = jnp.sum(grad_normed * unit_one, axis=0, keepdims=True)
    scaled_one = small[experts : experts + 1, :] * grad_normed
    grad_tokens[...] = grad_resid[...] + inv_one * (
        scaled_one - unit_one * jnp.mean(scaled_one * unit_one, axis=1, keepdims=True)
    )
    reached("tokens")


def backward_scratch(slots, width):
    return [
        pltpu.VMEM((slots, width), BF16),
        pltpu.VMEM((slots, 3 * width), BF16),
        pltpu.VMEM((slots, width), BF16),
        pltpu.VMEM((slots, width), BF16),
        pltpu.VMEM((slots, width), F32),
        pltpu.VMEM((HEADS, 2 * slots), F32),
    ]


def add_mixed(output, resid, length, parts):
    keep_row = lax.broadcasted_iota(jnp.int32, (resid.shape[0], 1), 0) < length[0, 0]
    total = resid[...]
    for part in parts:
        total = total + part[...].astype(F32)
    output[...] = jnp.where(keep_row, total, 0.0).astype(BF16)


def local_backward_kernel(experts, *refs):
    ins, mixed, output, outs, work = refs[:17], refs[17], refs[18], refs[19:24], refs[24:]
    backward_layer(experts, False, ins, outs, work, lambda name: None)
    add_mixed(output, ins[15], ins[7], [mixed.at[block] for block in range(mixed.shape[0])])


def local_backward(experts, *args):
    tokens, small = args[0], args[4]
    slots, width = tokens.shape
    return call(
        functools.partial(local_backward_kernel, experts),
        (
            jax.ShapeDtypeStruct((slots, width), BF16),
            jax.ShapeDtypeStruct((slots, width), F32),
            jax.ShapeDtypeStruct(small.shape, F32),
            jax.ShapeDtypeStruct((width, width), BF16),
            jax.ShapeDtypeStruct((width, 3 * width // 2), BF16),
            jax.ShapeDtypeStruct((width, 3 * width // 2), BF16),
        ),
        backward_scratch(slots, width),
        62 * MB,
        4 * slots * width * (4 * width + 2 * slots),
        *args,
    )


class DeviceSum:
    @staticmethod
    def scratch(share, width):
        return [
            pltpu.VMEM((4, 4 * share, width), BF16),
            pltpu.VMEM((4, 2, share, width), BF16),
            pltpu.VMEM((4, share, width), BF16),
            DMA((4, 4)),
            DMA((4, 4)),
        ] + LineSum.scratch(1, share, width, False)

    def __init__(self, partial, scratch):
        self.partial = partial
        self.theirs, self.first_in, self.second_in, self.send, self.recv = scratch[:5]
        self.line = LineSum(1, None, scratch[5:], False)
        self.share = self.second_in.shape[1]
        self.d, self.e, self.z, self.core = here()
        self.other = (2 * self.z + 1 - self.core, self.e)
        self.to_x, self.to_y = (self.d, flipped(self.e, 1)), (self.d, flipped(self.e, 2))

    def rows(self, k, core, start, count):
        row = (2 * flipped(self.z, k) + core) * 4 * self.share + start
        return self.partial.at[pl.ds(pl.multiple_of(row, self.share), count)]

    def piece(self, k, q):
        return self.rows(k, self.core, flipped(self.e, q) * self.share, self.share)

    def remote(self, src, dst, stage, k, to):
        return pltpu.make_async_remote_copy(
            src_ref=src,
            dst_ref=dst,
            send_sem=self.send.at[stage, k],
            recv_sem=self.recv.at[stage, k],
            device_id=to,
            device_id_type=MESH,
        )

    def swap(self, k):
        src = self.rows(k, 1 - self.core, 0, 4 * self.share)
        return self.remote(src, self.theirs.at[k], 0, k, self.other)

    def first(self, k, slot):
        near, to = (1, self.to_x) if k % 2 == 0 else (2, self.to_y)
        return self.remote(
            self.piece(k, 3 if slot else near), self.first_in.at[k, slot], 1 + slot, k, to
        )

    def far(self, k):
        return 2 if k % 2 == 0 else 1

    def second(self, k):
        to = self.to_y if k % 2 == 0 else self.to_x
        return self.remote(self.piece(k, self.far(k)), self.second_in.at[k], 3, k, to)

    def begin(self):
        for k in (3, 2, 1, 0):
            self.swap(k).start()

    def stage_one(self):
        for k in (3, 2, 1, 0):
            self.swap(k).wait_recv()

            @pl.loop(0, 4)
            def _(j):
                start = pl.multiple_of(j * self.share, self.share)
                mine = self.rows(k, self.core, start, self.share)
                mine[...] = (
                    mine[...].astype(F32) + self.theirs[k, pl.ds(start, self.share)].astype(F32)
                ).astype(BF16)

            self.first(k, 1).start()
            self.first(k, 0).start()

    def stage_two(self):
        for k in (3, 2, 1, 0):
            self.first(k, 1).wait_recv()
            source = self.piece(k, self.far(k))
            source[...] = (source[...].astype(F32) + self.first_in[k, 1].astype(F32)).astype(BF16)
            self.second(k).start()

    def stage_three(self):
        for k in (3, 2, 1, 0):
            self.first(k, 0).wait_recv()
            self.second(k).wait_recv()
            total = self.piece(k, 0)[...].astype(F32) + self.first_in[k, 0].astype(F32)
            self.line.theirs[0, k] = (total + self.second_in[k].astype(F32)).astype(BF16)
        self.line.hand_over(0)

    def settle(self):
        for k in range(4):
            self.swap(k).wait_send()
            self.first(k, 0).wait_send()
            self.first(k, 1).wait_send()
            self.second(k).wait_send()


class EverySum:
    @staticmethod
    def scratch(shape):
        return [
            pltpu.VMEM((6,) + shape, F32),
            pltpu.VMEM((5,) + shape, F32),
            DMA((5,)),
            DMA((5,)),
        ]

    def __init__(self, scratch):
        self.sums, self.landed, self.send, self.recv = scratch
        d, e, z, c = here()
        near = [(2 * flipped(z, k) + c, e) for k in (1, 2)]
        self.to = [(2 * z + 1 - c, e), (d, flipped(e, 1)), (d, flipped(e, 2))] + near

    def copy(self, at):
        return pltpu.make_async_remote_copy(
            src_ref=self.sums.at[at],
            dst_ref=self.landed.at[at],
            send_sem=self.send.at[at],
            recv_sem=self.recv.at[at],
            device_id=self.to[at],
            device_id_type=MESH,
        )

    def start(self, value):
        self.sums[0] = value
        self.copy(0).start()

    def step(self, at):
        self.copy(at).wait_recv()
        self.sums[at + 1] = self.sums[at] + self.landed[at]
        if at + 1 < len(self.to):
            self.copy(at + 1).start()

    def settle(self):
        for at in range(len(self.to)):
            self.copy(at).wait_send()


def down_source(array, z, share):
    def source(i, k, core):
        row = pl.multiple_of((2 * flipped(z, k) + core) * share, share)
        return array.at[pl.ds(row, share), pl.ds(pl.multiple_of(i * CHUNK, CHUNK), CHUNK)]

    return source


def backward_kernel(experts, *refs):
    refs = list(refs)

    def take(count):
        taken, refs[:] = refs[:count], refs[count:]
        return taken

    ins = take(17)
    mixed, grad_down = take(2)
    output, grad_tokens, qkv_sum, out_sum, small_sum, down_sum = take(6)
    grad_small, grad_out, *grad_halves = take(4)
    work = take(6)
    (half_sums,) = take(1)
    brought, (own_mixed, fetched) = take(len(FETCHED)), take(2)
    cut = brought[FETCHED.index(2)].shape[1]
    ins[2], ins[3] = ins[2].at[:, :cut], ins[3].at[:, cut:]
    fetches = {}
    for i, (at, ref) in enumerate(zip(FETCHED, brought)):
        fetches[at] = pltpu.make_async_copy(ins[at], ref, fetched.at[i])
        fetches[at].start()
        ins[at] = ref
    fetches["mixed"] = pltpu.make_async_copy(mixed.at[0], own_mixed, fetched.at[len(FETCHED)])
    fetches["mixed"].start()

    def bring(names):
        for name in names:
            fetches.pop(name).wait()

    mixed_full, mixed_send, mixed_recv = take(3)
    d, e, z, _ = here()
    width = out_sum.shape[1]
    down = LineSum(width // CHUNK, down_source(grad_down, z, down_sum.shape[0]), take(6), True)
    out = DeviceSum(grad_out, take(9))
    halves = [DeviceSum(grad_half, take(9)) for grad_half in grad_halves]
    every = EverySum(take(4))
    swap = Swap(mixed, mixed_full, mixed_send, mixed_recv, d, e)
    meet(group(d, e)[1:] + [down.other] + down.to[1:])
    for block in (3, 1, 2):
        swap.start(block)
    for i in range(down.count):
        down.begin(i)
    down.halve(0)

    def reached(name):
        if name == "branch":
            bring(tuple(fetches))
            down.halve(1)
        elif name == "out":
            out.begin()
        elif name == "attended":
            down.halve(2)
        elif name == "part0":
            out.stage_one()
            down.relay(0)
        elif name == "part1":
            out.stage_two()
        elif name == "half0":
            halves[0].begin()
            down.pass_on(0)
            down.relay(1)
        elif name == "part2":
            halves[0].stage_one()
            out.stage_three()
            down.halve(3)
        elif name == "part3":
            halves[0].stage_two()
            down.pass_on(1)
        elif name == "half1":
            halves[1].begin()
            down.relay(2)
        elif name == "tokens":
            every.start(grad_small[...])
            halves[1].stage_one()

    outs = [grad_tokens, grad_small, grad_out] + grad_halves
    bring((16, 10, 15, 1))
    backward_layer(experts, True, ins, outs, work, reached)
    halves[0].stage_three()
    every.step(0)
    halves[1].stage_two()
    out.line.relay(0)
    every.step(1)
    down.pass_on(2)
    down.relay(3)
    out.line.pass_on(0)
    halves[1].stage_three()
    every.step(2)
    halves[0].line.relay(0)
    down.pass_on(3)
    every.step(3)
    halves[0].line.pass_on(0)
    halves[1].line.relay(0)
    every.step(4)
    small_sum[...] = every.sums[5]
    for i in range(down.count):
        down.finish(i, down_sum.at[:, i * CHUNK : (i + 1) * CHUNK])
    halves[1].line.pass_on(0)
    swap.finish()
    add_mixed(output, ins[15], ins[7], [own_mixed] + [mixed_full.at[q] for q in (1, 2, 3)])
    out.line.finish(0, out_sum)
    wide = width // 2
    for half, sums in enumerate(halves):
        sums.line.finish(0, half_sums.at[half])
        for i in range(3):
            at = i * width + half * wide
            qkv_sum[:, at : at + wide] = half_sums[half, :, i * wide : (i + 1) * wide]
    for sums in [out] + halves:
        sums.settle()
    every.settle()


FETCHED = (16, 10, 15, 1, 13, 3, 0, 12, 14, 2, 6)


def fetched_shape(args, at):
    width = args[0].shape[1]
    if at in (2, 3):
        return (width, args[2].shape[1] - width if at == 2 else width)
    return args[at].shape


def backward(experts, *args):
    tokens, small, mixed, grad_down = args[0], args[4], args[17], args[18]
    slots, width = tokens.shape
    share, down_share = width // 32, grad_down.shape[0] // 8
    half = 3 * width // 2
    scratch = [
        pltpu.VMEM(small.shape, F32),
        pltpu.VMEM((width, width), BF16),
        pltpu.VMEM((width, half), BF16),
        pltpu.VMEM((width, half), BF16),
        *backward_scratch(slots, width),
        pltpu.VMEM((2, share, half), F32),
        *[pltpu.VMEM(fetched_shape(args, i), args[i].dtype) for i in FETCHED],
        pltpu.VMEM(mixed.shape[1:], BF16),
        DMA((len(FETCHED) + 1,)),
        pltpu.VMEM(mixed.shape, BF16),
        DMA((4,)),
        DMA((4,)),
        *LineSum.scratch(width // CHUNK, down_share, CHUNK, True),
        *DeviceSum.scratch(share, width),
        *DeviceSum.scratch(share, half),
        *DeviceSum.scratch(share, half),
        *EverySum.scratch(small.shape),
    ]
    return call(
        functools.partial(backward_kernel, experts),
        (
            jax.ShapeDtypeStruct((slots, width), BF16),
            jax.ShapeDtypeStruct((slots, width), F32),
            jax.ShapeDtypeStruct((share, 3 * width), F32),
            jax.ShapeDtypeStruct((share, width), F32),
            jax.ShapeDtypeStruct(small.shape, F32),
            jax.ShapeDtypeStruct((down_share, width), F32),
        ),
        scratch,
        63 * MB,
        4 * slots * width * (4 * width + 2 * slots),
        *args,
        stay=(17, 18) + FETCHED,
        link=3,
    )


def publish_kernel(experts, small, *refs):
    count = (len(refs) - 12) // 3
    refs = list(refs)
    ins, smalls, outs = refs[:count], refs[count : count + 4], refs[count + 4 : 2 * count + 4]
    held, small_in = refs[2 * count + 4 : 3 * count + 4], refs[3 * count + 4]
    parts, (loaded, stored, moved) = refs[3 * count + 5 : 3 * count + 9], refs[3 * count + 9 :]
    fetch = pltpu.make_async_copy(small, small_in, moved.at[4])
    loads = [pltpu.make_async_copy(ins[i], held[i], loaded.at[i]) for i in range(count)]
    stores = [pltpu.make_async_copy(held[i], outs[i], stored.at[i]) for i in range(count)]
    stores += [pltpu.make_async_copy(parts[i], smalls[i], moved.at[i]) for i in range(4)]
    fetch.start()
    for copy in loads:
        copy.start()
    router, first, second, bias = parts
    width, share = small_in.shape[1], first.shape[1]
    device = lax.axis_index("dp") * experts + lax.axis_index("expert")
    fetch.wait()
    turned = pltpu.roll(small_in[...], lax.rem(width - device * share, width), 1)
    router[...] = turned[:experts, :share]
    first[...] = turned[experts : experts + 1, :share]
    second[...] = turned[experts + 1 : experts + 2, :share]
    bias[...] = turned[experts + 2 : experts + 3, : bias.shape[1]]
    for copy in stores[count:]:
        copy.start()
    for load, store in zip(loads, stores):
        load.wait()
        store.start()
    for copy in stores:
        copy.wait()


def publish(experts, small, bias_share, *values):
    count = len(values)
    share = small.shape[1] // 32
    shapes = ((experts, share), (1, share), (1, share), (1, bias_share))
    return call(
        functools.partial(publish_kernel, experts),
        tuple(jax.ShapeDtypeStruct(shape, F32) for shape in shapes)
        + tuple(jax.ShapeDtypeStruct(value.shape, value.dtype) for value in values),
        [pltpu.VMEM(value.shape, value.dtype) for value in values]
        + [pltpu.VMEM(small.shape, F32)]
        + [pltpu.VMEM(shape, F32) for shape in shapes]
        + [DMA((count,)), DMA((count,)), DMA((5,))],
        60 * MB,
        0,
        small,
        *values,
        stay=tuple(range(count + 1)),
        land=tuple(range(count + 4)),
    )


READY = 2


def on_device(
    fast,
    tokens,
    cotangent,
    qkv_weight,
    out_weight,
    router_weight,
    first_gain,
    second_gain,
    bias_table,
    gate_weight,
    up_weight,
    down_weight,
    lengths,
    routes,
    priority,
):
    both = ("dp", "expert")
    slots, width = tokens.shape
    expert_count = lax.axis_size("expert")
    device_count = lax.axis_size("dp") * expert_count
    share, bias_share = first_gain.shape[0], bias_table.shape[0]
    device = lax.axis_index("dp") * expert_count + lax.axis_index("expert")
    own = lax.axis_index("expert").astype(jnp.int32).reshape(1, 1)
    small_rows = -(-(expert_count + 3) // 8) * 8

    def gathered(value, axes, axis=0, tiled=True):
        return lax.all_gather(value, axes, axis=axis, tiled=tiled)

    def scattered(value, axes):
        return lax.psum_scatter(value, axes, scatter_dimension=0, tiled=True).astype(F32)

    def exchanged(value):
        return lax.all_to_all(value, "expert", split_axis=0, concat_axis=0, tiled=True)

    rows_own, hidden = gate_weight.shape[1:]
    if not fast:
        gate_full, up_full, down_full = (
            gathered(value[0], "dp") for value in (gate_weight, up_weight, down_weight)
        )

    lane = np.arange(width)
    flat = lane // share * bias_share + lane % share
    in_table = lane % share < bias_share
    heads = np.arange(HEADS)[:, None] == np.where(in_table, flat // BUCKETS, -1)[None, :]
    heads = jnp.asarray(heads.astype(np.float32), BF16)
    ahead = np.arange(2 * slots)

    def hot(ahead):
        return jnp.asarray(
            np.where(in_table[:, None], diagonal_onehot(ahead)[flat % BUCKETS], 0.0), BF16
        )

    diagonals_hot = hot(np.where(ahead < slots, ahead, ahead - 2 * slots))
    if fast:
        *kept, buffer, scaled, plain, select, gate_column, meta_own, weights, early, down_full = forward(
            READY,
            expert_count,
            tokens,
            heads,
            diagonals_hot,
            lengths,
            cotangent,
            routes.T,
            priority,
            router_weight.T,
            first_gain[None],
            second_gain[None],
            bias_table[None],
            qkv_weight,
            out_weight,
            gate_weight[0],
            up_weight[0],
            down_weight[0],
        )
        out_full = weights
    else:
        beside = jnp.concatenate(
            [
                router_weight,
                first_gain[:, None],
                second_gain[:, None],
                jnp.pad(bias_table, (0, share - bias_share))[:, None],
                jnp.zeros((share, 128 - expert_count - 3), BF16),
            ],
            axis=1,
        )
        valid_rows = jnp.arange(slots, dtype=jnp.int32) < lengths[0, 0]
        meta_own = jnp.concatenate(
            [
                routes.T,
                priority,
                valid_rows.astype(jnp.int32)[None, :],
                jnp.zeros((4, slots), jnp.int32),
            ],
            axis=0,
        )
        weights = gathered(jnp.concatenate([qkv_weight, beside], axis=1), both)
        out_full = gathered(out_weight, both)
        kept = attention_forward(
            expert_count, tokens, weights, out_full, heads, diagonals_hot, lengths
        )
        rows, cots, meta = (
            gathered(value, "expert", tiled=False) for value in (kept[4], cotangent, meta_own)
        )
        buffer, scaled, plain, select, gate_column = dispatch(rows, cots, meta, kept[5], own)
    qkv, attended, probs, resid, normed_two, small = kept
    if fast:
        grad_gate, grad_up, grad_down, mixed, returned, inner_rows = sweep(
            READY,
            buffer,
            scaled,
            plain,
            gate_column,
            select,
            gate_weight[0],
            up_weight[0],
            early,
            down_full,
        )
    else:
        expert_out, grad_buffer, inner, *grad_experts = experts(
            buffer, scaled, plain, gate_full, up_full, down_full
        )
        mixed, returned, inner_rows = (
            exchanged(value)
            for value in give_back(select, expert_out, grad_buffer, inner, gate_column)
        )
        grad_gate, grad_up, grad_down = (scattered(value, "dp")[None] for value in grad_experts)
    layer = (
        tokens,
        cotangent,
        weights,
        out_full,
        small,
        heads,
        hot(ahead - (slots - 1)),
        lengths,
        meta_own,
        own,
        returned,
        inner_rows,
        qkv,
        attended,
        probs,
        resid,
        normed_two,
        mixed,
    )
    if fast:
        output, grad_tokens, grad_qkv, grad_out, grad_small, grad_down = backward(
            expert_count, *layer, grad_down
        )
        grad_router, grad_first, grad_second, grad_bias, *large = publish(
            expert_count,
            grad_small,
            bias_share,
            output,
            grad_tokens,
            grad_qkv,
            grad_out,
            grad_gate,
            grad_up,
            grad_down,
        )
        output, grad_tokens, grad_qkv, grad_out, grad_gate, grad_up, grad_down = large
        grad_gate, grad_up, grad_down = grad_gate[None], grad_up[None], grad_down[None]
    else:
        output, grad_tokens, grad_small, *grad_weights = local_backward(expert_count, *layer)
        grad_out, *halves = (scattered(value, both) for value in grad_weights)
        grad_qkv = jnp.stack([half.reshape(share, 3, width // 2) for half in halves], axis=2)
        grad_qkv = grad_qkv.reshape(share, 3 * width)
        grad_small = lax.psum(grad_small, both)
        grad_small = lax.dynamic_slice(grad_small, (0, device * share), (small_rows, share))
        grad_router, grad_first, grad_second, grad_bias = (
            grad_small[:expert_count],
            grad_small[expert_count : expert_count + 1],
            grad_small[expert_count + 1 : expert_count + 2],
            grad_small[expert_count + 2 : expert_count + 3, :bias_share],
        )
    return (
        output,
        grad_tokens,
        grad_qkv,
        grad_out,
        grad_router.T,
        grad_first[0],
        grad_second[0],
        grad_bias[0],
        grad_gate,
        grad_up,
        grad_down,
    )


def solution(mesh):
    fast = dict(mesh.shape) == {"dp": 8, "expert": 4}
    rows = P(("dp", "expert"), None)
    flat = P(("dp", "expert"))
    expert = P("expert", "dp", None)
    grid = P("dp", "expert")
    return jax.shard_map(
        functools.partial(on_device, fast),
        mesh=mesh,
        in_specs=(rows,) * 5 + (flat,) * 3 + (expert,) * 3 + (grid, rows, grid),
        out_specs=(rows,) * 5 + (flat,) * 3 + (expert,) * 3,
        check_vma=False,
    )
```

```python
import functools
import math

import jax
import jax.numpy as jnp
import numpy as np
from jax import lax
from jax.experimental import pallas as pl
from jax.experimental.pallas import tpu as pltpu
from jax.sharding import PartitionSpec as P

HEADS = 16
HD = 64
BUCKETS = 32
CAP = 480
PAIRS = HEADS // 2
LANES = 2 * HD
PARTS = 4
CHUNK = 256
TILE = 2 * CHUNK

epsilon = 1e-06
masked_value = -1e30
max_distance = 128.0
SCALE = 1.0 / math.sqrt(HD)
MB = 1 << 20
F32 = jnp.float32
BF16 = jnp.bfloat16


def bucket_of(offset, bucket_count):
    halfway = bucket_count // 2
    exact_span = bucket_count // 4
    distance = np.abs(offset)
    log_part = np.log(np.maximum(distance, 1) / float(exact_span)) / np.log(
        max_distance / exact_span
    )
    far_bucket = np.minimum(
        exact_span + np.floor(log_part * exact_span).astype(np.int64), halfway - 1
    )
    inside = np.where(distance < exact_span, distance, far_bucket)
    return np.where(offset < 0, halfway, 0) + inside


def diagonal_onehot(ahead):
    return (bucket_of(-ahead, BUCKETS)[None, :] == np.arange(BUCKETS)[:, None]).astype(np.float32)


def dot(a, b):
    return jnp.dot(a, b, preferred_element_type=F32)


def dot_nt(a, b):
    return lax.dot_general(a, b, (((1,), (1,)), ((), ())), preferred_element_type=F32)


def dot_tn(a, b):
    return lax.dot_general(a, b, (((0,), (0,)), ((), ())), preferred_element_type=F32)


def two_halves(value):
    high = value.astype(BF16)
    return high, (value - high.astype(F32)).astype(BF16)


def columns(index, width):
    return pl.ds(pl.multiple_of(index * width, width), width)


VMEM_SPEC = pl.BlockSpec(memory_space=pltpu.VMEM)


ANY_SPEC = pl.BlockSpec(memory_space=pl.ANY)
MESH = pl.DeviceIdType.MESH
DMA = pltpu.SemaphoreType.DMA


def call(kernel, out_shape, scratch, vmem, flops, *args, stay=(), land=(), link=None, aliases=None):
    nbytes = sum(a.size * a.dtype.itemsize for a in args)
    params = dict(vmem_limit_bytes=vmem)
    if link is not None:
        params.update(collective_id=link, has_side_effects=True)
    return pl.pallas_call(
        kernel,
        out_shape=out_shape,
        in_specs=[ANY_SPEC if i in stay else VMEM_SPEC for i in range(len(args))],
        out_specs=tuple(ANY_SPEC if i in land else VMEM_SPEC for i in range(len(out_shape))),
        scratch_shapes=scratch,
        input_output_aliases=aliases or {},
        compiler_params=pltpu.CompilerParams(**params),
        cost_estimate=pl.CostEstimate(flops=flops, bytes_accessed=nbytes, transcendentals=0),
    )(*args)


def here():
    d, e = lax.axis_index("dp"), lax.axis_index("expert")
    return d, e, d // 2, lax.rem(d, 2)


def flipped(value, bits):
    low, high = lax.rem(value, 2), value // 2
    low = 1 - low if bits & 1 else low
    high = 1 - high if bits & 2 else high
    return 2 * high + low


def meet(partners):
    barrier = pltpu.get_barrier_semaphore()
    for partner in partners:
        pl.semaphore_signal(barrier, inc=1, device_id=partner, device_id_type=MESH)
    pl.semaphore_wait(barrier, len(partners))


def push(src, dst, send, recv, to):
    copy = pltpu.make_async_remote_copy(
        src_ref=src, dst_ref=dst, send_sem=send, recv_sem=recv, device_id=to, device_id_type=MESH
    )
    copy.start()
    return copy


def group(d, e):
    return [None] + [(d, flipped(e, q)) for q in (1, 2, 3)]


class Spread:
    def __init__(self, src, dst, send, recv, d, e):
        self.src, self.dst, self.send, self.recv = src, dst, send, recv
        self.to = group(d, e)
        self.half = src.shape[0] // 2
        self.copies = {}

    def part(self, ref, half):
        return ref.at[pl.ds(half * self.half, self.half)]

    def start(self):
        for turn in range(2):
            for q in (1, 2):
                half = turn if q == 1 else 1 - turn
                at = 2 * (q - 1) + half
                self.copies[q, half] = push(
                    self.part(self.src, half),
                    self.part(self.dst.at[q], half),
                    self.send.at[at],
                    self.recv.at[at],
                    self.to[q],
                )

    def forward(self):
        for q, half, across, at in ((1, 0, 2, 4), (2, 1, 1, 5)):
            self.copies[q, half].wait_recv()
            self.copies[3, half] = push(
                self.part(self.dst.at[q], half),
                self.part(self.dst.at[3], half),
                self.send.at[at],
                self.recv.at[at],
                self.to[across],
            )

    def arrived(self, q):
        for half in {1: (1,), 2: (0,), 3: (0, 1)}[q]:
            self.copies[q, half].wait_recv()

    def sent(self):
        for copy in self.copies.values():
            copy.wait_send()

    def finish(self):
        for q in (1, 2, 3):
            self.arrived(q)
        self.sent()


class Swap:
    def __init__(self, src, dst, send, recv, d, e):
        self.src, self.dst, self.send, self.recv = src, dst, send, recv
        self.to = group(d, e)
        self.copies = {}

    def start(self, q):
        self.copies[q] = push(
            self.src.at[q], self.dst.at[q], self.send.at[q], self.recv.at[q], self.to[q]
        )

    def finish(self):
        for copy in self.copies.values():
            copy.wait_recv()
        for copy in self.copies.values():
            copy.wait_send()


class DeviceGather:
    WAYS = 5

    def __init__(self, full, share, send, recv):
        self.full, self.share, self.send, self.recv = full, share, send, recv
        self.d, self.e, self.z, self.core = d, e, z, c = here()
        self.to_x, self.to_y = (d, flipped(e, 1)), (d, flipped(e, 2))
        self.other = (2 * z + 1 - c, e)
        self.to_z = [None] + [(2 * flipped(z, k) + c, e) for k in (1, 2, 3)]
        self.end = jnp.logical_or(z == 0, z == 3)
        self.middle = jnp.logical_not(self.end)

    def item(self, k, q, core=None):
        device = 2 * flipped(self.z, k) + (self.core if core is None else core)
        row = (device * 4 + flipped(self.e, q)) * self.share
        return self.full.at[pl.ds(pl.multiple_of(row, self.share), self.share)]

    def pass_on(self, k, q, way, at, to, into=None):
        piece = self.item(k, q)
        return pltpu.make_async_remote_copy(
            src_ref=piece,
            dst_ref=piece,
            send_sem=self.send.at[way, at],
            recv_sem=self.recv.at[way, at if into is None else into],
            device_id=to,
            device_id_type=MESH,
        )

    def along_z(self, k):
        return self.pass_on(0, 0, 0, k, self.to_z[k])

    def relay_z(self, k):
        return self.pass_on(k, 0, 0, 2 + k, self.to_z[1], 5 - k)

    def along_x(self, k):
        return self.pass_on(k, 0, 1, k, self.to_x)

    def along_y(self, k):
        return self.pass_on(k, 0, 2, k, self.to_y)

    def across(self, k):
        return self.pass_on(k, 1, 3, k, self.to_y) if k % 2 == 0 else self.pass_on(k, 2, 3, k, self.to_x)

    def over(self, k, q):
        return self.pass_on(k, q, 4, 4 * q + k, self.other)

    def start(self):
        self.along_z(1).start()

        @pl.when(self.middle)
        def _():
            self.along_z(3).start()

        @pl.when(self.end)
        def _():
            self.along_z(2).start()

    def spread_out(self, k):
        self.along_x(k).start()
        self.along_y(k).start()
        self.over(k, 0).start()

    def from_z(self, k):
        self.along_z(k).wait_recv()
        if k > 1:

            @pl.when(self.middle)
            def _():
                self.relay_z(k).start()

        self.spread_out(k)

    def from_neighbours(self, k):
        self.along_x(k).wait_recv()
        if k % 2 == 0:
            self.across(k).start()
        self.over(k, 1).start()
        self.along_y(k).wait_recv()
        if k % 2 == 1:
            self.across(k).start()
        self.over(k, 2).start()

    def from_across(self, k):
        self.across(k).wait_recv()
        self.over(k, 3).start()

    def complete(self):
        for q in range(4):
            for k in range(4):
                self.over(k, q).wait_recv()

    def settle(self):
        self.along_z(1).wait_send()

        @pl.when(self.middle)
        def _():
            self.along_z(3).wait_send()
            self.relay_z(2).wait_send()
            self.relay_z(3).wait_send()

        @pl.when(self.end)
        def _():
            self.along_z(2).wait_send()

        for k in range(4):
            self.along_x(k).wait_send()
            self.along_y(k).wait_send()
            self.across(k).wait_send()
            for q in range(4):
                self.over(k, q).wait_send()


class LineSum:
    def __init__(self, count, source, scratch, load):
        self.count, self.source, self.load_first = count, source, load
        scratch = list(scratch)
        self.theirs, self.landed, self.send, self.recv = scratch[:4]
        if load:
            self.loads, self.loaded = scratch[4:]
        self.d, self.e, self.z, self.core = here()
        self.other = (2 * self.z + 1 - self.core, self.e)
        self.to = [None] + [(2 * flipped(self.z, k) + self.core, self.e) for k in (1, 2, 3)]
        self.end = jnp.logical_or(self.z == 0, self.z == 3)
        self.middle = jnp.logical_not(self.end)

    @staticmethod
    def scratch(count, rows, width, load):
        part = (rows, width)
        parts = [
            pltpu.VMEM((count, 4) + part, BF16),
            pltpu.VMEM((count, 5) + part, BF16),
            DMA((count, 3, 5)),
            DMA((count, 3, 5)),
        ]
        return parts + ([pltpu.VMEM((count, 4) + part, BF16), DMA((count, 4))] if load else [])

    def remote(self, i, src, dst, stage, out, into, to):
        return pltpu.make_async_remote_copy(
            src_ref=src,
            dst_ref=dst,
            send_sem=self.send.at[i, stage, out],
            recv_sem=self.recv.at[i, stage, into],
            device_id=to,
            device_id_type=MESH,
        )

    def load(self, i, k):
        return pltpu.make_async_copy(
            self.source(i, k, self.core), self.loads.at[i, k], self.loaded.at[i, k]
        )

    def swap(self, i, k):
        src = self.source(i, k, 1 - self.core)
        return self.remote(i, src, self.theirs.at[i, k], 0, k, k, self.other)

    def hand(self, i, k):
        at = 1 if k == 1 else 5 - k
        return self.remote(i, self.theirs.at[i, k], self.landed.at[i, at], 1, k, at, self.to[1])

    def handed(self, i, at):
        return self.remote(i, self.theirs.at[i, at], self.landed.at[i, at], 1, at, at, self.to[1])

    def deliver(self, i, k):
        at = 0 if k == 3 else 4
        return self.remote(i, self.theirs.at[i, k], self.landed.at[i, at], 2, k, at, self.to[3])

    def for_partner(self, i):
        return self.remote(i, self.theirs.at[i, 0], self.landed.at[i, 4], 2, 4, 4, self.to[3])

    def last(self, i):
        return self.remote(i, self.theirs.at[i, 1], self.landed.at[i, 0], 2, 0, 0, self.to[1])

    def add(self, i, k, more):
        self.theirs[i, k] = (self.theirs[i, k].astype(F32) + more[...].astype(F32)).astype(BF16)

    def begin(self, i):
        for k in (3, 2, 1, 0):
            self.swap(i, k).start()
            if self.load_first:
                self.load(i, k).start()

    def halve(self, i):
        for k in (3, 2, 1, 0):
            if self.load_first:
                self.load(i, k).wait()
            self.swap(i, k).wait_recv()
            self.add(i, k, self.loads.at[i, k] if self.load_first else self.source(i, k, self.core))
        self.hand_over(i)

    def hand_over(self, i):
        @pl.when(self.end)
        def _():
            for k in (3, 2, 1):
                self.hand(i, k).start()

    def relay(self, i):
        @pl.when(self.middle)
        def _():
            for k in (2, 3):
                self.handed(i, k).wait_recv()
                self.add(i, k, self.landed.at[i, k])
                self.deliver(i, k).start()

    def pass_on(self, i):
        @pl.when(self.middle)
        def _():
            self.for_partner(i).wait_recv()
            self.add(i, 1, self.landed.at[i, 4])
            self.last(i).start()

    def finish(self, i, out):
        self.last(i).wait_recv()
        out[...] = self.theirs[i, 0].astype(F32) + self.landed[i, 0].astype(F32)
        if self.source is not None:
            for k in range(4):
                self.swap(i, k).wait_send()

        @pl.when(self.end)
        def _():
            for k in (3, 2, 1):
                self.hand(i, k).wait_send()

        @pl.when(self.middle)
        def _():
            self.handed(i, 1).wait_recv()
            out[...] += self.landed[i, 1].astype(F32)
            self.deliver(i, 2).wait_send()
            self.deliver(i, 3).wait_send()
            self.last(i).wait_send()


class LineSpread:
    def __init__(self, halves, place, scratch):
        self.halves, self.place = halves, place
        self.copied, self.send, self.recv = scratch
        self.d, self.e, self.z, self.core = here()
        self.other = (2 * self.z + 1 - self.core, self.e)
        self.to = [None] + [(2 * flipped(self.z, k) + self.core, self.e) for k in (1, 2, 3)]
        self.end = jnp.logical_or(self.z == 0, self.z == 3)
        self.middle = jnp.logical_not(self.end)

    @staticmethod
    def scratch(count):
        return [DMA((count,)), DMA((count, 9)), DMA((count, 8))]

    def from_chip(self, j, k, core=None):
        return self.place(j, 2 * flipped(self.z, k) + (self.core if core is None else core))

    def remote(self, j, src, dst, out, into, to):
        return pltpu.make_async_remote_copy(
            src_ref=src,
            dst_ref=dst,
            send_sem=self.send.at[j, out],
            recv_sem=self.recv.at[j, into],
            device_id=to,
            device_id_type=MESH,
        )

    def parts(self, j):
        piece, halves = self.place(j, self.d), self.halves(j)
        width = piece.shape[1] // len(halves)
        for i, half in enumerate(halves):
            yield half, piece.at[:, i * width : (i + 1) * width]

    def keep(self, j):
        piece = self.place(j, self.d)
        return pltpu.make_async_copy(piece, piece, self.copied.at[j])

    def first(self, j, way):
        piece = self.place(j, self.d)
        return self.remote(j, piece, piece, *self.way(way))

    def way(self, way):
        return min(way, 2), 4 if way == 0 else way, self.to[way] if way else self.other

    def send_own(self, j, way):
        for src, dst in self.parts(j):
            self.remote(j, src, dst, *self.way(way)).start()

    def share(self, j, k):
        piece = self.from_chip(j, k)
        return self.remote(j, piece, piece, 2 + k, 4 + k, self.other)

    def pass_on(self, j, k):
        piece = self.from_chip(j, k)
        return self.remote(j, piece, piece, 4 + k, 5 - k, self.to[1])

    def arrival(self, j, k):
        piece = self.from_chip(j, k)
        return self.remote(j, piece, piece, k, k, self.to[1])

    def shared(self, j, k):
        piece = self.from_chip(j, k, 1 - self.core)
        return self.remote(j, piece, piece, 4 + k if k else 0, 4 + k, self.other)

    def across(self, j):
        piece = self.from_chip(j, 1)
        return self.remote(j, piece, piece, 8, 2, self.to[3])

    def start(self, j):
        self.send_own(j, 1)

        @pl.when(self.middle)
        def _():
            self.send_own(j, 3)

        self.send_own(j, 0)
        for src, dst in self.parts(j):
            pltpu.make_async_copy(src, dst, self.copied.at[j]).start()

    def relay_near(self, j):
        self.arrival(j, 1).wait_recv()

        @pl.when(self.middle)
        def _():
            self.across(j).start()

        self.share(j, 1).start()

    def relay_far(self, j):
        for k in (3, 2):
            self.arrival(j, k).wait_recv()

            @pl.when(self.middle)
            def _():
                self.pass_on(j, k).start()

            self.share(j, k).start()

    def complete(self, j):
        self.keep(j).wait()
        for k in range(4):
            self.shared(j, k).wait_recv()

    def settle(self, j):
        self.first(j, 0).wait_send()
        self.first(j, 1).wait_send()

        @pl.when(self.middle)
        def _():
            self.first(j, 3).wait_send()
            self.across(j).wait_send()
            self.pass_on(j, 2).wait_send()
            self.pass_on(j, 3).wait_send()

        for k in (1, 2, 3):
            self.share(j, k).wait_send()


def pair_gates(logits, route_zero, route_one):
    experts = logits.shape[0]
    which = lax.broadcasted_iota(jnp.int32, logits.shape, 0)
    zero = jnp.sum(jnp.where(which == route_zero, logits, 0.0), axis=0, keepdims=True)
    one = jnp.sum(jnp.where(which == route_one, logits, 0.0), axis=0, keepdims=True)
    top = jnp.maximum(zero, one)
    zero, one = jnp.exp(zero - top), jnp.exp(one - top)
    total = zero + one
    return zero / total, one / total


class Dispatch:
    def __init__(self, expert, meta, rank, places):
        self.expert, self.meta, self.rank, self.places = expert, meta, rank, places
        self.blocks, _, self.slots = meta.shape

    def names(self, block):
        info = self.meta[block]
        valid = info[3:4, :] > 0
        zero = jnp.logical_and(valid, info[0:1, :] == self.expert)
        one = jnp.logical_and(valid, info[1:2, :] == self.expert)
        return info, zero, one

    def find_places(self):
        row_of = lax.broadcasted_iota(jnp.int32, (16, self.slots), 0)
        total_zero = jnp.zeros((1, 1), F32)
        for block in range(self.blocks):
            _, zero, _ = self.names(block)
            total_zero = total_zero + jnp.sum(zero.astype(F32), axis=1, keepdims=True)
            self.rank[block] = jnp.transpose(self.meta[block].astype(F32))

        def block_places(block, _):
            info, zero, one = self.names(block)
            mine = info[2:3, :].astype(F32)

            def earlier(other, counts):
                _, other_zero, other_one = self.names(other)
                marks = jnp.where(row_of == 0, other_zero.astype(F32), 0.0) + jnp.where(
                    row_of == 1, other_one.astype(F32), 0.0
                )
                before = (self.rank[other][:, 2:3] < mine).astype(F32).astype(BF16)
                return counts + dot(marks.astype(BF16), before)

            counts = lax.fori_loop(0, self.blocks, earlier, jnp.zeros((16, self.slots), F32))
            place = jnp.where(
                zero, counts[0:1, :], jnp.where(one, counts[1:2, :] + total_zero, -1.0)
            ).astype(jnp.int32)
            self.places[block] = jnp.broadcast_to(place, self.places.shape[1:])
            return 0

        lax.fori_loop(0, self.blocks, block_places, 0)

    def hot(self, block):
        return lax.broadcasted_iota(jnp.int32, (CAP, self.slots), 0) == self.places[block][0:1, :]

    def gates(self, block, rows, router_t):
        info, zero, one = self.names(block)
        gate_zero, gate_one = pair_gates(dot_nt(router_t, rows), info[0:1, :], info[1:2, :])
        gate = jnp.where(zero, gate_zero, jnp.where(one, gate_one, 0.0))
        return jnp.sum(jnp.where(self.hot(block), gate, 0.0), axis=1, keepdims=True)


def attend_forward(experts, tokens, weights, out_weight, heads, hot, length, out, between):
    qkv, attended, probs, resid, normed_two, small, normed, diagonals = out
    slots, width = tokens.shape
    small[...] = jnp.transpose(weights[:, 3 * width :].astype(F32))[: small.shape[0], :]
    x = tokens[...].astype(F32)
    inv_one = lax.rsqrt(jnp.mean(x * x, axis=1, keepdims=True) + epsilon)
    normed[...] = (x * inv_one * small[experts : experts + 1, :]).astype(BF16)
    spread_bias = heads[...].astype(F32) * small[experts + 2 : experts + 3, :]
    diagonals[...] = dot(spread_bias.astype(BF16), hot[...])

    @pl.loop(0, 3 * width // 512)
    def _(j):
        qkv[:, columns(j, 512)] = dot(normed[...], weights[:, columns(j, 512)]).astype(BF16)

    lane = lax.broadcasted_iota(jnp.int32, (slots, LANES), 1)
    first = lane < HD
    live = lax.broadcasted_iota(jnp.int32, (slots, slots), 1) < length[0, 0]

    def attend(pair):
        q = qkv[:, columns(pair, LANES)]
        k = qkv[:, columns(PAIRS + pair, LANES)]
        v = qkv[:, columns(2 * PAIRS + pair, LANES)]
        outs = []
        for half in range(2):
            head = 2 * pair + half
            own = first if half == 0 else jnp.logical_not(first)
            row = jnp.broadcast_to(diagonals[pl.ds(head, 1), :], (slots, 2 * slots))
            bias = pltpu.roll(row, 0, 1, stride=1, stride_axis=0)[:, :slots]
            scores = dot_nt(jnp.where(own, q, jnp.zeros_like(q)), k) * SCALE + bias
            scores = jnp.where(live, scores, masked_value)
            exponent = jnp.exp(scores - jnp.max(scores, axis=1, keepdims=True))
            low = (exponent / jnp.sum(exponent, axis=1, keepdims=True)).astype(BF16)
            probs[head] = low
            outs.append(dot(low, v))
        attended[:, columns(pair, LANES)] = jnp.where(first, outs[0], outs[1]).astype(BF16)

    for part in range(PARTS):
        pl.loop(part * PAIRS // PARTS, (part + 1) * PAIRS // PARTS)(attend)
        between(part)

    @pl.loop(0, width // 512)
    def _(j):
        resid[:, columns(j, 512)] = tokens[:, columns(j, 512)].astype(F32) + dot(
            attended[...], out_weight[:, columns(j, 512)]
        )

    r = resid[...]
    inv_two = lax.rsqrt(jnp.mean(r * r, axis=1, keepdims=True) + epsilon)
    normed_two[...] = (r * inv_two * small[experts + 1 : experts + 2, :]).astype(BF16)


def attention_forward_kernel(
    experts,
    tokens,
    weights,
    out_weight,
    heads,
    hot,
    length,
    qkv,
    attended,
    probs,
    resid,
    normed_two,
    small,
    *scratch,
):
    out = (qkv, attended, probs, resid, normed_two, small) + scratch
    attend_forward(
        experts, tokens, weights, out_weight, heads, hot, length, out, lambda part: None
    )


def attention_shapes(experts, tokens):
    slots, width = tokens.shape
    return (
        jax.ShapeDtypeStruct((slots, 3 * width), BF16),
        jax.ShapeDtypeStruct((slots, width), BF16),
        jax.ShapeDtypeStruct((HEADS, slots, slots), BF16),
        jax.ShapeDtypeStruct((slots, width), F32),
        jax.ShapeDtypeStruct((slots, width), BF16),
        jax.ShapeDtypeStruct((-(-(experts + 3) // 8) * 8, width), F32),
    )


def attention_forward(experts, tokens, weights, out_weight, heads, hot, length):
    slots, width = tokens.shape
    return call(
        functools.partial(attention_forward_kernel, experts),
        attention_shapes(experts, tokens),
        [pltpu.VMEM((slots, width), BF16), pltpu.VMEM((HEADS, 2 * slots), F32)],
        48 * MB,
        2 * slots * width * (4 * width + 2 * slots),
        tokens,
        weights,
        out_weight,
        heads,
        hot,
        length,
    )


def dispatch_kernel(
    rows, cots, meta, small, own, buffer, scaled, plain, select, gate_column, acc, acc_cot, rank, places
):
    work = Dispatch(own[0, 0], meta, rank, places)
    work.find_places()
    acc[...] = jnp.zeros_like(acc)
    acc_cot[...] = jnp.zeros_like(acc_cot)
    gate_column[...] = jnp.zeros_like(gate_column)
    router_t = small[...].astype(BF16)
    for block in range(work.blocks):
        picked = work.hot(block).astype(F32).astype(BF16)
        select[block] = picked
        gate_column[...] += work.gates(block, rows[block], router_t)
        acc[...] += dot(picked, rows[block])
        acc_cot[...] += dot(picked, cots[block])
    buffer[...] = acc[...].astype(BF16)
    plain[...] = acc_cot[...].astype(BF16)
    scaled[...] = (acc_cot[...] * gate_column[:, 0:1]).astype(BF16)


def dispatch_shapes(blocks, slots, width):
    return (
        jax.ShapeDtypeStruct((CAP, width), BF16),
        jax.ShapeDtypeStruct((CAP, width), BF16),
        jax.ShapeDtypeStruct((CAP, width), BF16),
        jax.ShapeDtypeStruct((blocks, CAP, slots), BF16),
        jax.ShapeDtypeStruct((CAP, 128), F32),
    )


def dispatch_scratch(blocks, slots, width):
    return [
        pltpu.VMEM((CAP, width), F32),
        pltpu.VMEM((CAP, width), F32),
        pltpu.VMEM((blocks, slots, 8), F32),
        pltpu.VMEM((blocks, 8, slots), jnp.int32),
    ]


def dispatch(rows, cots, meta, small, own):
    blocks, slots, width = rows.shape
    return call(
        dispatch_kernel,
        dispatch_shapes(blocks, slots, width),
        dispatch_scratch(blocks, slots, width),
        60 * MB,
        4 * CAP * blocks * slots * width,
        rows,
        cots,
        meta,
        small,
        own,
    )


def forward_kernel(
    experts,
    tokens,
    heads,
    hot,
    length,
    cotangent,
    routes,
    priority,
    router,
    first_gain,
    second_gain,
    bias,
    qkv_own,
    out_own,
    gate_own,
    up_own,
    down_own,
    qkv_kept,
    attended_kept,
    probs_kept,
    resid_kept,
    normed_kept,
    small,
    buffer,
    scaled,
    plain_kept,
    select_kept,
    gate_column,
    meta,
    kept,
    early_kept,
    down_kept,
    early,
    down,
    acc,
    acc_cot,
    rank,
    places,
    weights,
    rows,
    cots,
    metas,
    normed,
    diagonals,
    local,
    send,
    recv,
    gather_send,
    gather_recv,
    piece_stored,
    own_small,
    qkv,
    attended,
    probs,
    resid,
    normed_two,
    plain,
    select,
    result_stored,
    *scratch,
):
    d, e, z, c = here()
    slots, width = tokens.shape
    share = qkv_own.shape[0]
    gather = DeviceGather(weights, share, gather_send, gather_recv)
    rows_spread = Spread(normed_two, rows, send.at[0], recv.at[0], d, e)
    cots_spread = Spread(cotangent, cots, send.at[1], recv.at[1], d, e)
    work = Dispatch(e, metas, rank, places)
    tile_share, down_share = gate_own.shape[0], down_own.shape[0]
    tile_spread = LineSpread(
        lambda j: [own.at[:, j * CHUNK : (j + 1) * CHUNK] for own in (gate_own, up_own)],
        lambda j, device: early.at[
            j, pl.ds(pl.multiple_of(device * tile_share, tile_share), tile_share)
        ],
        scratch[:3],
    )
    down_spread = LineSpread(
        lambda j: [down_own.at[:, j * CHUNK : (j + 1) * CHUNK]],
        lambda j, device: down.at[
            pl.ds(pl.multiple_of(device * down_share, down_share), down_share),
            j * CHUNK : (j + 1) * CHUNK,
        ],
        scratch[3:],
    )
    pieces = [(tile_spread, j) for j in range(early.shape[0])]
    pieces += [(down_spread, j) for j in range(width // CHUNK)]

    def near(i):
        if 0 <= i < len(pieces):
            pieces[i][0].relay_near(pieces[i][1])

    def far(i):
        if 0 <= i < len(pieces):
            pieces[i][0].relay_far(pieces[i][1])
        begin(i + AHEAD)

    def begin(i):
        if i < len(pieces):
            pieces[i][0].start(pieces[i][1])

    def store(i):
        spread, j = pieces[i]
        if spread is tile_spread:
            src, dst = early.at[j], early_kept.at[j]
        else:
            at = slice(j * CHUNK, (j + 1) * CHUNK)
            src, dst = down.at[:, at], down_kept.at[:, at]
        return pltpu.make_async_copy(src, dst, piece_stored.at[i])

    cut = weights.shape[1] - width
    mine = gather.item(0, 0)
    own_parts = [
        pltpu.make_async_copy(qkv_own, mine.at[:, : 3 * width], local.at[0]),
        pltpu.make_async_copy(out_own, mine.at[:, cut:], local.at[1]),
    ]
    own_cots = pltpu.make_async_copy(cotangent, cots.at[0], local.at[3])
    for copy in own_parts:
        copy.start()
    meta[0:2, :] = routes[...]
    meta[2:3, :] = priority[...]
    slot = lax.broadcasted_iota(jnp.int32, (1, slots), 1)
    meta[3:4, :] = (slot < length[0, 0]).astype(jnp.int32)
    meta[4:8, :] = jnp.zeros((4, slots), jnp.int32)
    own_small[...] = jnp.zeros_like(own_small)
    row = 0
    for part in (router, first_gain, second_gain, bias):
        own_small[row : row + part.shape[0], : part.shape[1]] = part[...].astype(F32)
        row += part.shape[0]
    mine[:, 3 * width : cut] = jnp.zeros((share, cut - 3 * width), BF16)
    mine[:, 3 * width : 3 * width + own_small.shape[0]] = jnp.transpose(own_small[...])[
        :share, :
    ].astype(BF16)
    meet(group(d, e)[1:] + [gather.other] + gather.to_z[1:])
    meta_copies = [
        push(meta, metas.at[q], send.at[2, q], recv.at[2, q], group(d, e)[q]) for q in (1, 2, 3)
    ]
    for copy in own_parts:
        copy.wait()
    gather.start()
    gather.spread_out(0)
    own_cots.start()
    metas[0] = meta[...]
    for copy in meta_copies:
        copy.wait_recv()
    work.find_places()
    gather.from_z(1)
    gather.from_neighbours(0)
    gather.from_z(3)
    gather.from_z(2)
    for i in range(AHEAD):
        begin(i)
    gather.from_neighbours(1)
    near(0)
    gather.from_neighbours(3)
    near(1)
    far(0)
    gather.from_neighbours(2)
    cots_spread.start()
    far(1)
    for k in (0, 1, 3, 2):
        gather.from_across(k)
    near(2)
    gather.complete()
    far(2)
    keep = pltpu.make_async_copy(weights, kept, local.at[4])
    keep.start()

    def between(part):
        if part == 0:
            near(3)
        elif part == 1:
            cots_spread.forward()
            far(3)
        elif part == 2:
            near(4)
        else:
            far(4)

    out = (qkv, attended, probs, resid, normed_two, small, normed, diagonals)
    projections, out_weight = weights.at[:, :cut], weights.at[:, cut:]
    attend_forward(experts, tokens, projections, out_weight, heads, hot, length, out, between)

    rows_spread.start()
    results = [
        pltpu.make_async_copy(src, dst, result_stored.at[i])
        for i, (src, dst) in enumerate(
            (
                (qkv, qkv_kept),
                (attended, attended_kept),
                (probs, probs_kept),
                (resid, resid_kept),
                (normed_two, normed_kept),
            )
        )
    ]
    for copy in results:
        copy.start()
    own_cots.wait()
    cots_spread.finish()
    router_t = small[...].astype(BF16)

    def take_cots(block):
        picked = work.hot(block).astype(F32).astype(BF16)
        select[block] = picked
        more = dot(picked, cots[block])
        if block:
            acc_cot[...] += more
        else:
            acc_cot[...] = more

    def take_rows(block, ref):
        gate = work.gates(block, ref[...], router_t)
        more = dot(select[block], ref[...])
        if block:
            gate_column[...] += gate
            acc[...] += more
        else:
            gate_column[...] = jnp.broadcast_to(gate, gate_column.shape)
            acc[...] = more

    take_cots(0)
    take_cots(1)
    rows_spread.forward()
    take_cots(2)
    near(5)
    take_cots(3)
    plain[...] = acc_cot[...].astype(BF16)
    results += [
        pltpu.make_async_copy(plain, plain_kept, result_stored.at[5]),
        pltpu.make_async_copy(select, select_kept, result_stored.at[6]),
    ]
    for copy in results[5:]:
        copy.start()
    take_rows(0, normed_two)
    far(5)
    near(6)
    rows_spread.arrived(1)
    take_rows(1, rows.at[1])
    rows_spread.arrived(2)
    take_rows(2, rows.at[2])
    rows_spread.arrived(3)
    take_rows(3, rows.at[3])
    buffer[...] = acc[...].astype(BF16)
    scaled[...] = (acc_cot[...] * gate_column[:, 0:1]).astype(BF16)
    far(6)
    for i, (spread, j) in enumerate(pieces):
        spread.complete(j)
        store(i).start()
    rows_spread.sent()
    for copy in results:
        copy.wait()
    gather.settle()
    for i, (spread, j) in enumerate(pieces):
        spread.settle(j)
        store(i).wait()
    for copy in meta_copies:
        copy.wait_send()
    keep.wait()


AHEAD = 3


def forward(ready, experts, *args):
    tokens, cotangent, qkv_own, gate_own, down_own = args[0], args[4], args[11], args[13], args[15]
    slots, width = tokens.shape
    full = (32 * qkv_own.shape[0], 4 * width + 128)
    meta = jax.ShapeDtypeStruct((8, slots), jnp.int32)
    block = (experts, slots, width)
    tiles, down_full = (ready, width, TILE), (8 * down_own.shape[0], width)
    pieces = ready + width // CHUNK
    scratch = [pltpu.VMEM(tiles, BF16), pltpu.VMEM(down_full, BF16)]
    scratch += dispatch_scratch(*block) + [
        pltpu.VMEM(full, BF16),
        pltpu.VMEM(block, BF16),
        pltpu.VMEM(block, BF16),
        pltpu.VMEM((experts,) + meta.shape, meta.dtype),
        pltpu.VMEM((slots, width), BF16),
        pltpu.VMEM((HEADS, 2 * slots), F32),
        DMA((5,)),
        DMA((3, 6)),
        DMA((3, 6)),
        DMA((5, 16)),
        DMA((5, 16)),
        DMA((pieces,)),
        pltpu.VMEM((8, 128), F32),
        *[pltpu.VMEM(value.shape, value.dtype) for value in attention_shapes(experts, tokens)[:5]],
        *[pltpu.VMEM(value.shape, value.dtype) for value in dispatch_shapes(*block)[2:4]],
        DMA((7,)),
        *LineSpread.scratch(ready),
        *LineSpread.scratch(width // CHUNK),
    ]
    shapes = attention_shapes(experts, tokens) + dispatch_shapes(*block) + (meta,)
    return call(
        functools.partial(forward_kernel, experts),
        shapes
        + tuple(jax.ShapeDtypeStruct(shape, BF16) for shape in (full, tiles, down_full)),
        scratch,
        62 * MB,
        2 * slots * width * (4 * width + 2 * slots),
        *args,
        stay=(4, 11, 12, 13, 14, 15),
        land=tuple(range(5)) + (8, 9) + tuple(len(shapes) + i for i in range(3)),
        link=0,
    )


GELU_A = math.sqrt(2.0 / math.pi)
GELU_B = 0.044715


def expert_chunk(buffer, scaled, gate, up, down):
    gate_in, up_in = dot(buffer, gate), dot(buffer, up)
    square = gate_in * gate_in
    wave = jnp.tanh(GELU_A * gate_in * (1.0 + GELU_B * square))
    half = 0.5 * (1.0 + wave)
    activated = gate_in * half
    slope = half + (0.5 * GELU_A) * gate_in * (1.0 - wave * wave) * (1.0 + 3.0 * GELU_B * square)
    hidden = (activated * up_in).astype(BF16)
    grad_hidden = dot_nt(scaled, down)
    grad_gate_in = (grad_hidden * up_in * slope).astype(BF16)
    grad_up_in = (grad_hidden * activated).astype(BF16)
    grad_buffer = dot_nt(grad_gate_in, gate) + dot_nt(grad_up_in, up)
    return (
        dot(hidden, down),
        grad_buffer,
        dot_tn(buffer, grad_gate_in),
        dot_tn(buffer, grad_up_in),
        dot_tn(hidden, scaled),
    )


def expert_kernel(
    buffer,
    scaled,
    plain,
    gate,
    up,
    down,
    out,
    grad_buffer,
    inner,
    grad_gate,
    grad_up,
    grad_down,
    acc_out,
    acc_grad,
):
    step = pl.program_id(0)

    @pl.when(step == 0)
    def _():
        acc_out[...] = jnp.zeros_like(acc_out)
        acc_grad[...] = jnp.zeros_like(acc_grad)

    more_out, more_grad, d_gate, d_up, d_down = expert_chunk(
        buffer[...], scaled[...], gate[...], up[...], down[...]
    )
    acc_out[...] += more_out
    acc_grad[...] += more_grad
    grad_gate[...] = d_gate.astype(BF16)
    grad_up[...] = d_up.astype(BF16)
    grad_down[...] = d_down.astype(BF16)

    @pl.when(step == pl.num_programs(0) - 1)
    def _():
        low = acc_out[...].astype(BF16)
        out[...] = low
        grad_buffer[...] = acc_grad[...].astype(BF16)
        inner[...] = jnp.broadcast_to(
            jnp.sum(low.astype(F32) * plain[...].astype(F32), axis=1, keepdims=True), inner.shape
        )


def experts(buffer, scaled, plain, gate, up, down):
    rows, width = buffer.shape
    hidden = gate.shape[1]
    whole = pl.BlockSpec((rows, width), lambda j: (0, 0))
    tall = pl.BlockSpec((width, CHUNK), lambda j: (0, j))
    wide = pl.BlockSpec((CHUNK, width), lambda j: (j, 0))
    shapes = (
        jax.ShapeDtypeStruct((rows, width), BF16),
        jax.ShapeDtypeStruct((rows, width), BF16),
        jax.ShapeDtypeStruct((rows, 128), F32),
        jax.ShapeDtypeStruct((width, hidden), BF16),
        jax.ShapeDtypeStruct((width, hidden), BF16),
        jax.ShapeDtypeStruct((hidden, width), BF16),
    )
    return pl.pallas_call(
        expert_kernel,
        out_shape=shapes,
        grid=(hidden // CHUNK,),
        in_specs=[whole, whole, whole, tall, tall, wide],
        out_specs=(whole, whole, pl.BlockSpec((rows, 128), lambda j: (0, 0)), tall, tall, wide),
        scratch_shapes=[pltpu.VMEM((rows, width), F32), pltpu.VMEM((rows, width), F32)],
        compiler_params=pltpu.CompilerParams(
            vmem_limit_bytes=48 * MB, dimension_semantics=("arbitrary",)
        ),
        cost_estimate=pl.CostEstimate(
            flops=18 * rows * width * hidden,
            bytes_accessed=12 * width * hidden,
            transcendentals=rows * hidden,
        ),
    )(buffer, scaled, plain, gate, up, down)


def give_back_kernel(select, out, grad_buffer, inner, gate_column, mixed, grads, inner_rows):
    weighted = (out[...].astype(F32) * gate_column[:, 0:1]).astype(BF16)
    for block in range(select.shape[0]):
        row = jnp.sum(select[block].astype(F32) * inner[:, 0:1], axis=0, keepdims=True)
        inner_rows[block] = jnp.broadcast_to(row, inner_rows.shape[1:])
        grads[block] = dot_tn(select[block], grad_buffer[...]).astype(BF16)
        mixed[block] = dot_tn(select[block], weighted).astype(BF16)


def give_back(select, out, grad_buffer, inner, gate_column):
    blocks, rows, slots = select.shape
    width = out.shape[1]
    wide = (blocks, slots, width)
    return call(
        give_back_kernel,
        (
            jax.ShapeDtypeStruct(wide, BF16),
            jax.ShapeDtypeStruct(wide, BF16),
            jax.ShapeDtypeStruct((blocks, 8, slots), F32),
        ),
        [],
        56 * MB,
        4 * rows * blocks * slots * width,
        select,
        out,
        grad_buffer,
        inner,
        gate_column,
    )


def sweep_kernel(
    ready,
    buffer,
    scaled,
    plain,
    gate_column,
    select,
    gate_own,
    up_own,
    early,
    down_full,
    gate_sum,
    up_sum,
    grad_down,
    mixed_kept,
    returned,
    inner_full,
    mixed,
    sums,
    both,
    down,
    acc_out,
    acc_grad,
    down_stage,
    grads,
    inner_rows,
    buffer_in,
    scaled_in,
    plain_in,
    column_in,
    select_in,
    fetched,
    loaded,
    stored,
    local,
    swap_send,
    swap_recv,
    *scratch,
):
    tiles, width = both.shape[0], both.shape[1]
    share = gate_own.shape[0]
    coming = tiles - ready
    d, e, z, c = here()

    def rows_of(device):
        return pl.ds(pl.multiple_of(device * share, share), share)

    spread = LineSpread(
        lambda j: [own.at[:, columns(ready + j, CHUNK)] for own in (gate_own, up_own)],
        lambda j, device: both.at[ready + j, rows_of(device)],
        scratch[:3],
    )
    line = LineSum(
        tiles,
        lambda i, k, core: both.at[i, rows_of(2 * flipped(z, k) + core)],
        scratch[3:],
        load=False,
    )
    swap = Swap(grads, returned, swap_send.at[0], swap_recv.at[0], d, e)
    inner_swap = Swap(inner_rows, inner_full, swap_send.at[1], swap_recv.at[1], d, e)
    meet(group(d, e)[1:] + [line.other] + line.to[1:])

    def early_load(t):
        return pltpu.make_async_copy(early.at[t], both.at[t], loaded.at[t])

    for j in range(min(DEPTH, coming)):
        spread.start(j)
    fetches = []
    for i, (src, dst) in enumerate(
        (
            (buffer, buffer_in),
            (scaled, scaled_in),
            (plain, plain_in),
            (gate_column, column_in),
            (select, select_in),
        )
    ):
        fetches.append(pltpu.make_async_copy(src, dst, fetched.at[i]))
        fetches[-1].start()
    buffer, scaled, plain, gate_column, select = buffer_in, scaled_in, plain_in, column_in, select_in
    down_load = pltpu.make_async_copy(down_full, down, loaded.at[tiles])
    for t in range(ready):
        early_load(t).start()
        if t == 0:
            down_load.start()
    acc_out[...] = jnp.zeros_like(acc_out)
    acc_grad[...] = jnp.zeros_like(acc_grad)
    for copy in fetches:
        copy.wait()
    down_load.wait()

    def down_rows(t):
        return pl.ds(pl.multiple_of(t * CHUNK, CHUNK), CHUNK)

    def down_store(t, slot):
        return pltpu.make_async_copy(
            down_stage.at[slot], grad_down.at[down_rows(t)], stored.at[slot]
        )

    def between(low, value, high):
        return jnp.logical_and(value >= low, value < high)

    def tile_step(t, _):
        @pl.when(t < ready)
        def _():
            early_load(t).wait()

        near = t - ready + NEAR

        @pl.when(between(0, near, coming))
        def _():
            spread.relay_near(near)

        @pl.when(between(0, near - 1, coming))
        def _():
            spread.relay_far(near - 1)

        @pl.when(between(DEPTH, near - 1 + DEPTH, coming))
        def _():
            spread.start(near - 1 + DEPTH)

        @pl.when(t >= ready)
        def _():
            spread.complete(t - ready)

        @pl.when(t >= 1)
        def _():
            line.halve(t - 1)

        @pl.when(t >= LAG)
        def _():
            line.relay(t - LAG)

        @pl.when(t >= LAG + 1)
        def _():
            line.pass_on(t - LAG - 1)

        more_out, more_grad, d_gate, d_up, d_down = expert_chunk(
            buffer[...], scaled[...], both[t, :, :CHUNK], both[t, :, CHUNK:], down[down_rows(t)]
        )
        acc_out[...] += more_out
        acc_grad[...] += more_grad

        @pl.when(t >= ready)
        def _():
            spread.settle(t - ready)

        both[t, :, :CHUNK] = d_gate.astype(BF16)
        both[t, :, CHUNK:] = d_up.astype(BF16)
        slot = lax.rem(t, 2)

        @pl.when(t >= 2)
        def _():
            down_store(t - 2, slot).wait()

        down_stage[slot] = d_down.astype(BF16)
        down_store(t, slot).start()
        line.begin(t)
        return 0

    lax.fori_loop(0, tiles, tile_step, 0)

    low = acc_out[...].astype(BF16)
    inner = jnp.sum(low.astype(F32) * plain[...].astype(F32), axis=1, keepdims=True)
    grad_low = acc_grad[...].astype(BF16)
    order = (3, 1, 2, 0)
    for block in order:
        row = jnp.sum(select[block].astype(F32) * inner, axis=0, keepdims=True)
        inner_rows[block] = jnp.broadcast_to(row, inner_rows.shape[1:])
        grads[block] = dot_tn(select[block], grad_low).astype(BF16)
        if block:
            inner_swap.start(block)
            swap.start(block)
    own_copies = [
        pltpu.make_async_copy(grads.at[0], returned.at[0], local.at[0]),
        pltpu.make_async_copy(inner_rows.at[0], inner_full.at[0], local.at[1]),
    ]
    for copy in own_copies:
        copy.start()
    line.halve(tiles - 1)
    weighted = (low.astype(F32) * gate_column[:, 0:1]).astype(BF16)
    for block in order:
        mixed[block] = dot_tn(select[block], weighted).astype(BF16)
    own_copies.append(pltpu.make_async_copy(mixed, mixed_kept, local.at[3]))
    own_copies[-1].start()

    @pl.loop(tiles - LAG, tiles + 1)
    def _(i):
        @pl.when(i < tiles)
        def _():
            line.relay(i)

        line.pass_on(i - 1)

    @pl.loop(0, tiles)
    def _(i):
        line.finish(i, sums.at[i])
        for copy in result_stores(sums.at[i], gate_sum, up_sum, i, local.at[2]):
            copy.start()

    @pl.loop(0, tiles)
    def _(i):
        for copy in result_stores(sums.at[i], gate_sum, up_sum, i, local.at[2]):
            copy.wait()

    for t in range(tiles - 2, tiles):
        down_store(t, t % 2).wait()
    for copy in own_copies:
        copy.wait()
    inner_swap.finish()
    swap.finish()


def result_stores(value, gate_sum, up_sum, tile, sem):
    return [
        pltpu.make_async_copy(
            value.at[:, i * CHUNK : (i + 1) * CHUNK], array.at[:, columns(tile, CHUNK)], sem
        )
        for i, array in enumerate((gate_sum, up_sum))
    ]


LAG = 5

DEPTH = 6
NEAR = 2


def sweep(ready, buffer, scaled, plain, gate_column, select, gate_own, up_own, early, down_full):
    rows, width = buffer.shape
    tiles = gate_own.shape[1] // CHUNK
    share = gate_own.shape[0]
    block = (select.shape[0], select.shape[2], width)
    thin = (select.shape[0], 8, select.shape[2])
    hidden = tiles * CHUNK
    shapes = (
        jax.ShapeDtypeStruct(gate_own.shape, F32),
        jax.ShapeDtypeStruct(gate_own.shape, F32),
        jax.ShapeDtypeStruct(down_full.shape, BF16),
        jax.ShapeDtypeStruct(block, BF16),
        jax.ShapeDtypeStruct(block, BF16),
        jax.ShapeDtypeStruct(thin, F32),
    )
    scratch = [
        pltpu.VMEM(block, BF16),
        pltpu.VMEM((tiles, share, TILE), F32),
        pltpu.VMEM((tiles, width, TILE), BF16),
        pltpu.VMEM(down_full.shape, BF16),
        pltpu.VMEM((rows, width), F32),
        pltpu.VMEM((rows, width), F32),
        pltpu.VMEM((2, CHUNK, width), BF16),
        pltpu.VMEM(block, BF16),
        pltpu.VMEM(thin, F32),
        *[
            pltpu.VMEM(value.shape, value.dtype)
            for value in (buffer, scaled, plain, gate_column, select)
        ],
        DMA((5,)),
        DMA((tiles + 1,)),
        DMA((2,)),
        DMA((4,)),
        DMA((2, 4)),
        DMA((2, 4)),
    ]
    scratch += LineSpread.scratch(tiles - ready) + LineSum.scratch(tiles, share, TILE, False)
    return call(
        functools.partial(sweep_kernel, ready),
        shapes,
        scratch,
        62 * MB,
        18 * rows * width * hidden,
        buffer,
        scaled,
        plain,
        gate_column,
        select,
        gate_own,
        up_own,
        early,
        down_full,
        stay=tuple(range(9)),
        land=tuple(range(6)),
        link=2,
    )


def backward_layer(experts, relative, ins, outs, work, reached):
    tokens, cotangent, weights, out_weight, small, heads, hot_back, length, meta, own = ins[:10]
    returned, inner_rows, qkv, attended, probs, resid, normed_two = ins[10:]
    grad_tokens, grad_small, grad_out, *grad_halves = outs
    grad_attended, grad_qkv, branch, normed, grad_resid, grad_diagonals = work
    slots, width = tokens.shape
    blocks = returned.shape[0]
    router_t = small[...].astype(BF16)
    keep_row = lax.broadcasted_iota(jnp.int32, (slots, 1), 0) < length[0, 0]
    logits = dot_nt(router_t, normed_two[...])
    zero_route, one_route = meta[0:1, :], meta[1:2, :]
    gate_zero, gate_one = pair_gates(logits, zero_route, one_route)
    which = lax.broadcasted_iota(jnp.int32, logits.shape, 0)
    grad_zero = jnp.zeros((1, slots), F32)
    grad_one = jnp.zeros((1, slots), F32)
    for block in range(blocks):
        row = inner_rows[block][0:1, :]
        expert = jnp.bitwise_xor(own[0, 0], block) if relative else block
        grad_zero = grad_zero + jnp.where(zero_route == expert, row, 0.0)
        grad_one = grad_one + jnp.where(one_route == expert, row, 0.0)
    shared = gate_zero * grad_zero + gate_one * grad_one
    grad_zero = gate_zero * (grad_zero - shared)
    grad_one = gate_one * (grad_one - shared)
    grad_logits = jnp.where(which == zero_route, grad_zero, 0.0) + jnp.where(
        which == one_route, grad_one, 0.0
    )
    high, low = two_halves(grad_logits)
    grad_small[...] = dot(high, normed_two[...]) + dot(low, normed_two[...])
    grad_normed_two = dot_tn(high, router_t) + dot_tn(low, router_t)
    for block in range(blocks):
        grad_normed_two = grad_normed_two + returned[block].astype(F32)
    r = resid[...]
    inv_two = lax.rsqrt(jnp.mean(r * r, axis=1, keepdims=True) + epsilon)
    unit_two = r * inv_two
    grad_small[experts + 1 : experts + 2, :] = jnp.sum(
        grad_normed_two * unit_two, axis=0, keepdims=True
    )
    scaled_two = small[experts + 1 : experts + 2, :] * grad_normed_two
    grad_resid[...] = jnp.where(keep_row, cotangent[...].astype(F32), 0.0) + inv_two * (
        scaled_two - unit_two * jnp.mean(scaled_two * unit_two, axis=1, keepdims=True)
    )
    branch[...] = grad_resid[...].astype(BF16)
    reached("branch")

    @pl.loop(0, width // 256)
    def _(j):
        grad_out[:, columns(j, 256)] = dot_tn(attended[...], branch[:, columns(j, 256)]).astype(
            BF16
        )

    reached("out")
    grad_attended[...] = dot_nt(branch[...], out_weight[...]).astype(BF16)
    x = tokens[...].astype(F32)
    inv_one = lax.rsqrt(jnp.mean(x * x, axis=1, keepdims=True) + epsilon)
    normed[...] = (x * inv_one * small[experts : experts + 1, :]).astype(BF16)
    reached("attended")

    lane = lax.broadcasted_iota(jnp.int32, (slots, LANES), 1)
    first = lane < HD
    square = (slots, slots)
    flip = (
        lax.broadcasted_iota(jnp.int32, square, 0) + lax.broadcasted_iota(jnp.int32, square, 1)
        == slots - 1
    )
    flip = flip.astype(F32).astype(BF16)

    def attend_back(pair):
        q = qkv[:, columns(pair, LANES)]
        k = qkv[:, columns(PAIRS + pair, LANES)]
        v = qkv[:, columns(2 * PAIRS + pair, LANES)]
        g = grad_attended[:, columns(pair, LANES)]
        dq, dk, dv = [], [], []
        for half in range(2):
            head = 2 * pair + half
            mine = first if half == 0 else jnp.logical_not(first)
            low = probs[head]
            p = low.astype(F32)
            grad_probs = dot_nt(jnp.where(mine, g, jnp.zeros_like(g)), v)
            ds = p * (grad_probs - jnp.sum(p * grad_probs, axis=1, keepdims=True))
            ds = ds.astype(BF16)
            wide = jnp.concatenate([dot(flip, ds), jnp.zeros((slots, slots), F32)], axis=1)
            skewed = pltpu.roll(wide, 0, 1, stride=1, stride_axis=0)
            grad_diagonals[pl.ds(head, 1), :] = jnp.sum(skewed, axis=0, keepdims=True)
            dq.append(dot(ds, k))
            dk.append(dot_tn(ds, q))
            dv.append(dot_tn(low, g))
        grad_qkv[:, columns(pair, LANES)] = (jnp.where(first, dq[0], dq[1]) * SCALE).astype(BF16)
        grad_qkv[:, columns(PAIRS + pair, LANES)] = (
            jnp.where(first, dk[0], dk[1]) * SCALE
        ).astype(BF16)
        grad_qkv[:, columns(2 * PAIRS + pair, LANES)] = jnp.where(first, dv[0], dv[1]).astype(BF16)

    for part in range(PARTS):
        pl.loop(part * PAIRS // PARTS, (part + 1) * PAIRS // PARTS)(attend_back)
        reached(f"part{part}")
        if part % 2 == 1:
            half, wide = part // 2, width // 2
            for i in range(3):
                for j in range(wide // 256):
                    source = i * width + half * wide + j * 256
                    at = i * wide + j * 256
                    grad_halves[half][:, at : at + 256] = dot_tn(
                        normed[...], grad_qkv[:, source : source + 256]
                    ).astype(BF16)
            reached(f"half{half}")

    high, low = two_halves(grad_diagonals[...])
    by_lane = dot_nt(high, hot_back[...]) + dot_nt(low, hot_back[...])
    grad_small[experts + 2 : experts + 3, :] = jnp.sum(
        by_lane * heads[...].astype(F32), axis=0, keepdims=True
    )
    grad_normed = dot_nt(grad_qkv[...], weights[:, : 3 * width])
    x = tokens[...].astype(F32)
    inv_one = lax.rsqrt(jnp.mean(x * x, axis=1, keepdims=True) + epsilon)
    unit_one = x * inv_one
    grad_small[experts : experts + 1, :] = jnp.sum(grad_normed * unit_one, axis=0, keepdims=True)
    scaled_one = small[experts : experts + 1, :] * grad_normed
    grad_tokens[...] = grad_resid[...] + inv_one * (
        scaled_one - unit_one * jnp.mean(scaled_one * unit_one, axis=1, keepdims=True)
    )
    reached("tokens")


def backward_scratch(slots, width):
    return [
        pltpu.VMEM((slots, width), BF16),
        pltpu.VMEM((slots, 3 * width), BF16),
        pltpu.VMEM((slots, width), BF16),
        pltpu.VMEM((slots, width), BF16),
        pltpu.VMEM((slots, width), F32),
        pltpu.VMEM((HEADS, 2 * slots), F32),
    ]


def add_mixed(output, resid, length, parts):
    keep_row = lax.broadcasted_iota(jnp.int32, (resid.shape[0], 1), 0) < length[0, 0]
    total = resid[...]
    for part in parts:
        total = total + part[...].astype(F32)
    output[...] = jnp.where(keep_row, total, 0.0).astype(BF16)


def local_backward_kernel(experts, *refs):
    ins, mixed, output, outs, work = refs[:17], refs[17], refs[18], refs[19:24], refs[24:]
    backward_layer(experts, False, ins, outs, work, lambda name: None)
    add_mixed(output, ins[15], ins[7], [mixed.at[block] for block in range(mixed.shape[0])])


def local_backward(experts, *args):
    tokens, small = args[0], args[4]
    slots, width = tokens.shape
    return call(
        functools.partial(local_backward_kernel, experts),
        (
            jax.ShapeDtypeStruct((slots, width), BF16),
            jax.ShapeDtypeStruct((slots, width), F32),
            jax.ShapeDtypeStruct(small.shape, F32),
            jax.ShapeDtypeStruct((width, width), BF16),
            jax.ShapeDtypeStruct((width, 3 * width // 2), BF16),
            jax.ShapeDtypeStruct((width, 3 * width // 2), BF16),
        ),
        backward_scratch(slots, width),
        62 * MB,
        4 * slots * width * (4 * width + 2 * slots),
        *args,
    )


class DeviceSum:
    @staticmethod
    def scratch(share, width):
        return [
            pltpu.VMEM((4, 4 * share, width), BF16),
            pltpu.VMEM((4, 2, share, width), BF16),
            pltpu.VMEM((4, share, width), BF16),
            DMA((4, 4)),
            DMA((4, 4)),
        ] + LineSum.scratch(1, share, width, False)

    def __init__(self, partial, scratch):
        self.partial = partial
        self.theirs, self.first_in, self.second_in, self.send, self.recv = scratch[:5]
        self.line = LineSum(1, None, scratch[5:], False)
        self.share = self.second_in.shape[1]
        self.d, self.e, self.z, self.core = here()
        self.other = (2 * self.z + 1 - self.core, self.e)
        self.to_x, self.to_y = (self.d, flipped(self.e, 1)), (self.d, flipped(self.e, 2))

    def rows(self, k, core, start, count):
        row = (2 * flipped(self.z, k) + core) * 4 * self.share + start
        return self.partial.at[pl.ds(pl.multiple_of(row, self.share), count)]

    def piece(self, k, q):
        return self.rows(k, self.core, flipped(self.e, q) * self.share, self.share)

    def remote(self, src, dst, stage, k, to):
        return pltpu.make_async_remote_copy(
            src_ref=src,
            dst_ref=dst,
            send_sem=self.send.at[stage, k],
            recv_sem=self.recv.at[stage, k],
            device_id=to,
            device_id_type=MESH,
        )

    def swap(self, k):
        src = self.rows(k, 1 - self.core, 0, 4 * self.share)
        return self.remote(src, self.theirs.at[k], 0, k, self.other)

    def first(self, k, slot):
        near, to = (1, self.to_x) if k % 2 == 0 else (2, self.to_y)
        return self.remote(
            self.piece(k, 3 if slot else near), self.first_in.at[k, slot], 1 + slot, k, to
        )

    def far(self, k):
        return 2 if k % 2 == 0 else 1

    def second(self, k):
        to = self.to_y if k % 2 == 0 else self.to_x
        return self.remote(self.piece(k, self.far(k)), self.second_in.at[k], 3, k, to)

    def begin(self):
        for k in (3, 2, 1, 0):
            self.swap(k).start()

    def stage_one(self):
        for k in (3, 2, 1, 0):
            self.swap(k).wait_recv()

            @pl.loop(0, 4)
            def _(j):
                start = pl.multiple_of(j * self.share, self.share)
                mine = self.rows(k, self.core, start, self.share)
                mine[...] = (
                    mine[...].astype(F32) + self.theirs[k, pl.ds(start, self.share)].astype(F32)
                ).astype(BF16)

            self.first(k, 1).start()
            self.first(k, 0).start()

    def stage_two(self):
        for k in (3, 2, 1, 0):
            self.first(k, 1).wait_recv()
            source = self.piece(k, self.far(k))
            source[...] = (source[...].astype(F32) + self.first_in[k, 1].astype(F32)).astype(BF16)
            self.second(k).start()

    def stage_three(self):
        for k in (3, 2, 1, 0):
            self.first(k, 0).wait_recv()
            self.second(k).wait_recv()
            total = self.piece(k, 0)[...].astype(F32) + self.first_in[k, 0].astype(F32)
            self.line.theirs[0, k] = (total + self.second_in[k].astype(F32)).astype(BF16)
        self.line.hand_over(0)

    def settle(self):
        for k in range(4):
            self.swap(k).wait_send()
            self.first(k, 0).wait_send()
            self.first(k, 1).wait_send()
            self.second(k).wait_send()


class EverySum:
    @staticmethod
    def scratch(shape):
        return [
            pltpu.VMEM((6,) + shape, F32),
            pltpu.VMEM((5,) + shape, F32),
            DMA((5,)),
            DMA((5,)),
        ]

    def __init__(self, scratch):
        self.sums, self.landed, self.send, self.recv = scratch
        d, e, z, c = here()
        near = [(2 * flipped(z, k) + c, e) for k in (1, 2)]
        self.to = [(2 * z + 1 - c, e), (d, flipped(e, 1)), (d, flipped(e, 2))] + near

    def copy(self, at):
        return pltpu.make_async_remote_copy(
            src_ref=self.sums.at[at],
            dst_ref=self.landed.at[at],
            send_sem=self.send.at[at],
            recv_sem=self.recv.at[at],
            device_id=self.to[at],
            device_id_type=MESH,
        )

    def start(self, value):
        self.sums[0] = value
        self.copy(0).start()

    def step(self, at):
        self.copy(at).wait_recv()
        self.sums[at + 1] = self.sums[at] + self.landed[at]
        if at + 1 < len(self.to):
            self.copy(at + 1).start()

    def settle(self):
        for at in range(len(self.to)):
            self.copy(at).wait_send()


def down_source(array, z, share):
    def source(i, k, core):
        row = pl.multiple_of((2 * flipped(z, k) + core) * share, share)
        return array.at[pl.ds(row, share), pl.ds(pl.multiple_of(i * CHUNK, CHUNK), CHUNK)]

    return source


def backward_kernel(experts, *refs):
    refs = list(refs)

    def take(count):
        taken, refs[:] = refs[:count], refs[count:]
        return taken

    ins = take(17)
    mixed, grad_down = take(2)
    output, grad_tokens, qkv_sum, out_sum, small_sum, down_sum = take(6)
    grad_small, grad_out, *grad_halves = take(4)
    work = take(6)
    (half_sums,) = take(1)
    brought, (own_mixed, fetched) = take(len(FETCHED)), take(2)
    cut = brought[FETCHED.index(2)].shape[1]
    ins[2], ins[3] = ins[2].at[:, :cut], ins[3].at[:, cut:]
    fetches = {}
    for i, (at, ref) in enumerate(zip(FETCHED, brought)):
        fetches[at] = pltpu.make_async_copy(ins[at], ref, fetched.at[i])
        fetches[at].start()
        ins[at] = ref
    fetches["mixed"] = pltpu.make_async_copy(mixed.at[0], own_mixed, fetched.at[len(FETCHED)])
    fetches["mixed"].start()

    def bring(names):
        for name in names:
            fetches.pop(name).wait()

    mixed_full, mixed_send, mixed_recv = take(3)
    d, e, z, _ = here()
    width = out_sum.shape[1]
    down = LineSum(width // CHUNK, down_source(grad_down, z, down_sum.shape[0]), take(6), True)
    out = DeviceSum(grad_out, take(9))
    halves = [DeviceSum(grad_half, take(9)) for grad_half in grad_halves]
    every = EverySum(take(4))
    swap = Swap(mixed, mixed_full, mixed_send, mixed_recv, d, e)
    meet(group(d, e)[1:] + [down.other] + down.to[1:])
    for block in (3, 1, 2):
        swap.start(block)
    for i in range(down.count):
        down.begin(i)
    down.halve(0)

    def reached(name):
        if name == "branch":
            bring(tuple(fetches))
            down.halve(1)
        elif name == "out":
            out.begin()
        elif name == "attended":
            down.halve(2)
        elif name == "part0":
            out.stage_one()
            down.relay(0)
        elif name == "part1":
            out.stage_two()
        elif name == "half0":
            halves[0].begin()
            down.pass_on(0)
            down.relay(1)
        elif name == "part2":
            halves[0].stage_one()
            out.stage_three()
            down.halve(3)
        elif name == "part3":
            halves[0].stage_two()
            down.pass_on(1)
        elif name == "half1":
            halves[1].begin()
            down.relay(2)
        elif name == "tokens":
            every.start(grad_small[...])
            halves[1].stage_one()

    outs = [grad_tokens, grad_small, grad_out] + grad_halves
    bring((16, 10, 15, 1))
    backward_layer(experts, True, ins, outs, work, reached)
    halves[0].stage_three()
    every.step(0)
    halves[1].stage_two()
    out.line.relay(0)
    every.step(1)
    down.pass_on(2)
    down.relay(3)
    out.line.pass_on(0)
    halves[1].stage_three()
    every.step(2)
    halves[0].line.relay(0)
    down.pass_on(3)
    every.step(3)
    halves[0].line.pass_on(0)
    halves[1].line.relay(0)
    every.step(4)
    small_sum[...] = every.sums[5]
    for i in range(down.count):
        down.finish(i, down_sum.at[:, i * CHUNK : (i + 1) * CHUNK])
    halves[1].line.pass_on(0)
    swap.finish()
    add_mixed(output, ins[15], ins[7], [own_mixed] + [mixed_full.at[q] for q in (1, 2, 3)])
    out.line.finish(0, out_sum)
    wide = width // 2
    for half, sums in enumerate(halves):
        sums.line.finish(0, half_sums.at[half])
        for i in range(3):
            at = i * width + half * wide
            qkv_sum[:, at : at + wide] = half_sums[half, :, i * wide : (i + 1) * wide]
    for sums in [out] + halves:
        sums.settle()
    every.settle()


FETCHED = (16, 10, 15, 1, 13, 3, 0, 12, 14, 2, 6)


def fetched_shape(args, at):
    width = args[0].shape[1]
    if at in (2, 3):
        return (width, args[2].shape[1] - width if at == 2 else width)
    return args[at].shape


def backward(experts, *args):
    tokens, small, mixed, grad_down = args[0], args[4], args[17], args[18]
    slots, width = tokens.shape
    share, down_share = width // 32, grad_down.shape[0] // 8
    half = 3 * width // 2
    scratch = [
        pltpu.VMEM(small.shape, F32),
        pltpu.VMEM((width, width), BF16),
        pltpu.VMEM((width, half), BF16),
        pltpu.VMEM((width, half), BF16),
        *backward_scratch(slots, width),
        pltpu.VMEM((2, share, half), F32),
        *[pltpu.VMEM(fetched_shape(args, i), args[i].dtype) for i in FETCHED],
        pltpu.VMEM(mixed.shape[1:], BF16),
        DMA((len(FETCHED) + 1,)),
        pltpu.VMEM(mixed.shape, BF16),
        DMA((4,)),
        DMA((4,)),
        *LineSum.scratch(width // CHUNK, down_share, CHUNK, True),
        *DeviceSum.scratch(share, width),
        *DeviceSum.scratch(share, half),
        *DeviceSum.scratch(share, half),
        *EverySum.scratch(small.shape),
    ]
    return call(
        functools.partial(backward_kernel, experts),
        (
            jax.ShapeDtypeStruct((slots, width), BF16),
            jax.ShapeDtypeStruct((slots, width), F32),
            jax.ShapeDtypeStruct((share, 3 * width), F32),
            jax.ShapeDtypeStruct((share, width), F32),
            jax.ShapeDtypeStruct(small.shape, F32),
            jax.ShapeDtypeStruct((down_share, width), F32),
        ),
        scratch,
        63 * MB,
        4 * slots * width * (4 * width + 2 * slots),
        *args,
        stay=(17, 18) + FETCHED,
        link=3,
    )


def publish_kernel(experts, small, *refs):
    count = (len(refs) - 12) // 3
    refs = list(refs)
    ins, smalls, outs = refs[:count], refs[count : count + 4], refs[count + 4 : 2 * count + 4]
    held, small_in = refs[2 * count + 4 : 3 * count + 4], refs[3 * count + 4]
    parts, (loaded, stored, moved) = refs[3 * count + 5 : 3 * count + 9], refs[3 * count + 9 :]
    fetch = pltpu.make_async_copy(small, small_in, moved.at[4])
    loads = [pltpu.make_async_copy(ins[i], held[i], loaded.at[i]) for i in range(count)]
    stores = [pltpu.make_async_copy(held[i], outs[i], stored.at[i]) for i in range(count)]
    stores += [pltpu.make_async_copy(parts[i], smalls[i], moved.at[i]) for i in range(4)]
    fetch.start()
    for copy in loads:
        copy.start()
    router, first, second, bias = parts
    width, share = small_in.shape[1], first.shape[1]
    device = lax.axis_index("dp") * experts + lax.axis_index("expert")
    fetch.wait()
    turned = pltpu.roll(small_in[...], lax.rem(width - device * share, width), 1)
    router[...] = turned[:experts, :share]
    first[...] = turned[experts : experts + 1, :share]
    second[...] = turned[experts + 1 : experts + 2, :share]
    bias[...] = turned[experts + 2 : experts + 3, : bias.shape[1]]
    for copy in stores[count:]:
        copy.start()
    for load, store in zip(loads, stores):
        load.wait()
        store.start()
    for copy in stores:
        copy.wait()


def publish(experts, small, bias_share, *values):
    count = len(values)
    share = small.shape[1] // 32
    shapes = ((experts, share), (1, share), (1, share), (1, bias_share))
    return call(
        functools.partial(publish_kernel, experts),
        tuple(jax.ShapeDtypeStruct(shape, F32) for shape in shapes)
        + tuple(jax.ShapeDtypeStruct(value.shape, value.dtype) for value in values),
        [pltpu.VMEM(value.shape, value.dtype) for value in values]
        + [pltpu.VMEM(small.shape, F32)]
        + [pltpu.VMEM(shape, F32) for shape in shapes]
        + [DMA((count,)), DMA((count,)), DMA((5,))],
        60 * MB,
        0,
        small,
        *values,
        stay=tuple(range(count + 1)),
        land=tuple(range(count + 4)),
    )


READY = 2


def on_device(
    fast,
    tokens,
    cotangent,
    qkv_weight,
    out_weight,
    router_weight,
    first_gain,
    second_gain,
    bias_table,
    gate_weight,
    up_weight,
    down_weight,
    lengths,
    routes,
    priority,
):
    both = ("dp", "expert")
    slots, width = tokens.shape
    expert_count = lax.axis_size("expert")
    device_count = lax.axis_size("dp") * expert_count
    share, bias_share = first_gain.shape[0], bias_table.shape[0]
    device = lax.axis_index("dp") * expert_count + lax.axis_index("expert")
    own = lax.axis_index("expert").astype(jnp.int32).reshape(1, 1)
    small_rows = -(-(expert_count + 3) // 8) * 8

    def gathered(value, axes, axis=0, tiled=True):
        return lax.all_gather(value, axes, axis=axis, tiled=tiled)

    def scattered(value, axes):
        return lax.psum_scatter(value, axes, scatter_dimension=0, tiled=True).astype(F32)

    def exchanged(value):
        return lax.all_to_all(value, "expert", split_axis=0, concat_axis=0, tiled=True)

    rows_own, hidden = gate_weight.shape[1:]
    if not fast:
        gate_full, up_full, down_full = (
            gathered(value[0], "dp") for value in (gate_weight, up_weight, down_weight)
        )

    lane = np.arange(width)
    flat = lane // share * bias_share + lane % share
    in_table = lane % share < bias_share
    heads = np.arange(HEADS)[:, None] == np.where(in_table, flat // BUCKETS, -1)[None, :]
    heads = jnp.asarray(heads.astype(np.float32), BF16)
    ahead = np.arange(2 * slots)

    def hot(ahead):
        return jnp.asarray(
            np.where(in_table[:, None], diagonal_onehot(ahead)[flat % BUCKETS], 0.0), BF16
        )

    diagonals_hot = hot(np.where(ahead < slots, ahead, ahead - 2 * slots))
    if fast:
        *kept, buffer, scaled, plain, select, gate_column, meta_own, weights, early, down_full = forward(
            READY,
            expert_count,
            tokens,
            heads,
            diagonals_hot,
            lengths,
            cotangent,
            routes.T,
            priority,
            router_weight.T,
            first_gain[None],
            second_gain[None],
            bias_table[None],
            qkv_weight,
            out_weight,
            gate_weight[0],
            up_weight[0],
            down_weight[0],
        )
        out_full = weights
    else:
        beside = jnp.concatenate(
            [
                router_weight,
                first_gain[:, None],
                second_gain[:, None],
                jnp.pad(bias_table, (0, share - bias_share))[:, None],
                jnp.zeros((share, 128 - expert_count - 3), BF16),
            ],
            axis=1,
        )
        valid_rows = jnp.arange(slots, dtype=jnp.int32) < lengths[0, 0]
        meta_own = jnp.concatenate(
            [
                routes.T,
                priority,
                valid_rows.astype(jnp.int32)[None, :],
                jnp.zeros((4, slots), jnp.int32),
            ],
            axis=0,
        )
        weights = gathered(jnp.concatenate([qkv_weight, beside], axis=1), both)
        out_full = gathered(out_weight, both)
        kept = attention_forward(
            expert_count, tokens, weights, out_full, heads, diagonals_hot, lengths
        )
        rows, cots, meta = (
            gathered(value, "expert", tiled=False) for value in (kept[4], cotangent, meta_own)
        )
        buffer, scaled, plain, select, gate_column = dispatch(rows, cots, meta, kept[5], own)
    qkv, attended, probs, resid, normed_two, small = kept
    if fast:
        grad_gate, grad_up, grad_down, mixed, returned, inner_rows = sweep(
            READY,
            buffer,
            scaled,
            plain,
            gate_column,
            select,
            gate_weight[0],
            up_weight[0],
            early,
            down_full,
        )
    else:
        expert_out, grad_buffer, inner, *grad_experts = experts(
            buffer, scaled, plain, gate_full, up_full, down_full
        )
        mixed, returned, inner_rows = (
            exchanged(value)
            for value in give_back(select, expert_out, grad_buffer, inner, gate_column)
        )
        grad_gate, grad_up, grad_down = (scattered(value, "dp")[None] for value in grad_experts)
    layer = (
        tokens,
        cotangent,
        weights,
        out_full,
        small,
        heads,
        hot(ahead - (slots - 1)),
        lengths,
        meta_own,
        own,
        returned,
        inner_rows,
        qkv,
        attended,
        probs,
        resid,
        normed_two,
        mixed,
    )
    if fast:
        output, grad_tokens, grad_qkv, grad_out, grad_small, grad_down = backward(
            expert_count, *layer, grad_down
        )
        grad_router, grad_first, grad_second, grad_bias, *large = publish(
            expert_count,
            grad_small,
            bias_share,
            output,
            grad_tokens,
            grad_qkv,
            grad_out,
            grad_gate,
            grad_up,
            grad_down,
        )
        output, grad_tokens, grad_qkv, grad_out, grad_gate, grad_up, grad_down = large
        grad_gate, grad_up, grad_down = grad_gate[None], grad_up[None], grad_down[None]
    else:
        output, grad_tokens, grad_small, *grad_weights = local_backward(expert_count, *layer)
        grad_out, *halves = (scattered(value, both) for value in grad_weights)
        grad_qkv = jnp.stack([half.reshape(share, 3, width // 2) for half in halves], axis=2)
        grad_qkv = grad_qkv.reshape(share, 3 * width)
        grad_small = lax.psum(grad_small, both)
        grad_small = lax.dynamic_slice(grad_small, (0, device * share), (small_rows, share))
        grad_router, grad_first, grad_second, grad_bias = (
            grad_small[:expert_count],
            grad_small[expert_count : expert_count + 1],
            grad_small[expert_count + 1 : expert_count + 2],
            grad_small[expert_count + 2 : expert_count + 3, :bias_share],
        )
    return (
        output,
        grad_tokens,
        grad_qkv,
        grad_out,
        grad_router.T,
        grad_first[0],
        grad_second[0],
        grad_bias[0],
        grad_gate,
        grad_up,
        grad_down,
    )


def solution(mesh):
    fast = dict(mesh.shape) == {"dp": 8, "expert": 4}
    rows = P(("dp", "expert"), None)
    flat = P(("dp", "expert"))
    expert = P("expert", "dp", None)
    grid = P("dp", "expert")
    return jax.shard_map(
        functools.partial(on_device, fast),
        mesh=mesh,
        in_specs=(rows,) * 5 + (flat,) * 3 + (expert,) * 3 + (grid, rows, grid),
        out_specs=(rows,) * 5 + (flat,) * 3 + (expert,) * 3,
        check_vma=False,
    )
```
